32 devices in a mesh: dp: 8 (over y, x, core), hor: 4 (over z).
Axes of the slice: x: 2, y: 2, z: 4, core: 2. Of those that a mesh axis runs over, the one named last changes fastest.
Arguments:
- trajectories: float32 [32, 3584, 23], P('dp', 'hor'), may hold values from -12 to 12
- dim_means: float32 [23], replicated, may hold values from -1 to 1
- dim_stds: float32 [23], replicated, may hold values from 0.5 to 3
- noise_draw: float32 [32, 3584, 23], P('dp', 'hor'), may hold values from -6 to 6
- diffusion_steps: int32 [32], P('dp'), may hold values from 0 to 99
- valid_mask: int32 [32, 3584], P('dp', 'hor'), may hold values from 0 to 1, as said below
- kernels: float32 [2136128], replicated, as said below
- affine: float32 [7511], replicated, as said below
- kernel_momentum: float32 [2136128], P('dp'), may hold values from -8.879071e-05 to 8.879071e-05
- kernel_average: float32 [2136128], P('dp'), as said below
- affine_momentum: float32 [7511], replicated, may hold values from -0.00040980327 to 0.00040980327
- affine_average: float32 [7511], replicated, as said below
Outputs:
- noise_loss: float32 [], replicated
- grad_norm: float32 [], replicated
- kernel_new: float32 [2136128], P('dp')
- kernel_mom_new: float32 [2136128], P('dp')
- kernel_ema_new: float32 [2136128], P('dp')
- kernel_low: bfloat16 [2136128], P('dp')
- affine_new: float32 [7511], replicated
- affine_mom_new: float32 [7511], replicated
- affine_ema_new: float32 [7511], replicated
- affine_low: bfloat16 [7511], replicated
The draws below stay inside these ranges and needn't reach their ends.
Inputs may be any that keep to these rules, and one draw needn't show every extreme that they name: `valid_mask`: within each horizon the ones form a prefix that holds the horizon's first frame. `kernels`: each matrix's entries have a standard deviation of one over the root of its number of rows. `affine`: gains lie near 1, the other entries near 0. `kernel_average`: entries as those of kernels. `affine_average`: entries as those of affine.
All inputs are finite; a program needn't handle non-finite values.
Results may differ from the reference program's by a relative error of at most 0.0033.
The reference program's roundings to bfloat16 on the way count: a program that leaves them out, or rounds other values in their place, can miss the bound.
Values may be sent and summed in bfloat16 or wider, within the bound.
No kernel may reach another device: no remote copies, remote signals or barrier semaphores. Data moves between devices by JAX's collectives and lax.ppermute only.
A program may use at most 256 MiB of HBM per device.

```python
import math
import jax
import jax.numpy as jnp
from jax import lax

TD = 23
C1 = 64
C2 = 128
C3 = 256
TE = 128
TH = 256
KSIZE = 5
GROUPS = 8
NSTEPS = 100
SEG = 3584
HORIZONS = 32
NKER = 2136128
NAFF = 7511


def layout_shapes_drawn():
    kernel_shapes = []
    affine_shapes = []
    for width_in, width_out in [(TD, C1), (C1, C2), (C2, C3), (C3, C3), (C3 + C3, C2), (C2 + C2, C1)]:
        matrices = [('conv_one', KSIZE * width_in, width_out), ('conv_two', KSIZE * width_out, width_out), ('time_proj', TE, width_out)]
        vectors = [(entry_name, width_out) for entry_name in ['bias_one', 'gain_one', 'shift_one', 'time_bias', 'bias_two', 'gain_two', 'shift_two']]
        if width_in != width_out:
            matrices.append(('res_proj', width_in, width_out))
            vectors.append(('res_bias', width_out))
        kernel_shapes.append(matrices)
        affine_shapes.append(vectors)
    kernel_shapes.append([('head_conv', KSIZE * C1, C1), ('head_out', C1, TD), ('embed_one', TE, TH), ('embed_two', TH, TE)])
    affine_shapes.append([('head_bias', C1), ('head_gain', C1), ('head_shift', C1), ('out_bias', TD), ('embed_bias_one', TH), ('embed_bias_two', TE)])
    return (kernel_shapes, affine_shapes)


def kernel_fill(key):
    kernel_shapes, _ = layout_shapes_drawn()
    pieces = []
    number = 0
    for entries in kernel_shapes:
        for entry_name, height, breadth in entries:
            sample = jax.random.normal(jax.random.fold_in(key, number), (height * breadth,), jnp.float32)
            pieces.append(sample * float(height) ** (-0.5))
            number += 1
    return jnp.concatenate(pieces)


def affine_fill(key):
    _, affine_shapes = layout_shapes_drawn()
    pieces = []
    number = 0
    for entries in affine_shapes:
        for entry_name, length in entries:
            sample = jax.random.normal(jax.random.fold_in(key, number), (length,), jnp.float32)
            if 'gain' in entry_name:
                pieces.append(1.0 + 0.15 * sample)
            else:
                pieces.append(0.3 * sample)
            number += 1
    return jnp.concatenate(pieces)


def draw_kernels(key, part):
    return kernel_fill(jax.random.fold_in(key, 11))


def draw_kernel_average(key, part):
    return kernel_fill(jax.random.fold_in(key, 12))


def draw_affine(key, part):
    return affine_fill(jax.random.fold_in(key, 13))


def draw_affine_average(key, part):
    return affine_fill(jax.random.fold_in(key, 14))


def draw_valid_mask(key, part):
    lengths = jax.random.randint(jax.random.fold_in(key, 15), (HORIZONS,), SEG // 4, SEG + 1)
    frame_ids = jnp.arange(SEG, dtype=jnp.int32)
    return (frame_ids[None, :] < lengths[:, None]).astype(jnp.int32)


def place_ends(values, stream_key, least, high):
    longest = values.shape.index(max(values.shape))
    spots = []
    for shift in (0, 1):
        where = [jax.random.randint(jax.random.fold_in(stream_key, axis), (), 0, length) for axis, length in enumerate(values.shape)]
        where[longest] = (where[longest] + shift) % values.shape[longest]
        spots.append(tuple(where))
    return values.at[spots[0]].set(least).at[spots[1]].set(high)


def block_levels(rng, dims, split, least, high):
    level = 1.0
    for axis_at, parts in split:
        heights = jax.random.uniform(jax.random.fold_in(jax.random.fold_in(rng, 6), axis_at), (parts,), jnp.float32, least / len(split), high / len(split))
        level = level * jnp.repeat(jnp.exp(heights), dims[axis_at] // parts).reshape((-1,) + (1,) * (len(dims) - 1 - axis_at))
    return level


def scatter_about(stream_key, shape, spread, most, split=(), held_as=jnp.bfloat16):
    values = spread * jax.random.normal(stream_key, shape, jnp.float32)
    if split:
        values = values * block_levels(stream_key, shape, split, -0.22, 0.18)
    return jnp.clip(values, -most, most).astype(held_as)


def setup_inputs(seed: int = 0) -> dict:
    seeds = jax.random.split(jax.random.key(seed), 13)
    trajectories = scatter_about(seeds[0], (HORIZONS, SEG, TD), 2.0, 12.0, ((0, 8), (1, 4)), jnp.float32)
    dim_means = jnp.clip(jax.random.uniform(seeds[1], (TD,), jnp.float32, -1.0, 1.0), -1.0, 1.0)
    dim_stds = jnp.clip(jnp.exp(jax.random.uniform(seeds[2], (TD,), jnp.float32, math.log(0.5), math.log(3.0))), 0.5, 3.0)
    noise_draw = scatter_about(seeds[3], (HORIZONS, SEG, TD), 1.0, 6.0, ((0, 8), (1, 4)), jnp.float32)
    diffusion_steps = place_ends(jax.random.randint(seeds[4], (HORIZONS,), 0, NSTEPS), jax.random.fold_in(seeds[4], 1), 0, NSTEPS - 1).astype(jnp.int32)
    valid_mask = draw_valid_mask(jax.random.fold_in(seeds[12], 71), 0)
    kernels = draw_kernels(jax.random.fold_in(seeds[12], 71), 0)
    affine = draw_affine(jax.random.fold_in(seeds[12], 71), 0)
    kernel_momentum = scatter_about(seeds[8], (NKER,), (0.022 / (NKER + NAFF) ** 0.5), 8.879070810507983e-05, ((0, 8),), jnp.float32)
    kernel_average = draw_kernel_average(jax.random.fold_in(seeds[12], 71), 0)
    affine_momentum = scatter_about(seeds[10], (NAFF,), (0.1 / (NKER + NAFF) ** 0.5), 0.00040980327, (), jnp.float32)
    affine_average = draw_affine_average(jax.random.fold_in(seeds[12], 71), 0)
    return dict(trajectories=trajectories, dim_means=dim_means, dim_stds=dim_stds, noise_draw=noise_draw, diffusion_steps=diffusion_steps, valid_mask=valid_mask, kernels=kernels, affine=affine, kernel_momentum=kernel_momentum, kernel_average=kernel_average, affine_momentum=affine_momentum, affine_average=affine_average)


PRECISE = lax.Precision.HIGHEST
EPSILON = 1e-05
MAX_NORM = 0.02
LEARN_RATE = 200.0
AFFINE_RATE = 1500.0
MOMENTUM = 0.9
EMA_DECAY = 0.5

@jax.custom_vjp
def low(v):
    return lax.optimization_barrier(v.astype(jnp.bfloat16)).astype(jnp.float32)

@jax.custom_vjp
def low_back(v):
    return v

def low_keep(v):
    return (low(v), None)

def low_pass(kept, grad):
    return (grad,)

def back_keep(v):
    return (v, None)

def back_low(kept, grad):
    return (low(grad),)
low.defvjp(low_keep, low_pass)
low_back.defvjp(back_keep, back_low)

def layout_shapes():
    kernel_shapes = []
    affine_shapes = []
    for width_in, width_out in [(TD, C1), (C1, C2), (C2, C3), (C3, C3), (C3 + C3, C2), (C2 + C2, C1)]:
        matrices = [('conv_one', KSIZE * width_in, width_out), ('conv_two', KSIZE * width_out, width_out), ('time_proj', TE, width_out)]
        vectors = [(entry_name, width_out) for entry_name in ['bias_one', 'gain_one', 'shift_one', 'time_bias', 'bias_two', 'gain_two', 'shift_two']]
        if width_in != width_out:
            matrices.append(('res_proj', width_in, width_out))
            vectors.append(('res_bias', width_out))
        kernel_shapes.append(matrices)
        affine_shapes.append(vectors)
    kernel_shapes.append([('head_conv', KSIZE * C1, C1), ('head_out', C1, TD), ('embed_one', TE, TH), ('embed_two', TH, TE)])
    affine_shapes.append([('head_bias', C1), ('head_gain', C1), ('head_shift', C1), ('out_bias', TD), ('embed_bias_one', TH), ('embed_bias_two', TE)])
    return (kernel_shapes, affine_shapes)

def unpack(kernels, affine):
    kernel_shapes, affine_shapes = layout_shapes()
    members_all = []
    cursor = 0
    for entries in kernel_shapes:
        members = {}
        for entry_name, height, breadth in entries:
            members[entry_name] = kernels[cursor:cursor + height * breadth].reshape(height, breadth)
            cursor += height * breadth
        members_all.append(members)
    cursor = 0
    for position, entries in enumerate(affine_shapes):
        for entry_name, length in entries:
            members_all[position][entry_name] = affine[cursor:cursor + length]
            cursor += length
    return members_all

def mish_act(value):
    return value * jnp.tanh(jax.nn.softplus(value))

def sinusoid(steps_vec):
    half_width = TE // 2
    ladder = jnp.exp(-math.log(10000.0) * jnp.arange(half_width).astype(jnp.float32) / (half_width - 1))
    angles = steps_vec.astype(jnp.float32)[:, None] * ladder[None, :]
    return jnp.concatenate([jnp.sin(angles), jnp.cos(angles)], axis=1)

def signal_level(steps_vec):
    ratio = (steps_vec.astype(jnp.float32) + 1.0) / NSTEPS
    cosine_now = jnp.cos((ratio + 0.008) / 1.008 * math.pi / 2)
    cosine_zero = math.cos(0.008 / 1.008 * math.pi / 2)
    return (cosine_now / cosine_zero) ** 2

def time_parts(members_all, steps_vec):
    last_group = members_all[6]
    hidden = mish_act(jnp.dot(sinusoid(steps_vec), last_group['embed_one'], precision=PRECISE) + last_group['embed_bias_one'])
    feature = mish_act(jnp.dot(hidden, last_group['embed_two'], precision=PRECISE) + last_group['embed_bias_two'])
    return [jnp.dot(feature, members_all[block_index]['time_proj'], precision=PRECISE) + members_all[block_index]['time_bias'] for block_index in range(6)]

def conv_apply(values_low, weight):
    frames = values_low.shape[1]
    channels = values_low.shape[2]
    padded = jnp.pad(values_low, ((0, 0), (2, 2), (0, 0)))
    weight_low = low(weight)
    running = jnp.zeros((values_low.shape[0], frames, weight.shape[1]), jnp.float32)
    for offset in range(KSIZE):
        running = running + jnp.einsum('blc,cd->bld', padded[:, offset:offset + frames], weight_low[offset * channels:(offset + 1) * channels], precision=PRECISE)
    return low_back(running)

def group_norm(values, gain_vec, shift_vec):
    horizons, frames, channels = values.shape
    grouped = values.reshape(horizons, frames, GROUPS, channels // GROUPS)
    average = lax.optimization_barrier(jnp.mean(grouped, axis=(1, 3), keepdims=True))
    variance = lax.optimization_barrier(jnp.mean(grouped * grouped, axis=(1, 3), keepdims=True)) - average * average
    normed = (grouped - average) * lax.rsqrt(variance + EPSILON)
    return normed.reshape(horizons, frames, channels) * gain_vec + shift_vec

def block_apply(inputs, members, time_term):
    inputs_low = low(inputs)
    pre_one = conv_apply(inputs_low, members['conv_one']) + members['bias_one']
    hidden = mish_act(group_norm(pre_one, members['gain_one'], members['shift_one'])) + time_term[:, None, :]
    pre_two = conv_apply(low(hidden), members['conv_two']) + members['bias_two']
    result = mish_act(group_norm(pre_two, members['gain_two'], members['shift_two']))
    if 'res_proj' in members:
        side = low_back(jnp.einsum('blc,cd->bld', inputs_low, low(members['res_proj']), precision=PRECISE)) + members['res_bias']
    else:
        side = inputs
    return result + side

def network(members_all, noisy_frames, steps_vec):
    time_list = time_parts(members_all, steps_vec)
    down_one = block_apply(noisy_frames, members_all[0], time_list[0])
    down_two = block_apply(down_one, members_all[1], time_list[1])
    down_three = block_apply(down_two, members_all[2], time_list[2])
    middle = block_apply(down_three, members_all[3], time_list[3])
    up_one = block_apply(jnp.concatenate([middle, down_three], axis=2), members_all[4], time_list[4])
    up_two = block_apply(jnp.concatenate([up_one, down_two], axis=2), members_all[5], time_list[5])
    head = members_all[6]
    pre_head = conv_apply(low(up_two), head['head_conv']) + head['head_bias']
    feature_low = low(mish_act(group_norm(pre_head, head['head_gain'], head['head_shift'])))
    return low_back(jnp.einsum('blc,cd->bld', feature_low, low(head['head_out']), precision=PRECISE)) + head['out_bias']

def reference(trajectories, dim_means, dim_stds, noise_draw, diffusion_steps, valid_mask, kernels, affine, kernel_momentum, kernel_average, affine_momentum, affine_average):
    valid_total = jnp.sum(valid_mask.astype(jnp.float32))

    def group_loss(kernel_flat, affine_flat, trajectory_group, noise_group, step_group, mask_group):
        members_all = unpack(kernel_flat, affine_flat)
        signal_now = signal_level(step_group)[:, None, None]
        clean_frames = (trajectory_group - dim_means) / dim_stds
        noisy_frames = jnp.sqrt(signal_now) * clean_frames + jnp.sqrt(1.0 - signal_now) * noise_group
        predicted = network(members_all, noisy_frames, step_group)
        difference = predicted - noise_group
        return jnp.sum(mask_group.astype(jnp.float32)[:, :, None] * difference * difference) / (valid_total * TD)

    def scan_step(carried, group_data):
        loss_sum, kernel_acc, affine_acc = carried
        trajectory_group, noise_group, step_group, mask_group = group_data

        def closed_loss(kernel_flat, affine_flat):
            return group_loss(kernel_flat, affine_flat, trajectory_group, noise_group, step_group, mask_group)
        outcome, pullback = jax.vjp(closed_loss, kernels, affine)
        kernel_grad, affine_grad = pullback(jnp.ones_like(outcome))
        return ((loss_sum + outcome, kernel_acc + kernel_grad, affine_acc + affine_grad), None)
    group_data = (trajectories.reshape(-1, 1, SEG, TD), noise_draw.reshape(-1, 1, SEG, TD), diffusion_steps.reshape(-1, 1), valid_mask.reshape(-1, 1, SEG))
    start = (jnp.zeros((), jnp.float32), jnp.zeros_like(kernels), jnp.zeros_like(affine))
    (noise_loss, kernel_grad, affine_grad), _ = lax.scan(scan_step, start, group_data)
    grad_norm = jnp.sqrt(jnp.sum(kernel_grad * kernel_grad) + jnp.sum(affine_grad * affine_grad))
    factor = jnp.minimum(1.0, MAX_NORM / (grad_norm + 1e-06))
    kernel_step = kernel_grad * factor
    kernel_mom_new = MOMENTUM * kernel_momentum + kernel_step
    kernel_new = kernels - LEARN_RATE * (kernel_step + MOMENTUM * kernel_mom_new)
    kernel_ema_new = EMA_DECAY * kernel_average + (1.0 - EMA_DECAY) * kernel_new
    affine_step = affine_grad * factor
    affine_mom_new = MOMENTUM * affine_momentum + affine_step
    affine_new = affine - AFFINE_RATE * (affine_step + MOMENTUM * affine_mom_new)
    affine_ema_new = EMA_DECAY * affine_average + (1.0 - EMA_DECAY) * affine_new
    return (noise_loss, grad_norm, kernel_new, kernel_mom_new, kernel_ema_new, kernel_new.astype(jnp.bfloat16), affine_new, affine_mom_new, affine_ema_new, affine_new.astype(jnp.bfloat16))
```

```python
import math

import jax
import jax.numpy as jnp
from jax import lax
from jax.sharding import PartitionSpec as P

TD = 23
C1 = 64
C2 = 128
C3 = 256
TE = 128
TH = 256
KSIZE = 5
GROUPS = 8
NSTEPS = 100


PRECISE = lax.Precision.HIGHEST
EPSILON = 1e-05
MAX_NORM = 0.02
LEARN_RATE = 200.0
AFFINE_RATE = 1500.0
MOMENTUM = 0.9
EMA_DECAY = 0.5


def padded_2(cells, sides, width):
    for axis, dim in sides:
        if axis is None:
            pads = [(0, 0)] * cells.ndim
            pads[dim] = (width, width)
            cells = jnp.pad(cells, pads)
            continue
        count = lax.axis_size(axis)
        ends = count - 1
        head = lax.slice_in_dim(cells, 0, width, axis=dim)
        tail = lax.slice_in_dim(cells, cells.shape[dim] - width, cells.shape[dim], axis=dim)
        cells = jnp.concatenate(
            [
                lax.ppermute(tail, axis, [(i, (i + 1) % count) for i in range(ends)]),
                cells,
                lax.ppermute(head, axis, [((i + 1) % count, i) for i in range(ends)]),
            ],
            axis=dim,
        )
    return cells


def sum_over(values, axis):
    return values if axis is None else lax.psum(values, axis)


def axis_length(axis):
    return 1 if axis is None else lax.axis_size(axis)


def layout_shapes():
    kernel_shapes = []
    affine_shapes = []
    for width_in, width_out in [
        (TD, C1),
        (C1, C2),
        (C2, C3),
        (C3, C3),
        (C3 + C3, C2),
        (C2 + C2, C1),
    ]:
        matrices = [
            ("conv_one", KSIZE * width_in, width_out),
            ("conv_two", KSIZE * width_out, width_out),
            ("time_proj", TE, width_out),
        ]
        vectors = [
            (entry_name, width_out)
            for entry_name in [
                "bias_one",
                "gain_one",
                "shift_one",
                "time_bias",
                "bias_two",
                "gain_two",
                "shift_two",
            ]
        ]
        if width_in != width_out:
            matrices.append(("res_proj", width_in, width_out))
            vectors.append(("res_bias", width_out))
        kernel_shapes.append(matrices)
        affine_shapes.append(vectors)
    kernel_shapes.append(
        [
            ("head_conv", KSIZE * C1, C1),
            ("head_out", C1, TD),
            ("embed_one", TE, TH),
            ("embed_two", TH, TE),
        ]
    )
    affine_shapes.append(
        [
            ("head_bias", C1),
            ("head_gain", C1),
            ("head_shift", C1),
            ("out_bias", TD),
            ("embed_bias_one", TH),
            ("embed_bias_two", TE),
        ]
    )
    return (kernel_shapes, affine_shapes)


def unpack(kernels, affine):
    kernel_shapes, affine_shapes = layout_shapes()
    members_all = []
    cursor = 0
    for entries in kernel_shapes:
        members = {}
        for entry_name, height, breadth in entries:
            members[entry_name] = kernels[cursor : cursor + height * breadth].reshape(
                height, breadth
            )
            cursor += height * breadth
        members_all.append(members)
    cursor = 0
    for position, entries in enumerate(affine_shapes):
        for entry_name, length in entries:
            members_all[position][entry_name] = affine[cursor : cursor + length]
            cursor += length
    return members_all


def pack_flat(grad_list):
    kernel_shapes, affine_shapes = layout_shapes()
    kernel_pieces = []
    affine_pieces = []
    for position, entries in enumerate(kernel_shapes):
        for entry_name, height, breadth in entries:
            kernel_pieces.append(
                grad_list[position]
                .get(entry_name, jnp.zeros((height, breadth), jnp.float32))
                .reshape(-1)
            )
    for position, entries in enumerate(affine_shapes):
        for entry_name, length in entries:
            affine_pieces.append(
                grad_list[position].get(entry_name, jnp.zeros((length,), jnp.float32))
            )
    return (jnp.concatenate(kernel_pieces), jnp.concatenate(affine_pieces))


def mish_act(value):
    return value * jnp.tanh(jax.nn.softplus(value))


def mish_grad(value, upstream):
    return jax.vjp(mish_act, value)[1](upstream)[0]


def sinusoid(steps_vec):
    half_width = TE // 2
    ladder = jnp.exp(
        -math.log(10000.0) * jnp.arange(half_width).astype(jnp.float32) / (half_width - 1)
    )
    angles = steps_vec.astype(jnp.float32)[:, None] * ladder[None, :]
    return jnp.concatenate([jnp.sin(angles), jnp.cos(angles)], axis=1)


def signal_level(steps_vec):
    ratio = (steps_vec.astype(jnp.float32) + 1.0) / NSTEPS
    cosine_now = jnp.cos((ratio + 0.008) / 1.008 * math.pi / 2)
    cosine_zero = math.cos(0.008 / 1.008 * math.pi / 2)
    return (cosine_now / cosine_zero) ** 2


def time_parts(kernel_flat, affine_flat, steps_vec):
    members_all = unpack(kernel_flat, affine_flat)
    last_group = members_all[6]
    hidden = mish_act(
        jnp.dot(sinusoid(steps_vec), last_group["embed_one"], precision=PRECISE)
        + last_group["embed_bias_one"]
    )
    feature = mish_act(
        jnp.dot(hidden, last_group["embed_two"], precision=PRECISE) + last_group["embed_bias_two"]
    )
    return tuple(
        (
            jnp.dot(feature, members_all[block_index]["time_proj"], precision=PRECISE)
            + members_all[block_index]["time_bias"]
            for block_index in range(6)
        )
    )


def conv_forward(inputs_low, weight_low, axis):
    padded = padded_2(inputs_low, ((axis, 1),), 2)
    frames = inputs_low.shape[1]
    channels = inputs_low.shape[2]
    running = 0.0
    for offset in range(KSIZE):
        running = running + jnp.einsum(
            "blc,cd->bld",
            padded[:, offset : offset + frames],
            weight_low[offset * channels : (offset + 1) * channels],
            preferred_element_type=jnp.float32,
        )
    return (running, padded)


def conv_backward(grad_low, padded, weight_low, axis):
    grad_padded = padded_2(grad_low, ((axis, 1),), 2)
    frames = grad_low.shape[1]
    channels = padded.shape[2]
    pieces = []
    running = 0.0
    for offset in range(KSIZE):
        pieces.append(
            jnp.einsum(
                "blc,bld->cd",
                padded[:, offset : offset + frames],
                grad_low,
                preferred_element_type=jnp.float32,
            )
        )
        start_row = KSIZE - 1 - offset
        running = running + jnp.einsum(
            "bld,cd->blc",
            grad_padded[:, start_row : start_row + frames],
            weight_low[offset * channels : (offset + 1) * channels],
            preferred_element_type=jnp.float32,
        )
    return (running, jnp.concatenate(pieces, axis=0))


def group_norm(values, gain_vec, shift_vec, axis):
    horizons, frames, channels = values.shape
    grouped = values.reshape(horizons, frames, GROUPS, channels // GROUPS)
    sum_one, sum_two = sum_over(
        (jnp.sum(grouped, axis=(1, 3)), jnp.sum(grouped * grouped, axis=(1, 3))), axis
    )
    group_count = frames * axis_length(axis) * (channels // GROUPS)
    average = sum_one / group_count
    inverse = lax.rsqrt(sum_two / group_count - average * average + EPSILON)
    normed = ((grouped - average[:, None, :, None]) * inverse[:, None, :, None]).reshape(
        horizons, frames, channels
    )
    return (normed * gain_vec + shift_vec, (normed, inverse))


def group_norm_back(upstream, norm_stats, gain_vec, axis):
    normed, inverse = norm_stats
    horizons, frames, channels = normed.shape
    grad_gain = jnp.sum(upstream * normed, axis=(0, 1))
    grad_shift = jnp.sum(upstream, axis=(0, 1))
    scaled = (upstream * gain_vec).reshape(horizons, frames, GROUPS, channels // GROUPS)
    grouped = normed.reshape(horizons, frames, GROUPS, channels // GROUPS)
    sum_one, sum_two = sum_over(
        (jnp.sum(scaled, axis=(1, 3)), jnp.sum(scaled * grouped, axis=(1, 3))), axis
    )
    group_count = frames * axis_length(axis) * (channels // GROUPS)
    result = inverse[:, None, :, None] * (
        scaled
        - sum_one[:, None, :, None] / group_count
        - grouped * sum_two[:, None, :, None] / group_count
    )
    return (result.reshape(horizons, frames, channels), grad_gain, grad_shift)


def block_forward(inputs, members, time_term, axis):
    inputs_low = inputs.astype(jnp.bfloat16)
    weight_one = members["conv_one"].astype(jnp.bfloat16)
    weight_two = members["conv_two"].astype(jnp.bfloat16)
    conv_out, padded_one = conv_forward(inputs_low, weight_one, axis)
    normed_one, stats_one = group_norm(
        conv_out + members["bias_one"], members["gain_one"], members["shift_one"], axis
    )
    hidden = mish_act(normed_one) + time_term[:, None, :]
    conv_out, padded_two = conv_forward(hidden.astype(jnp.bfloat16), weight_two, axis)
    normed_two, stats_two = group_norm(
        conv_out + members["bias_two"], members["gain_two"], members["shift_two"], axis
    )
    result = mish_act(normed_two)
    if "res_proj" in members:
        weight_side = members["res_proj"].astype(jnp.bfloat16)
        result = (
            result
            + jnp.einsum("blc,cd->bld", inputs_low, weight_side, preferred_element_type=jnp.float32)
            + members["res_bias"]
        )
    else:
        weight_side = None
        result = result + inputs
    return (
        result,
        (
            padded_one,
            stats_one,
            padded_two,
            stats_two,
            inputs_low,
            weight_one,
            weight_two,
            weight_side,
        ),
    )


def block_backward(upstream, kept, members, axis):
    (
        padded_one,
        stats_one,
        padded_two,
        stats_two,
        inputs_low,
        weight_one,
        weight_two,
        weight_side,
    ) = kept
    grad_map = {}
    grad_normed = mish_grad(stats_two[0] * members["gain_two"] + members["shift_two"], upstream)
    grad_pre, grad_map["gain_two"], grad_map["shift_two"] = group_norm_back(
        grad_normed, stats_two, members["gain_two"], axis
    )
    grad_map["bias_two"] = jnp.sum(grad_pre, axis=(0, 1))
    grad_hidden, grad_map["conv_two"] = conv_backward(
        grad_pre.astype(jnp.bfloat16), padded_two, weight_two, axis
    )
    time_grad = jnp.sum(grad_hidden, axis=1)
    grad_normed = mish_grad(stats_one[0] * members["gain_one"] + members["shift_one"], grad_hidden)
    grad_pre, grad_map["gain_one"], grad_map["shift_one"] = group_norm_back(
        grad_normed, stats_one, members["gain_one"], axis
    )
    grad_map["bias_one"] = jnp.sum(grad_pre, axis=(0, 1))
    grad_inputs, grad_map["conv_one"] = conv_backward(
        grad_pre.astype(jnp.bfloat16), padded_one, weight_one, axis
    )
    if weight_side is not None:
        upstream_low = upstream.astype(jnp.bfloat16)
        grad_map["res_bias"] = jnp.sum(upstream, axis=(0, 1))
        grad_map["res_proj"] = jnp.einsum(
            "blc,bld->cd", inputs_low, upstream_low, preferred_element_type=jnp.float32
        )
        grad_inputs = grad_inputs + jnp.einsum(
            "bld,cd->blc", upstream_low, weight_side, preferred_element_type=jnp.float32
        )
    else:
        grad_inputs = grad_inputs + upstream
    return (grad_inputs, time_grad, grad_map)


def head_forward(inputs, members, axis):
    weight_conv = members["head_conv"].astype(jnp.bfloat16)
    weight_out = members["head_out"].astype(jnp.bfloat16)
    conv_out, padded = conv_forward(inputs.astype(jnp.bfloat16), weight_conv, axis)
    normed, norm_stats = group_norm(
        conv_out + members["head_bias"], members["head_gain"], members["head_shift"], axis
    )
    feature_low = mish_act(normed).astype(jnp.bfloat16)
    predicted = (
        jnp.einsum("blc,cd->bld", feature_low, weight_out, preferred_element_type=jnp.float32)
        + members["out_bias"]
    )
    return (predicted, (padded, norm_stats, feature_low, weight_conv, weight_out))


def head_backward(upstream, kept, members, axis):
    padded, norm_stats, feature_low, weight_conv, weight_out = kept
    grad_map = {}
    upstream_low = upstream.astype(jnp.bfloat16)
    grad_map["out_bias"] = jnp.sum(upstream, axis=(0, 1))
    grad_map["head_out"] = jnp.einsum(
        "blc,bld->cd", feature_low, upstream_low, preferred_element_type=jnp.float32
    )
    grad_feature = jnp.einsum(
        "bld,cd->blc", upstream_low, weight_out, preferred_element_type=jnp.float32
    )
    grad_normed = mish_grad(
        norm_stats[0] * members["head_gain"] + members["head_shift"], grad_feature
    )
    grad_pre, grad_map["head_gain"], grad_map["head_shift"] = group_norm_back(
        grad_normed, norm_stats, members["head_gain"], axis
    )
    grad_map["head_bias"] = jnp.sum(grad_pre, axis=(0, 1))
    grad_inputs, grad_map["head_conv"] = conv_backward(
        grad_pre.astype(jnp.bfloat16), padded, weight_conv, axis
    )
    return (grad_inputs, grad_map)


def on_device(
    trajectories,
    dim_means,
    dim_stds,
    noise_draw,
    diffusion_steps,
    valid_mask,
    kernels,
    affine,
    kernel_momentum,
    kernel_average,
    affine_momentum,
    affine_average,
):
    members_all = unpack(kernels, affine)
    valid_total = lax.psum(jnp.sum(valid_mask.astype(jnp.float32)), ("dp", "hor"))
    signal_now = signal_level(diffusion_steps)[:, None, None]
    clean_frames = (trajectories - dim_means) / dim_stds
    noisy_frames = jnp.sqrt(signal_now) * clean_frames + jnp.sqrt(1.0 - signal_now) * noise_draw

    ring = lax.axis_size("hor")
    axis = "hor"
    if trajectories.shape[0] % ring == 0:
        axis = None
        local = trajectories.shape[0] // ring
        part = lax.axis_index("hor") * local
        low_frames = noisy_frames.astype(jnp.bfloat16)
        noisy_frames = lax.all_to_all(low_frames, "hor", 0, 1, tiled=True).astype(jnp.float32)
        noise_draw = lax.all_to_all(noise_draw, "hor", 0, 1, tiled=True)
        valid_mask = lax.all_to_all(valid_mask, "hor", 0, 1, tiled=True)
        diffusion_steps = lax.dynamic_slice_in_dim(diffusion_steps, part, local)

    def time_closed(kernel_flat, affine_flat):
        return time_parts(kernel_flat, affine_flat, diffusion_steps)

    time_list, time_pullback = jax.vjp(time_closed, kernels, affine)
    down_one, kept_one = block_forward(noisy_frames, members_all[0], time_list[0], axis)
    down_two, kept_two = block_forward(down_one, members_all[1], time_list[1], axis)
    down_three, kept_three = block_forward(down_two, members_all[2], time_list[2], axis)
    middle, kept_middle = block_forward(down_three, members_all[3], time_list[3], axis)
    up_one, kept_upper = block_forward(
        jnp.concatenate([middle, down_three], axis=2), members_all[4], time_list[4], axis)
    up_two, kept_lower = block_forward(
        jnp.concatenate([up_one, down_two], axis=2), members_all[5], time_list[5], axis)
    predicted, kept_head = head_forward(up_two, members_all[6], axis)
    weight_rows = valid_mask.astype(jnp.float32)[:, :, None]
    difference = predicted - noise_draw
    loss_scale = 1.0 / (valid_total * TD)
    loss_part = jnp.sum(weight_rows * difference * difference) * loss_scale
    grad_predicted = 2.0 * weight_rows * difference * loss_scale
    grad_up_two, head_grads = head_backward(grad_predicted, kept_head, members_all[6], axis)
    grad_joined, time_six, grads_six = block_backward(grad_up_two, kept_lower, members_all[5], axis)
    grad_up_one = grad_joined[:, :, :C2]
    grad_down_two = grad_joined[:, :, C2:]
    grad_joined, time_five, grads_five = block_backward(grad_up_one, kept_upper, members_all[4], axis)
    grad_middle = grad_joined[:, :, :C3]
    grad_down_three = grad_joined[:, :, C3:]
    grad_inputs, time_four, grads_four = block_backward(grad_middle, kept_middle, members_all[3], axis)
    grad_inputs, time_three, grads_three = block_backward(
        grad_down_three + grad_inputs, kept_three, members_all[2], axis
    )
    grad_inputs, time_two, grads_two = block_backward(
        grad_down_two + grad_inputs, kept_two, members_all[1], axis
    )
    grad_inputs, time_one, grads_one = block_backward(grad_inputs, kept_one, members_all[0], axis)
    kernel_grad, affine_grad = pack_flat(
        [grads_one, grads_two, grads_three, grads_four, grads_five, grads_six, head_grads]
    )
    time_kernel, time_affine = time_pullback(
        (time_one, time_two, time_three, time_four, time_five, time_six)
    )
    kernel_grad = kernel_grad + time_kernel
    affine_grad = affine_grad + time_affine
    share_len = kernels.shape[0] // lax.axis_size("dp")
    owner_start = lax.axis_index("dp") * share_len
    kernel_sum, affine_sum, noise_loss = lax.psum(
        (kernel_grad, affine_grad, loss_part), ("dp", "hor")
    )
    kernel_own = lax.dynamic_slice_in_dim(kernel_sum, owner_start, share_len)
    squares = jnp.sum(kernel_sum * kernel_sum) + jnp.sum(affine_sum * affine_sum)
    grad_norm = jnp.sqrt(squares)
    factor = jnp.minimum(1.0, MAX_NORM / (grad_norm + 1e-06))
    kernel_step = kernel_own * factor
    kernel_old = lax.dynamic_slice_in_dim(kernels, owner_start, share_len)
    kernel_mom_new = MOMENTUM * kernel_momentum + kernel_step
    kernel_new = kernel_old - LEARN_RATE * (kernel_step + MOMENTUM * kernel_mom_new)
    kernel_ema_new = EMA_DECAY * kernel_average + (1.0 - EMA_DECAY) * kernel_new
    affine_step = affine_sum * factor
    affine_mom_new = MOMENTUM * affine_momentum + affine_step
    affine_new = affine - AFFINE_RATE * (affine_step + MOMENTUM * affine_mom_new)
    affine_ema_new = EMA_DECAY * affine_average + (1.0 - EMA_DECAY) * affine_new
    return (
        noise_loss,
        grad_norm,
        kernel_new,
        kernel_mom_new,
        kernel_ema_new,
        kernel_new.astype(jnp.bfloat16),
        affine_new,
        affine_mom_new,
        affine_ema_new,
        affine_new.astype(jnp.bfloat16),
    )


def solution(mesh):
    in_specs = (
        P("dp", "hor", None),
        P(),
        P(),
        P("dp", "hor", None),
        P("dp"),
        P("dp", "hor"),
        P(),
        P(),
        P("dp"),
        P("dp"),
        P(),
        P(),
    )
    out_specs = (P(), P(), P("dp"), P("dp"), P("dp"), P("dp"), P(), P(), P(), P())
    return jax.shard_map(
        on_device, mesh=mesh, in_specs=in_specs, out_specs=out_specs, check_vma=False
    )
```

```python
import functools
import math

import jax
import jax.numpy as jnp
from jax import lax
from jax.experimental import pallas as pl
from jax.experimental.pallas import tpu as pltpu
from jax.sharding import PartitionSpec as P

TD = 23
C1 = 64
C2 = 128
C3 = 256
TE = 128
TH = 256
KSIZE = 5
GROUPS = 8
NSTEPS = 100


PRECISE = lax.Precision.HIGHEST
EPSILON = 1e-05
MAX_NORM = 0.02
LEARN_RATE = 200.0
AFFINE_RATE = 1500.0
MOMENTUM = 0.9
EMA_DECAY = 0.5


def padded_2(cells, sides, width):
    for axis, dim in sides:
        if axis is None:
            pads = [(0, 0)] * cells.ndim
            pads[dim] = (width, width)
            cells = jnp.pad(cells, pads)
            continue
        count = lax.axis_size(axis)
        ends = count - 1
        head = lax.slice_in_dim(cells, 0, width, axis=dim)
        tail = lax.slice_in_dim(cells, cells.shape[dim] - width, cells.shape[dim], axis=dim)
        cells = jnp.concatenate(
            [
                lax.ppermute(tail, axis, [(i, (i + 1) % count) for i in range(ends)]),
                cells,
                lax.ppermute(head, axis, [((i + 1) % count, i) for i in range(ends)]),
            ],
            axis=dim,
        )
    return cells


def sum_over(values, axis):
    return values if axis is None else lax.psum(values, axis)


def axis_length(axis):
    return 1 if axis is None else lax.axis_size(axis)


def layout_shapes():
    kernel_shapes = []
    affine_shapes = []
    for width_in, width_out in [
        (TD, C1),
        (C1, C2),
        (C2, C3),
        (C3, C3),
        (C3 + C3, C2),
        (C2 + C2, C1),
    ]:
        matrices = [
            ("conv_one", KSIZE * width_in, width_out),
            ("conv_two", KSIZE * width_out, width_out),
            ("time_proj", TE, width_out),
        ]
        vectors = [
            (entry_name, width_out)
            for entry_name in [
                "bias_one",
                "gain_one",
                "shift_one",
                "time_bias",
                "bias_two",
                "gain_two",
                "shift_two",
            ]
        ]
        if width_in != width_out:
            matrices.append(("res_proj", width_in, width_out))
            vectors.append(("res_bias", width_out))
        kernel_shapes.append(matrices)
        affine_shapes.append(vectors)
    kernel_shapes.append(
        [
            ("head_conv", KSIZE * C1, C1),
            ("head_out", C1, TD),
            ("embed_one", TE, TH),
            ("embed_two", TH, TE),
        ]
    )
    affine_shapes.append(
        [
            ("head_bias", C1),
            ("head_gain", C1),
            ("head_shift", C1),
            ("out_bias", TD),
            ("embed_bias_one", TH),
            ("embed_bias_two", TE),
        ]
    )
    return (kernel_shapes, affine_shapes)


def unpack(kernels, affine):
    kernel_shapes, affine_shapes = layout_shapes()
    members_all = []
    cursor = 0
    for entries in kernel_shapes:
        members = {}
        for entry_name, height, breadth in entries:
            members[entry_name] = kernels[cursor : cursor + height * breadth].reshape(
                height, breadth
            )
            cursor += height * breadth
        members_all.append(members)
    cursor = 0
    for position, entries in enumerate(affine_shapes):
        for entry_name, length in entries:
            members_all[position][entry_name] = affine[cursor : cursor + length]
            cursor += length
    return members_all


def pack_flat(grad_list):
    kernel_shapes, affine_shapes = layout_shapes()
    kernel_pieces = []
    affine_pieces = []
    for position, entries in enumerate(kernel_shapes):
        for entry_name, height, breadth in entries:
            kernel_pieces.append(
                grad_list[position]
                .get(entry_name, jnp.zeros((height, breadth), jnp.float32))
                .reshape(-1)
            )
    for position, entries in enumerate(affine_shapes):
        for entry_name, length in entries:
            affine_pieces.append(
                grad_list[position].get(entry_name, jnp.zeros((length,), jnp.float32))
            )
    return (jnp.concatenate(kernel_pieces), jnp.concatenate(affine_pieces))


def mish_act(value):
    return value * jnp.tanh(jax.nn.softplus(value))


def mish_grad(value, upstream):
    return jax.vjp(mish_act, value)[1](upstream)[0]


def sinusoid(steps_vec):
    half_width = TE // 2
    ladder = jnp.exp(
        -math.log(10000.0) * jnp.arange(half_width).astype(jnp.float32) / (half_width - 1)
    )
    angles = steps_vec.astype(jnp.float32)[:, None] * ladder[None, :]
    return jnp.concatenate([jnp.sin(angles), jnp.cos(angles)], axis=1)


def signal_level(steps_vec):
    ratio = (steps_vec.astype(jnp.float32) + 1.0) / NSTEPS
    cosine_now = jnp.cos((ratio + 0.008) / 1.008 * math.pi / 2)
    cosine_zero = math.cos(0.008 / 1.008 * math.pi / 2)
    return (cosine_now / cosine_zero) ** 2


def time_parts(kernel_flat, affine_flat, steps_vec):
    members_all = unpack(kernel_flat, affine_flat)
    last_group = members_all[6]
    hidden = mish_act(
        jnp.dot(sinusoid(steps_vec), last_group["embed_one"], precision=PRECISE)
        + last_group["embed_bias_one"]
    )
    feature = mish_act(
        jnp.dot(hidden, last_group["embed_two"], precision=PRECISE) + last_group["embed_bias_two"]
    )
    return tuple(
        (
            jnp.dot(feature, members_all[block_index]["time_proj"], precision=PRECISE)
            + members_all[block_index]["time_bias"]
            for block_index in range(6)
        )
    )


def conv_forward(inputs_low, weight_low, axis):
    padded = padded_2(inputs_low, ((axis, 1),), 2)
    frames = inputs_low.shape[1]
    channels = inputs_low.shape[2]
    running = 0.0
    for offset in range(KSIZE):
        running = running + jnp.einsum(
            "blc,cd->bld",
            padded[:, offset : offset + frames],
            weight_low[offset * channels : (offset + 1) * channels],
            preferred_element_type=jnp.float32,
        )
    return (running, padded)


def conv_backward(grad_low, padded, weight_low, axis):
    grad_padded = padded_2(grad_low, ((axis, 1),), 2)
    frames = grad_low.shape[1]
    channels = padded.shape[2]
    pieces = []
    running = 0.0
    for offset in range(KSIZE):
        pieces.append(
            jnp.einsum(
                "blc,bld->cd",
                padded[:, offset : offset + frames],
                grad_low,
                preferred_element_type=jnp.float32,
            )
        )
        start_row = KSIZE - 1 - offset
        running = running + jnp.einsum(
            "bld,cd->blc",
            grad_padded[:, start_row : start_row + frames],
            weight_low[offset * channels : (offset + 1) * channels],
            preferred_element_type=jnp.float32,
        )
    return (running, jnp.concatenate(pieces, axis=0))


def group_norm(values, gain_vec, shift_vec, axis):
    horizons, frames, channels = values.shape
    grouped = values.reshape(horizons, frames, GROUPS, channels // GROUPS)
    sum_one, sum_two = sum_over(
        (jnp.sum(grouped, axis=(1, 3)), jnp.sum(grouped * grouped, axis=(1, 3))), axis
    )
    group_count = frames * axis_length(axis) * (channels // GROUPS)
    average = sum_one / group_count
    inverse = lax.rsqrt(sum_two / group_count - average * average + EPSILON)
    normed = ((grouped - average[:, None, :, None]) * inverse[:, None, :, None]).reshape(
        horizons, frames, channels
    )
    return (normed * gain_vec + shift_vec, (normed, inverse))


def group_norm_back(upstream, norm_stats, gain_vec, axis):
    normed, inverse = norm_stats
    horizons, frames, channels = normed.shape
    grad_gain = jnp.sum(upstream * normed, axis=(0, 1))
    grad_shift = jnp.sum(upstream, axis=(0, 1))
    scaled = (upstream * gain_vec).reshape(horizons, frames, GROUPS, channels // GROUPS)
    grouped = normed.reshape(horizons, frames, GROUPS, channels // GROUPS)
    sum_one, sum_two = sum_over(
        (jnp.sum(scaled, axis=(1, 3)), jnp.sum(scaled * grouped, axis=(1, 3))), axis
    )
    group_count = frames * axis_length(axis) * (channels // GROUPS)
    result = inverse[:, None, :, None] * (
        scaled
        - sum_one[:, None, :, None] / group_count
        - grouped * sum_two[:, None, :, None] / group_count
    )
    return (result.reshape(horizons, frames, channels), grad_gain, grad_shift)


def block_forward(inputs, members, time_term, axis):
    inputs_low = inputs.astype(jnp.bfloat16)
    weight_one = members["conv_one"].astype(jnp.bfloat16)
    weight_two = members["conv_two"].astype(jnp.bfloat16)
    conv_out, padded_one = conv_forward(inputs_low, weight_one, axis)
    normed_one, stats_one = group_norm(
        conv_out + members["bias_one"], members["gain_one"], members["shift_one"], axis
    )
    hidden = mish_act(normed_one) + time_term[:, None, :]
    conv_out, padded_two = conv_forward(hidden.astype(jnp.bfloat16), weight_two, axis)
    normed_two, stats_two = group_norm(
        conv_out + members["bias_two"], members["gain_two"], members["shift_two"], axis
    )
    result = mish_act(normed_two)
    if "res_proj" in members:
        weight_side = members["res_proj"].astype(jnp.bfloat16)
        result = (
            result
            + jnp.einsum("blc,cd->bld", inputs_low, weight_side, preferred_element_type=jnp.float32)
            + members["res_bias"]
        )
    else:
        weight_side = None
        result = result + inputs
    return (
        result,
        (
            padded_one,
            stats_one,
            padded_two,
            stats_two,
            inputs_low,
            weight_one,
            weight_two,
            weight_side,
        ),
    )


def block_backward(upstream, kept, members, axis):
    (
        padded_one,
        stats_one,
        padded_two,
        stats_two,
        inputs_low,
        weight_one,
        weight_two,
        weight_side,
    ) = kept
    grad_map = {}
    grad_normed = mish_grad(stats_two[0] * members["gain_two"] + members["shift_two"], upstream)
    grad_pre, grad_map["gain_two"], grad_map["shift_two"] = group_norm_back(
        grad_normed, stats_two, members["gain_two"], axis
    )
    grad_map["bias_two"] = jnp.sum(grad_pre, axis=(0, 1))
    grad_hidden, grad_map["conv_two"] = conv_backward(
        grad_pre.astype(jnp.bfloat16), padded_two, weight_two, axis
    )
    time_grad = jnp.sum(grad_hidden, axis=1)
    grad_normed = mish_grad(stats_one[0] * members["gain_one"] + members["shift_one"], grad_hidden)
    grad_pre, grad_map["gain_one"], grad_map["shift_one"] = group_norm_back(
        grad_normed, stats_one, members["gain_one"], axis
    )
    grad_map["bias_one"] = jnp.sum(grad_pre, axis=(0, 1))
    grad_inputs, grad_map["conv_one"] = conv_backward(
        grad_pre.astype(jnp.bfloat16), padded_one, weight_one, axis
    )
    if weight_side is not None:
        upstream_low = upstream.astype(jnp.bfloat16)
        grad_map["res_bias"] = jnp.sum(upstream, axis=(0, 1))
        grad_map["res_proj"] = jnp.einsum(
            "blc,bld->cd", inputs_low, upstream_low, preferred_element_type=jnp.float32
        )
        grad_inputs = grad_inputs + jnp.einsum(
            "bld,cd->blc", upstream_low, weight_side, preferred_element_type=jnp.float32
        )
    else:
        grad_inputs = grad_inputs + upstream
    return (grad_inputs, time_grad, grad_map)


def head_forward(inputs, members, axis):
    weight_conv = members["head_conv"].astype(jnp.bfloat16)
    weight_out = members["head_out"].astype(jnp.bfloat16)
    conv_out, padded = conv_forward(inputs.astype(jnp.bfloat16), weight_conv, axis)
    normed, norm_stats = group_norm(
        conv_out + members["head_bias"], members["head_gain"], members["head_shift"], axis
    )
    feature_low = mish_act(normed).astype(jnp.bfloat16)
    predicted = (
        jnp.einsum("blc,cd->bld", feature_low, weight_out, preferred_element_type=jnp.float32)
        + members["out_bias"]
    )
    return (predicted, (padded, norm_stats, feature_low, weight_conv, weight_out))


def head_backward(upstream, kept, members, axis):
    padded, norm_stats, feature_low, weight_conv, weight_out = kept
    grad_map = {}
    upstream_low = upstream.astype(jnp.bfloat16)
    grad_map["out_bias"] = jnp.sum(upstream, axis=(0, 1))
    grad_map["head_out"] = jnp.einsum(
        "blc,bld->cd", feature_low, upstream_low, preferred_element_type=jnp.float32
    )
    grad_feature = jnp.einsum(
        "bld,cd->blc", upstream_low, weight_out, preferred_element_type=jnp.float32
    )
    grad_normed = mish_grad(
        norm_stats[0] * members["head_gain"] + members["head_shift"], grad_feature
    )
    grad_pre, grad_map["head_gain"], grad_map["head_shift"] = group_norm_back(
        grad_normed, norm_stats, members["head_gain"], axis
    )
    grad_map["head_bias"] = jnp.sum(grad_pre, axis=(0, 1))
    grad_inputs, grad_map["head_conv"] = conv_backward(
        grad_pre.astype(jnp.bfloat16), padded, weight_conv, axis
    )
    return (grad_inputs, grad_map)


BF = jnp.bfloat16
F32 = jnp.float32
HALO = 32
ROW_STARTS = (0, 293, 1445, 5797, 11173, 15013)
LOAD_ROWS = (0, 296, 1448, 5800, 11176, 15016, 16008, 16696)
HEAD_ROW = 16005
OUT_ROW = 16165
EMB_ROW = 16176
FLAT_ROWS = 16696
TABLE_ROWS = 16720
LATE_START = 5792
LATE_ROWS = 16168 - LATE_START
OWN_ROWS = 2112
NKER_ROWS = 2086
OUT_START = OUT_ROW * 128
WIDTHS = ((TD, C1), (C1, C2), (C2, C3), (C3, C3), (C3 + C3, C2), (C2 + C2, C1))
AFF_ROWS = (0, 4, 12, 28, 42, 50)
LAYER_OUT = ((1, 128), (2, 128), (2, 256), (2, 256), (2, 128), (1, 128), (1, 128))
W_ONE = ((640, 128), (640, 256), (640, 256), (1280, 256), (2560, 128), (2560, 128), (640, 128))
W_TWO = ((640, 128), (640, 128), (1280, 256), (1280, 256), (640, 128), (640, 128))
W_RES = ((128, 128), (128, 256), (128, 256), None, (512, 128), (512, 128))
TN = (((0,), (0,)), ((), ()))
NT = (((1,), (1,)), ((), ()))


def lanes_of(shape):
    return lax.broadcasted_iota(jnp.int32, shape, 1)


def rows_of(shape):
    return lax.broadcasted_iota(jnp.int32, shape, 0)


def fill_halo(ref):
    halves, padded_rows, lanes = ref.shape
    inner = padded_rows - 2 * HALO
    row = rows_of((16, lanes))
    lane = lanes_of((16, lanes))
    for group in range(2):
        start = inner + 16 * group
        moved = [pltpu.roll(ref[q, start : start + 16, :].astype(F32), 1, 0) for q in range(halves)]
        into = pl.ds(16 * group, 16)
        if halves == 1:
            edge = jnp.where(lane >= 64, pltpu.roll(moved[0], 64, 1), 0.0)
            ref[0, into, :] = jnp.where(row == 0, edge, moved[0]).astype(BF)
        else:
            ref[0, into, :] = jnp.where(row == 0, 0.0, moved[0]).astype(BF)
            ref[1, into, :] = jnp.where(row == 0, moved[0], moved[1]).astype(BF)
        start = HALO + 16 * group
        moved = [pltpu.roll(ref[q, start : start + 16, :].astype(F32), 15, 0) for q in range(halves)]
        into = pl.ds(HALO + inner + 16 * group, 16)
        if halves == 1:
            edge = jnp.where(lane < 64, pltpu.roll(moved[0], 64, 1), 0.0)
            ref[0, into, :] = jnp.where(row == 15, edge, moved[0]).astype(BF)
        else:
            ref[0, into, :] = jnp.where(row == 15, moved[1], moved[0]).astype(BF)
            ref[1, into, :] = jnp.where(row == 15, 0.0, moved[1]).astype(BF)


def mish_fast(value):
    grown = jnp.exp(jnp.minimum(value, 20.0))
    top = grown * (grown + 2.0)
    return value * (top / (top + 2.0))


def mish_both(value):
    grown = jnp.exp(jnp.minimum(value, 20.0))
    top = grown * (grown + 2.0)
    inverse = 1.0 / (top + 2.0)
    ratio = top * inverse
    slope = ratio + 4.0 * value * (top - grown) * (inverse * inverse)
    return value * ratio, slope


def fold_rows(value):
    rows, lanes = value.shape
    return jnp.sum(value.reshape(rows // 8, 8, lanes), axis=0)


def down_one_row(value):
    return jnp.sum(value, axis=0, keepdims=True)


def both_halves(row):
    return row + pltpu.roll(row, 64, 1)


def group_sums(first, second, packed):
    lanes = first.shape[1]
    row = rows_of((8, lanes))
    stacked = jnp.where(row == 0, first, jnp.where(row == 1, second, 0.0))
    left = rows_of((lanes, lanes))
    right = lanes_of((lanes, lanes))
    if packed:
        same = (left % 64) // 8 == (right % 64) // 8
    else:
        size = lanes // GROUPS
        same = left // size == right // size
    summed = jnp.dot(stacked, same.astype(F32), precision=PRECISE, preferred_element_type=F32)
    return summed[0:1, :], summed[1:2, :]


def tile_rows(inner):
    for rows in (256, 128, 64, 32, 16):
        if inner % rows == 0:
            return rows


def sweep(halves, inner, body, carry):
    rows = tile_rows(inner)
    per_half = inner // rows

    def step(index, state):
        q = index // per_half
        start = pl.multiple_of((index - q * per_half) * rows, rows)
        return body(q, start, rows, state)

    return lax.fori_loop(0, halves * per_half, step, carry)


def vector(aff, row, width):
    if width == 256:
        base = int(row)
        return jnp.concatenate([aff[base : base + 1, :], aff[base + 1 : base + 2, :]], axis=1)
    base = int(row)
    whole = aff[base : base + 1, :]
    if width == 128:
        return whole
    turned = pltpu.roll(whole, 64, 1)
    lane = lanes_of((1, 128))
    if row == base:
        return jnp.where(lane < 64, whole, turned)
    return jnp.where(lane < 64, turned, whole)


def block_vector(aff, block, number):
    width = WIDTHS[block][1]
    return vector(aff, AFF_ROWS[block] + number * width / 128, width)


def head_vector(aff, number):
    return vector(aff, 54 + number / 2, 64)


def conv_input(xs, q, tap, inner):
    parts = [x[q, pl.ds(16 * tap, inner), :] for x in xs]
    return parts[0] if len(parts) == 1 else jnp.concatenate(parts, axis=1)


def conv_to(xs, weight, bias, out, crossing):
    halves, inner, lanes = out.shape
    zero = jnp.zeros((8, lanes), F32)

    def finish(q, total, state):
        total = total + bias
        out[q] = total
        return state[0] + fold_rows(total), state[1] + fold_rows(total * total)

    if crossing == "up":
        wide = jnp.concatenate([conv_input(xs, 0, k, inner) for k in range(KSIZE)], axis=1)
        total = jnp.dot(wide, weight[...], preferred_element_type=F32)
        state = finish(0, total[:, :lanes], (zero, zero))
        return finish(1, total[:, lanes:], state)
    if crossing == "down":
        wide = jnp.concatenate(
            [conv_input(xs, q, k, inner) for k in range(KSIZE) for q in range(2)], axis=1
        )
        return finish(0, jnp.dot(wide, weight[...], preferred_element_type=F32), (zero, zero))

    def half(q, state):
        wide = jnp.concatenate([conv_input(xs, q, k, inner) for k in range(KSIZE)], axis=1)
        return finish(q, jnp.dot(wide, weight[...], preferred_element_type=F32), state)

    return lax.fori_loop(0, halves, half, (zero, zero))


def norm_fit(sums, gain, shift, count, packed, stats, layer):
    lanes = gain.shape[1]
    one = down_one_row(sums[0])
    two = down_one_row(sums[1])
    group_one, group_two = group_sums(one, two, packed)
    mean = group_one / count
    inverse = lax.rsqrt(group_two / count - mean * mean + EPSILON)
    scale = inverse * gain
    offset = shift - mean * scale
    for number, row in enumerate((scale, offset, mean, inverse, one)):
        stats[8 * layer + number : 8 * layer + number + 1, 0:lanes] = row
    return scale, offset


def norm_kept(stats, layer, lanes):
    return [stats[8 * layer + n : 8 * layer + n + 1, 0:lanes] for n in range(5)]


def norm_back_fit(sums, kept, gain, count, rows, packed):
    scale, _, mean, inverse, one = kept
    grad_shift = down_one_row(sums[0])
    grad_gain = inverse * (down_one_row(sums[1]) - mean * grad_shift)
    first, second = group_sums(gain * grad_shift, gain * grad_gain, packed)
    first = first / count
    second = second / count
    slope = -inverse * inverse * second
    level = -inverse * first - slope * mean
    grad_bias = scale * grad_shift + slope * one + level * rows
    if packed:
        grad_shift, grad_gain, grad_bias = [both_halves(v) for v in (grad_shift, grad_gain, grad_bias)]
    return slope, level, grad_bias, grad_gain, grad_shift


def unpack_pairs(flat, start, count, out):
    step = 8

    def move(index, carry):
        at = pl.multiple_of(index * step, step)
        rows = flat[pl.ds(start + at, step), :]
        turned = pltpu.roll(rows, 64, 1)
        lane = lanes_of(rows.shape)
        out[pl.ds(2 * at, step, stride=2), :] = jnp.where(lane < 64, rows, turned)
        out[pl.ds(2 * at + 1, step, stride=2), :] = jnp.where(lane < 64, turned, rows)
        return carry

    lax.fori_loop(0, count // step, move, 0)


def pack_pairs(source, out, start, count):
    step = 8

    def move(index, carry):
        at = pl.multiple_of(index * step, step)
        even = source[pl.ds(2 * at, step, stride=2), :]
        odd = pltpu.roll(source[pl.ds(2 * at + 1, step, stride=2), :], 64, 1)
        out[pl.ds(start + at, step), :] = jnp.where(lanes_of(even.shape) < 64, even, odd)
        return carry

    lax.fori_loop(0, count // step, move, 0)


def spread_pairs(pairs, start, count, weight, to, size):
    rows = min(-(-count // 32) * 32, size)
    value = pairs[start : start + rows, :]
    keep = rows_of(value.shape) < count
    lane = lanes_of(value.shape)
    weight[to : to + rows, :] = jnp.where(keep & (lane < 64), value, 0.0).astype(BF)
    weight[to + size : to + size + rows, :] = jnp.where(keep & (lane >= 64), value, 0.0).astype(BF)


def straight_rows(flat, start, count, out, to):
    step = 128

    def move(index, carry):
        at = pl.multiple_of(index * step, step)
        out[pl.ds(to + at, step), :] = flat[pl.ds(start + at, step), :].astype(out.dtype)
        return carry

    lax.fori_loop(0, count // step, move, 0)


def wide_rows(flat, start, count, out, to):
    step = 64

    def move(index, carry):
        at = pl.multiple_of(index * step, step)
        for half in range(2):
            out[pl.ds(to + at, step), 128 * half : 128 * half + 128] = flat[
                pl.ds(start + 2 * at + half, step, stride=2), :
            ].astype(out.dtype)
        return carry

    lax.fori_loop(0, count // step, move, 0)


def prepare_block(block, c):
    flat = c["flat"]
    start = ROW_STARTS[block]
    width_in, width_out = WIDTHS[block]
    one, two = c[f"one{block}"], c[f"two{block}"]
    res = c.get(f"res{block}")
    proj, at = c["proj"], TE * block
    pairs = c["pairs"]
    if width_out == 64:
        chunks = 592 if block == 0 else 1984
        unpack_pairs(flat, start, chunks // 2, pairs)
        size = 64 if block == 0 else 256
        if block == 0:
            one[...] = jnp.zeros_like(one)
            res[...] = jnp.zeros_like(res)
        for k in range(KSIZE):
            spread_pairs(pairs, width_in * k, width_in, one, 2 * size * k, size)
            spread_pairs(pairs, KSIZE * width_in + 64 * k, 64, two, 128 * k, 64)
        cursor = KSIZE * (width_in + 64)
        proj[at : at + TE, 0:128] = pairs[cursor : cursor + TE, :]
        spread_pairs(pairs, cursor + TE, width_in, res, 0, size)
    elif width_out == 128:
        if block == 1:
            one[...] = jnp.zeros_like(one)
            res[...] = jnp.zeros_like(res)
            for k in range(KSIZE + 1):
                source = start + 64 * k if k < KSIZE else start + 320 + 640 + TE
                value = flat[source : source + 64, :].astype(BF)
                into, base = (one, 128 * k) if k < KSIZE else (res, 0)
                into[base : base + 64, 0:128] = value
                into[base + 64 : base + 128, 128:256] = value
        else:
            straight_rows(flat, start, KSIZE * width_in, one, 0)
            straight_rows(flat, start + KSIZE * width_in + 640 + TE, width_in, res, 0)
        straight_rows(flat, start + KSIZE * width_in, 640, two, 0)
        cursor = start + KSIZE * width_in + 640
        proj[at : at + TE, 0:128] = flat[cursor : cursor + TE, :]
    else:
        wide_rows(flat, start, KSIZE * width_in, one, 0)
        wide_rows(flat, start + 2 * KSIZE * width_in, 1280, two, 0)
        cursor = start + 2 * (KSIZE * width_in + 1280)
        wide_rows(flat, cursor, TE, proj, at)
        if res is not None:
            wide_rows(flat, cursor + 2 * TE, width_in, res, 0)


def exact_dot(left, right, dims=(((1,), (0,)), ((), ()))):
    return lax.dot_general(left, right, dims, precision=PRECISE, preferred_element_type=F32)


CROSSING = (None, "up", None, None, None, "down")


def counts_of(frames, block):
    width = WIDTHS[block][1] if block < 6 else C1
    return frames * (width // GROUPS)


def forward_kernel(names, *refs):
    c = dict(zip(names, refs))
    sems = c["sems"]
    aff, stats, terms = c["aff"], c["stats"], c["terms"]
    inner = c["pre_a0"].shape[1]
    frames = 2 * inner
    saves = []

    def save(name):
        copy = pltpu.make_async_copy(c[name], c["out_" + name], sems.at[16 + len(saves)])
        copy.start()
        saves.append(copy)

    loads = []
    for number, (low, high) in enumerate(zip(LOAD_ROWS[:-1], LOAD_ROWS[1:])):
        part = pl.ds(low, high - low)
        copy = pltpu.make_async_copy(c["in_flat"].at[part, :], c["flat"].at[part, :], sems.at[number])
        loads.append(copy)
    order = (6, 0, 1, 2, 3, 4, 5)
    for number in order:
        loads[number].start()
    loads[6].wait()
    flat, pairs, embed = c["flat"], c["pairs"], c["embed_two"]
    unpack_pairs(flat, EMB_ROW, FLAT_ROWS - EMB_ROW, pairs)
    quarter = [pairs[pl.ds(1 + n, TE, stride=4), :] for n in range(4)]
    lane = lanes_of((TE, 128))
    embed_one = jnp.concatenate(
        [jnp.where(lane < 64, quarter[0], quarter[1]), jnp.where(lane < 64, quarter[2], quarter[3])], axis=1
    )
    embed[...] = jnp.where(
        lanes_of((TH, 128)) < 64, pairs[pl.ds(513, TH, stride=2), :], pairs[pl.ds(514, TH, stride=2), :]
    )
    sinus = c["sinus"][...]
    bias = vector(aff, 56, 256)
    kept = c["kept"]
    hidden_pre = exact_dot(sinus, embed_one) + bias
    hidden = mish_fast(hidden_pre)
    feature_pre = exact_dot(hidden, embed[...]) + vector(aff, 58, 128)
    feature = mish_fast(feature_pre)
    for number, value in enumerate((hidden_pre, hidden, feature_pre, feature)):
        kept[8 * number : 8 * number + 8, 0 : value.shape[1]] = value
    save("embed_two")
    x0 = c["x0"]
    x0[0, HALO : HALO + inner, :] = c["noisy"][...]
    fill_halo(x0)
    save("x0")

    inputs = (("x0",), ("x1",), ("x2",), ("x3",), ("x4", "x3"), ("x5", "x2"))
    for block in range(6):
        loads[block].wait()
        prepare_block(block, c)
        for name in ("one", "two", "res"):
            if f"{name}{block}" in c:
                save(f"{name}{block}")
        halves, lanes = LAYER_OUT[block]
        packed = halves == 1
        count = counts_of(frames, block)
        width = WIDTHS[block][1]
        lane_bias = block_vector(aff, block, 3)
        term = exact_dot(feature, c["proj"][TE * block : TE * block + TE, 0:lanes])[0:1, :] + lane_bias
        terms[8 * block : 8 * block + 1, 0:lanes] = term
        xs = [c[name] for name in inputs[block]]
        pre_a, pre_b = c[f"pre_a{block}"], c[f"pre_b{block}"]
        sums = conv_to(xs, c[f"one{block}"], block_vector(aff, block, 0), pre_a, CROSSING[block])
        save(f"pre_a{block}")
        scale, offset = norm_fit(
            sums, block_vector(aff, block, 1), block_vector(aff, block, 2), count, packed, stats, 2 * block
        )
        hid = c["hid"].at[0:halves, :, 0:lanes]

        def to_hidden(q, start, rows, carry):
            value = mish_fast(pre_a[q, pl.ds(start, rows), :] * scale + offset) + term
            hid[q, pl.ds(HALO + start, rows), :] = value.astype(BF)
            return carry

        sweep(halves, inner, to_hidden, 0)
        fill_halo(hid)
        sums = conv_to([hid], c[f"two{block}"], block_vector(aff, block, 4), pre_b, None)
        save(f"pre_b{block}")
        scale_b, offset_b = norm_fit(
            sums, block_vector(aff, block, 5), block_vector(aff, block, 6), count, packed, stats, 2 * block + 1
        )
        side = c["side"]
        res = c.get(f"res{block}")
        if res is not None:
            res_bias = block_vector(aff, block, 7)
            if CROSSING[block] == "up":
                total = jnp.dot(conv_input(xs, 0, 2, inner), res[...], preferred_element_type=F32)
                side[0, :, 0:lanes] = total[:, :lanes] + res_bias
                side[1, :, 0:lanes] = total[:, lanes:] + res_bias
            elif CROSSING[block] == "down":
                wide = jnp.concatenate([conv_input(xs, q, 2, inner) for q in range(2)], axis=1)
                side[0, :, 0:lanes] = jnp.dot(wide, res[...], preferred_element_type=F32) + res_bias
            else:
                for q in range(halves):
                    side[q, :, 0:lanes] = (
                        jnp.dot(conv_input(xs, q, 2, inner), res[...], preferred_element_type=F32) + res_bias
                    )
        out = c[f"x{block + 1}"]

        def to_output(q, start, rows, carry):
            value = mish_fast(pre_b[q, pl.ds(start, rows), :] * scale_b + offset_b)
            value = value + side[q, pl.ds(start, rows), 0:lanes]
            if block == 2:
                side[q, pl.ds(start, rows), 0:lanes] = value
            out[q, pl.ds(HALO + start, rows), :] = value.astype(BF)
            return carry

        sweep(halves, inner, to_output, 0)
        fill_halo(out)
        save(f"x{block + 1}")
    unpack_pairs(flat, HEAD_ROW, 160, pairs)
    for k in range(KSIZE):
        spread_pairs(pairs, 64 * k, 64, c["one6"], 128 * k, 64)
    save("one6")
    sums = conv_to([c["x6"]], c["one6"], head_vector(aff, 0), c["pre_a6"], None)
    save("pre_a6")
    norm_fit(sums, head_vector(aff, 1), head_vector(aff, 2), counts_of(frames, 6), True, stats, 12)
    for name in ("stats", "terms", "kept", "proj"):
        save(name)
    for copy in saves:
        copy.wait()


def put_rows(value, out, start):
    rows, lanes = value.shape
    if lanes == 128:
        out[start : start + rows, :] = value
    else:
        out[pl.ds(start, rows, stride=2), :] = value[:, 0:128]
        out[pl.ds(start + 1, rows, stride=2), :] = value[:, 128:256]


def conv_dx(dy, weight, size, inner, crossing, emit):
    halves = dy.shape[0]

    def taps(pick):
        total = 0.0
        for k in range(KSIZE):
            total = total + lax.dot_general(
                pick(KSIZE - 1 - k), weight[size * k : size * k + size, :], NT, preferred_element_type=F32
            )
        return total

    if crossing == "up":
        emit(0, taps(lambda k: jnp.concatenate([conv_input([dy], q, k, inner) for q in range(2)], axis=1)))
    elif halves == 1:
        emit(0, taps(lambda k: conv_input([dy], 0, k, inner)))
    else:

        def half(q, carry):
            emit(q, taps(lambda k: conv_input([dy], q, k, inner)))
            return carry

        lax.fori_loop(0, halves, half, 0)


def conv_dw(xs, dy, inner, crossing, acc, extra=None):
    def dys(q):
        parts = [conv_input([dy], q, KSIZE - 1 - k, inner) for k in range(KSIZE)]
        if extra is not None:
            parts.append(extra[q, :, 0 : dy.shape[2]])
        return parts

    def product(left, right):
        return lax.dot_general(left, right, TN, preferred_element_type=F32)

    if crossing == "up":
        both = zip(dys(0), dys(1))
        value = product(conv_input(xs, 0, 2, inner), jnp.concatenate([p for pair in both for p in pair], axis=1))
        acc[0 : value.shape[0], 0 : value.shape[1]] = value
        return
    if crossing == "down":
        left = jnp.concatenate([conv_input(xs, q, 2, inner) for q in range(2)], axis=1)
        value = product(left, jnp.concatenate(dys(0), axis=1))
        acc[0 : value.shape[0], 0 : value.shape[1]] = value
        return
    for q in range(dy.shape[0]):
        value = product(conv_input(xs, q, 2, inner), jnp.concatenate(dys(q), axis=1))
        if q == 0:
            acc[0 : value.shape[0], 0 : value.shape[1]] = value
        else:
            acc[0 : value.shape[0], 0 : value.shape[1]] += value


def fold_pairs(acc, tap, size, rows):
    lanes = slice(128 * tap, 128 * tap + 128)
    return acc[0:rows, lanes] + pltpu.roll(acc[size : size + rows, lanes], 64, 1)


def put_vector(grads, row, width, value):
    base = int(row)
    if width == 256:
        grads[base : base + 1, :] = value[:, 0:128]
        grads[base + 1 : base + 2, :] = value[:, 128:256]
    elif width == 128:
        grads[base : base + 1, :] = value
    else:
        lane = lanes_of((1, 128))
        keep = lane < 64 if row == base else lane >= 64
        grads[base : base + 1, :] = jnp.where(keep, value, grads[base : base + 1, :])


def norm_backward(c, layer, pre, gain, count, packed, upstream, dy, also=None):
    halves, inner, lanes = pre.shape
    kept = norm_kept(c["stats"], layer, lanes)
    dv = c["dv"]
    zero = jnp.zeros((8, lanes), F32)

    def first(q, start, rows, state):
        here = pl.ds(start, rows)
        value = pre[q, here, :]
        act, slope = mish_both(value * kept[0] + kept[1])
        up = upstream(q, here)
        if also is not None:
            also(q, here, act, up)
        grad = up * slope
        dv[q, here, 0:lanes] = grad
        return state[0] + fold_rows(grad), state[1] + fold_rows(grad * value), state[2] + fold_rows(up)

    sums = sweep(halves, inner, first, (zero, zero, zero))
    rows_each = float(inner * halves)
    slope, level, grad_bias, grad_gain, grad_shift = norm_back_fit(sums, kept, gain, count, rows_each, packed)
    scale = kept[0]

    def second(q, start, rows, carry):
        here = pl.ds(start, rows)
        value = scale * dv[q, here, 0:lanes] + (slope * pre[q, here, :] + level)
        dy[q, pl.ds(HALO + start, rows), :] = value.astype(BF)
        return carry

    sweep(halves, inner, second, 0)
    fill_halo(dy)
    total = down_one_row(sums[2])
    return grad_bias, grad_gain, grad_shift, both_halves(total) if packed else total


def backward_block(block, c, base):
    aff, grads, table, acc = c["aff"], c["agrad"], c["table"], c["acc"]
    halves, lanes = LAYER_OUT[block]
    packed = halves == 1
    width_in, width_out = WIDTHS[block]
    inner = c[f"pre_a{block}"].shape[1]
    count = counts_of(2 * inner, block)
    up = c[f"up{block}"]
    low = c["low"]
    dy = c["dy"].at[0:halves, :, 0:lanes]
    act_low = c["act"]
    res = c.get(f"res{block}")
    inputs = (("x0",), ("x1",), ("x2",), ("x3",), ("x4", "x3"), ("x5", "x2"))
    xs = [c[name] for name in inputs[block]]
    start = ROW_STARTS[block] - base
    spot = AFF_ROWS[block]
    unit = width_out / 128

    def keep_low(q, here, act, value):
        low[q, here, 0:lanes] = value.astype(BF)

    got = norm_backward(
        c, 2 * block + 1, c[f"pre_b{block}"], block_vector(aff, block, 5), count, packed,
        lambda q, here: up[q, here, :], dy, keep_low if res is not None else None,
    )
    for number, value in zip((4, 5, 6, 7), got):
        if number < 7 or res is not None:
            put_vector(grads, spot + number * unit, width_out, value)
    dv = c["dv"]

    def emit_hidden(q, value):
        dv[q, :, 0:lanes] = value

    conv_dx(dy, c[f"two{block}"], lanes, inner, None, emit_hidden)
    term = c["terms"][8 * block : 8 * block + 1, 0:lanes]
    dy_two = dy
    dy_one = c["ey"].at[0:halves, :, 0:lanes]

    def keep_act(q, here, act, value):
        act_low[q, here, 0:lanes] = (act + term).astype(BF)

    got = norm_backward(
        c, 2 * block, c[f"pre_a{block}"], block_vector(aff, block, 1), count, packed,
        lambda q, here: dv[q, here, 0:lanes], dy_one, keep_act,
    )
    for number, value in zip((0, 1, 2, 3), got):
        put_vector(grads, spot + number * unit, width_out, value)
    time_row = got[3]
    c["tgrad"][8 * block : 8 * block + 1, 0:lanes] = time_row

    def plain_dw(left, right_ref):
        for q in range(halves):
            parts = jnp.concatenate([conv_input([right_ref], q, KSIZE - 1 - k, inner) for k in range(KSIZE)], axis=1)
            value = lax.dot_general(left[q, :, 0:lanes], parts, TN, preferred_element_type=F32)
            if q == 0:
                acc[0:lanes, 0 : KSIZE * lanes] = value
            else:
                acc[0:lanes, 0 : KSIZE * lanes] += value

    plain_dw(act_low, dy_two)
    pairs = c["pairs"]
    feature = c["kept"][24:32, 0:128]
    row = rows_of((8, lanes))
    outer = exact_dot(
        jnp.where(rows_of((8, 128)) == 0, feature, 0.0), jnp.where(row == 0, time_row, 0.0), TN
    )
    if width_out == 64:
        at = KSIZE * width_in
        for k in range(KSIZE):
            pairs[at + 64 * k : at + 64 * k + 64, :] = fold_pairs(acc, k, 64, 64)
        pairs[at + 320 : at + 320 + TE, :] = outer
    else:
        at = start + KSIZE * width_in * (width_out // 128)
        for k in range(KSIZE):
            put_rows(acc[0:lanes, lanes * k : lanes * k + lanes], table, at + k * lanes * (width_out // 128))
        put_rows(outer, table, at + 5 * lanes * (width_out // 128))
    crossing = CROSSING[block]
    if block > 0:
        size = {None: sum(x.shape[2] for x in xs), "up": 128, "down": 512}[crossing]

        def emit(q, value):
            if res is not None:
                if crossing == "up":
                    side = jnp.concatenate([low[0, :, 0:lanes], low[1, :, 0:lanes]], axis=1)
                else:
                    side = low[q, :, 0:lanes]
                value = value + lax.dot_general(side, res[...], NT, preferred_element_type=F32)
            if block == 5:
                for h in range(2):
                    c["up4"][h] = value[:, 256 * h : 256 * h + 128]
                    c["up1"][h] = value[:, 256 * h + 128 : 256 * h + 256]
            elif block == 4:
                c["up3"][q] = value[:, 0:256]
                c["up2"][q] = value[:, 256:512]
            elif block == 3:
                c["up2"][q] = c["up2"][q] + (value + up[q])
            elif block == 2:
                c["up1"][q] = c["up1"][q] + value
            else:
                c["up0"][0] = value

        conv_dx(dy_one, c[f"one{block}"], size, inner, crossing, emit)
    conv_dw(xs, dy_one, inner, crossing, acc, low if res is not None else None)
    if width_out == 64:
        size = 64 if block == 0 else 256
        rows = 24 if block == 0 else 256
        for k in range(KSIZE):
            value = fold_pairs(acc, k, size, rows)
            pairs[width_in * k : width_in * k + width_in, :] = value[0:width_in]
        at = KSIZE * (width_in + 64) + TE
        pairs[at : at + width_in, :] = fold_pairs(acc, KSIZE, size, rows)[0:width_in]
        if block == 0:
            after = table[288:296, :]
            pack_pairs(pairs, table, start, 296)
            table[288:296, :] = jnp.where(rows_of((8, 128)) < 5, table[288:296, :], after)
        else:
            pack_pairs(pairs, table, start, 992)
    else:
        unit_rows = width_out // 128
        for k in range(KSIZE + (0 if res is None else 1)):
            at = start + k * width_in * unit_rows
            if k == KSIZE:
                at = start + (KSIZE * (width_in + width_out) + TE) * unit_rows
            if crossing == "up":
                value = acc[0:64, 256 * k : 256 * k + 128] + acc[64:128, 256 * k + 128 : 256 * k + 256]
            else:
                value = acc[0:width_in, width_out * k : width_out * k + width_out]
            put_rows(value, table, at)


def load_all(c, names, sems, first=0):
    copies = {}
    for number, name in enumerate(names):
        copy = pltpu.make_async_copy(c["in_" + name], c[name], sems.at[first + number])
        copy.start()
        copies[name] = copy
    return copies


def late_kernel(loaded, names, *refs):
    c = dict(zip(names, refs))
    copies = load_all(c, loaded, c["sems"])
    aff, grads = c["aff"], c["agrad"]

    def need(*wanted):
        for name in wanted:
            copy = copies.pop(name, None)
            if copy is not None:
                copy.wait()

    grads[...] = jnp.zeros_like(grads)
    need("stats", "terms", "kept", "pre_a6", "noise")
    pre = c["pre_a6"]
    inner = pre.shape[1]
    kept = norm_kept(c["stats"], 12, 128)
    act, low, up = c["act"], c["low"], c["up5"]
    scale_out = c["scalars"][0:1, :]
    lane = lanes_of((1, 128))
    spot = lane % 64
    out_row = aff[55:56, :]
    out_bias = jnp.where(spot < TD, jnp.where(lane < 64, pltpu.roll(out_row, 64, 1), out_row), 0.0)
    length = c["length"][0]
    segment = inner // 16

    def to_feature(q, start, rows, carry):
        here = pl.ds(start, rows)
        act[0, here, 0:128] = mish_fast(pre[0, here, :] * kept[0] + kept[1]).astype(BF)
        return carry

    sweep(1, inner, to_feature, 0)
    dv = c["dv"]
    dv[0, :, 0:128] = jnp.dot(act[0, :, 0:128], c["wout"][...], preferred_element_type=F32)

    def to_loss(q, start, rows, state):
        here = pl.ds(start, rows)
        shape = (rows, 128)
        place = rows_of(shape) + start
        lanes = lanes_of(shape)
        frame = (place % 16 + jnp.where(lanes >= 64, 16, 0)) * segment + place // 16
        weight = jnp.where((frame < length) & (lanes % 64 < TD), 1.0, 0.0)
        difference = weight * (dv[0, here, 0:128] + out_bias - c["noise"][here, :])
        grad = 2.0 * difference * scale_out
        low[0, here, 0:128] = grad.astype(BF)
        return state[0] + fold_rows(difference * difference), state[1] + fold_rows(grad)

    zero = jnp.zeros((8, 128), F32)
    loss, out_sum = sweep(1, inner, to_loss, (zero, zero))
    c["loss"][...] = loss * scale_out
    out_sum = both_halves(down_one_row(out_sum))
    c["gout"][...] = lax.dot_general(act[0, :, 0:128], low[0, :, 0:128], TN, preferred_element_type=F32)
    dv[0, :, 0:128] = lax.dot_general(low[0, :, 0:128], c["wout"][...], NT, preferred_element_type=F32)
    dy = c["dy"].at[0:1, :, 0:128]
    got = norm_backward(
        c, 12, pre, head_vector(aff, 1), counts_of(2 * inner, 6), True, lambda q, here: dv[q, here, 0:128], dy
    )
    grads[54:55, :] = jnp.where(lane < 64, got[0], got[1])
    grads[55:56, :] = jnp.where(lane < 64, got[2], jnp.where(spot < TD, out_sum, 0.0))

    def emit_head(q, value):
        up[0] = value

    need("one6", "x6")
    conv_dx(dy, c["one6"], 128, inner, None, emit_head)
    conv_dw([c["x6"]], dy, inner, None, c["acc"])
    for k in range(KSIZE):
        c["pairs"][64 * k : 64 * k + 64, :] = fold_pairs(c["acc"], k, 64, 64)
    pack_pairs(c["pairs"], c["table"], HEAD_ROW - LATE_START, 160)
    c["tgrad"][...] = jnp.zeros_like(c["tgrad"])
    need("pre_a5", "pre_b5", "one5", "two5", "res5", "x5", "x2")
    backward_block(5, c, LATE_START)
    need("pre_a4", "pre_b4", "one4", "two4", "res4", "x4", "x3")
    backward_block(4, c, LATE_START)
    need("pre_a3", "pre_b3", "one3", "two3")
    backward_block(3, c, LATE_START)
    need(*list(copies))
    outs = []
    for number, name in enumerate(("table", "up1", "up2", "tgrad", "agrad")):
        copy = pltpu.make_async_copy(c[name], c["out_" + name], c["sems"].at[len(loaded) + number])
        copy.start()
        outs.append(copy)
    for copy in outs:
        copy.wait()


def early_kernel(loaded, names, *refs):
    c = dict(zip(names, refs))
    copies = load_all(c, loaded, c["sems"])
    aff, grads, table = c["aff"], c["agrad"], c["table"]
    late_copy = pltpu.make_async_copy(
        c["in_late"], table.at[pl.ds(LATE_START, LATE_ROWS), :], c["sems"].at[len(loaded) + 4]
    )
    late_copy.start()

    def need(*wanted):
        for name in wanted:
            copy = copies.pop(name, None)
            if copy is not None:
                copy.wait()

    need("stats", "terms", "kept", "agrad", "tgrad", "up2", "pre_b2", "two2", "pre_a2", "one2", "res2", "x2", "up1")
    late_copy.wait()
    backward_block(2, c, 0)
    need("pre_a1", "pre_b1", "one1", "two1", "res1", "x1")
    backward_block(1, c, 0)
    need("pre_a0", "pre_b0", "one0", "two0", "res0", "x0")
    backward_block(0, c, 0)
    need(*list(copies))
    total = jnp.zeros((8, TE), F32)
    row = rows_of((8, 256))
    for block in range(6):
        lanes = LAYER_OUT[block][1]
        first = jnp.where(rows_of((8, lanes)) == 0, c["tgrad"][8 * block : 8 * block + 8, 0:lanes], 0.0)
        if WIDTHS[block][1] == 64:
            first = jnp.where(lanes_of((8, lanes)) < 64, first, 0.0)
        total = total + exact_dot(first, c["proj"][TE * block : TE * block + TE, 0:lanes], NT)
    kept = c["kept"]
    hidden_pre, hidden = kept[0:8, :], kept[8:16, :]
    feature_pre = kept[16:24, 0:128]
    grad_feature = total * mish_both(feature_pre)[1]
    pairs = c["pairs"]
    second = exact_dot(jnp.where(row == 0, hidden, 0.0), grad_feature, TN)
    put_vector(grads, 58, 128, grad_feature[0:1, :])
    grad_hidden = exact_dot(grad_feature, c["embed_two"][...], NT) * mish_both(hidden_pre)[1]
    only = jnp.where(row == 0, grad_hidden, 0.0)
    first = exact_dot(c["sinus"][...], only, TN)
    put_vector(grads, 56, 256, grad_hidden[0:1, :])
    grads[60:61, :] = down_one_row(c["loss"][...])
    table[OUT_ROW : OUT_ROW + 12, :] = c["hograd"][0:12, :]
    table[FLAT_ROWS:TABLE_ROWS, :] = jnp.zeros((TABLE_ROWS - FLAT_ROWS, 128), F32)
    pairs[1024:1040, :] = jnp.zeros((16, 128), F32)
    pairs[0:1, :] = c["hograd"][11:12, :]
    for half in range(2):
        value = first[:, 128 * half : 128 * half + 128]
        pairs[pl.ds(1 + 2 * half, TE, stride=4), :] = value
        pairs[pl.ds(2 + 2 * half, TE, stride=4), :] = pltpu.roll(value, 64, 1)
    pairs[pl.ds(513, TH, stride=2), :] = second
    pairs[pl.ds(514, TH, stride=2), :] = pltpu.roll(second, 64, 1)
    pack_pairs(pairs, table, EMB_ROW, FLAT_ROWS - EMB_ROW)
    core = c["core"][0]
    keep, send = c["keep"], c["send"]
    share = NKER_ROWS
    step = 32

    for pair in range(4):

        def split(index, carry):
            at = pl.multiple_of(index * step, step)
            even = table[pl.ds(share * (2 * pair) + at, step), :]
            odd = table[pl.ds(share * (2 * pair + 1) + at, step), :]
            keep[pair, pl.ds(at, step), :] = jnp.where(core == 0, even, odd)
            send[pair, pl.ds(at, step), :] = jnp.where(core == 0, odd, even).astype(BF)
            return carry

        lax.fori_loop(0, OWN_ROWS // step, split, 0)
    outs = []
    for number, name in enumerate(("send", "keep", "agrad")):
        copy = pltpu.make_async_copy(c[name], c["out_" + name], c["sems"].at[len(loaded) + number])
        copy.start()
        outs.append(copy)
    for copy in outs:
        copy.wait()


def shape_table(inner):
    padded = inner + 2 * HALO
    table = {
        "x0": ((1, padded, 128), BF),
        "x1": ((1, padded, 128), BF),
        "x2": ((2, padded, 128), BF),
        "x3": ((2, padded, 256), BF),
        "x4": ((2, padded, 256), BF),
        "x5": ((2, padded, 128), BF),
        "x6": ((1, padded, 128), BF),
        "stats": ((104, 256), F32),
        "terms": ((48, 256), F32),
        "tgrad": ((48, 256), F32),
        "kept": ((32, 256), F32),
        "proj": ((6 * TE, 256), F32),
        "embed_two": ((256, 128), F32),
        "agrad": ((64, 128), F32),
        "flat": ((FLAT_ROWS, 128), F32),
        "pairs": ((2048, 128), F32),
        "table": ((TABLE_ROWS, 128), F32),
        "send": ((4, OWN_ROWS, 128), BF),
        "keep": ((4, OWN_ROWS, 128), F32),
        "acc": ((512, 1536), F32),
        "side": ((2, inner, 256), F32),
        "dv": ((2, inner, 256), F32),
        "low": ((2, inner, 256), BF),
        "act": ((2, inner, 256), BF),
        "noise": ((inner, 128), F32),
    }
    for block in range(7):
        halves, lanes = LAYER_OUT[block]
        table[f"pre_a{block}"] = ((halves, inner, lanes), F32)
        table[f"one{block}"] = (W_ONE[block], BF)
        if block < 6:
            table[f"up{block}"] = ((halves, inner, lanes), F32)
            table[f"pre_b{block}"] = ((halves, inner, lanes), F32)
            table[f"two{block}"] = (W_TWO[block], BF)
            if W_RES[block] is not None:
                table[f"res{block}"] = (W_RES[block], BF)
    for stem in ("hid", "dy", "ey"):
        table[stem] = ((2, padded, 256), BF)
    return table


def run_kernel(body, vmem_in, smem_in, any_in, outs_vmem, outs_any, scratch, sems, table, cost):
    names = list(vmem_in) + list(smem_in) + ["in_" + n for n in any_in]
    operands = list(vmem_in.values()) + list(smem_in.values()) + list(any_in.values())
    in_specs = (
        [pl.BlockSpec(memory_space=pltpu.VMEM)] * len(vmem_in)
        + [pl.BlockSpec(memory_space=pltpu.SMEM)] * len(smem_in)
        + [pl.BlockSpec(memory_space=pl.ANY)] * len(any_in)
    )
    out_shape, out_specs = [], []
    for name, (shape, kind) in outs_vmem.items():
        names.append(name)
        out_shape.append(jax.ShapeDtypeStruct(shape, kind))
        out_specs.append(pl.BlockSpec(memory_space=pltpu.VMEM))
    for name in outs_any:
        names.append("out_" + name)
        out_shape.append(jax.ShapeDtypeStruct(*table[name]))
        out_specs.append(pl.BlockSpec(memory_space=pl.ANY))
    buffers = []
    for name in scratch:
        names.append(name)
        buffers.append(pltpu.VMEM(*table[name]))
    names.append("sems")
    buffers.append(pltpu.SemaphoreType.DMA((sems,)))
    results = pl.pallas_call(
        functools.partial(body, names),
        out_shape=out_shape,
        in_specs=in_specs,
        out_specs=out_specs,
        scratch_shapes=buffers,
        compiler_params=pltpu.CompilerParams(vmem_limit_bytes=VMEM_LIMIT),
        cost_estimate=pl.CostEstimate(flops=cost, bytes_accessed=40000000, transcendentals=0),
    )(*operands)
    return dict(zip(list(outs_vmem) + list(outs_any), results))


VMEM_LIMIT = 67043328


def whole_horizon(noisy, noise, length, loss_scale, sinus, core, kernels, affine):
    frames = noisy.shape[0]
    inner = frames // 2
    segment = frames // 32
    table = shape_table(inner)

    def packed(values):
        cells = values.reshape(2, 16, segment, TD).transpose(2, 1, 0, 3)
        cells = jnp.pad(cells, ((0, 0), (0, 0), (0, 0), (0, 64 - TD)))
        return cells.reshape(inner, 128)

    flat = jnp.pad(kernels, (0, FLAT_ROWS * 128 - kernels.shape[0])).reshape(FLAT_ROWS, 128)
    aff = jnp.concatenate(
        [affine[:7127], jnp.zeros((41,), F32), affine[7127:], jnp.zeros((640,), F32)]
    ).reshape(64, 128)
    head_out = kernels[OUT_START : OUT_START + C1 * TD].reshape(C1, TD).astype(BF)
    wide_out = jnp.pad(head_out, ((0, 0), (0, 64 - TD)))
    nothing = jnp.zeros((C1, 64), BF)
    wout = jnp.concatenate(
        [jnp.concatenate([wide_out, nothing], axis=1), jnp.concatenate([nothing, wide_out], axis=1)], axis=0
    )
    weights = [n for n in table if n[:3] in ("one", "two", "res") and n[3:].isdigit()]
    saved = [n for n in table if n.startswith("pre_") or (n[0] == "x" and n[1:].isdigit())]
    saved += weights + ["stats", "terms", "kept", "proj", "embed_two"]
    kept = run_kernel(
        forward_kernel,
        {"noisy": packed(noisy).astype(BF), "aff": aff, "sinus": sinus},
        {},
        {"flat": flat},
        {},
        saved,
        saved + ["flat", "pairs", "side", "hid"],
        16 + len(saved),
        table,
        14000000000,
    )
    late_table = dict(table)
    late_table["table"] = ((LATE_ROWS, 128), F32)
    late_in = ["stats", "terms", "kept", "pre_a6", "noise", "one6", "x6"]
    late_in += ["pre_b5", "two5", "pre_a5", "one5", "res5", "x5", "x2"]
    late_in += ["pre_b4", "two4", "pre_a4", "one4", "res4", "x4", "x3"]
    late_in += ["pre_b3", "two3", "pre_a3", "one3"]
    sources = dict(kept, noise=packed(noise))
    late_out = ["table", "up1", "up2", "tgrad", "agrad"]
    late = run_kernel(
        functools.partial(late_kernel, late_in),
        {"aff": aff, "wout": wout, "scalars": jnp.broadcast_to(loss_scale, (8, 128))},
        {"length": length.reshape(1)},
        {n: sources[n] for n in late_in},
        {"loss": ((8, 128), F32), "gout": ((128, 128), F32)},
        late_out,
        late_in + late_out + ["up5", "up4", "up3", "dv", "low", "act", "acc", "pairs"]
        + ["dy", "ey"],
        len(late_in) + len(late_out),
        late_table,
        16000000000,
    )
    sources.update(late)
    gout = late["gout"]
    head_grad = (gout[0:64, 0:TD] + gout[64:128, 64 : 64 + TD]).reshape(-1)
    early_in = ["stats", "terms", "kept", "agrad", "tgrad", "up2", "pre_b2", "two2", "pre_a2", "one2", "res2", "x2", "up1"]
    early_in += ["pre_b1", "two1", "pre_a1", "one1", "res1", "x1"]
    early_in += ["pre_b0", "two0", "pre_a0", "one0", "res0", "x0", "proj", "embed_two"]
    any_in = {n: sources[n] for n in early_in}
    any_in["late"] = late["table"]
    early = run_kernel(
        functools.partial(early_kernel, early_in),
        {
            "aff": aff,
            "sinus": jnp.where(jnp.arange(8)[:, None] == 0, sinus, 0.0),
            "loss": late["loss"],
            "hograd": jnp.pad(head_grad, (0, 2048 - C1 * TD)).reshape(16, 128),
        },
        {"core": core.reshape(1)},
        any_in,
        {},
        ["send", "keep", "agrad"],
        early_in + ["table", "send", "keep", "up0", "dv", "low", "act", "acc", "pairs"]
        + ["dy", "ey"],
        len(early_in) + 5,
        table,
        10000000000,
    )
    return early["send"], early["keep"], early["agrad"]


def on_device_xla(
    trajectories,
    dim_means,
    dim_stds,
    noise_draw,
    diffusion_steps,
    valid_mask,
    kernels,
    affine,
    kernel_momentum,
    kernel_average,
    affine_momentum,
    affine_average,
):
    members_all = unpack(kernels, affine)
    valid_total = lax.psum(jnp.sum(valid_mask.astype(jnp.float32)), ("dp", "hor"))
    signal_now = signal_level(diffusion_steps)[:, None, None]
    clean_frames = (trajectories - dim_means) / dim_stds
    noisy_frames = jnp.sqrt(signal_now) * clean_frames + jnp.sqrt(1.0 - signal_now) * noise_draw

    ring = lax.axis_size("hor")
    axis = "hor"
    if trajectories.shape[0] % ring == 0:
        axis = None
        local = trajectories.shape[0] // ring
        part = lax.axis_index("hor") * local
        low_frames = noisy_frames.astype(jnp.bfloat16)
        noisy_frames = lax.all_to_all(low_frames, "hor", 0, 1, tiled=True).astype(jnp.float32)
        noise_draw = lax.all_to_all(noise_draw, "hor", 0, 1, tiled=True)
        valid_mask = lax.all_to_all(valid_mask, "hor", 0, 1, tiled=True)
        diffusion_steps = lax.dynamic_slice_in_dim(diffusion_steps, part, local)

    def time_closed(kernel_flat, affine_flat):
        return time_parts(kernel_flat, affine_flat, diffusion_steps)

    time_list, time_pullback = jax.vjp(time_closed, kernels, affine)
    down_one, kept_one = block_forward(noisy_frames, members_all[0], time_list[0], axis)
    down_two, kept_two = block_forward(down_one, members_all[1], time_list[1], axis)
    down_three, kept_three = block_forward(down_two, members_all[2], time_list[2], axis)
    middle, kept_middle = block_forward(down_three, members_all[3], time_list[3], axis)
    up_one, kept_upper = block_forward(
        jnp.concatenate([middle, down_three], axis=2), members_all[4], time_list[4], axis)
    up_two, kept_lower = block_forward(
        jnp.concatenate([up_one, down_two], axis=2), members_all[5], time_list[5], axis)
    predicted, kept_head = head_forward(up_two, members_all[6], axis)
    weight_rows = valid_mask.astype(jnp.float32)[:, :, None]
    difference = predicted - noise_draw
    loss_scale = 1.0 / (valid_total * TD)
    loss_part = jnp.sum(weight_rows * difference * difference) * loss_scale
    grad_predicted = 2.0 * weight_rows * difference * loss_scale
    grad_up_two, head_grads = head_backward(grad_predicted, kept_head, members_all[6], axis)
    grad_joined, time_six, grads_six = block_backward(grad_up_two, kept_lower, members_all[5], axis)
    grad_up_one = grad_joined[:, :, :C2]
    grad_down_two = grad_joined[:, :, C2:]
    grad_joined, time_five, grads_five = block_backward(grad_up_one, kept_upper, members_all[4], axis)
    grad_middle = grad_joined[:, :, :C3]
    grad_down_three = grad_joined[:, :, C3:]
    grad_inputs, time_four, grads_four = block_backward(grad_middle, kept_middle, members_all[3], axis)
    grad_inputs, time_three, grads_three = block_backward(
        grad_down_three + grad_inputs, kept_three, members_all[2], axis
    )
    grad_inputs, time_two, grads_two = block_backward(
        grad_down_two + grad_inputs, kept_two, members_all[1], axis
    )
    grad_inputs, time_one, grads_one = block_backward(grad_inputs, kept_one, members_all[0], axis)
    kernel_grad, affine_grad = pack_flat(
        [grads_one, grads_two, grads_three, grads_four, grads_five, grads_six, head_grads]
    )
    time_kernel, time_affine = time_pullback(
        (time_one, time_two, time_three, time_four, time_five, time_six)
    )
    kernel_grad = kernel_grad + time_kernel
    affine_grad = affine_grad + time_affine
    share_len = kernels.shape[0] // lax.axis_size("dp")
    owner_start = lax.axis_index("dp") * share_len
    kernel_sum, affine_sum, noise_loss = lax.psum(
        (kernel_grad, affine_grad, loss_part), ("dp", "hor")
    )
    kernel_own = lax.dynamic_slice_in_dim(kernel_sum, owner_start, share_len)
    squares = jnp.sum(kernel_sum * kernel_sum) + jnp.sum(affine_sum * affine_sum)
    grad_norm = jnp.sqrt(squares)
    factor = jnp.minimum(1.0, MAX_NORM / (grad_norm + 1e-06))
    kernel_step = kernel_own * factor
    kernel_old = lax.dynamic_slice_in_dim(kernels, owner_start, share_len)
    kernel_mom_new = MOMENTUM * kernel_momentum + kernel_step
    kernel_new = kernel_old - LEARN_RATE * (kernel_step + MOMENTUM * kernel_mom_new)
    kernel_ema_new = EMA_DECAY * kernel_average + (1.0 - EMA_DECAY) * kernel_new
    affine_step = affine_sum * factor
    affine_mom_new = MOMENTUM * affine_momentum + affine_step
    affine_new = affine - AFFINE_RATE * (affine_step + MOMENTUM * affine_mom_new)
    affine_ema_new = EMA_DECAY * affine_average + (1.0 - EMA_DECAY) * affine_new
    return (
        noise_loss,
        grad_norm,
        kernel_new,
        kernel_mom_new,
        kernel_ema_new,
        kernel_new.astype(jnp.bfloat16),
        affine_new,
        affine_mom_new,
        affine_ema_new,
        affine_new.astype(jnp.bfloat16),
    )


def swap(value, axis, bit):
    return lax.ppermute(value, axis, [(i, i ^ bit) for i in range(lax.axis_size(axis))])


def total_over(value, hops):
    for axis, bit in hops:
        value = value + swap(value, axis, bit)
    return value


def bits_of(axis):
    return [(axis, 1 << n) for n in range(lax.axis_size(axis).bit_length() - 1)]


def pick(stack, index):
    return lax.dynamic_index_in_dim(stack, index, 0, keepdims=False)


def share_sums(send, keep, small):
    low = jnp.bfloat16
    place = lax.axis_index("dp")
    seat_x = (place >> 1) & 1
    seat_y = (place >> 2) & 1
    layer = lax.axis_index("hor")
    part_rows = OWN_ROWS // 4
    pairs = keep + swap(send, "dp", 1).astype(jnp.float32)
    small = small + swap(small, "dp", 1)
    half = OWN_ROWS // 2
    grid = pairs.reshape(2, 2, OWN_ROWS, 128)
    first, second = grid[:, :, :half], grid[:, :, half:]
    first_out = lax.dynamic_index_in_dim(first, 1 - seat_x, 1, keepdims=False).astype(low)
    second_out = lax.dynamic_index_in_dim(second, 1 - seat_y, 0, keepdims=False).astype(low)
    first_in = swap(first_out, "dp", 2)
    second_in = swap(second_out, "dp", 4)
    small = small + swap(small, "dp", 2)
    first = lax.dynamic_index_in_dim(first, seat_x, 1, keepdims=False) + first_in.astype(jnp.float32)
    second = lax.dynamic_index_in_dim(second, seat_y, 0, keepdims=False) + second_in.astype(jnp.float32)
    first_in = swap(pick(first, 1 - seat_y).astype(low), "dp", 4)
    second_in = swap(pick(second, 1 - seat_x).astype(low), "dp", 2)
    small = small + swap(small, "dp", 4)
    own = jnp.concatenate(
        [
            pick(first, seat_y) + first_in.astype(jnp.float32),
            pick(second, seat_x) + second_in.astype(jnp.float32),
        ],
        axis=0,
    ).reshape(4, part_rows, 128)
    arrived = [swap(pick(own, layer ^ bits).astype(low), "hor", bits) for bits in (1, 2, 3)]
    small = total_over(small, bits_of("hor"))
    part = pick(own, layer)
    for value in arrived:
        part = part + value.astype(jnp.float32)
    part_low = part.astype(low)
    parts = jnp.stack([part_low] + [swap(part_low, "hor", bits) for bits in (1, 2, 3)])
    whole = jnp.concatenate([pick(parts, layer ^ n) for n in range(4)], axis=0)
    return part, whole, small


def on_device(
    trajectories,
    dim_means,
    dim_stds,
    noise_draw,
    diffusion_steps,
    valid_mask,
    kernels,
    affine,
    kernel_momentum,
    kernel_average,
    affine_momentum,
    affine_average,
):
    ring = lax.axis_size("hor")
    frames = trajectories.shape[1] * ring
    if trajectories.shape[0] != ring or ring != 4 or frames % 512 or lax.axis_size("dp") != 8:
        return on_device_xla(
            trajectories,
            dim_means,
            dim_stds,
            noise_draw,
            diffusion_steps,
            valid_mask,
            kernels,
            affine,
            kernel_momentum,
            kernel_average,
            affine_momentum,
            affine_average,
        )
    signal_all = signal_level(diffusion_steps)[:, None, None]
    clean_frames = (trajectories - dim_means) / dim_stds
    noisy_frames = jnp.sqrt(signal_all) * clean_frames + jnp.sqrt(1.0 - signal_all) * noise_draw
    counts = jnp.sum(valid_mask, axis=1)
    noisy = lax.all_to_all(noisy_frames.astype(jnp.bfloat16), "hor", 0, 1, tiled=True)[0]
    noise = lax.all_to_all(noise_draw, "hor", 0, 1, tiled=True)[0]
    length = jnp.sum(lax.all_to_all(counts, "hor", 0, 0, tiled=True))
    valid_total = total_over(length.astype(jnp.float32), bits_of("hor") + bits_of("dp"))
    own_step = lax.dynamic_slice_in_dim(diffusion_steps, lax.axis_index("hor"), 1)
    sinus = jnp.broadcast_to(sinusoid(own_step), (8, TE))
    loss_scale = 1.0 / (valid_total * TD)
    place = lax.axis_index("dp")
    send, keep, small = whole_horizon(
        noisy, noise, length, loss_scale, sinus, place & 1, kernels, affine
    )
    part, whole, small = share_sums(send, keep, small)
    share_len = kernels.shape[0] // lax.axis_size("dp")
    owner_start = place * share_len
    lead = owner_start - place * NKER_ROWS * 128
    number = (
        lax.axis_index("hor") * part.size
        + lax.broadcasted_iota(jnp.int32, part.shape, 0) * 128
        + lax.broadcasted_iota(jnp.int32, part.shape, 1)
    )
    inside = (number >= lead) & (number < lead + share_len)
    squares = total_over(jnp.sum(jnp.where(inside, part * part, 0.0)), bits_of("dp") + bits_of("hor"))
    small_flat = small.reshape(-1)
    affine_sum = jnp.concatenate([small_flat[:7127], small_flat[7168:7552]])
    noise_loss = jnp.sum(small[60])
    grad_norm = jnp.sqrt(squares + jnp.sum(affine_sum * affine_sum))
    kernel_own = lax.dynamic_slice_in_dim(whole.astype(jnp.float32).reshape(-1), lead, share_len)
    factor = jnp.minimum(1.0, MAX_NORM / (grad_norm + 1e-06))
    kernel_step = kernel_own * factor
    kernel_old = lax.dynamic_slice_in_dim(kernels, owner_start, share_len)
    kernel_mom_new = MOMENTUM * kernel_momentum + kernel_step
    kernel_new = kernel_old - LEARN_RATE * (kernel_step + MOMENTUM * kernel_mom_new)
    kernel_ema_new = EMA_DECAY * kernel_average + (1.0 - EMA_DECAY) * kernel_new
    affine_step = affine_sum * factor
    affine_mom_new = MOMENTUM * affine_momentum + affine_step
    affine_new = affine - AFFINE_RATE * (affine_step + MOMENTUM * affine_mom_new)
    affine_ema_new = EMA_DECAY * affine_average + (1.0 - EMA_DECAY) * affine_new
    return (
        noise_loss,
        grad_norm,
        kernel_new,
        kernel_mom_new,
        kernel_ema_new,
        kernel_new.astype(jnp.bfloat16),
        affine_new,
        affine_mom_new,
        affine_ema_new,
        affine_new.astype(jnp.bfloat16),
    )


def solution(mesh):
    in_specs = (
        P("dp", "hor", None),
        P(),
        P(),
        P("dp", "hor", None),
        P("dp"),
        P("dp", "hor"),
        P(),
        P(),
        P("dp"),
        P("dp"),
        P(),
        P(),
    )
    out_specs = (P(), P(), P("dp"), P("dp"), P("dp"), P("dp"), P(), P(), P(), P())
    return jax.shard_map(
        on_device, mesh=mesh, in_specs=in_specs, out_specs=out_specs, check_vma=False
    )
```

```python
import functools
import math

import jax
import jax.numpy as jnp
from jax import lax
from jax.experimental import pallas as pl
from jax.experimental.pallas import tpu as pltpu
from jax.sharding import PartitionSpec as P

TD = 23
C1 = 64
C2 = 128
C3 = 256
TE = 128
TH = 256
KSIZE = 5
GROUPS = 8
NSTEPS = 100


PRECISE = lax.Precision.HIGHEST
EPSILON = 1e-05
MAX_NORM = 0.02
LEARN_RATE = 200.0
AFFINE_RATE = 1500.0
MOMENTUM = 0.9
EMA_DECAY = 0.5


def padded_2(cells, sides, width):
    for axis, dim in sides:
        if axis is None:
            pads = [(0, 0)] * cells.ndim
            pads[dim] = (width, width)
            cells = jnp.pad(cells, pads)
            continue
        count = lax.axis_size(axis)
        ends = count - 1
        head = lax.slice_in_dim(cells, 0, width, axis=dim)
        tail = lax.slice_in_dim(cells, cells.shape[dim] - width, cells.shape[dim], axis=dim)
        cells = jnp.concatenate(
            [
                lax.ppermute(tail, axis, [(i, (i + 1) % count) for i in range(ends)]),
                cells,
                lax.ppermute(head, axis, [((i + 1) % count, i) for i in range(ends)]),
            ],
            axis=dim,
        )
    return cells


def sum_over(values, axis):
    return values if axis is None else lax.psum(values, axis)


def axis_length(axis):
    return 1 if axis is None else lax.axis_size(axis)


def layout_shapes():
    kernel_shapes = []
    affine_shapes = []
    for width_in, width_out in [
        (TD, C1),
        (C1, C2),
        (C2, C3),
        (C3, C3),
        (C3 + C3, C2),
        (C2 + C2, C1),
    ]:
        matrices = [
            ("conv_one", KSIZE * width_in, width_out),
            ("conv_two", KSIZE * width_out, width_out),
            ("time_proj", TE, width_out),
        ]
        vectors = [
            (entry_name, width_out)
            for entry_name in [
                "bias_one",
                "gain_one",
                "shift_one",
                "time_bias",
                "bias_two",
                "gain_two",
                "shift_two",
            ]
        ]
        if width_in != width_out:
            matrices.append(("res_proj", width_in, width_out))
            vectors.append(("res_bias", width_out))
        kernel_shapes.append(matrices)
        affine_shapes.append(vectors)
    kernel_shapes.append(
        [
            ("head_conv", KSIZE * C1, C1),
            ("head_out", C1, TD),
            ("embed_one", TE, TH),
            ("embed_two", TH, TE),
        ]
    )
    affine_shapes.append(
        [
            ("head_bias", C1),
            ("head_gain", C1),
            ("head_shift", C1),
            ("out_bias", TD),
            ("embed_bias_one", TH),
            ("embed_bias_two", TE),
        ]
    )
    return (kernel_shapes, affine_shapes)


def unpack(kernels, affine):
    kernel_shapes, affine_shapes = layout_shapes()
    members_all = []
    cursor = 0
    for entries in kernel_shapes:
        members = {}
        for entry_name, height, breadth in entries:
            members[entry_name] = kernels[cursor : cursor + height * breadth].reshape(
                height, breadth
            )
            cursor += height * breadth
        members_all.append(members)
    cursor = 0
    for position, entries in enumerate(affine_shapes):
        for entry_name, length in entries:
            members_all[position][entry_name] = affine[cursor : cursor + length]
            cursor += length
    return members_all


def pack_flat(grad_list):
    kernel_shapes, affine_shapes = layout_shapes()
    kernel_pieces = []
    affine_pieces = []
    for position, entries in enumerate(kernel_shapes):
        for entry_name, height, breadth in entries:
            kernel_pieces.append(
                grad_list[position]
                .get(entry_name, jnp.zeros((height, breadth), jnp.float32))
                .reshape(-1)
            )
    for position, entries in enumerate(affine_shapes):
        for entry_name, length in entries:
            affine_pieces.append(
                grad_list[position].get(entry_name, jnp.zeros((length,), jnp.float32))
            )
    return (jnp.concatenate(kernel_pieces), jnp.concatenate(affine_pieces))


def mish_act(value):
    return value * jnp.tanh(jax.nn.softplus(value))


def mish_grad(value, upstream):
    return jax.vjp(mish_act, value)[1](upstream)[0]


def sinusoid(steps_vec):
    half_width = TE // 2
    ladder = jnp.exp(
        -math.log(10000.0) * jnp.arange(half_width).astype(jnp.float32) / (half_width - 1)
    )
    angles = steps_vec.astype(jnp.float32)[:, None] * ladder[None, :]
    return jnp.concatenate([jnp.sin(angles), jnp.cos(angles)], axis=1)


def signal_level(steps_vec):
    ratio = (steps_vec.astype(jnp.float32) + 1.0) / NSTEPS
    cosine_now = jnp.cos((ratio + 0.008) / 1.008 * math.pi / 2)
    cosine_zero = math.cos(0.008 / 1.008 * math.pi / 2)
    return (cosine_now / cosine_zero) ** 2


def time_parts(kernel_flat, affine_flat, steps_vec):
    members_all = unpack(kernel_flat, affine_flat)
    last_group = members_all[6]
    hidden = mish_act(
        jnp.dot(sinusoid(steps_vec), last_group["embed_one"], precision=PRECISE)
        + last_group["embed_bias_one"]
    )
    feature = mish_act(
        jnp.dot(hidden, last_group["embed_two"], precision=PRECISE) + last_group["embed_bias_two"]
    )
    return tuple(
        (
            jnp.dot(feature, members_all[block_index]["time_proj"], precision=PRECISE)
            + members_all[block_index]["time_bias"]
            for block_index in range(6)
        )
    )


def conv_forward(inputs_low, weight_low, axis):
    padded = padded_2(inputs_low, ((axis, 1),), 2)
    frames = inputs_low.shape[1]
    channels = inputs_low.shape[2]
    running = 0.0
    for offset in range(KSIZE):
        running = running + jnp.einsum(
            "blc,cd->bld",
            padded[:, offset : offset + frames],
            weight_low[offset * channels : (offset + 1) * channels],
            preferred_element_type=jnp.float32,
        )
    return (running, padded)


def conv_backward(grad_low, padded, weight_low, axis):
    grad_padded = padded_2(grad_low, ((axis, 1),), 2)
    frames = grad_low.shape[1]
    channels = padded.shape[2]
    pieces = []
    running = 0.0
    for offset in range(KSIZE):
        pieces.append(
            jnp.einsum(
                "blc,bld->cd",
                padded[:, offset : offset + frames],
                grad_low,
                preferred_element_type=jnp.float32,
            )
        )
        start_row = KSIZE - 1 - offset
        running = running + jnp.einsum(
            "bld,cd->blc",
            grad_padded[:, start_row : start_row + frames],
            weight_low[offset * channels : (offset + 1) * channels],
            preferred_element_type=jnp.float32,
        )
    return (running, jnp.concatenate(pieces, axis=0))


def group_norm(values, gain_vec, shift_vec, axis):
    horizons, frames, channels = values.shape
    grouped = values.reshape(horizons, frames, GROUPS, channels // GROUPS)
    sum_one, sum_two = sum_over(
        (jnp.sum(grouped, axis=(1, 3)), jnp.sum(grouped * grouped, axis=(1, 3))), axis
    )
    group_count = frames * axis_length(axis) * (channels // GROUPS)
    average = sum_one / group_count
    inverse = lax.rsqrt(sum_two / group_count - average * average + EPSILON)
    normed = ((grouped - average[:, None, :, None]) * inverse[:, None, :, None]).reshape(
        horizons, frames, channels
    )
    return (normed * gain_vec + shift_vec, (normed, inverse))


def group_norm_back(upstream, norm_stats, gain_vec, axis):
    normed, inverse = norm_stats
    horizons, frames, channels = normed.shape
    grad_gain = jnp.sum(upstream * normed, axis=(0, 1))
    grad_shift = jnp.sum(upstream, axis=(0, 1))
    scaled = (upstream * gain_vec).reshape(horizons, frames, GROUPS, channels // GROUPS)
    grouped = normed.reshape(horizons, frames, GROUPS, channels // GROUPS)
    sum_one, sum_two = sum_over(
        (jnp.sum(scaled, axis=(1, 3)), jnp.sum(scaled * grouped, axis=(1, 3))), axis
    )
    group_count = frames * axis_length(axis) * (channels // GROUPS)
    result = inverse[:, None, :, None] * (
        scaled
        - sum_one[:, None, :, None] / group_count
        - grouped * sum_two[:, None, :, None] / group_count
    )
    return (result.reshape(horizons, frames, channels), grad_gain, grad_shift)


def block_forward(inputs, members, time_term, axis):
    inputs_low = inputs.astype(jnp.bfloat16)
    weight_one = members["conv_one"].astype(jnp.bfloat16)
    weight_two = members["conv_two"].astype(jnp.bfloat16)
    conv_out, padded_one = conv_forward(inputs_low, weight_one, axis)
    normed_one, stats_one = group_norm(
        conv_out + members["bias_one"], members["gain_one"], members["shift_one"], axis
    )
    hidden = mish_act(normed_one) + time_term[:, None, :]
    conv_out, padded_two = conv_forward(hidden.astype(jnp.bfloat16), weight_two, axis)
    normed_two, stats_two = group_norm(
        conv_out + members["bias_two"], members["gain_two"], members["shift_two"], axis
    )
    result = mish_act(normed_two)
    if "res_proj" in members:
        weight_side = members["res_proj"].astype(jnp.bfloat16)
        result = (
            result
            + jnp.einsum("blc,cd->bld", inputs_low, weight_side, preferred_element_type=jnp.float32)
            + members["res_bias"]
        )
    else:
        weight_side = None
        result = result + inputs
    return (
        result,
        (
            padded_one,
            stats_one,
            padded_two,
            stats_two,
            inputs_low,
            weight_one,
            weight_two,
            weight_side,
        ),
    )


def block_backward(upstream, kept, members, axis):
    (
        padded_one,
        stats_one,
        padded_two,
        stats_two,
        inputs_low,
        weight_one,
        weight_two,
        weight_side,
    ) = kept
    grad_map = {}
    grad_normed = mish_grad(stats_two[0] * members["gain_two"] + members["shift_two"], upstream)
    grad_pre, grad_map["gain_two"], grad_map["shift_two"] = group_norm_back(
        grad_normed, stats_two, members["gain_two"], axis
    )
    grad_map["bias_two"] = jnp.sum(grad_pre, axis=(0, 1))
    grad_hidden, grad_map["conv_two"] = conv_backward(
        grad_pre.astype(jnp.bfloat16), padded_two, weight_two, axis
    )
    time_grad = jnp.sum(grad_hidden, axis=1)
    grad_normed = mish_grad(stats_one[0] * members["gain_one"] + members["shift_one"], grad_hidden)
    grad_pre, grad_map["gain_one"], grad_map["shift_one"] = group_norm_back(
        grad_normed, stats_one, members["gain_one"], axis
    )
    grad_map["bias_one"] = jnp.sum(grad_pre, axis=(0, 1))
    grad_inputs, grad_map["conv_one"] = conv_backward(
        grad_pre.astype(jnp.bfloat16), padded_one, weight_one, axis
    )
    if weight_side is not None:
        upstream_low = upstream.astype(jnp.bfloat16)
        grad_map["res_bias"] = jnp.sum(upstream, axis=(0, 1))
        grad_map["res_proj"] = jnp.einsum(
            "blc,bld->cd", inputs_low, upstream_low, preferred_element_type=jnp.float32
        )
        grad_inputs = grad_inputs + jnp.einsum(
            "bld,cd->blc", upstream_low, weight_side, preferred_element_type=jnp.float32
        )
    else:
        grad_inputs = grad_inputs + upstream
    return (grad_inputs, time_grad, grad_map)


def head_forward(inputs, members, axis):
    weight_conv = members["head_conv"].astype(jnp.bfloat16)
    weight_out = members["head_out"].astype(jnp.bfloat16)
    conv_out, padded = conv_forward(inputs.astype(jnp.bfloat16), weight_conv, axis)
    normed, norm_stats = group_norm(
        conv_out + members["head_bias"], members["head_gain"], members["head_shift"], axis
    )
    feature_low = mish_act(normed).astype(jnp.bfloat16)
    predicted = (
        jnp.einsum("blc,cd->bld", feature_low, weight_out, preferred_element_type=jnp.float32)
        + members["out_bias"]
    )
    return (predicted, (padded, norm_stats, feature_low, weight_conv, weight_out))


def head_backward(upstream, kept, members, axis):
    padded, norm_stats, feature_low, weight_conv, weight_out = kept
    grad_map = {}
    upstream_low = upstream.astype(jnp.bfloat16)
    grad_map["out_bias"] = jnp.sum(upstream, axis=(0, 1))
    grad_map["head_out"] = jnp.einsum(
        "blc,bld->cd", feature_low, upstream_low, preferred_element_type=jnp.float32
    )
    grad_feature = jnp.einsum(
        "bld,cd->blc", upstream_low, weight_out, preferred_element_type=jnp.float32
    )
    grad_normed = mish_grad(
        norm_stats[0] * members["head_gain"] + members["head_shift"], grad_feature
    )
    grad_pre, grad_map["head_gain"], grad_map["head_shift"] = group_norm_back(
        grad_normed, norm_stats, members["head_gain"], axis
    )
    grad_map["head_bias"] = jnp.sum(grad_pre, axis=(0, 1))
    grad_inputs, grad_map["head_conv"] = conv_backward(
        grad_pre.astype(jnp.bfloat16), padded, weight_conv, axis
    )
    return (grad_inputs, grad_map)


BF = jnp.bfloat16
F32 = jnp.float32
HALO = 32
ROW_STARTS = (0, 293, 1445, 5797, 11173, 15013)
LOAD_ROWS = (0, 296, 1448, 5800, 11176, 15016, 16008, 16696)
HEAD_ROW = 16005
OUT_ROW = 16165
EMB_ROW = 16176
FLAT_ROWS = 16696
TABLE_ROWS = 16720
LATE_START = 5792
LATE_ROWS = 16168 - LATE_START
OWN_ROWS = 2112
NKER_ROWS = 2086
OUT_START = OUT_ROW * 128
WIDTHS = ((TD, C1), (C1, C2), (C2, C3), (C3, C3), (C3 + C3, C2), (C2 + C2, C1))
AFF_ROWS = (0, 4, 12, 28, 42, 50)
LAYER_OUT = ((1, 128), (2, 128), (2, 256), (2, 256), (2, 128), (1, 128), (1, 128))
W_ONE = ((640, 128), (640, 256), (640, 256), (1280, 256), (2560, 128), (2560, 128), (640, 128))
W_TWO = ((640, 128), (640, 128), (1280, 256), (1280, 256), (640, 128), (640, 128))
W_RES = ((128, 128), (128, 256), (128, 256), None, (512, 128), (512, 128))
TN = (((0,), (0,)), ((), ()))
NT = (((1,), (1,)), ((), ()))


def lanes_of(shape):
    return lax.broadcasted_iota(jnp.int32, shape, 1)


def rows_of(shape):
    return lax.broadcasted_iota(jnp.int32, shape, 0)


def fill_halo(ref):
    halves, padded_rows, lanes = ref.shape
    inner = padded_rows - 2 * HALO
    row = rows_of((16, lanes))
    lane = lanes_of((16, lanes))
    for group in range(2):
        start = inner + 16 * group
        moved = [pltpu.roll(ref[q, start : start + 16, :].astype(F32), 1, 0) for q in range(halves)]
        into = pl.ds(16 * group, 16)
        if halves == 1:
            edge = jnp.where(lane >= 64, pltpu.roll(moved[0], 64, 1), 0.0)
            ref[0, into, :] = jnp.where(row == 0, edge, moved[0]).astype(BF)
        else:
            ref[0, into, :] = jnp.where(row == 0, 0.0, moved[0]).astype(BF)
            ref[1, into, :] = jnp.where(row == 0, moved[0], moved[1]).astype(BF)
        start = HALO + 16 * group
        moved = [pltpu.roll(ref[q, start : start + 16, :].astype(F32), 15, 0) for q in range(halves)]
        into = pl.ds(HALO + inner + 16 * group, 16)
        if halves == 1:
            edge = jnp.where(lane < 64, pltpu.roll(moved[0], 64, 1), 0.0)
            ref[0, into, :] = jnp.where(row == 15, edge, moved[0]).astype(BF)
        else:
            ref[0, into, :] = jnp.where(row == 15, moved[1], moved[0]).astype(BF)
            ref[1, into, :] = jnp.where(row == 15, 0.0, moved[1]).astype(BF)


def exchange_kernel(traj, noise, mask, scale, mean, std, noisy_out, noise_out, counts, noisy_wide, noise_wide):
    pieces, frames, wide = traj.shape
    segment = frames // 8
    quarter = segment // 4
    rows = tile_rows(frames // 7) * 7 if frames % 7 == 0 else tile_rows(frames)

    for piece in range(pieces):

        def fill(index, carry):
            here = pl.ds(pl.multiple_of(index * rows, rows), rows)
            value = noise[piece, here, :]
            clean = (traj[piece, here, :] - mean[...]) / std[...]
            noisy_wide[here, 0:wide] = scale[piece : piece + 1, 0:wide] * clean + (
                scale[4 + piece : 5 + piece, 0:wide] * value
            )
            noise_wide[here, 0:wide] = value
            return carry

        lax.fori_loop(0, frames // rows, fill, 0)
        step = quarter // 2 if quarter % 4 == 0 else quarter

        def gather(index, carry):
            lane = lanes_of((8, 128))

            def one(source, place):
                total = 0.0
                for number in range(4):
                    value = source[pl.ds(quarter * number + place, 8, stride=segment), :]
                    value = jnp.where(lane < wide, value, 0.0)
                    total = total + (pltpu.roll(value, 32 * number, 1) if number else value)
                return total

            for inner in range(0, step, 2):
                place = index * step + inner
                at = pl.multiple_of(8 * place, 16)
                noisy_out[piece, pl.ds(at, 16), :] = jnp.concatenate(
                    [one(noisy_wide, place), one(noisy_wide, place + 1)], axis=0
                ).astype(BF)
                noise_out[piece, pl.ds(at, 8), :] = one(noise_wide, place)
                noise_out[piece, pl.ds(at + 8, 8), :] = one(noise_wide, place + 1)
            return carry

        lax.fori_loop(0, quarter // step, gather, 0)
        total = jnp.sum(mask[piece : piece + 1, :].astype(F32), axis=1, keepdims=True)
        counts[piece : piece + 1, :] = jnp.broadcast_to(total, (1, 128))


def take_apart(source, quarter, store):
    lane = lanes_of((16, 128))

    def step(index, carry):
        at = pl.multiple_of(16 * index, 16)
        got = [source[piece, pl.ds(at, 16), :].astype(F32) for piece in range(4)]
        for inner in range(2):
            here = slice(8 * inner, 8 * inner + 8)
            low = jnp.concatenate([got[0][here], got[1][here]], axis=0)
            high = jnp.concatenate([got[2][here], got[3][here]], axis=0)
            for number in range(4):
                left = pltpu.roll(low, (128 - 32 * number) % 128, 1) if number else low
                right = pltpu.roll(high, (192 - 32 * number) % 128, 1) if number != 2 else high
                value = jnp.where(lane < 64, left, right)
                store(quarter * number + 2 * index + inner, jnp.where(lane % 64 < 32, value, 0.0))
        return carry

    lax.fori_loop(0, quarter // 2, step, 0)


def mish_fast(value):
    grown = jnp.exp(jnp.minimum(value, 20.0))
    top = grown * (grown + 2.0)
    return value * (top / (top + 2.0))


def mish_both(value):
    grown = jnp.exp(jnp.minimum(value, 20.0))
    top = grown * (grown + 2.0)
    inverse = 1.0 / (top + 2.0)
    ratio = top * inverse
    slope = ratio + 4.0 * value * (top - grown) * (inverse * inverse)
    return value * ratio, slope


def fold_rows(value):
    rows, lanes = value.shape
    return jnp.sum(value.reshape(rows // 8, 8, lanes), axis=0)


def down_one_row(value):
    return jnp.sum(value, axis=0, keepdims=True)


def both_halves(row):
    return row + pltpu.roll(row, 64, 1)


def group_sums(first, second, packed):
    lanes = first.shape[1]
    row = rows_of((8, lanes))
    stacked = jnp.where(row == 0, first, jnp.where(row == 1, second, 0.0))
    left = rows_of((lanes, lanes))
    right = lanes_of((lanes, lanes))
    if packed:
        same = (left % 64) // 8 == (right % 64) // 8
    else:
        size = lanes // GROUPS
        same = left // size == right // size
    summed = jnp.dot(stacked, same.astype(F32), precision=PRECISE, preferred_element_type=F32)
    return summed[0:1, :], summed[1:2, :]


def tile_rows(inner):
    for rows in (256, 128, 64, 32, 16):
        if inner % rows == 0:
            return rows


def sweep(halves, inner, body, carry):
    rows = tile_rows(inner)
    per_half = inner // rows

    def step(index, state):
        q = index // per_half
        start = pl.multiple_of((index - q * per_half) * rows, rows)
        return body(q, start, rows, state)

    return lax.fori_loop(0, halves * per_half, step, carry)


def vector(aff, row, width):
    if width == 256:
        base = int(row)
        return jnp.concatenate([aff[base : base + 1, :], aff[base + 1 : base + 2, :]], axis=1)
    base = int(row)
    whole = aff[base : base + 1, :]
    if width == 128:
        return whole
    turned = pltpu.roll(whole, 64, 1)
    lane = lanes_of((1, 128))
    if row == base:
        return jnp.where(lane < 64, whole, turned)
    return jnp.where(lane < 64, turned, whole)


def block_vector(aff, block, number):
    width = WIDTHS[block][1]
    return vector(aff, AFF_ROWS[block] + number * width / 128, width)


def head_vector(aff, number):
    return vector(aff, 54 + number / 2, 64)


def conv_input(xs, q, tap, inner):
    parts = [x[q, pl.ds(16 * tap, inner), :] for x in xs]
    return parts[0] if len(parts) == 1 else jnp.concatenate(parts, axis=1)


def conv_to(xs, weight, bias, out, crossing):
    halves, inner, lanes = out.shape
    zero = jnp.zeros((8, lanes), F32)

    def finish(q, total, state):
        total = total + bias
        out[q] = total
        return state[0] + fold_rows(total), state[1] + fold_rows(total * total)

    if crossing == "up":
        wide = jnp.concatenate([conv_input(xs, 0, k, inner) for k in range(KSIZE)], axis=1)
        total = jnp.dot(wide, weight[...], preferred_element_type=F32)
        state = finish(0, total[:, :lanes], (zero, zero))
        return finish(1, total[:, lanes:], state)
    if crossing == "down":
        wide = jnp.concatenate(
            [conv_input(xs, q, k, inner) for k in range(KSIZE) for q in range(2)], axis=1
        )
        return finish(0, jnp.dot(wide, weight[...], preferred_element_type=F32), (zero, zero))

    def half(q, state):
        wide = jnp.concatenate([conv_input(xs, q, k, inner) for k in range(KSIZE)], axis=1)
        return finish(q, jnp.dot(wide, weight[...], preferred_element_type=F32), state)

    return lax.fori_loop(0, halves, half, (zero, zero))


def norm_fit(sums, gain, shift, count, packed, stats, layer):
    lanes = gain.shape[1]
    one = down_one_row(sums[0])
    two = down_one_row(sums[1])
    group_one, group_two = group_sums(one, two, packed)
    mean = group_one / count
    inverse = lax.rsqrt(group_two / count - mean * mean + EPSILON)
    scale = inverse * gain
    offset = shift - mean * scale
    for number, row in enumerate((scale, offset, mean, inverse, one)):
        stats[8 * layer + number : 8 * layer + number + 1, 0:lanes] = row
    return scale, offset


def norm_kept(stats, layer, lanes):
    return [stats[8 * layer + n : 8 * layer + n + 1, 0:lanes] for n in range(5)]


def norm_back_fit(sums, kept, gain, count, rows, packed):
    scale, _, mean, inverse, one = kept
    grad_shift = down_one_row(sums[0])
    grad_gain = inverse * (down_one_row(sums[1]) - mean * grad_shift)
    first, second = group_sums(gain * grad_shift, gain * grad_gain, packed)
    first = first / count
    second = second / count
    slope = -inverse * inverse * second
    level = -inverse * first - slope * mean
    grad_bias = scale * grad_shift + slope * one + level * rows
    if packed:
        grad_shift, grad_gain, grad_bias = [both_halves(v) for v in (grad_shift, grad_gain, grad_bias)]
    return slope, level, grad_bias, grad_gain, grad_shift


def in_steps(count, step, body):
    full = count // step

    def move(index, carry):
        body(pl.multiple_of(index * step, step), step)
        return carry

    if full > 1:
        lax.fori_loop(0, full, move, 0)
    elif full:
        body(0, step)
    if count % step:
        body(full * step, count % step)


def unpack_pairs(flat, start, count, out):
    def move(at, step):
        rows = flat[pl.ds(start + at, step), :]
        turned = pltpu.roll(rows, 64, 1)
        lane = lanes_of(rows.shape)
        out[pl.ds(2 * at, step, stride=2), :] = jnp.where(lane < 64, rows, turned)
        out[pl.ds(2 * at + 1, step, stride=2), :] = jnp.where(lane < 64, turned, rows)

    in_steps(count, 128, move)


def pack_pairs(source, out, start, count):
    def move(at, step):
        even = source[pl.ds(2 * at, step, stride=2), :]
        odd = pltpu.roll(source[pl.ds(2 * at + 1, step, stride=2), :], 64, 1)
        out[pl.ds(start + at, step), :] = jnp.where(lanes_of(even.shape) < 64, even, odd)

    in_steps(count, 128, move)


def spread_pairs(pairs, start, count, weight, to, size):
    rows = min(-(-count // 32) * 32, size)
    value = pairs[start : start + rows, :]
    keep = rows_of(value.shape) < count
    lane = lanes_of(value.shape)
    weight[to : to + rows, :] = jnp.where(keep & (lane < 64), value, 0.0).astype(BF)
    weight[to + size : to + size + rows, :] = jnp.where(keep & (lane >= 64), value, 0.0).astype(BF)


def straight_rows(flat, start, count, out, to):
    def move(at, step):
        out[pl.ds(to + at, step), :] = flat[pl.ds(start + at, step), :].astype(out.dtype)

    in_steps(count, 256, move)


def wide_rows(flat, start, count, out, to):
    def move(at, step):
        for half in range(2):
            out[pl.ds(to + at, step), 128 * half : 128 * half + 128] = flat[
                pl.ds(start + 2 * at + half, step, stride=2), :
            ].astype(out.dtype)

    in_steps(count, 128, move)


def prepare_block(block, c):
    flat = c["flat"]
    start = ROW_STARTS[block]
    width_in, width_out = WIDTHS[block]
    one, two = c[f"one{block}"], c[f"two{block}"]
    res = c.get(f"res{block}")
    proj, at = c["proj"], TE * block
    pairs = c["pairs"]
    if width_out == 64:
        chunks = 592 if block == 0 else 1984
        unpack_pairs(flat, start, chunks // 2, pairs)
        size = 64 if block == 0 else 256
        if block == 0:
            one[...] = jnp.zeros_like(one)
            res[...] = jnp.zeros_like(res)
        for k in range(KSIZE):
            spread_pairs(pairs, width_in * k, width_in, one, 2 * size * k, size)
            spread_pairs(pairs, KSIZE * width_in + 64 * k, 64, two, 128 * k, 64)
        cursor = KSIZE * (width_in + 64)
        proj[at : at + TE, 0:128] = pairs[cursor : cursor + TE, :]
        spread_pairs(pairs, cursor + TE, width_in, res, 0, size)
    elif width_out == 128:
        if block == 1:
            one[...] = jnp.zeros_like(one)
            res[...] = jnp.zeros_like(res)
            for k in range(KSIZE + 1):
                source = start + 64 * k if k < KSIZE else start + 320 + 640 + TE
                value = flat[source : source + 64, :].astype(BF)
                into, base = (one, 128 * k) if k < KSIZE else (res, 0)
                into[base : base + 64, 0:128] = value
                into[base + 64 : base + 128, 128:256] = value
        else:
            straight_rows(flat, start, KSIZE * width_in, one, 0)
            straight_rows(flat, start + KSIZE * width_in + 640 + TE, width_in, res, 0)
        straight_rows(flat, start + KSIZE * width_in, 640, two, 0)
        cursor = start + KSIZE * width_in + 640
        proj[at : at + TE, 0:128] = flat[cursor : cursor + TE, :]
    else:
        wide_rows(flat, start, KSIZE * width_in, one, 0)
        wide_rows(flat, start + 2 * KSIZE * width_in, 1280, two, 0)
        cursor = start + 2 * (KSIZE * width_in + 1280)
        wide_rows(flat, cursor, TE, proj, at)
        if res is not None:
            wide_rows(flat, cursor + 2 * TE, width_in, res, 0)


def exact_dot(left, right, dims=(((1,), (0,)), ((), ()))):
    return lax.dot_general(left, right, dims, precision=PRECISE, preferred_element_type=F32)


CROSSING = (None, "up", None, None, None, "down")


def counts_of(frames, block):
    width = WIDTHS[block][1] if block < 6 else C1
    return frames * (width // GROUPS)


def forward_kernel(names, *refs):
    c = dict(zip(names, refs))
    sems = c["sems"]
    aff, stats, terms = c["aff"], c["stats"], c["terms"]
    inner = c["pre_a0"].shape[1]
    frames = 2 * inner
    saves = []

    def save(name):
        copy = pltpu.make_async_copy(c[name], c["out_" + name], sems.at[16 + len(saves)])
        copy.start()
        saves.append(copy)

    loads = []
    for number, (low, high) in enumerate(zip(LOAD_ROWS[:-1], LOAD_ROWS[1:])):
        part = pl.ds(low, high - low)
        copy = pltpu.make_async_copy(c["in_flat"].at[part, :], c["flat"].at[part, :], sems.at[number])
        loads.append(copy)
    order = (6, 0, 1, 2, 3, 4, 5)
    for number in order:
        loads[number].start()
    loads[6].wait()
    flat, pairs, embed = c["flat"], c["pairs"], c["embed_two"]
    unpack_pairs(flat, EMB_ROW, FLAT_ROWS - EMB_ROW, pairs)
    quarter = [pairs[pl.ds(1 + n, TE, stride=4), :] for n in range(4)]
    lane = lanes_of((TE, 128))
    embed_one = jnp.concatenate(
        [jnp.where(lane < 64, quarter[0], quarter[1]), jnp.where(lane < 64, quarter[2], quarter[3])], axis=1
    )
    embed[...] = jnp.where(
        lanes_of((TH, 128)) < 64, pairs[pl.ds(513, TH, stride=2), :], pairs[pl.ds(514, TH, stride=2), :]
    )
    sinus = c["sinus"][...]
    bias = vector(aff, 56, 256)
    kept = c["kept"]
    hidden_pre = exact_dot(sinus, embed_one) + bias
    hidden = mish_fast(hidden_pre)
    feature_pre = exact_dot(hidden, embed[...]) + vector(aff, 58, 128)
    feature = mish_fast(feature_pre)
    for number, value in enumerate((hidden_pre, hidden, feature_pre, feature)):
        kept[8 * number : 8 * number + 8, 0 : value.shape[1]] = value
    save("embed_two")
    x0 = c["x0"]

    def put_noisy(group, value):
        x0[0, pl.ds(pl.multiple_of(HALO + 16 * group, 16), 16), :] = value.astype(BF)

    take_apart(c["noisy"], inner // 64, put_noisy)
    fill_halo(x0)
    save("x0")

    inputs = (("x0",), ("x1",), ("x2",), ("x3",), ("x4", "x3"), ("x5", "x2"))
    for block in range(6):
        loads[block].wait()
        prepare_block(block, c)
        for name in ("one", "two", "res"):
            if f"{name}{block}" in c:
                save(f"{name}{block}")
        halves, lanes = LAYER_OUT[block]
        packed = halves == 1
        count = counts_of(frames, block)
        width = WIDTHS[block][1]
        lane_bias = block_vector(aff, block, 3)
        term = exact_dot(feature, c["proj"][TE * block : TE * block + TE, 0:lanes])[0:1, :] + lane_bias
        terms[8 * block : 8 * block + 1, 0:lanes] = term
        xs = [c[name] for name in inputs[block]]
        pre_a, pre_b = c[f"pre_a{block}"], c[f"pre_b{block}"]
        sums = conv_to(xs, c[f"one{block}"], block_vector(aff, block, 0), pre_a, CROSSING[block])
        save(f"pre_a{block}")
        scale, offset = norm_fit(
            sums, block_vector(aff, block, 1), block_vector(aff, block, 2), count, packed, stats, 2 * block
        )
        hid = c["hid"].at[0:halves, :, 0:lanes]

        def to_hidden(q, start, rows, carry):
            value = mish_fast(pre_a[q, pl.ds(start, rows), :] * scale + offset) + term
            hid[q, pl.ds(HALO + start, rows), :] = value.astype(BF)
            return carry

        sweep(halves, inner, to_hidden, 0)
        fill_halo(hid)
        sums = conv_to([hid], c[f"two{block}"], block_vector(aff, block, 4), pre_b, None)
        save(f"pre_b{block}")
        scale_b, offset_b = norm_fit(
            sums, block_vector(aff, block, 5), block_vector(aff, block, 6), count, packed, stats, 2 * block + 1
        )
        side = c["side"]
        res = c.get(f"res{block}")
        if res is not None:
            res_bias = block_vector(aff, block, 7)
            if CROSSING[block] == "up":
                total = jnp.dot(conv_input(xs, 0, 2, inner), res[...], preferred_element_type=F32)
                side[0, :, 0:lanes] = total[:, :lanes] + res_bias
                side[1, :, 0:lanes] = total[:, lanes:] + res_bias
            elif CROSSING[block] == "down":
                wide = jnp.concatenate([conv_input(xs, q, 2, inner) for q in range(2)], axis=1)
                side[0, :, 0:lanes] = jnp.dot(wide, res[...], preferred_element_type=F32) + res_bias
            else:
                for q in range(halves):
                    side[q, :, 0:lanes] = (
                        jnp.dot(conv_input(xs, q, 2, inner), res[...], preferred_element_type=F32) + res_bias
                    )
        out = c[f"x{block + 1}"]

        def to_output(q, start, rows, carry):
            value = mish_fast(pre_b[q, pl.ds(start, rows), :] * scale_b + offset_b)
            value = value + side[q, pl.ds(start, rows), 0:lanes]
            if block == 2:
                side[q, pl.ds(start, rows), 0:lanes] = value
            out[q, pl.ds(HALO + start, rows), :] = value.astype(BF)
            return carry

        sweep(halves, inner, to_output, 0)
        fill_halo(out)
        save(f"x{block + 1}")
    unpack_pairs(flat, HEAD_ROW, 160, pairs)
    for k in range(KSIZE):
        spread_pairs(pairs, 64 * k, 64, c["one6"], 128 * k, 64)
    save("one6")
    sums = conv_to([c["x6"]], c["one6"], head_vector(aff, 0), c["pre_a6"], None)
    save("pre_a6")
    norm_fit(sums, head_vector(aff, 1), head_vector(aff, 2), counts_of(frames, 6), True, stats, 12)
    for name in ("stats", "terms", "kept", "proj"):
        save(name)
    for copy in saves:
        copy.wait()


def put_rows(value, out, start):
    rows, lanes = value.shape
    if lanes == 128:
        out[start : start + rows, :] = value
    else:
        out[pl.ds(start, rows, stride=2), :] = value[:, 0:128]
        out[pl.ds(start + 1, rows, stride=2), :] = value[:, 128:256]


def conv_dx(dy, weight, size, inner, crossing, emit):
    halves = dy.shape[0]

    def taps(pick):
        total = 0.0
        for k in range(KSIZE):
            total = total + lax.dot_general(
                pick(KSIZE - 1 - k), weight[size * k : size * k + size, :], NT, preferred_element_type=F32
            )
        return total

    if crossing == "up":
        emit(0, taps(lambda k: jnp.concatenate([conv_input([dy], q, k, inner) for q in range(2)], axis=1)))
    elif halves == 1:
        emit(0, taps(lambda k: conv_input([dy], 0, k, inner)))
    else:

        def half(q, carry):
            emit(q, taps(lambda k: conv_input([dy], q, k, inner)))
            return carry

        lax.fori_loop(0, halves, half, 0)


def conv_dw(xs, dy, inner, crossing, acc, extra=None):
    def dys(q):
        parts = [conv_input([dy], q, KSIZE - 1 - k, inner) for k in range(KSIZE)]
        if extra is not None:
            parts.append(extra[q, :, 0 : dy.shape[2]])
        return parts

    def product(left, right):
        return lax.dot_general(left, right, TN, preferred_element_type=F32)

    if crossing == "up":
        both = zip(dys(0), dys(1))
        value = product(conv_input(xs, 0, 2, inner), jnp.concatenate([p for pair in both for p in pair], axis=1))
        acc[0 : value.shape[0], 0 : value.shape[1]] = value
        return
    if crossing == "down":
        left = jnp.concatenate([conv_input(xs, q, 2, inner) for q in range(2)], axis=1)
        value = product(left, jnp.concatenate(dys(0), axis=1))
        acc[0 : value.shape[0], 0 : value.shape[1]] = value
        return
    for q in range(dy.shape[0]):
        value = product(conv_input(xs, q, 2, inner), jnp.concatenate(dys(q), axis=1))
        if q == 0:
            acc[0 : value.shape[0], 0 : value.shape[1]] = value
        else:
            acc[0 : value.shape[0], 0 : value.shape[1]] += value


def fold_pairs(acc, tap, size, rows):
    lanes = slice(128 * tap, 128 * tap + 128)
    return acc[0:rows, lanes] + pltpu.roll(acc[size : size + rows, lanes], 64, 1)


def put_vector(grads, row, width, value):
    base = int(row)
    if width == 256:
        grads[base : base + 1, :] = value[:, 0:128]
        grads[base + 1 : base + 2, :] = value[:, 128:256]
    elif width == 128:
        grads[base : base + 1, :] = value
    else:
        lane = lanes_of((1, 128))
        keep = lane < 64 if row == base else lane >= 64
        grads[base : base + 1, :] = jnp.where(keep, value, grads[base : base + 1, :])


def norm_backward(c, layer, pre, gain, count, packed, upstream, dy, also=None):
    halves, inner, lanes = pre.shape
    kept = norm_kept(c["stats"], layer, lanes)
    dv = c["dv"]
    zero = jnp.zeros((8, lanes), F32)

    def first(q, start, rows, state):
        here = pl.ds(start, rows)
        value = pre[q, here, :]
        act, slope = mish_both(value * kept[0] + kept[1])
        up = upstream(q, here)
        if also is not None:
            also(q, here, act, up)
        grad = up * slope
        dv[q, here, 0:lanes] = grad
        return state[0] + fold_rows(grad), state[1] + fold_rows(grad * value), state[2] + fold_rows(up)

    sums = sweep(halves, inner, first, (zero, zero, zero))
    rows_each = float(inner * halves)
    slope, level, grad_bias, grad_gain, grad_shift = norm_back_fit(sums, kept, gain, count, rows_each, packed)
    scale = kept[0]

    def second(q, start, rows, carry):
        here = pl.ds(start, rows)
        value = scale * dv[q, here, 0:lanes] + (slope * pre[q, here, :] + level)
        dy[q, pl.ds(HALO + start, rows), :] = value.astype(BF)
        return carry

    sweep(halves, inner, second, 0)
    fill_halo(dy)
    total = down_one_row(sums[2])
    return grad_bias, grad_gain, grad_shift, both_halves(total) if packed else total


def backward_block(block, c, base):
    aff, grads, table, acc = c["aff"], c["agrad"], c["table"], c["acc"]
    halves, lanes = LAYER_OUT[block]
    packed = halves == 1
    width_in, width_out = WIDTHS[block]
    inner = c[f"pre_a{block}"].shape[1]
    count = counts_of(2 * inner, block)
    up = c[f"up{block}"]
    low = c["low"]
    dy = c["dy"].at[0:halves, :, 0:lanes]
    act_low = c["act"]
    res = c.get(f"res{block}")
    inputs = (("x0",), ("x1",), ("x2",), ("x3",), ("x4", "x3"), ("x5", "x2"))
    xs = [c[name] for name in inputs[block]]
    start = ROW_STARTS[block] - base
    spot = AFF_ROWS[block]
    unit = width_out / 128

    def keep_low(q, here, act, value):
        low[q, here, 0:lanes] = value.astype(BF)

    got = norm_backward(
        c, 2 * block + 1, c[f"pre_b{block}"], block_vector(aff, block, 5), count, packed,
        lambda q, here: up[q, here, :], dy, keep_low if res is not None else None,
    )
    for number, value in zip((4, 5, 6, 7), got):
        if number < 7 or res is not None:
            put_vector(grads, spot + number * unit, width_out, value)
    dv = c["dv"]

    def emit_hidden(q, value):
        dv[q, :, 0:lanes] = value

    conv_dx(dy, c[f"two{block}"], lanes, inner, None, emit_hidden)
    term = c["terms"][8 * block : 8 * block + 1, 0:lanes]
    dy_two = dy
    dy_one = c["ey"].at[0:halves, :, 0:lanes]

    def keep_act(q, here, act, value):
        act_low[q, here, 0:lanes] = (act + term).astype(BF)

    got = norm_backward(
        c, 2 * block, c[f"pre_a{block}"], block_vector(aff, block, 1), count, packed,
        lambda q, here: dv[q, here, 0:lanes], dy_one, keep_act,
    )
    for number, value in zip((0, 1, 2, 3), got):
        put_vector(grads, spot + number * unit, width_out, value)
    time_row = got[3]
    c["tgrad"][8 * block : 8 * block + 1, 0:lanes] = time_row

    def plain_dw(left, right_ref):
        for q in range(halves):
            parts = jnp.concatenate([conv_input([right_ref], q, KSIZE - 1 - k, inner) for k in range(KSIZE)], axis=1)
            value = lax.dot_general(left[q, :, 0:lanes], parts, TN, preferred_element_type=F32)
            if q == 0:
                acc[0:lanes, 0 : KSIZE * lanes] = value
            else:
                acc[0:lanes, 0 : KSIZE * lanes] += value

    plain_dw(act_low, dy_two)
    pairs = c["pairs"]
    feature = c["kept"][24:32, 0:128]
    row = rows_of((8, lanes))
    outer = exact_dot(
        jnp.where(rows_of((8, 128)) == 0, feature, 0.0), jnp.where(row == 0, time_row, 0.0), TN
    )
    if width_out == 64:
        at = KSIZE * width_in
        for k in range(KSIZE):
            pairs[at + 64 * k : at + 64 * k + 64, :] = fold_pairs(acc, k, 64, 64)
        pairs[at + 320 : at + 320 + TE, :] = outer
    else:
        at = start + KSIZE * width_in * (width_out // 128)
        for k in range(KSIZE):
            put_rows(acc[0:lanes, lanes * k : lanes * k + lanes], table, at + k * lanes * (width_out // 128))
        put_rows(outer, table, at + 5 * lanes * (width_out // 128))
    crossing = CROSSING[block]
    if block > 0:
        size = {None: sum(x.shape[2] for x in xs), "up": 128, "down": 512}[crossing]

        def emit(q, value):
            if res is not None:
                if crossing == "up":
                    side = jnp.concatenate([low[0, :, 0:lanes], low[1, :, 0:lanes]], axis=1)
                else:
                    side = low[q, :, 0:lanes]
                value = value + lax.dot_general(side, res[...], NT, preferred_element_type=F32)
            if block == 5:
                for h in range(2):
                    c["up4"][h] = value[:, 256 * h : 256 * h + 128]
                    c["up1"][h] = value[:, 256 * h + 128 : 256 * h + 256]
            elif block == 4:
                c["up3"][q] = value[:, 0:256]
                c["up2"][q] = value[:, 256:512]
            elif block == 3:
                c["up2"][q] = c["up2"][q] + (value + up[q])
            elif block == 2:
                c["up1"][q] = c["up1"][q] + value
            else:
                c["up0"][0] = value

        conv_dx(dy_one, c[f"one{block}"], size, inner, crossing, emit)
    conv_dw(xs, dy_one, inner, crossing, acc, low if res is not None else None)
    if width_out == 64:
        size = 64 if block == 0 else 256
        rows = 24 if block == 0 else 256
        for k in range(KSIZE):
            value = fold_pairs(acc, k, size, rows)
            pairs[width_in * k : width_in * k + width_in, :] = value[0:width_in]
        at = KSIZE * (width_in + 64) + TE
        pairs[at : at + width_in, :] = fold_pairs(acc, KSIZE, size, rows)[0:width_in]
        if block == 0:
            after = table[288:296, :]
            pack_pairs(pairs, table, start, 296)
            table[288:296, :] = jnp.where(rows_of((8, 128)) < 5, table[288:296, :], after)
        else:
            pack_pairs(pairs, table, start, 992)
    else:
        unit_rows = width_out // 128
        for k in range(KSIZE + (0 if res is None else 1)):
            at = start + k * width_in * unit_rows
            if k == KSIZE:
                at = start + (KSIZE * (width_in + width_out) + TE) * unit_rows
            if crossing == "up":
                value = acc[0:64, 256 * k : 256 * k + 128] + acc[64:128, 256 * k + 128 : 256 * k + 256]
            else:
                value = acc[0:width_in, width_out * k : width_out * k + width_out]
            put_rows(value, table, at)


def load_all(c, names, sems, first=0):
    copies = {}
    for number, name in enumerate(names):
        copy = pltpu.make_async_copy(c["in_" + name], c[name], sems.at[first + number])
        copy.start()
        copies[name] = copy
    return copies


def late_kernel(loaded, names, *refs):
    c = dict(zip(names, refs))
    copies = load_all(c, loaded, c["sems"])
    aff, grads = c["aff"], c["agrad"]

    def need(*wanted):
        for name in wanted:
            copy = copies.pop(name, None)
            if copy is not None:
                copy.wait()

    grads[...] = jnp.zeros_like(grads)
    need("noise_in")
    noise_in, noise = c["noise_in"], c["noise"]
    last = noise_in.shape[1] - 8

    def put_noise(group, value):
        noise[pl.ds(pl.multiple_of(16 * group, 16), 16), :] = value

    take_apart(noise_in, c["pre_a6"].shape[1] // 64, put_noise)
    tail = noise_in[0, last:, :] + noise_in[1, last:, :] + noise_in[2, last:, :] + noise_in[3, last:, :]
    length = tail[0:1, :]
    scale_out = 1.0 / (tail[1:2, :] * TD)
    need("stats", "terms", "kept", "pre_a6")
    pre = c["pre_a6"]
    inner = pre.shape[1]
    kept = norm_kept(c["stats"], 12, 128)
    act, low, up = c["act"], c["low"], c["up5"]
    lane = lanes_of((1, 128))
    spot = lane % 64
    out_row = aff[55:56, :]
    out_bias = jnp.where(spot < TD, jnp.where(lane < 64, pltpu.roll(out_row, 64, 1), out_row), 0.0)
    segment = inner // 16

    def to_feature(q, start, rows, carry):
        here = pl.ds(start, rows)
        act[0, here, 0:128] = mish_fast(pre[0, here, :] * kept[0] + kept[1]).astype(BF)
        return carry

    sweep(1, inner, to_feature, 0)
    dv = c["dv"]
    dv[0, :, 0:128] = jnp.dot(act[0, :, 0:128], c["wout"][...], preferred_element_type=F32)

    def to_loss(q, start, rows, state):
        here = pl.ds(start, rows)
        shape = (rows, 128)
        place = rows_of(shape) + start
        lanes = lanes_of(shape)
        frame = (place % 16 + jnp.where(lanes >= 64, 16, 0)) * segment + place // 16
        weight = jnp.where((frame.astype(F32) < length) & (lanes % 64 < TD), 1.0, 0.0)
        difference = weight * (dv[0, here, 0:128] + out_bias - noise[here, :])
        grad = 2.0 * difference * scale_out
        low[0, here, 0:128] = grad.astype(BF)
        return state[0] + fold_rows(difference * difference), state[1] + fold_rows(grad)

    zero = jnp.zeros((8, 128), F32)
    loss, out_sum = sweep(1, inner, to_loss, (zero, zero))
    c["loss"][...] = loss * scale_out
    out_sum = both_halves(down_one_row(out_sum))
    c["gout"][...] = lax.dot_general(act[0, :, 0:128], low[0, :, 0:128], TN, preferred_element_type=F32)
    dv[0, :, 0:128] = lax.dot_general(low[0, :, 0:128], c["wout"][...], NT, preferred_element_type=F32)
    dy = c["dy"].at[0:1, :, 0:128]
    got = norm_backward(
        c, 12, pre, head_vector(aff, 1), counts_of(2 * inner, 6), True, lambda q, here: dv[q, here, 0:128], dy
    )
    grads[54:55, :] = jnp.where(lane < 64, got[0], got[1])
    grads[55:56, :] = jnp.where(lane < 64, got[2], jnp.where(spot < TD, out_sum, 0.0))

    def emit_head(q, value):
        up[0] = value

    need("one6", "x6")
    conv_dx(dy, c["one6"], 128, inner, None, emit_head)
    conv_dw([c["x6"]], dy, inner, None, c["acc"])
    for k in range(KSIZE):
        c["pairs"][64 * k : 64 * k + 64, :] = fold_pairs(c["acc"], k, 64, 64)
    pack_pairs(c["pairs"], c["table"], HEAD_ROW - LATE_START, 160)
    c["tgrad"][...] = jnp.zeros_like(c["tgrad"])
    need("pre_a5", "pre_b5", "one5", "two5", "res5", "x5", "x2")
    backward_block(5, c, LATE_START)
    need("pre_a4", "pre_b4", "one4", "two4", "res4", "x4", "x3")
    backward_block(4, c, LATE_START)
    need("pre_a3", "pre_b3", "one3", "two3")
    backward_block(3, c, LATE_START)
    need(*list(copies))
    outs = []
    for number, name in enumerate(("table", "up1", "up2", "tgrad", "agrad")):
        copy = pltpu.make_async_copy(c[name], c["out_" + name], c["sems"].at[len(loaded) + number])
        copy.start()
        outs.append(copy)
    for copy in outs:
        copy.wait()


def early_kernel(loaded, names, *refs):
    c = dict(zip(names, refs))
    copies = load_all(c, loaded, c["sems"])
    aff, grads, table = c["aff"], c["agrad"], c["table"]
    late_copy = pltpu.make_async_copy(
        c["in_late"], table.at[pl.ds(LATE_START, LATE_ROWS), :], c["sems"].at[len(loaded) + 4]
    )
    late_copy.start()

    def need(*wanted):
        for name in wanted:
            copy = copies.pop(name, None)
            if copy is not None:
                copy.wait()

    need("stats", "terms", "kept", "agrad", "tgrad", "up2", "pre_b2", "two2", "pre_a2", "one2", "res2", "x2", "up1")
    late_copy.wait()
    backward_block(2, c, 0)
    need("pre_a1", "pre_b1", "one1", "two1", "res1", "x1")
    backward_block(1, c, 0)
    need("pre_a0", "pre_b0", "one0", "two0", "res0", "x0")
    backward_block(0, c, 0)
    need(*list(copies))
    total = jnp.zeros((8, TE), F32)
    row = rows_of((8, 256))
    for block in range(6):
        lanes = LAYER_OUT[block][1]
        first = jnp.where(rows_of((8, lanes)) == 0, c["tgrad"][8 * block : 8 * block + 8, 0:lanes], 0.0)
        if WIDTHS[block][1] == 64:
            first = jnp.where(lanes_of((8, lanes)) < 64, first, 0.0)
        total = total + exact_dot(first, c["proj"][TE * block : TE * block + TE, 0:lanes], NT)
    kept = c["kept"]
    hidden_pre, hidden = kept[0:8, :], kept[8:16, :]
    feature_pre = kept[16:24, 0:128]
    grad_feature = total * mish_both(feature_pre)[1]
    pairs = c["pairs"]
    second = exact_dot(jnp.where(row == 0, hidden, 0.0), grad_feature, TN)
    put_vector(grads, 58, 128, grad_feature[0:1, :])
    grad_hidden = exact_dot(grad_feature, c["embed_two"][...], NT) * mish_both(hidden_pre)[1]
    only = jnp.where(row == 0, grad_hidden, 0.0)
    first = exact_dot(c["sinus"][...], only, TN)
    put_vector(grads, 56, 256, grad_hidden[0:1, :])
    grads[60:61, :] = down_one_row(c["loss"][...])
    table[OUT_ROW : OUT_ROW + 12, :] = c["hograd"][0:12, :]
    table[FLAT_ROWS:TABLE_ROWS, :] = jnp.zeros((TABLE_ROWS - FLAT_ROWS, 128), F32)
    pairs[1024:1040, :] = jnp.zeros((16, 128), F32)
    pairs[0:1, :] = c["hograd"][11:12, :]
    for half in range(2):
        value = first[:, 128 * half : 128 * half + 128]
        pairs[pl.ds(1 + 2 * half, TE, stride=4), :] = value
        pairs[pl.ds(2 + 2 * half, TE, stride=4), :] = pltpu.roll(value, 64, 1)
    pairs[pl.ds(513, TH, stride=2), :] = second
    pairs[pl.ds(514, TH, stride=2), :] = pltpu.roll(second, 64, 1)
    pack_pairs(pairs, table, EMB_ROW, FLAT_ROWS - EMB_ROW)
    core = c["core"][0]
    keep, send = c["keep"], c["send"]
    share = NKER_ROWS
    step = 176

    for pair in range(4):

        def split(index, carry):
            at = pl.multiple_of(index * step, step)
            even = table[pl.ds(share * (2 * pair) + at, step), :]
            odd = table[pl.ds(share * (2 * pair + 1) + at, step), :]
            keep[pair, pl.ds(at, step), :] = jnp.where(core == 0, even, odd)
            send[pl.ds(OWN_ROWS * pair + at, step), :] = jnp.where(core == 0, odd, even).astype(BF)
            return carry

        lax.fori_loop(0, OWN_ROWS // step, split, 0)
    value = grads[...]
    high = value.astype(BF)
    rest = (value - high.astype(F32)).astype(BF)
    send[4 * OWN_ROWS : 4 * OWN_ROWS + 64, :] = high
    send[4 * OWN_ROWS + 64 : 4 * OWN_ROWS + 128, :] = rest
    grads[...] = high.astype(F32) + rest.astype(F32)
    outs = []
    for number, name in enumerate(("send", "keep", "agrad")):
        copy = pltpu.make_async_copy(c[name], c["out_" + name], c["sems"].at[len(loaded) + number])
        copy.start()
        outs.append(copy)
    for copy in outs:
        copy.wait()


def shape_table(inner):
    padded = inner + 2 * HALO
    table = {
        "x0": ((1, padded, 128), BF),
        "x1": ((1, padded, 128), BF),
        "x2": ((2, padded, 128), BF),
        "x3": ((2, padded, 256), BF),
        "x4": ((2, padded, 256), BF),
        "x5": ((2, padded, 128), BF),
        "x6": ((1, padded, 128), BF),
        "stats": ((104, 256), F32),
        "terms": ((48, 256), F32),
        "tgrad": ((48, 256), F32),
        "kept": ((32, 256), F32),
        "proj": ((6 * TE, 256), F32),
        "embed_two": ((256, 128), F32),
        "agrad": ((64, 128), F32),
        "flat": ((FLAT_ROWS, 128), F32),
        "pairs": ((2048, 128), F32),
        "table": ((TABLE_ROWS, 128), F32),
        "send": ((4 * OWN_ROWS + 128, 128), BF),
        "keep": ((4, OWN_ROWS, 128), F32),
        "acc": ((512, 1536), F32),
        "side": ((2, inner, 256), F32),
        "dv": ((2, inner, 256), F32),
        "low": ((2, inner, 256), BF),
        "act": ((2, inner, 256), BF),
        "noise": ((inner, 128), F32),
        "noise_in": ((4, inner // 8 + 8, 128), F32),
    }
    for block in range(7):
        halves, lanes = LAYER_OUT[block]
        table[f"pre_a{block}"] = ((halves, inner, lanes), F32)
        table[f"one{block}"] = (W_ONE[block], BF)
        if block < 6:
            table[f"up{block}"] = ((halves, inner, lanes), F32)
            table[f"pre_b{block}"] = ((halves, inner, lanes), F32)
            table[f"two{block}"] = (W_TWO[block], BF)
            if W_RES[block] is not None:
                table[f"res{block}"] = (W_RES[block], BF)
    for stem in ("hid", "dy", "ey"):
        table[stem] = ((2, padded, 256), BF)
    return table


def run_kernel(body, vmem_in, smem_in, any_in, outs_vmem, outs_any, scratch, sems, table, cost):
    names = list(vmem_in) + list(smem_in) + ["in_" + n for n in any_in]
    operands = list(vmem_in.values()) + list(smem_in.values()) + list(any_in.values())
    in_specs = (
        [pl.BlockSpec(memory_space=pltpu.VMEM)] * len(vmem_in)
        + [pl.BlockSpec(memory_space=pltpu.SMEM)] * len(smem_in)
        + [pl.BlockSpec(memory_space=pl.ANY)] * len(any_in)
    )
    out_shape, out_specs = [], []
    for name, (shape, kind) in outs_vmem.items():
        names.append(name)
        out_shape.append(jax.ShapeDtypeStruct(shape, kind))
        out_specs.append(pl.BlockSpec(memory_space=pltpu.VMEM))
    for name in outs_any:
        names.append("out_" + name)
        out_shape.append(jax.ShapeDtypeStruct(*table[name]))
        out_specs.append(pl.BlockSpec(memory_space=pl.ANY))
    buffers = []
    for name in scratch:
        names.append(name)
        buffers.append(pltpu.VMEM(*table[name]))
    names.append("sems")
    buffers.append(pltpu.SemaphoreType.DMA((sems,)))
    results = pl.pallas_call(
        functools.partial(body, names),
        out_shape=out_shape,
        in_specs=in_specs,
        out_specs=out_specs,
        scratch_shapes=buffers,
        compiler_params=pltpu.CompilerParams(vmem_limit_bytes=VMEM_LIMIT),
        cost_estimate=pl.CostEstimate(flops=cost, bytes_accessed=40000000, transcendentals=0),
    )(*operands)
    return dict(zip(list(outs_vmem) + list(outs_any), results))


VMEM_LIMIT = 67043328


def exchange_pieces(traj, noise, mask, signal, mean, std):
    pieces, frames, wide = traj.shape
    scale = jnp.concatenate([jnp.sqrt(signal), jnp.sqrt(1.0 - signal)])
    vmem = pl.BlockSpec(memory_space=pltpu.VMEM)
    return pl.pallas_call(
        exchange_kernel,
        out_shape=[
            jax.ShapeDtypeStruct((pieces, frames // 4, 128), BF),
            jax.ShapeDtypeStruct((pieces, frames // 4 + 8, 128), F32),
            jax.ShapeDtypeStruct((8, 128), F32),
        ],
        in_specs=[vmem] * 6,
        out_specs=[vmem] * 3,
        scratch_shapes=[pltpu.VMEM((frames, 128), F32)] * 2,
    )(traj, noise, mask, jnp.broadcast_to(scale[:, None], (2 * pieces, 128)), mean[None, :], std[None, :])


def whole_horizon(noisy, noise, sinus, core, kernels, affine):
    inner = 4 * noisy.shape[1] * 2
    table = shape_table(inner)
    flat = jnp.pad(kernels, (0, FLAT_ROWS * 128 - kernels.shape[0])).reshape(FLAT_ROWS, 128)
    aff = jnp.concatenate(
        [affine[:7127], jnp.zeros((41,), F32), affine[7127:], jnp.zeros((640,), F32)]
    ).reshape(64, 128)
    head_out = kernels[OUT_START : OUT_START + C1 * TD].reshape(C1, TD).astype(BF)
    wide_out = jnp.pad(head_out, ((0, 0), (0, 64 - TD)))
    nothing = jnp.zeros((C1, 64), BF)
    wout = jnp.concatenate(
        [jnp.concatenate([wide_out, nothing], axis=1), jnp.concatenate([nothing, wide_out], axis=1)], axis=0
    )
    weights = [n for n in table if n[:3] in ("one", "two", "res") and n[3:].isdigit()]
    saved = [n for n in table if n.startswith("pre_") or (n[0] == "x" and n[1:].isdigit())]
    saved += weights + ["stats", "terms", "kept", "proj", "embed_two"]
    kept = run_kernel(
        forward_kernel,
        {"noisy": noisy, "aff": aff, "sinus": sinus},
        {},
        {"flat": flat},
        {},
        saved,
        saved + ["flat", "pairs", "side", "hid"],
        16 + len(saved),
        table,
        14000000000,
    )
    late_table = dict(table)
    late_table["table"] = ((LATE_ROWS, 128), F32)
    late_in = ["noise_in", "stats", "terms", "kept", "pre_a6", "one6", "x6"]
    late_in += ["pre_b5", "two5", "pre_a5", "one5", "res5", "x5", "x2"]
    late_in += ["pre_b4", "two4", "pre_a4", "one4", "res4", "x4", "x3"]
    late_in += ["pre_b3", "two3", "pre_a3", "one3"]
    sources = dict(kept, noise_in=noise)
    late_out = ["table", "up1", "up2", "tgrad", "agrad"]
    late = run_kernel(
        functools.partial(late_kernel, late_in),
        {"aff": aff, "wout": wout},
        {},
        {n: sources[n] for n in late_in},
        {"loss": ((8, 128), F32), "gout": ((128, 128), F32)},
        late_out,
        late_in + late_out + ["noise", "up5", "up4", "up3", "dv", "low", "act", "acc", "pairs"]
        + ["dy", "ey"],
        len(late_in) + len(late_out),
        late_table,
        16000000000,
    )
    sources.update(late)
    gout = late["gout"]
    head_grad = (gout[0:64, 0:TD] + gout[64:128, 64 : 64 + TD]).reshape(-1)
    early_in = ["stats", "terms", "kept", "agrad", "tgrad", "up2", "pre_b2", "two2", "pre_a2", "one2", "res2", "x2", "up1"]
    early_in += ["pre_b1", "two1", "pre_a1", "one1", "res1", "x1"]
    early_in += ["pre_b0", "two0", "pre_a0", "one0", "res0", "x0", "proj", "embed_two"]
    any_in = {n: sources[n] for n in early_in}
    any_in["late"] = late["table"]
    early = run_kernel(
        functools.partial(early_kernel, early_in),
        {
            "aff": aff,
            "sinus": jnp.where(jnp.arange(8)[:, None] == 0, sinus, 0.0),
            "loss": late["loss"],
            "hograd": jnp.pad(head_grad, (0, 2048 - C1 * TD)).reshape(16, 128),
        },
        {"core": core.reshape(1)},
        any_in,
        {},
        ["send", "keep", "agrad"],
        early_in + ["table", "send", "keep", "up0", "dv", "low", "act", "acc", "pairs"]
        + ["dy", "ey"],
        len(early_in) + 5,
        table,
        10000000000,
    )
    return early["send"], early["keep"], early["agrad"]


def on_device_xla(
    trajectories,
    dim_means,
    dim_stds,
    noise_draw,
    diffusion_steps,
    valid_mask,
    kernels,
    affine,
    kernel_momentum,
    kernel_average,
    affine_momentum,
    affine_average,
):
    members_all = unpack(kernels, affine)
    valid_total = lax.psum(jnp.sum(valid_mask.astype(jnp.float32)), ("dp", "hor"))
    signal_now = signal_level(diffusion_steps)[:, None, None]
    clean_frames = (trajectories - dim_means) / dim_stds
    noisy_frames = jnp.sqrt(signal_now) * clean_frames + jnp.sqrt(1.0 - signal_now) * noise_draw

    ring = lax.axis_size("hor")
    axis = "hor"
    if trajectories.shape[0] % ring == 0:
        axis = None
        local = trajectories.shape[0] // ring
        part = lax.axis_index("hor") * local
        low_frames = noisy_frames.astype(jnp.bfloat16)
        noisy_frames = lax.all_to_all(low_frames, "hor", 0, 1, tiled=True).astype(jnp.float32)
        noise_draw = lax.all_to_all(noise_draw, "hor", 0, 1, tiled=True)
        valid_mask = lax.all_to_all(valid_mask, "hor", 0, 1, tiled=True)
        diffusion_steps = lax.dynamic_slice_in_dim(diffusion_steps, part, local)

    def time_closed(kernel_flat, affine_flat):
        return time_parts(kernel_flat, affine_flat, diffusion_steps)

    time_list, time_pullback = jax.vjp(time_closed, kernels, affine)
    down_one, kept_one = block_forward(noisy_frames, members_all[0], time_list[0], axis)
    down_two, kept_two = block_forward(down_one, members_all[1], time_list[1], axis)
    down_three, kept_three = block_forward(down_two, members_all[2], time_list[2], axis)
    middle, kept_middle = block_forward(down_three, members_all[3], time_list[3], axis)
    up_one, kept_upper = block_forward(
        jnp.concatenate([middle, down_three], axis=2), members_all[4], time_list[4], axis)
    up_two, kept_lower = block_forward(
        jnp.concatenate([up_one, down_two], axis=2), members_all[5], time_list[5], axis)
    predicted, kept_head = head_forward(up_two, members_all[6], axis)
    weight_rows = valid_mask.astype(jnp.float32)[:, :, None]
    difference = predicted - noise_draw
    loss_scale = 1.0 / (valid_total * TD)
    loss_part = jnp.sum(weight_rows * difference * difference) * loss_scale
    grad_predicted = 2.0 * weight_rows * difference * loss_scale
    grad_up_two, head_grads = head_backward(grad_predicted, kept_head, members_all[6], axis)
    grad_joined, time_six, grads_six = block_backward(grad_up_two, kept_lower, members_all[5], axis)
    grad_up_one = grad_joined[:, :, :C2]
    grad_down_two = grad_joined[:, :, C2:]
    grad_joined, time_five, grads_five = block_backward(grad_up_one, kept_upper, members_all[4], axis)
    grad_middle = grad_joined[:, :, :C3]
    grad_down_three = grad_joined[:, :, C3:]
    grad_inputs, time_four, grads_four = block_backward(grad_middle, kept_middle, members_all[3], axis)
    grad_inputs, time_three, grads_three = block_backward(
        grad_down_three + grad_inputs, kept_three, members_all[2], axis
    )
    grad_inputs, time_two, grads_two = block_backward(
        grad_down_two + grad_inputs, kept_two, members_all[1], axis
    )
    grad_inputs, time_one, grads_one = block_backward(grad_inputs, kept_one, members_all[0], axis)
    kernel_grad, affine_grad = pack_flat(
        [grads_one, grads_two, grads_three, grads_four, grads_five, grads_six, head_grads]
    )
    time_kernel, time_affine = time_pullback(
        (time_one, time_two, time_three, time_four, time_five, time_six)
    )
    kernel_grad = kernel_grad + time_kernel
    affine_grad = affine_grad + time_affine
    share_len = kernels.shape[0] // lax.axis_size("dp")
    owner_start = lax.axis_index("dp") * share_len
    kernel_sum, affine_sum, noise_loss = lax.psum(
        (kernel_grad, affine_grad, loss_part), ("dp", "hor")
    )
    kernel_own = lax.dynamic_slice_in_dim(kernel_sum, owner_start, share_len)
    squares = jnp.sum(kernel_sum * kernel_sum) + jnp.sum(affine_sum * affine_sum)
    grad_norm = jnp.sqrt(squares)
    factor = jnp.minimum(1.0, MAX_NORM / (grad_norm + 1e-06))
    kernel_step = kernel_own * factor
    kernel_old = lax.dynamic_slice_in_dim(kernels, owner_start, share_len)
    kernel_mom_new = MOMENTUM * kernel_momentum + kernel_step
    kernel_new = kernel_old - LEARN_RATE * (kernel_step + MOMENTUM * kernel_mom_new)
    kernel_ema_new = EMA_DECAY * kernel_average + (1.0 - EMA_DECAY) * kernel_new
    affine_step = affine_sum * factor
    affine_mom_new = MOMENTUM * affine_momentum + affine_step
    affine_new = affine - AFFINE_RATE * (affine_step + MOMENTUM * affine_mom_new)
    affine_ema_new = EMA_DECAY * affine_average + (1.0 - EMA_DECAY) * affine_new
    return (
        noise_loss,
        grad_norm,
        kernel_new,
        kernel_mom_new,
        kernel_ema_new,
        kernel_new.astype(jnp.bfloat16),
        affine_new,
        affine_mom_new,
        affine_ema_new,
        affine_new.astype(jnp.bfloat16),
    )


def swap(value, axis, bit):
    return lax.ppermute(value, axis, [(i, i ^ bit) for i in range(lax.axis_size(axis))])


def total_over(value, hops):
    for axis, bit in hops:
        value = value + swap(value, axis, bit)
    return value


def bits_of(axis):
    return [(axis, 1 << n) for n in range(lax.axis_size(axis).bit_length() - 1)]


def pick(stack, index):
    return lax.dynamic_index_in_dim(stack, index, 0, keepdims=False)


def in_low(value):
    return lax.reduce_precision(value, 8, 7)


def two_parts(value):
    high = in_low(value)
    return high, in_low(value - high)


def share_sums(send, keep, small):
    low, wide = jnp.bfloat16, jnp.float32
    place = lax.axis_index("dp")
    seat_x = (place >> 1) & 1
    seat_y = (place >> 2) & 1
    layer = lax.axis_index("hor")
    part_rows = OWN_ROWS // 4
    half = OWN_ROWS // 2

    def with_small(value, parts):
        return jnp.concatenate([value.reshape(-1, 128), parts[0], parts[1]], axis=0).astype(low)

    def small_of(got):
        tail = got[-128:].astype(wide)
        return tail[:64] + tail[64:]

    got = swap(send, "dp", 1)
    grid = (keep + got[:-128].reshape(keep.shape).astype(wide)).reshape(2, 2, OWN_ROWS, 128)
    parts = two_parts(small + small_of(got))
    first, second = grid[:, :, :half], grid[:, :, half:]
    first_in = swap(
        with_small(lax.dynamic_index_in_dim(first, 1 - seat_x, 1, keepdims=False), parts), "dp", 2
    )
    second_in = swap(pick(second, 1 - seat_y).astype(low), "dp", 4)
    parts = two_parts(parts[0] + parts[1] + small_of(first_in))
    first = lax.dynamic_index_in_dim(first, seat_x, 1, keepdims=False)
    first = first + first_in[:-128].reshape(first.shape).astype(wide)
    second = pick(second, seat_y) + second_in.astype(wide)
    first_in = swap(with_small(pick(first, 1 - seat_y), parts), "dp", 4)
    second_in = swap(pick(second, 1 - seat_x).astype(low), "dp", 2)
    parts = two_parts(parts[0] + parts[1] + small_of(first_in))
    own = jnp.concatenate(
        [
            pick(first, seat_y) + first_in[:-128].astype(wide),
            pick(second, seat_x) + second_in.astype(wide),
        ],
        axis=0,
    ).reshape(4, part_rows, 128)
    arrived = [swap(with_small(pick(own, layer ^ bits), parts), "hor", bits) for bits in (1, 2, 3)]
    part = pick(own, layer)
    for value in arrived:
        part = part + value[:-128].astype(wide)
    smalls = jnp.stack([parts[0] + parts[1]] + [small_of(value) for value in arrived])
    small = sum(pick(smalls, layer ^ n) for n in range(4))
    return part, small


def all_parts(part):
    layer = lax.axis_index("hor")
    part_low = in_low(part).astype(jnp.bfloat16)
    parts = jnp.stack([part_low] + [swap(part_low, "hor", bits) for bits in (1, 2, 3)])
    return jnp.concatenate([pick(parts, layer ^ n) for n in range(4)], axis=0)


def on_device(
    trajectories,
    dim_means,
    dim_stds,
    noise_draw,
    diffusion_steps,
    valid_mask,
    kernels,
    affine,
    kernel_momentum,
    kernel_average,
    affine_momentum,
    affine_average,
):
    ring = lax.axis_size("hor")
    frames = trajectories.shape[1] * ring
    if trajectories.shape[0] != ring or ring != 4 or frames % 512 or lax.axis_size("dp") != 8:
        return on_device_xla(
            trajectories,
            dim_means,
            dim_stds,
            noise_draw,
            diffusion_steps,
            valid_mask,
            kernels,
            affine,
            kernel_momentum,
            kernel_average,
            affine_momentum,
            affine_average,
        )
    low_out, noise_out, counts = exchange_pieces(
        trajectories, noise_draw, valid_mask, signal_level(diffusion_steps), dim_means, dim_stds
    )
    noisy = lax.all_to_all(low_out, "hor", 0, 0, tiled=True)
    total = total_over(jnp.sum(counts[:4, 0]), bits_of("dp"))
    row = lax.broadcasted_iota(jnp.int32, (4, 8, 128), 1)
    extra = jnp.where(row == 0, counts[:4, None, :], jnp.where(row == 1, total, 0.0))
    noise_out = lax.dynamic_update_slice(noise_out, extra, (0, noise_out.shape[1] - 8, 0))
    noise = lax.all_to_all(noise_out, "hor", 0, 0, tiled=True)
    own_step = lax.dynamic_slice_in_dim(diffusion_steps, lax.axis_index("hor"), 1)
    sinus = jnp.broadcast_to(sinusoid(own_step), (8, TE))
    place = lax.axis_index("dp")
    send, keep, small = whole_horizon(noisy, noise, sinus, place & 1, kernels, affine)
    part, small = share_sums(send, keep, small)
    share_len = kernels.shape[0] // lax.axis_size("dp")
    owner_start = place * share_len
    lead = owner_start - place * NKER_ROWS * 128
    number = (
        lax.axis_index("hor") * part.size
        + lax.broadcasted_iota(jnp.int32, part.shape, 0) * 128
        + lax.broadcasted_iota(jnp.int32, part.shape, 1)
    )
    inside = (number >= lead) & (number < lead + share_len)
    squares = total_over(jnp.sum(jnp.where(inside, part * part, 0.0)), bits_of("dp"))
    whole = all_parts(part)
    squares = total_over(squares, bits_of("hor"))
    small_flat = small.reshape(-1)
    affine_sum = jnp.concatenate([small_flat[:7127], small_flat[7168:7552]])
    noise_loss = jnp.sum(small[60])
    grad_norm = jnp.sqrt(squares + jnp.sum(affine_sum * affine_sum))
    kernel_own = lax.dynamic_slice_in_dim(whole.astype(jnp.float32).reshape(-1), lead, share_len)
    factor = jnp.minimum(1.0, MAX_NORM / (grad_norm + 1e-06))
    kernel_step = kernel_own * factor
    kernel_old = lax.dynamic_slice_in_dim(kernels, owner_start, share_len)
    kernel_mom_new = MOMENTUM * kernel_momentum + kernel_step
    kernel_new = kernel_old - LEARN_RATE * (kernel_step + MOMENTUM * kernel_mom_new)
    kernel_ema_new = EMA_DECAY * kernel_average + (1.0 - EMA_DECAY) * kernel_new
    affine_step = affine_sum * factor
    affine_mom_new = MOMENTUM * affine_momentum + affine_step
    affine_new = affine - AFFINE_RATE * (affine_step + MOMENTUM * affine_mom_new)
    affine_ema_new = EMA_DECAY * affine_average + (1.0 - EMA_DECAY) * affine_new
    return (
        noise_loss,
        grad_norm,
        kernel_new,
        kernel_mom_new,
        kernel_ema_new,
        kernel_new.astype(jnp.bfloat16),
        affine_new,
        affine_mom_new,
        affine_ema_new,
        affine_new.astype(jnp.bfloat16),
    )


def solution(mesh):
    in_specs = (
        P("dp", "hor", None),
        P(),
        P(),
        P("dp", "hor", None),
        P("dp"),
        P("dp", "hor"),
        P(),
        P(),
        P("dp"),
        P("dp"),
        P(),
        P(),
    )
    out_specs = (P(), P(), P("dp"), P("dp"), P("dp"), P("dp"), P(), P(), P(), P())
    return jax.shard_map(
        on_device, mesh=mesh, in_specs=in_specs, out_specs=out_specs, check_vma=False
    )
```

```python
import functools
import math
from types import SimpleNamespace

import jax
import jax.numpy as jnp
from jax import lax
from jax.experimental import pallas as pl
from jax.experimental.pallas import tpu as pltpu
from jax.sharding import PartitionSpec as P

TD = 23
C1 = 64
C2 = 128
C3 = 256
TE = 128
TH = 256
KSIZE = 5
GROUPS = 8
NSTEPS = 100


DP, HOR = "dp", "hor"
PRECISE = lax.Precision.HIGHEST
EPSILON = 1e-05
MAX_NORM = 0.02
LEARN_RATE = 200.0
AFFINE_RATE = 1500.0
MOMENTUM = 0.9
EMA_DECAY = 0.5


def padded_2(cells, sides, width):
    for axis, dim in sides:
        if axis is None:
            pads = [(0, 0)] * cells.ndim
            pads[dim] = (width, width)
            cells = jnp.pad(cells, pads)
            continue
        count = lax.axis_size(axis)
        ends = count - 1
        head = lax.slice_in_dim(cells, 0, width, axis=dim)
        tail = lax.slice_in_dim(cells, cells.shape[dim] - width, cells.shape[dim], axis=dim)
        cells = jnp.concatenate(
            [
                lax.ppermute(tail, axis, [(i, (i + 1) % count) for i in range(ends)]),
                cells,
                lax.ppermute(head, axis, [((i + 1) % count, i) for i in range(ends)]),
            ],
            axis=dim,
        )
    return cells


def sum_over(values, axis):
    return values if axis is None else lax.psum(values, axis)


def axis_length(axis):
    return 1 if axis is None else lax.axis_size(axis)


def layout_shapes():
    kernel_shapes = []
    affine_shapes = []
    for width_in, width_out in [
        (TD, C1),
        (C1, C2),
        (C2, C3),
        (C3, C3),
        (C3 + C3, C2),
        (C2 + C2, C1),
    ]:
        matrices = [
            ("conv_one", KSIZE * width_in, width_out),
            ("conv_two", KSIZE * width_out, width_out),
            ("time_proj", TE, width_out),
        ]
        vectors = [
            (entry_name, width_out)
            for entry_name in [
                "bias_one",
                "gain_one",
                "shift_one",
                "time_bias",
                "bias_two",
                "gain_two",
                "shift_two",
            ]
        ]
        if width_in != width_out:
            matrices.append(("res_proj", width_in, width_out))
            vectors.append(("res_bias", width_out))
        kernel_shapes.append(matrices)
        affine_shapes.append(vectors)
    kernel_shapes.append(
        [
            ("head_conv", KSIZE * C1, C1),
            ("head_out", C1, TD),
            ("embed_one", TE, TH),
            ("embed_two", TH, TE),
        ]
    )
    affine_shapes.append(
        [
            ("head_bias", C1),
            ("head_gain", C1),
            ("head_shift", C1),
            ("out_bias", TD),
            ("embed_bias_one", TH),
            ("embed_bias_two", TE),
        ]
    )
    return (kernel_shapes, affine_shapes)


def unpack(kernels, affine):
    kernel_shapes, affine_shapes = layout_shapes()
    members_all = []
    cursor = 0
    for entries in kernel_shapes:
        members = SimpleNamespace()
        for entry_name, height, breadth in entries:
            piece = kernels[cursor : cursor + height * breadth].reshape(height, breadth)
            setattr(members, entry_name, piece)
            cursor += height * breadth
        members_all.append(members)
    cursor = 0
    for position, entries in enumerate(affine_shapes):
        for entry_name, length in entries:
            setattr(members_all[position], entry_name, affine[cursor : cursor + length])
            cursor += length
    return members_all


def pack_flat(grad_list):
    kernel_shapes, affine_shapes = layout_shapes()
    kernel_pieces = []
    affine_pieces = []
    for position, entries in enumerate(kernel_shapes):
        for entry_name, height, breadth in entries:
            kernel_pieces.append(
                vars(grad_list[position])
                .get(entry_name, jnp.zeros((height, breadth), jnp.float32))
                .reshape(-1)
            )
    for position, entries in enumerate(affine_shapes):
        for entry_name, length in entries:
            affine_pieces.append(
                vars(grad_list[position]).get(entry_name, jnp.zeros((length,), jnp.float32))
            )
    return (jnp.concatenate(kernel_pieces), jnp.concatenate(affine_pieces))


def mish_act(value):
    return value * jnp.tanh(jax.nn.softplus(value))


def mish_grad(value, upstream):
    return jax.vjp(mish_act, value)[1](upstream)[0]


def sinusoid(steps_vec):
    half_width = TE // 2
    ladder = jnp.exp(
        -math.log(10000.0) * jnp.arange(half_width).astype(jnp.float32) / (half_width - 1)
    )
    angles = steps_vec.astype(jnp.float32)[:, None] * ladder[None, :]
    return jnp.concatenate([jnp.sin(angles), jnp.cos(angles)], axis=1)


def signal_level(steps_vec):
    ratio = (steps_vec.astype(jnp.float32) + 1.0) / NSTEPS
    cosine_now = jnp.cos((ratio + 0.008) / 1.008 * math.pi / 2)
    cosine_zero = math.cos(0.008 / 1.008 * math.pi / 2)
    return (cosine_now / cosine_zero) ** 2


def time_parts(kernel_flat, affine_flat, steps_vec):
    members_all = unpack(kernel_flat, affine_flat)
    last_group = members_all[6]
    hidden = mish_act(
        jnp.dot(sinusoid(steps_vec), last_group.embed_one, precision=PRECISE)
        + last_group.embed_bias_one
    )
    feature = mish_act(
        jnp.dot(hidden, last_group.embed_two, precision=PRECISE) + last_group.embed_bias_two
    )
    return tuple(
        (
            jnp.dot(feature, members_all[block_index].time_proj, precision=PRECISE)
            + members_all[block_index].time_bias
            for block_index in range(6)
        )
    )


def conv_forward(inputs_low, weight_low, axis):
    padded = padded_2(inputs_low, ((axis, 1),), 2)
    frames = inputs_low.shape[1]
    channels = inputs_low.shape[2]
    running = 0.0
    for offset in range(KSIZE):
        running = running + jnp.einsum(
            "blc,cd->bld",
            padded[:, offset : offset + frames],
            weight_low[offset * channels : (offset + 1) * channels],
            preferred_element_type=jnp.float32,
        )
    return (running, padded)


def conv_backward(grad_low, padded, weight_low, axis):
    grad_padded = padded_2(grad_low, ((axis, 1),), 2)
    frames = grad_low.shape[1]
    channels = padded.shape[2]
    pieces = []
    running = 0.0
    for offset in range(KSIZE):
        pieces.append(
            jnp.einsum(
                "blc,bld->cd",
                padded[:, offset : offset + frames],
                grad_low,
                preferred_element_type=jnp.float32,
            )
        )
        start_row = KSIZE - 1 - offset
        running = running + jnp.einsum(
            "bld,cd->blc",
            grad_padded[:, start_row : start_row + frames],
            weight_low[offset * channels : (offset + 1) * channels],
            preferred_element_type=jnp.float32,
        )
    return (running, jnp.concatenate(pieces, axis=0))


def group_norm(values, gain_vec, shift_vec, axis):
    horizons, frames, channels = values.shape
    grouped = values.reshape(horizons, frames, GROUPS, channels // GROUPS)
    sum_one, sum_two = sum_over(
        (jnp.sum(grouped, axis=(1, 3)), jnp.sum(grouped * grouped, axis=(1, 3))), axis
    )
    group_count = frames * axis_length(axis) * (channels // GROUPS)
    average = sum_one / group_count
    inverse = lax.rsqrt(sum_two / group_count - average * average + EPSILON)
    normed = ((grouped - average[:, None, :, None]) * inverse[:, None, :, None]).reshape(
        horizons, frames, channels
    )
    return (normed * gain_vec + shift_vec, (normed, inverse))


def group_norm_back(upstream, norm_stats, gain_vec, axis):
    normed, inverse = norm_stats
    horizons, frames, channels = normed.shape
    grad_gain = jnp.sum(upstream * normed, axis=(0, 1))
    grad_shift = jnp.sum(upstream, axis=(0, 1))
    scaled = (upstream * gain_vec).reshape(horizons, frames, GROUPS, channels // GROUPS)
    grouped = normed.reshape(horizons, frames, GROUPS, channels // GROUPS)
    sum_one, sum_two = sum_over(
        (jnp.sum(scaled, axis=(1, 3)), jnp.sum(scaled * grouped, axis=(1, 3))), axis
    )
    group_count = frames * axis_length(axis) * (channels // GROUPS)
    result = inverse[:, None, :, None] * (
        scaled
        - sum_one[:, None, :, None] / group_count
        - grouped * sum_two[:, None, :, None] / group_count
    )
    return (result.reshape(horizons, frames, channels), grad_gain, grad_shift)


def block_forward(inputs, members, time_term, axis):
    inputs_low = inputs.astype(jnp.bfloat16)
    weight_one = members.conv_one.astype(jnp.bfloat16)
    weight_two = members.conv_two.astype(jnp.bfloat16)
    conv_out, padded_one = conv_forward(inputs_low, weight_one, axis)
    normed_one, stats_one = group_norm(
        conv_out + members.bias_one, members.gain_one, members.shift_one, axis
    )
    hidden = mish_act(normed_one) + time_term[:, None, :]
    conv_out, padded_two = conv_forward(hidden.astype(jnp.bfloat16), weight_two, axis)
    normed_two, stats_two = group_norm(
        conv_out + members.bias_two, members.gain_two, members.shift_two, axis
    )
    result = mish_act(normed_two)
    if "res_proj" in vars(members):
        weight_side = members.res_proj.astype(jnp.bfloat16)
        result = (
            result
            + jnp.einsum("blc,cd->bld", inputs_low, weight_side, preferred_element_type=jnp.float32)
            + members.res_bias
        )
    else:
        weight_side = None
        result = result + inputs
    return (
        result,
        (
            padded_one,
            stats_one,
            padded_two,
            stats_two,
            inputs_low,
            weight_one,
            weight_two,
            weight_side,
        ),
    )


def block_backward(upstream, kept, members, axis):
    (
        padded_one,
        stats_one,
        padded_two,
        stats_two,
        inputs_low,
        weight_one,
        weight_two,
        weight_side,
    ) = kept
    grad_map = SimpleNamespace()
    grad_normed = mish_grad(stats_two[0] * members.gain_two + members.shift_two, upstream)
    grad_pre, grad_map.gain_two, grad_map.shift_two = group_norm_back(
        grad_normed, stats_two, members.gain_two, axis
    )
    grad_map.bias_two = jnp.sum(grad_pre, axis=(0, 1))
    grad_hidden, grad_map.conv_two = conv_backward(
        grad_pre.astype(jnp.bfloat16), padded_two, weight_two, axis
    )
    time_grad = jnp.sum(grad_hidden, axis=1)
    grad_normed = mish_grad(stats_one[0] * members.gain_one + members.shift_one, grad_hidden)
    grad_pre, grad_map.gain_one, grad_map.shift_one = group_norm_back(
        grad_normed, stats_one, members.gain_one, axis
    )
    grad_map.bias_one = jnp.sum(grad_pre, axis=(0, 1))
    grad_inputs, grad_map.conv_one = conv_backward(
        grad_pre.astype(jnp.bfloat16), padded_one, weight_one, axis
    )
    if weight_side is not None:
        upstream_low = upstream.astype(jnp.bfloat16)
        grad_map.res_bias = jnp.sum(upstream, axis=(0, 1))
        grad_map.res_proj = jnp.einsum(
            "blc,bld->cd", inputs_low, upstream_low, preferred_element_type=jnp.float32
        )
        grad_inputs = grad_inputs + jnp.einsum(
            "bld,cd->blc", upstream_low, weight_side, preferred_element_type=jnp.float32
        )
    else:
        grad_inputs = grad_inputs + upstream
    return (grad_inputs, time_grad, grad_map)


def head_forward(inputs, members, axis):
    weight_conv = members.head_conv.astype(jnp.bfloat16)
    weight_out = members.head_out.astype(jnp.bfloat16)
    conv_out, padded = conv_forward(inputs.astype(jnp.bfloat16), weight_conv, axis)
    normed, norm_stats = group_norm(
        conv_out + members.head_bias, members.head_gain, members.head_shift, axis
    )
    feature_low = mish_act(normed).astype(jnp.bfloat16)
    predicted = (
        jnp.einsum("blc,cd->bld", feature_low, weight_out, preferred_element_type=jnp.float32)
        + members.out_bias
    )
    return (predicted, (padded, norm_stats, feature_low, weight_conv, weight_out))


def head_backward(upstream, kept, members, axis):
    padded, norm_stats, feature_low, weight_conv, weight_out = kept
    grad_map = SimpleNamespace()
    upstream_low = upstream.astype(jnp.bfloat16)
    grad_map.out_bias = jnp.sum(upstream, axis=(0, 1))
    grad_map.head_out = jnp.einsum(
        "blc,bld->cd", feature_low, upstream_low, preferred_element_type=jnp.float32
    )
    grad_feature = jnp.einsum(
        "bld,cd->blc", upstream_low, weight_out, preferred_element_type=jnp.float32
    )
    grad_normed = mish_grad(
        norm_stats[0] * members.head_gain + members.head_shift, grad_feature
    )
    grad_pre, grad_map.head_gain, grad_map.head_shift = group_norm_back(
        grad_normed, norm_stats, members.head_gain, axis
    )
    grad_map.head_bias = jnp.sum(grad_pre, axis=(0, 1))
    grad_inputs, grad_map.head_conv = conv_backward(
        grad_pre.astype(jnp.bfloat16), padded, weight_conv, axis
    )
    return (grad_inputs, grad_map)


BF = jnp.bfloat16
F32 = jnp.float32
HALO = 32
ROW_STARTS = (0, 293, 1445, 5797, 11173, 15013)
LOAD_ROWS = (0, 296, 1448, 5800, 11176, 15016, 16008, 16696)
HEAD_ROW = 16005
OUT_ROW = 16165
EMB_ROW = 16176
FLAT_ROWS = 16696
TABLE_ROWS = 16720
LATE_START = 5792
LATE_ROWS = 16168 - LATE_START
OWN_ROWS = 2112
NKER_ROWS = 2086
OUT_START = OUT_ROW * 128
WIDTHS = ((TD, C1), (C1, C2), (C2, C3), (C3, C3), (C3 + C3, C2), (C2 + C2, C1))
AFF_ROWS = (0, 4, 12, 28, 42, 50)
LAYER_OUT = ((1, 128), (2, 128), (2, 256), (2, 256), (2, 128), (1, 128), (1, 128))
W_ONE = ((640, 128), (640, 256), (640, 256), (1280, 256), (2560, 128), (2560, 128), (640, 128))
W_TWO = ((640, 128), (640, 128), (1280, 256), (1280, 256), (640, 128), (640, 128))
W_RES = ((128, 128), (128, 256), (128, 256), None, (512, 128), (512, 128))
UP, DOWN = 1, 2
TN = (((0,), (0,)), ((), ()))
NT = (((1,), (1,)), ((), ()))


INPUTS = ((0,), (1,), (2,), (3,), (4, 3), (5, 2))


class Refs:
    def __init__(self, names, values):
        vars(self).update(zip(names, values))

    def of(self, kind, block):
        return vars(self).get(f"{kind}{block}")

    def one(self, block):
        return self.of("one", block)

    def two(self, block):
        return self.of("two", block)

    def res(self, block):
        return self.of("res", block)

    def pre_a(self, block):
        return self.of("pre_a", block)

    def pre_b(self, block):
        return self.of("pre_b", block)

    def up(self, block):
        return self.of("up", block)

    def x(self, number):
        return self.of("x", number)


def lanes_of(shape):
    return lax.broadcasted_iota(jnp.int32, shape, 1)


def rows_of(shape):
    return lax.broadcasted_iota(jnp.int32, shape, 0)


def fill_halo(ref):
    halves, padded_rows, lanes = ref.shape
    inner = padded_rows - 2 * HALO
    row = rows_of((16, lanes))
    lane = lanes_of((16, lanes))
    for group in range(2):
        start = inner + 16 * group
        moved = [pltpu.roll(ref[q, start : start + 16, :].astype(F32), 1, 0) for q in range(halves)]
        into = pl.ds(16 * group, 16)
        if halves == 1:
            edge = jnp.where(lane >= 64, pltpu.roll(moved[0], 64, 1), 0.0)
            ref[0, into, :] = jnp.where(row == 0, edge, moved[0]).astype(BF)
        else:
            ref[0, into, :] = jnp.where(row == 0, 0.0, moved[0]).astype(BF)
            ref[1, into, :] = jnp.where(row == 0, moved[0], moved[1]).astype(BF)
        start = HALO + 16 * group
        moved = [pltpu.roll(ref[q, start : start + 16, :].astype(F32), 15, 0) for q in range(halves)]
        into = pl.ds(HALO + inner + 16 * group, 16)
        if halves == 1:
            edge = jnp.where(lane < 64, pltpu.roll(moved[0], 64, 1), 0.0)
            ref[0, into, :] = jnp.where(row == 15, edge, moved[0]).astype(BF)
        else:
            ref[0, into, :] = jnp.where(row == 15, moved[1], moved[0]).astype(BF)
            ref[1, into, :] = jnp.where(row == 15, 0.0, moved[1]).astype(BF)


def exchange_kernel(traj, noise, mask, scale, mean, std, noisy_out, noise_out, counts, noisy_wide, noise_wide):
    pieces, frames, wide = traj.shape
    segment = frames // 8
    quarter = segment // 4
    rows = tile_rows(frames // 7) * 7 if frames % 7 == 0 else tile_rows(frames)

    for piece in range(pieces):

        def fill(index, carry):
            here = pl.ds(pl.multiple_of(index * rows, rows), rows)
            value = noise[piece, here, :]
            clean = (traj[piece, here, :] - mean[...]) / std[...]
            noisy_wide[here, 0:wide] = scale[piece : piece + 1, 0:wide] * clean + (
                scale[4 + piece : 5 + piece, 0:wide] * value
            )
            noise_wide[here, 0:wide] = value
            return carry

        lax.fori_loop(0, frames // rows, fill, 0)
        step = quarter // 2 if quarter % 4 == 0 else quarter

        def gather(index, carry):
            lane = lanes_of((8, 128))

            def one(source, place):
                total = 0.0
                for number in range(4):
                    value = source[pl.ds(quarter * number + place, 8, stride=segment), :]
                    value = jnp.where(lane < wide, value, 0.0)
                    total = total + (pltpu.roll(value, 32 * number, 1) if number else value)
                return total

            for inner in range(0, step, 2):
                place = index * step + inner
                at = pl.multiple_of(8 * place, 16)
                noisy_out[piece, pl.ds(at, 16), :] = jnp.concatenate(
                    [one(noisy_wide, place), one(noisy_wide, place + 1)], axis=0
                ).astype(BF)
                noise_out[piece, pl.ds(at, 8), :] = one(noise_wide, place)
                noise_out[piece, pl.ds(at + 8, 8), :] = one(noise_wide, place + 1)
            return carry

        lax.fori_loop(0, quarter // step, gather, 0)
        total = jnp.sum(mask[piece : piece + 1, :].astype(F32), axis=1, keepdims=True)
        counts[piece : piece + 1, :] = jnp.broadcast_to(total, (1, 128))


def take_apart(source, quarter, store):
    lane = lanes_of((16, 128))

    def step(index, carry):
        at = pl.multiple_of(16 * index, 16)
        got = [source[piece, pl.ds(at, 16), :].astype(F32) for piece in range(4)]
        for inner in range(2):
            here = slice(8 * inner, 8 * inner + 8)
            low = jnp.concatenate([got[0][here], got[1][here]], axis=0)
            high = jnp.concatenate([got[2][here], got[3][here]], axis=0)
            for number in range(4):
                left = pltpu.roll(low, (128 - 32 * number) % 128, 1) if number else low
                right = pltpu.roll(high, (192 - 32 * number) % 128, 1) if number != 2 else high
                value = jnp.where(lane < 64, left, right)
                store(quarter * number + 2 * index + inner, jnp.where(lane % 64 < 32, value, 0.0))
        return carry

    lax.fori_loop(0, quarter // 2, step, 0)


def mish_fast(value):
    grown = jnp.exp(jnp.minimum(value, 20.0))
    top = grown * (grown + 2.0)
    return value * (top / (top + 2.0))


def mish_both(value):
    grown = jnp.exp(jnp.minimum(value, 20.0))
    top = grown * (grown + 2.0)
    inverse = 1.0 / (top + 2.0)
    ratio = top * inverse
    slope = ratio + 4.0 * value * (top - grown) * (inverse * inverse)
    return value * ratio, slope


def fold_rows(value):
    rows, lanes = value.shape
    return jnp.sum(value.reshape(rows // 8, 8, lanes), axis=0)


def down_one_row(value):
    return jnp.sum(value, axis=0, keepdims=True)


def both_halves(row):
    return row + pltpu.roll(row, 64, 1)


def group_sums(first, second, packed):
    lanes = first.shape[1]
    row = rows_of((8, lanes))
    stacked = jnp.where(row == 0, first, jnp.where(row == 1, second, 0.0))
    left = rows_of((lanes, lanes))
    right = lanes_of((lanes, lanes))
    if packed:
        same = (left % 64) // 8 == (right % 64) // 8
    else:
        size = lanes // GROUPS
        same = left // size == right // size
    summed = jnp.dot(stacked, same.astype(F32), precision=PRECISE, preferred_element_type=F32)
    return summed[0:1, :], summed[1:2, :]


def tile_rows(inner):
    for rows in (256, 128, 64, 32, 16):
        if inner % rows == 0:
            return rows


def sweep(halves, inner, body, carry):
    rows = tile_rows(inner)
    per_half = inner // rows

    def step(index, state):
        q = index // per_half
        start = pl.multiple_of((index - q * per_half) * rows, rows)
        return body(q, start, rows, state)

    return lax.fori_loop(0, halves * per_half, step, carry)


def vector(aff, row, width):
    if width == 256:
        base = int(row)
        return jnp.concatenate([aff[base : base + 1, :], aff[base + 1 : base + 2, :]], axis=1)
    base = int(row)
    whole = aff[base : base + 1, :]
    if width == 128:
        return whole
    turned = pltpu.roll(whole, 64, 1)
    lane = lanes_of((1, 128))
    if row == base:
        return jnp.where(lane < 64, whole, turned)
    return jnp.where(lane < 64, turned, whole)


def block_vector(aff, block, number):
    width = WIDTHS[block][1]
    return vector(aff, AFF_ROWS[block] + number * width / 128, width)


def head_vector(aff, number):
    return vector(aff, 54 + number / 2, 64)


def conv_input(xs, q, tap, inner):
    parts = [x[q, pl.ds(16 * tap, inner), :] for x in xs]
    return parts[0] if len(parts) == 1 else jnp.concatenate(parts, axis=1)


def conv_to(xs, weight, bias, out, crossing):
    halves, inner, lanes = out.shape
    zero = jnp.zeros((8, lanes), F32)

    def finish(q, total, state):
        total = total + bias
        out[q] = total
        return state[0] + fold_rows(total), state[1] + fold_rows(total * total)

    if crossing == UP:
        wide = jnp.concatenate([conv_input(xs, 0, k, inner) for k in range(KSIZE)], axis=1)
        total = jnp.dot(wide, weight[...], preferred_element_type=F32)
        state = finish(0, total[:, :lanes], (zero, zero))
        return finish(1, total[:, lanes:], state)
    if crossing == DOWN:
        wide = jnp.concatenate(
            [conv_input(xs, q, k, inner) for k in range(KSIZE) for q in range(2)], axis=1
        )
        return finish(0, jnp.dot(wide, weight[...], preferred_element_type=F32), (zero, zero))

    def half(q, state):
        wide = jnp.concatenate([conv_input(xs, q, k, inner) for k in range(KSIZE)], axis=1)
        return finish(q, jnp.dot(wide, weight[...], preferred_element_type=F32), state)

    return lax.fori_loop(0, halves, half, (zero, zero))


def norm_fit(sums, gain, shift, count, packed, stats, layer):
    lanes = gain.shape[1]
    one = down_one_row(sums[0])
    two = down_one_row(sums[1])
    group_one, group_two = group_sums(one, two, packed)
    mean = group_one / count
    inverse = lax.rsqrt(group_two / count - mean * mean + EPSILON)
    scale = inverse * gain
    offset = shift - mean * scale
    for number, row in enumerate((scale, offset, mean, inverse, one)):
        stats[8 * layer + number : 8 * layer + number + 1, 0:lanes] = row
    return scale, offset


def norm_kept(stats, layer, lanes):
    return [stats[8 * layer + n : 8 * layer + n + 1, 0:lanes] for n in range(5)]


def norm_back_fit(sums, kept, gain, count, rows, packed):
    scale, _, mean, inverse, one = kept
    grad_shift = down_one_row(sums[0])
    grad_gain = inverse * (down_one_row(sums[1]) - mean * grad_shift)
    first, second = group_sums(gain * grad_shift, gain * grad_gain, packed)
    first = first / count
    second = second / count
    slope = -inverse * inverse * second
    level = -inverse * first - slope * mean
    grad_bias = scale * grad_shift + slope * one + level * rows
    if packed:
        grad_shift, grad_gain, grad_bias = [both_halves(v) for v in (grad_shift, grad_gain, grad_bias)]
    return slope, level, grad_bias, grad_gain, grad_shift


def in_steps(count, step, body):
    full = count // step

    def move(index, carry):
        body(pl.multiple_of(index * step, step), step)
        return carry

    if full > 1:
        lax.fori_loop(0, full, move, 0)
    elif full:
        body(0, step)
    if count % step:
        body(full * step, count % step)


def unpack_pairs(flat, start, count, out):
    def move(at, step):
        rows = flat[pl.ds(start + at, step), :]
        turned = pltpu.roll(rows, 64, 1)
        lane = lanes_of(rows.shape)
        out[pl.ds(2 * at, step, stride=2), :] = jnp.where(lane < 64, rows, turned)
        out[pl.ds(2 * at + 1, step, stride=2), :] = jnp.where(lane < 64, turned, rows)

    in_steps(count, 128, move)


def pack_pairs(source, out, start, count):
    def move(at, step):
        even = source[pl.ds(2 * at, step, stride=2), :]
        odd = pltpu.roll(source[pl.ds(2 * at + 1, step, stride=2), :], 64, 1)
        out[pl.ds(start + at, step), :] = jnp.where(lanes_of(even.shape) < 64, even, odd)

    in_steps(count, 128, move)


def spread_pairs(pairs, start, count, weight, to, size):
    rows = min(-(-count // 32) * 32, size)
    value = pairs[start : start + rows, :]
    keep = rows_of(value.shape) < count
    lane = lanes_of(value.shape)
    weight[to : to + rows, :] = jnp.where(keep & (lane < 64), value, 0.0).astype(BF)
    weight[to + size : to + size + rows, :] = jnp.where(keep & (lane >= 64), value, 0.0).astype(BF)


def straight_rows(flat, start, count, out, to):
    def move(at, step):
        out[pl.ds(to + at, step), :] = flat[pl.ds(start + at, step), :].astype(out.dtype)

    in_steps(count, 256, move)


def wide_rows(flat, start, count, out, to):
    def move(at, step):
        for half in range(2):
            out[pl.ds(to + at, step), 128 * half : 128 * half + 128] = flat[
                pl.ds(start + 2 * at + half, step, stride=2), :
            ].astype(out.dtype)

    in_steps(count, 128, move)


def prepare_block(block, c):
    flat = c.flat
    start = ROW_STARTS[block]
    width_in, width_out = WIDTHS[block]
    one, two = c.one(block), c.two(block)
    res = c.res(block)
    proj, at = c.proj, TE * block
    pairs = c.pairs
    if width_out == 64:
        chunks = 592 if block == 0 else 1984
        unpack_pairs(flat, start, chunks // 2, pairs)
        size = 64 if block == 0 else 256
        if block == 0:
            one[...] = jnp.zeros_like(one)
            res[...] = jnp.zeros_like(res)
        for k in range(KSIZE):
            spread_pairs(pairs, width_in * k, width_in, one, 2 * size * k, size)
            spread_pairs(pairs, KSIZE * width_in + 64 * k, 64, two, 128 * k, 64)
        cursor = KSIZE * (width_in + 64)
        proj[at : at + TE, 0:128] = pairs[cursor : cursor + TE, :]
        spread_pairs(pairs, cursor + TE, width_in, res, 0, size)
    elif width_out == 128:
        if block == 1:
            one[...] = jnp.zeros_like(one)
            res[...] = jnp.zeros_like(res)
            for k in range(KSIZE + 1):
                source = start + 64 * k if k < KSIZE else start + 320 + 640 + TE
                value = flat[source : source + 64, :].astype(BF)
                into, base = (one, 128 * k) if k < KSIZE else (res, 0)
                into[base : base + 64, 0:128] = value
                into[base + 64 : base + 128, 128:256] = value
        else:
            straight_rows(flat, start, KSIZE * width_in, one, 0)
            straight_rows(flat, start + KSIZE * width_in + 640 + TE, width_in, res, 0)
        straight_rows(flat, start + KSIZE * width_in, 640, two, 0)
        cursor = start + KSIZE * width_in + 640
        proj[at : at + TE, 0:128] = flat[cursor : cursor + TE, :]
    else:
        wide_rows(flat, start, KSIZE * width_in, one, 0)
        wide_rows(flat, start + 2 * KSIZE * width_in, 1280, two, 0)
        cursor = start + 2 * (KSIZE * width_in + 1280)
        wide_rows(flat, cursor, TE, proj, at)
        if res is not None:
            wide_rows(flat, cursor + 2 * TE, width_in, res, 0)


def exact_dot(left, right, dims=(((1,), (0,)), ((), ()))):
    return lax.dot_general(left, right, dims, precision=PRECISE, preferred_element_type=F32)


CROSSING = (None, UP, None, None, None, DOWN)


def counts_of(frames, block):
    width = WIDTHS[block][1] if block < 6 else C1
    return frames * (width // GROUPS)


def forward_kernel(c, far, into, sems):
    aff, stats, terms = c.aff, c.stats, c.terms
    inner = c.pre_a0.shape[1]
    frames = 2 * inner
    saves = []

    def save(source, target):
        copy = pltpu.make_async_copy(source, target, sems.at[16 + len(saves)])
        copy.start()
        saves.append(copy)

    loads = []
    for number, (low, high) in enumerate(zip(LOAD_ROWS[:-1], LOAD_ROWS[1:])):
        part = pl.ds(low, high - low)
        copy = pltpu.make_async_copy(far.flat.at[part, :], c.flat.at[part, :], sems.at[number])
        loads.append(copy)
    order = (6, 0, 1, 2, 3, 4, 5)
    for number in order:
        loads[number].start()
    loads[6].wait()
    flat, pairs, embed = c.flat, c.pairs, c.embed_two
    unpack_pairs(flat, EMB_ROW, FLAT_ROWS - EMB_ROW, pairs)
    quarter = [pairs[pl.ds(1 + n, TE, stride=4), :] for n in range(4)]
    lane = lanes_of((TE, 128))
    embed_one = jnp.concatenate(
        [jnp.where(lane < 64, quarter[0], quarter[1]), jnp.where(lane < 64, quarter[2], quarter[3])], axis=1
    )
    embed[...] = jnp.where(
        lanes_of((TH, 128)) < 64, pairs[pl.ds(513, TH, stride=2), :], pairs[pl.ds(514, TH, stride=2), :]
    )
    sinus = c.sinus[...]
    bias = vector(aff, 56, 256)
    kept = c.kept
    hidden_pre = exact_dot(sinus, embed_one) + bias
    hidden = mish_fast(hidden_pre)
    feature_pre = exact_dot(hidden, embed[...]) + vector(aff, 58, 128)
    feature = mish_fast(feature_pre)
    for number, value in enumerate((hidden_pre, hidden, feature_pre, feature)):
        kept[8 * number : 8 * number + 8, 0 : value.shape[1]] = value
    save(c.embed_two, into.embed_two)
    x0 = c.x0

    def put_noisy(group, value):
        x0[0, pl.ds(pl.multiple_of(HALO + 16 * group, 16), 16), :] = value.astype(BF)

    take_apart(c.noisy, inner // 64, put_noisy)
    fill_halo(x0)
    save(c.x0, into.x0)

    for block in range(6):
        loads[block].wait()
        prepare_block(block, c)
        for get in (Refs.one, Refs.two, Refs.res):
            if get(c, block) is not None:
                save(get(c, block), get(into, block))
        halves, lanes = LAYER_OUT[block]
        packed = halves == 1
        count = counts_of(frames, block)
        width = WIDTHS[block][1]
        lane_bias = block_vector(aff, block, 3)
        term = exact_dot(feature, c.proj[TE * block : TE * block + TE, 0:lanes])[0:1, :] + lane_bias
        terms[8 * block : 8 * block + 1, 0:lanes] = term
        xs = [c.x(number) for number in INPUTS[block]]
        pre_a, pre_b = c.pre_a(block), c.pre_b(block)
        sums = conv_to(xs, c.one(block), block_vector(aff, block, 0), pre_a, CROSSING[block])
        save(pre_a, into.pre_a(block))
        scale, offset = norm_fit(
            sums, block_vector(aff, block, 1), block_vector(aff, block, 2), count, packed, stats, 2 * block
        )
        hid = c.hid.at[0:halves, :, 0:lanes]

        def to_hidden(q, start, rows, carry):
            value = mish_fast(pre_a[q, pl.ds(start, rows), :] * scale + offset) + term
            hid[q, pl.ds(HALO + start, rows), :] = value.astype(BF)
            return carry

        sweep(halves, inner, to_hidden, 0)
        fill_halo(hid)
        sums = conv_to([hid], c.two(block), block_vector(aff, block, 4), pre_b, None)
        save(pre_b, into.pre_b(block))
        scale_b, offset_b = norm_fit(
            sums, block_vector(aff, block, 5), block_vector(aff, block, 6), count, packed, stats, 2 * block + 1
        )
        side = c.side
        res = c.res(block)
        if res is not None:
            res_bias = block_vector(aff, block, 7)
            if CROSSING[block] == UP:
                total = jnp.dot(conv_input(xs, 0, 2, inner), res[...], preferred_element_type=F32)
                side[0, :, 0:lanes] = total[:, :lanes] + res_bias
                side[1, :, 0:lanes] = total[:, lanes:] + res_bias
            elif CROSSING[block] == DOWN:
                wide = jnp.concatenate([conv_input(xs, q, 2, inner) for q in range(2)], axis=1)
                side[0, :, 0:lanes] = jnp.dot(wide, res[...], preferred_element_type=F32) + res_bias
            else:
                for q in range(halves):
                    side[q, :, 0:lanes] = (
                        jnp.dot(conv_input(xs, q, 2, inner), res[...], preferred_element_type=F32) + res_bias
                    )
        out = c.x(block + 1)

        def to_output(q, start, rows, carry):
            value = mish_fast(pre_b[q, pl.ds(start, rows), :] * scale_b + offset_b)
            value = value + side[q, pl.ds(start, rows), 0:lanes]
            if block == 2:
                side[q, pl.ds(start, rows), 0:lanes] = value
            out[q, pl.ds(HALO + start, rows), :] = value.astype(BF)
            return carry

        sweep(halves, inner, to_output, 0)
        fill_halo(out)
        save(out, into.x(block + 1))
    unpack_pairs(flat, HEAD_ROW, 160, pairs)
    for k in range(KSIZE):
        spread_pairs(pairs, 64 * k, 64, c.one6, 128 * k, 64)
    save(c.one6, into.one6)
    sums = conv_to([c.x6], c.one6, head_vector(aff, 0), c.pre_a6, None)
    save(c.pre_a6, into.pre_a6)
    norm_fit(sums, head_vector(aff, 1), head_vector(aff, 2), counts_of(frames, 6), True, stats, 12)
    for source, target in ((stats, into.stats), (terms, into.terms), (kept, into.kept), (c.proj, into.proj)):
        save(source, target)
    for copy in saves:
        copy.wait()


def put_rows(value, out, start):
    rows, lanes = value.shape
    if lanes == 128:
        out[start : start + rows, :] = value
    else:
        out[pl.ds(start, rows, stride=2), :] = value[:, 0:128]
        out[pl.ds(start + 1, rows, stride=2), :] = value[:, 128:256]


def conv_dx(dy, weight, size, inner, crossing, emit):
    halves = dy.shape[0]

    def taps(pick):
        total = 0.0
        for k in range(KSIZE):
            total = total + lax.dot_general(
                pick(KSIZE - 1 - k), weight[size * k : size * k + size, :], NT, preferred_element_type=F32
            )
        return total

    if crossing == UP:
        emit(0, taps(lambda k: jnp.concatenate([conv_input([dy], q, k, inner) for q in range(2)], axis=1)))
    elif halves == 1:
        emit(0, taps(lambda k: conv_input([dy], 0, k, inner)))
    else:

        def half(q, carry):
            emit(q, taps(lambda k: conv_input([dy], q, k, inner)))
            return carry

        lax.fori_loop(0, halves, half, 0)


def conv_dw(xs, dy, inner, crossing, acc, extra=None):
    def dys(q):
        parts = [conv_input([dy], q, KSIZE - 1 - k, inner) for k in range(KSIZE)]
        if extra is not None:
            parts.append(extra[q, :, 0 : dy.shape[2]])
        return parts

    def product(left, right):
        return lax.dot_general(left, right, TN, preferred_element_type=F32)

    if crossing == UP:
        both = zip(dys(0), dys(1))
        value = product(conv_input(xs, 0, 2, inner), jnp.concatenate([p for pair in both for p in pair], axis=1))
        acc[0 : value.shape[0], 0 : value.shape[1]] = value
        return
    if crossing == DOWN:
        left = jnp.concatenate([conv_input(xs, q, 2, inner) for q in range(2)], axis=1)
        value = product(left, jnp.concatenate(dys(0), axis=1))
        acc[0 : value.shape[0], 0 : value.shape[1]] = value
        return
    for q in range(dy.shape[0]):
        value = product(conv_input(xs, q, 2, inner), jnp.concatenate(dys(q), axis=1))
        if q == 0:
            acc[0 : value.shape[0], 0 : value.shape[1]] = value
        else:
            acc[0 : value.shape[0], 0 : value.shape[1]] += value


def fold_pairs(acc, tap, size, rows):
    lanes = slice(128 * tap, 128 * tap + 128)
    return acc[0:rows, lanes] + pltpu.roll(acc[size : size + rows, lanes], 64, 1)


def put_vector(grads, row, width, value):
    base = int(row)
    if width == 256:
        grads[base : base + 1, :] = value[:, 0:128]
        grads[base + 1 : base + 2, :] = value[:, 128:256]
    elif width == 128:
        grads[base : base + 1, :] = value
    else:
        lane = lanes_of((1, 128))
        keep = lane < 64 if row == base else lane >= 64
        grads[base : base + 1, :] = jnp.where(keep, value, grads[base : base + 1, :])


def norm_backward(c, layer, pre, gain, count, packed, upstream, dy, also=None):
    halves, inner, lanes = pre.shape
    kept = norm_kept(c.stats, layer, lanes)
    dv = c.dv
    zero = jnp.zeros((8, lanes), F32)

    def first(q, start, rows, state):
        here = pl.ds(start, rows)
        value = pre[q, here, :]
        act, slope = mish_both(value * kept[0] + kept[1])
        up = upstream(q, here)
        if also is not None:
            also(q, here, act, up)
        grad = up * slope
        dv[q, here, 0:lanes] = grad
        return state[0] + fold_rows(grad), state[1] + fold_rows(grad * value), state[2] + fold_rows(up)

    sums = sweep(halves, inner, first, (zero, zero, zero))
    rows_each = float(inner * halves)
    slope, level, grad_bias, grad_gain, grad_shift = norm_back_fit(sums, kept, gain, count, rows_each, packed)
    scale = kept[0]

    def second(q, start, rows, carry):
        here = pl.ds(start, rows)
        value = scale * dv[q, here, 0:lanes] + (slope * pre[q, here, :] + level)
        dy[q, pl.ds(HALO + start, rows), :] = value.astype(BF)
        return carry

    sweep(halves, inner, second, 0)
    fill_halo(dy)
    total = down_one_row(sums[2])
    return grad_bias, grad_gain, grad_shift, both_halves(total) if packed else total


def backward_block(block, c, base, copies, need):
    aff, grads, table, acc = c.aff, c.agrad, c.table, c.acc
    halves, lanes = LAYER_OUT[block]
    packed = halves == 1
    width_in, width_out = WIDTHS[block]
    inner = c.pre_a(block).shape[1]
    count = counts_of(2 * inner, block)
    up = c.up(block)
    low = c.low
    dy = c.dy.at[0:halves, :, 0:lanes]
    act_low = c.act
    res = c.res(block)
    xs = [c.x(number) for number in INPUTS[block]]
    start = ROW_STARTS[block] - base
    spot = AFF_ROWS[block]
    unit = width_out / 128

    def keep_low(q, here, act, value):
        low[q, here, 0:lanes] = value.astype(BF)

    need(copies.pre_b(block), copies.up(block))
    got = norm_backward(
        c, 2 * block + 1, c.pre_b(block), block_vector(aff, block, 5), count, packed,
        lambda q, here: up[q, here, :], dy, keep_low if res is not None else None,
    )
    for number, value in zip((4, 5, 6, 7), got):
        if number < 7 or res is not None:
            put_vector(grads, spot + number * unit, width_out, value)
    dv = c.dv

    def emit_hidden(q, value):
        dv[q, :, 0:lanes] = value

    need(copies.two(block))
    conv_dx(dy, c.two(block), lanes, inner, None, emit_hidden)
    term = c.terms[8 * block : 8 * block + 1, 0:lanes]
    dy_two = dy
    dy_one = c.ey.at[0:halves, :, 0:lanes]

    def keep_act(q, here, act, value):
        act_low[q, here, 0:lanes] = (act + term).astype(BF)

    need(copies.pre_a(block))
    got = norm_backward(
        c, 2 * block, c.pre_a(block), block_vector(aff, block, 1), count, packed,
        lambda q, here: dv[q, here, 0:lanes], dy_one, keep_act,
    )
    for number, value in zip((0, 1, 2, 3), got):
        put_vector(grads, spot + number * unit, width_out, value)
    time_row = got[3]
    c.tgrad[8 * block : 8 * block + 1, 0:lanes] = time_row

    def plain_dw(left, right_ref):
        for q in range(halves):
            parts = jnp.concatenate([conv_input([right_ref], q, KSIZE - 1 - k, inner) for k in range(KSIZE)], axis=1)
            value = lax.dot_general(left[q, :, 0:lanes], parts, TN, preferred_element_type=F32)
            if q == 0:
                acc[0:lanes, 0 : KSIZE * lanes] = value
            else:
                acc[0:lanes, 0 : KSIZE * lanes] += value

    plain_dw(act_low, dy_two)
    pairs = c.pairs
    feature = c.kept[24:32, 0:128]
    row = rows_of((8, lanes))
    outer = exact_dot(
        jnp.where(rows_of((8, 128)) == 0, feature, 0.0), jnp.where(row == 0, time_row, 0.0), TN
    )
    if width_out == 64:
        at = KSIZE * width_in
        for k in range(KSIZE):
            pairs[at + 64 * k : at + 64 * k + 64, :] = fold_pairs(acc, k, 64, 64)
        pairs[at + 320 : at + 320 + TE, :] = outer
    else:
        at = start + KSIZE * width_in * (width_out // 128)
        for k in range(KSIZE):
            put_rows(acc[0:lanes, lanes * k : lanes * k + lanes], table, at + k * lanes * (width_out // 128))
        put_rows(outer, table, at + 5 * lanes * (width_out // 128))
    crossing = CROSSING[block]
    need(copies.one(block), copies.res(block), *[copies.x(number) for number in INPUTS[block]])
    if block == 2:
        need(copies.up(1))
    if block > 0:
        size = {None: sum(x.shape[2] for x in xs), UP: 128, DOWN: 512}[crossing]

        def emit(q, value):
            if res is not None:
                if crossing == UP:
                    side = jnp.concatenate([low[0, :, 0:lanes], low[1, :, 0:lanes]], axis=1)
                else:
                    side = low[q, :, 0:lanes]
                value = value + lax.dot_general(side, res[...], NT, preferred_element_type=F32)
            if block == 5:
                for h in range(2):
                    c.up4[h] = value[:, 256 * h : 256 * h + 128]
                    c.up1[h] = value[:, 256 * h + 128 : 256 * h + 256]
            elif block == 4:
                c.up3[q] = value[:, 0:256]
                c.up2[q] = value[:, 256:512]
            elif block == 3:
                c.up2[q] = c.up2[q] + (value + up[q])
            elif block == 2:
                c.up1[q] = c.up1[q] + value
            else:
                c.up0[0] = value

        conv_dx(dy_one, c.one(block), size, inner, crossing, emit)
    conv_dw(xs, dy_one, inner, crossing, acc, low if res is not None else None)
    if width_out == 64:
        size = 64 if block == 0 else 256
        rows = 24 if block == 0 else 256
        for k in range(KSIZE):
            value = fold_pairs(acc, k, size, rows)
            pairs[width_in * k : width_in * k + width_in, :] = value[0:width_in]
        at = KSIZE * (width_in + 64) + TE
        pairs[at : at + width_in, :] = fold_pairs(acc, KSIZE, size, rows)[0:width_in]
        if block == 0:
            after = table[288:296, :]
            pack_pairs(pairs, table, start, 296)
            table[288:296, :] = jnp.where(rows_of((8, 128)) < 5, table[288:296, :], after)
        else:
            pack_pairs(pairs, table, start, 992)
    else:
        unit_rows = width_out // 128
        for k in range(KSIZE + (0 if res is None else 1)):
            at = start + k * width_in * unit_rows
            if k == KSIZE:
                at = start + (KSIZE * (width_in + width_out) + TE) * unit_rows
            if crossing == UP:
                value = acc[0:64, 256 * k : 256 * k + 128] + acc[64:128, 256 * k + 128 : 256 * k + 256]
            else:
                value = acc[0:width_in, width_out * k : width_out * k + width_out]
            put_rows(value, table, at)


def load_all(c, far, sems):
    copies = {}
    for number, (name, source) in enumerate(vars(far).items()):
        if name in vars(c):
            copies[name] = pltpu.make_async_copy(source, vars(c)[name], sems.at[number])
            copies[name].start()
    done = set()

    def need(*wanted):
        for copy in wanted:
            if copy is not None and id(copy) not in done:
                done.add(id(copy))
                copy.wait()

    return Refs(copies.keys(), copies.values()), need


def late_kernel(c, far, into, sems):
    copies, need = load_all(c, far, sems)
    aff, grads = c.aff, c.agrad
    outs = []

    def give(source, target):
        copy = pltpu.make_async_copy(source, target, sems.at[len(vars(far)) + len(outs)])
        copy.start()
        outs.append(copy)

    grads[...] = jnp.zeros_like(grads)
    need(copies.noise_in)
    noise_in, noise = c.noise_in, c.noise
    last = noise_in.shape[1] - 8

    def put_noise(group, value):
        noise[pl.ds(pl.multiple_of(16 * group, 16), 16), :] = value

    take_apart(noise_in, c.pre_a6.shape[1] // 64, put_noise)
    tail = noise_in[0, last:, :] + noise_in[1, last:, :] + noise_in[2, last:, :] + noise_in[3, last:, :]
    length = tail[0:1, :]
    scale_out = 1.0 / (tail[1:2, :] * TD)
    need(copies.stats, copies.terms, copies.kept, copies.pre_a6)
    pre = c.pre_a6
    inner = pre.shape[1]
    kept = norm_kept(c.stats, 12, 128)
    act, low, up = c.act, c.low, c.up5
    lane = lanes_of((1, 128))
    spot = lane % 64
    out_row = aff[55:56, :]
    out_bias = jnp.where(spot < TD, jnp.where(lane < 64, pltpu.roll(out_row, 64, 1), out_row), 0.0)
    segment = inner // 16

    def to_feature(q, start, rows, carry):
        here = pl.ds(start, rows)
        act[0, here, 0:128] = mish_fast(pre[0, here, :] * kept[0] + kept[1]).astype(BF)
        return carry

    sweep(1, inner, to_feature, 0)
    dv = c.dv
    dv[0, :, 0:128] = jnp.dot(act[0, :, 0:128], c.wout[...], preferred_element_type=F32)

    def to_loss(q, start, rows, state):
        here = pl.ds(start, rows)
        shape = (rows, 128)
        place = rows_of(shape) + start
        lanes = lanes_of(shape)
        frame = (place % 16 + jnp.where(lanes >= 64, 16, 0)) * segment + place // 16
        weight = jnp.where((frame.astype(F32) < length) & (lanes % 64 < TD), 1.0, 0.0)
        difference = weight * (dv[0, here, 0:128] + out_bias - noise[here, :])
        grad = 2.0 * difference * scale_out
        low[0, here, 0:128] = grad.astype(BF)
        return state[0] + fold_rows(difference * difference), state[1] + fold_rows(grad)

    zero = jnp.zeros((8, 128), F32)
    loss, out_sum = sweep(1, inner, to_loss, (zero, zero))
    c.loss[...] = loss * scale_out
    out_sum = both_halves(down_one_row(out_sum))
    c.gout[...] = lax.dot_general(act[0, :, 0:128], low[0, :, 0:128], TN, preferred_element_type=F32)
    dv[0, :, 0:128] = lax.dot_general(low[0, :, 0:128], c.wout[...], NT, preferred_element_type=F32)
    dy = c.dy.at[0:1, :, 0:128]
    got = norm_backward(
        c, 12, pre, head_vector(aff, 1), counts_of(2 * inner, 6), True, lambda q, here: dv[q, here, 0:128], dy
    )
    grads[54:55, :] = jnp.where(lane < 64, got[0], got[1])
    grads[55:56, :] = jnp.where(lane < 64, got[2], jnp.where(spot < TD, out_sum, 0.0))

    def emit_head(q, value):
        up[0] = value

    need(copies.one6, copies.x6)
    conv_dx(dy, c.one6, 128, inner, None, emit_head)
    conv_dw([c.x6], dy, inner, None, c.acc)
    for k in range(KSIZE):
        c.pairs[64 * k : 64 * k + 64, :] = fold_pairs(c.acc, k, 64, 64)
    pack_pairs(c.pairs, c.table, HEAD_ROW - LATE_START, 160)
    c.tgrad[...] = jnp.zeros_like(c.tgrad)
    backward_block(5, c, LATE_START, copies, need)
    give(c.up1, into.up1)
    backward_block(4, c, LATE_START, copies, need)
    split = -(-(ROW_STARTS[4] - LATE_START) // 8) * 8
    give(c.table.at[split:LATE_ROWS], into.table.at[split:LATE_ROWS])
    backward_block(3, c, LATE_START, copies, need)
    give(c.table.at[0:split], into.table.at[0:split])
    for source, target in ((c.up2, into.up2), (c.tgrad, into.tgrad), (grads, into.agrad)):
        give(source, target)
    need(*vars(copies).values())
    for copy in outs:
        copy.wait()


def early_kernel(c, far, into, sems):
    copies, need = load_all(c, far, sems)
    aff, grads, table = c.aff, c.agrad, c.table
    outs = []
    after = len(vars(far))

    def own_copy(source, target):
        copy = pltpu.make_async_copy(source, target, sems.at[after + len(outs)])
        copy.start()
        outs.append(copy)

    own_copy(far.late.at[0:8], c.edge)
    own_copy(far.late.at[8:LATE_ROWS], table.at[LATE_START + 8 : LATE_START + LATE_ROWS])
    late_edge, late_rest = outs
    need(copies.stats, copies.terms, copies.kept, copies.agrad, copies.tgrad)
    backward_block(2, c, 0, copies, need)
    late_edge.wait()
    lead = rows_of((8, 128)) < ROW_STARTS[3] - LATE_START
    table[LATE_START : LATE_START + 8, :] = jnp.where(lead, table[LATE_START : LATE_START + 8, :], c.edge[...])
    backward_block(1, c, 0, copies, need)
    backward_block(0, c, 0, copies, need)
    need(*vars(copies).values())
    late_rest.wait()
    total = jnp.zeros((8, TE), F32)
    row = rows_of((8, 256))
    for block in range(6):
        lanes = LAYER_OUT[block][1]
        first = jnp.where(rows_of((8, lanes)) == 0, c.tgrad[8 * block : 8 * block + 8, 0:lanes], 0.0)
        if WIDTHS[block][1] == 64:
            first = jnp.where(lanes_of((8, lanes)) < 64, first, 0.0)
        total = total + exact_dot(first, c.proj[TE * block : TE * block + TE, 0:lanes], NT)
    kept = c.kept
    hidden_pre, hidden = kept[0:8, :], kept[8:16, :]
    feature_pre = kept[16:24, 0:128]
    grad_feature = total * mish_both(feature_pre)[1]
    pairs = c.pairs
    second = exact_dot(jnp.where(row == 0, hidden, 0.0), grad_feature, TN)
    put_vector(grads, 58, 128, grad_feature[0:1, :])
    grad_hidden = exact_dot(grad_feature, c.embed_two[...], NT) * mish_both(hidden_pre)[1]
    only = jnp.where(row == 0, grad_hidden, 0.0)
    first = exact_dot(c.sinus[...], only, TN)
    put_vector(grads, 56, 256, grad_hidden[0:1, :])
    grads[60:61, :] = down_one_row(c.loss[...])
    table[OUT_ROW : OUT_ROW + 12, :] = c.hograd[0:12, :]
    table[FLAT_ROWS:TABLE_ROWS, :] = jnp.zeros((TABLE_ROWS - FLAT_ROWS, 128), F32)
    pairs[1024:1040, :] = jnp.zeros((16, 128), F32)
    pairs[0:1, :] = c.hograd[11:12, :]
    for half in range(2):
        value = first[:, 128 * half : 128 * half + 128]
        pairs[pl.ds(1 + 2 * half, TE, stride=4), :] = value
        pairs[pl.ds(2 + 2 * half, TE, stride=4), :] = pltpu.roll(value, 64, 1)
    pairs[pl.ds(513, TH, stride=2), :] = second
    pairs[pl.ds(514, TH, stride=2), :] = pltpu.roll(second, 64, 1)
    pack_pairs(pairs, table, EMB_ROW, FLAT_ROWS - EMB_ROW)
    core = c.core[0]
    keep, send = c.keep, c.send
    share = NKER_ROWS
    step = 176

    for pair in range(4):

        def split(index, carry):
            at = pl.multiple_of(index * step, step)
            even = table[pl.ds(share * (2 * pair) + at, step), :]
            odd = table[pl.ds(share * (2 * pair + 1) + at, step), :]
            keep[pair, pl.ds(at, step), :] = jnp.where(core == 0, even, odd)
            send[pl.ds(OWN_ROWS * pair + at, step), :] = jnp.where(core == 0, odd, even).astype(BF)
            return carry

        lax.fori_loop(0, OWN_ROWS // step, split, 0)
        own_copy(keep.at[pair], into.keep.at[pair])
        span = pl.ds(OWN_ROWS * pair, OWN_ROWS)
        own_copy(send.at[span, :], into.send.at[span, :])
    value = grads[...]
    high = value.astype(BF)
    rest = (value - high.astype(F32)).astype(BF)
    send[4 * OWN_ROWS : 4 * OWN_ROWS + 64, :] = high
    send[4 * OWN_ROWS + 64 : 4 * OWN_ROWS + 128, :] = rest
    grads[...] = high.astype(F32) + rest.astype(F32)
    span = pl.ds(4 * OWN_ROWS, 128)
    own_copy(send.at[span, :], into.send.at[span, :])
    own_copy(grads, into.agrad)
    for copy in outs[2:]:
        copy.wait()


def shape_tables(inner):
    padded = inner + 2 * HALO
    first = dict(
        stats=((104, 256), F32),
        terms=((48, 256), F32),
        kept=((32, 256), F32),
        proj=((6 * TE, 256), F32),
        embed_two=((256, 128), F32),
    )
    other = dict(
        tgrad=((48, 256), F32),
        agrad=((64, 128), F32),
        flat=((FLAT_ROWS, 128), F32),
        pairs=((2048, 128), F32),
        table=((TABLE_ROWS, 128), F32),
        edge=((8, 128), F32),
        send=((4 * OWN_ROWS + 128, 128), BF),
        keep=((4, OWN_ROWS, 128), F32),
        acc=((512, 1536), F32),
        side=((2, inner, 256), F32),
        dv=((2, inner, 256), F32),
        low=((2, inner, 256), BF),
        act=((2, inner, 256), BF),
        noise=((inner, 128), F32),
        noise_in=((4, inner // 8 + 8, 128), F32),
        hid=((2, padded, 256), BF),
        dy=((2, padded, 256), BF),
        ey=((2, padded, 256), BF),
    )
    for number, (halves, lanes) in enumerate(((1, 128),) + LAYER_OUT[:6]):
        first[f"x{number}"] = ((halves, padded, lanes), BF)
    for block in range(7):
        halves, lanes = LAYER_OUT[block]
        first[f"pre_a{block}"] = ((halves, inner, lanes), F32)
        first[f"one{block}"] = (W_ONE[block], BF)
        if block < 6:
            other[f"up{block}"] = ((halves, inner, lanes), F32)
            first[f"pre_b{block}"] = ((halves, inner, lanes), F32)
            first[f"two{block}"] = (W_TWO[block], BF)
            if W_RES[block] is not None:
                first[f"res{block}"] = (W_RES[block], BF)
    return first, other


def run_kernel(body, vmem_in, smem_in, any_in, outs_vmem, outs_any, scratch, sems, cost):
    operands = list(vmem_in.values()) + list(smem_in.values()) + list(any_in.values())
    in_specs = (
        [pl.BlockSpec(memory_space=pltpu.VMEM)] * len(vmem_in)
        + [pl.BlockSpec(memory_space=pltpu.SMEM)] * len(smem_in)
        + [pl.BlockSpec(memory_space=pl.ANY)] * len(any_in)
    )
    out_specs = [pl.BlockSpec(memory_space=pltpu.VMEM)] * len(outs_vmem)
    out_specs += [pl.BlockSpec(memory_space=pl.ANY)] * len(outs_any)
    out_kinds = list(outs_vmem.values()) + list(outs_any.values())
    near = list(vmem_in) + list(smem_in)
    places = (len(near), len(operands), len(operands) + len(outs_vmem), len(operands) + len(out_kinds))

    def call(*refs):
        here, there, results, left, buffers = [
            refs[low:high] for low, high in zip((0,) + places, places + (len(refs) - 1,))
        ]
        c = Refs(near + list(outs_vmem) + list(scratch), here + results + buffers)
        body(c, Refs(any_in, there), Refs(outs_any, left), refs[-1])

    results = pl.pallas_call(
        call,
        out_shape=[jax.ShapeDtypeStruct(*kind) for kind in out_kinds],
        in_specs=in_specs,
        out_specs=out_specs,
        scratch_shapes=[pltpu.VMEM(*kind) for kind in scratch.values()] + [pltpu.SemaphoreType.DMA((sems,))],
        compiler_params=pltpu.CompilerParams(vmem_limit_bytes=VMEM_LIMIT),
        cost_estimate=pl.CostEstimate(flops=cost, bytes_accessed=40000000, transcendentals=0),
    )(*operands)
    return SimpleNamespace(**dict(zip(list(outs_vmem) + list(outs_any), results)))


VMEM_LIMIT = 67043328


def exchange_pieces(traj, noise, mask, signal, mean, std):
    pieces, frames, wide = traj.shape
    scale = jnp.concatenate([jnp.sqrt(signal), jnp.sqrt(1.0 - signal)])
    vmem = pl.BlockSpec(memory_space=pltpu.VMEM)
    return pl.pallas_call(
        exchange_kernel,
        out_shape=[
            jax.ShapeDtypeStruct((pieces, frames // 4, 128), BF),
            jax.ShapeDtypeStruct((pieces, frames // 4 + 8, 128), F32),
            jax.ShapeDtypeStruct((8, 128), F32),
        ],
        in_specs=[vmem] * 6,
        out_specs=[vmem] * 3,
        scratch_shapes=[pltpu.VMEM((frames, 128), F32)] * 2,
    )(traj, noise, mask, jnp.broadcast_to(scale[:, None], (2 * pieces, 128)), mean[None, :], std[None, :])


def whole_horizon(noisy, noise, sinus, core, kernels, affine):
    inner = 4 * noisy.shape[1] * 2
    first, other = shape_tables(inner)
    t = SimpleNamespace(**first, **other)
    flat = jnp.pad(kernels, (0, FLAT_ROWS * 128 - kernels.shape[0])).reshape(FLAT_ROWS, 128)
    aff = jnp.concatenate(
        [affine[:7127], jnp.zeros((41,), F32), affine[7127:], jnp.zeros((640,), F32)]
    ).reshape(64, 128)
    head_out = kernels[OUT_START : OUT_START + C1 * TD].reshape(C1, TD).astype(BF)
    wide_out = jnp.pad(head_out, ((0, 0), (0, 64 - TD)))
    nothing = jnp.zeros((C1, 64), BF)
    wout = jnp.concatenate(
        [jnp.concatenate([wide_out, nothing], axis=1), jnp.concatenate([nothing, wide_out], axis=1)], axis=0
    )
    f = run_kernel(
        forward_kernel,
        dict(noisy=noisy, aff=aff, sinus=sinus),
        {},
        dict(flat=flat),
        {},
        first,
        dict(first, flat=t.flat, pairs=t.pairs, side=t.side, hid=t.hid),
        16 + len(first),
        14000000000,
    )
    late_in = dict(noise_in=noise, stats=f.stats, terms=f.terms, kept=f.kept, pre_a6=f.pre_a6, one6=f.one6, x6=f.x6)
    late_in.update(pre_b5=f.pre_b5, two5=f.two5, pre_a5=f.pre_a5, one5=f.one5, res5=f.res5, x5=f.x5, x2=f.x2)
    late_in.update(pre_b4=f.pre_b4, two4=f.two4, pre_a4=f.pre_a4, one4=f.one4, res4=f.res4, x4=f.x4, x3=f.x3)
    late_in.update(pre_b3=f.pre_b3, two3=f.two3, pre_a3=f.pre_a3, one3=f.one3)
    late_out = dict(table=((LATE_ROWS, 128), F32), up1=t.up1, up2=t.up2, tgrad=t.tgrad, agrad=t.agrad)
    work = dict(dv=t.dv, low=t.low, act=t.act, acc=t.acc, pairs=t.pairs, dy=t.dy, ey=t.ey)
    late = run_kernel(
        late_kernel,
        dict(aff=aff, wout=wout),
        {},
        late_in,
        dict(loss=((8, 128), F32), gout=((128, 128), F32)),
        late_out,
        dict({n: vars(t)[n] for n in late_in}, **late_out, noise=t.noise, up5=t.up5, up4=t.up4, up3=t.up3, **work),
        len(late_in) + len(late_out) + 1,
        16000000000,
    )
    gout = late.gout
    head_grad = (gout[0:64, 0:TD] + gout[64:128, 64 : 64 + TD]).reshape(-1)
    early_in = dict(stats=f.stats, terms=f.terms, kept=f.kept, agrad=late.agrad, tgrad=late.tgrad)
    early_in.update(up2=late.up2, pre_b2=f.pre_b2, two2=f.two2, pre_a2=f.pre_a2, one2=f.one2, res2=f.res2, x2=f.x2)
    early_in.update(up1=late.up1, pre_b1=f.pre_b1, two1=f.two1, pre_a1=f.pre_a1, one1=f.one1, res1=f.res1, x1=f.x1)
    early_in.update(pre_b0=f.pre_b0, two0=f.two0, pre_a0=f.pre_a0, one0=f.one0, res0=f.res0, x0=f.x0)
    early_in.update(proj=f.proj, embed_two=f.embed_two)
    early = run_kernel(
        early_kernel,
        dict(
            aff=aff,
            sinus=jnp.where(jnp.arange(8)[:, None] == 0, sinus, 0.0),
            loss=late.loss,
            hograd=jnp.pad(head_grad, (0, 2048 - C1 * TD)).reshape(16, 128),
        ),
        dict(core=core.reshape(1)),
        dict(early_in, late=late.table),
        {},
        dict(send=t.send, keep=t.keep, agrad=t.agrad),
        dict(
            {n: vars(t)[n] for n in early_in}, table=t.table, send=t.send, keep=t.keep, up0=t.up0, edge=t.edge, **work
        ),
        len(early_in) + 16,
        10000000000,
    )
    return early.send, early.keep, early.agrad


def on_device_xla(
    trajectories,
    dim_means,
    dim_stds,
    noise_draw,
    diffusion_steps,
    valid_mask,
    kernels,
    affine,
    kernel_momentum,
    kernel_average,
    affine_momentum,
    affine_average,
):
    members_all = unpack(kernels, affine)
    valid_total = lax.psum(jnp.sum(valid_mask.astype(jnp.float32)), (DP, HOR))
    signal_now = signal_level(diffusion_steps)[:, None, None]
    clean_frames = (trajectories - dim_means) / dim_stds
    noisy_frames = jnp.sqrt(signal_now) * clean_frames + jnp.sqrt(1.0 - signal_now) * noise_draw

    ring = lax.axis_size(HOR)
    axis = HOR
    if trajectories.shape[0] % ring == 0:
        axis = None
        local = trajectories.shape[0] // ring
        part = lax.axis_index(HOR) * local
        low_frames = noisy_frames.astype(jnp.bfloat16)
        noisy_frames = lax.all_to_all(low_frames, HOR, 0, 1, tiled=True).astype(jnp.float32)
        noise_draw = lax.all_to_all(noise_draw, HOR, 0, 1, tiled=True)
        valid_mask = lax.all_to_all(valid_mask, HOR, 0, 1, tiled=True)
        diffusion_steps = lax.dynamic_slice_in_dim(diffusion_steps, part, local)

    def time_closed(kernel_flat, affine_flat):
        return time_parts(kernel_flat, affine_flat, diffusion_steps)

    time_list, time_pullback = jax.vjp(time_closed, kernels, affine)
    down_one, kept_one = block_forward(noisy_frames, members_all[0], time_list[0], axis)
    down_two, kept_two = block_forward(down_one, members_all[1], time_list[1], axis)
    down_three, kept_three = block_forward(down_two, members_all[2], time_list[2], axis)
    middle, kept_middle = block_forward(down_three, members_all[3], time_list[3], axis)
    up_one, kept_upper = block_forward(
        jnp.concatenate([middle, down_three], axis=2), members_all[4], time_list[4], axis)
    up_two, kept_lower = block_forward(
        jnp.concatenate([up_one, down_two], axis=2), members_all[5], time_list[5], axis)
    predicted, kept_head = head_forward(up_two, members_all[6], axis)
    weight_rows = valid_mask.astype(jnp.float32)[:, :, None]
    difference = predicted - noise_draw
    loss_scale = 1.0 / (valid_total * TD)
    loss_part = jnp.sum(weight_rows * difference * difference) * loss_scale
    grad_predicted = 2.0 * weight_rows * difference * loss_scale
    grad_up_two, head_grads = head_backward(grad_predicted, kept_head, members_all[6], axis)
    grad_joined, time_six, grads_six = block_backward(grad_up_two, kept_lower, members_all[5], axis)
    grad_up_one = grad_joined[:, :, :C2]
    grad_down_two = grad_joined[:, :, C2:]
    grad_joined, time_five, grads_five = block_backward(grad_up_one, kept_upper, members_all[4], axis)
    grad_middle = grad_joined[:, :, :C3]
    grad_down_three = grad_joined[:, :, C3:]
    grad_inputs, time_four, grads_four = block_backward(grad_middle, kept_middle, members_all[3], axis)
    grad_inputs, time_three, grads_three = block_backward(
        grad_down_three + grad_inputs, kept_three, members_all[2], axis
    )
    grad_inputs, time_two, grads_two = block_backward(
        grad_down_two + grad_inputs, kept_two, members_all[1], axis
    )
    grad_inputs, time_one, grads_one = block_backward(grad_inputs, kept_one, members_all[0], axis)
    kernel_grad, affine_grad = pack_flat(
        [grads_one, grads_two, grads_three, grads_four, grads_five, grads_six, head_grads]
    )
    time_kernel, time_affine = time_pullback(
        (time_one, time_two, time_three, time_four, time_five, time_six)
    )
    kernel_grad = kernel_grad + time_kernel
    affine_grad = affine_grad + time_affine
    share_len = kernels.shape[0] // lax.axis_size(DP)
    owner_start = lax.axis_index(DP) * share_len
    kernel_sum, affine_sum, noise_loss = lax.psum(
        (kernel_grad, affine_grad, loss_part), (DP, HOR)
    )
    kernel_own = lax.dynamic_slice_in_dim(kernel_sum, owner_start, share_len)
    squares = jnp.sum(kernel_sum * kernel_sum) + jnp.sum(affine_sum * affine_sum)
    grad_norm = jnp.sqrt(squares)
    factor = jnp.minimum(1.0, MAX_NORM / (grad_norm + 1e-06))
    kernel_step = kernel_own * factor
    kernel_old = lax.dynamic_slice_in_dim(kernels, owner_start, share_len)
    kernel_mom_new = MOMENTUM * kernel_momentum + kernel_step
    kernel_new = kernel_old - LEARN_RATE * (kernel_step + MOMENTUM * kernel_mom_new)
    kernel_ema_new = EMA_DECAY * kernel_average + (1.0 - EMA_DECAY) * kernel_new
    affine_step = affine_sum * factor
    affine_mom_new = MOMENTUM * affine_momentum + affine_step
    affine_new = affine - AFFINE_RATE * (affine_step + MOMENTUM * affine_mom_new)
    affine_ema_new = EMA_DECAY * affine_average + (1.0 - EMA_DECAY) * affine_new
    return (
        noise_loss,
        grad_norm,
        kernel_new,
        kernel_mom_new,
        kernel_ema_new,
        kernel_new.astype(jnp.bfloat16),
        affine_new,
        affine_mom_new,
        affine_ema_new,
        affine_new.astype(jnp.bfloat16),
    )


def swap(value, axis, bit):
    return lax.ppermute(value, axis, [(i, i ^ bit) for i in range(lax.axis_size(axis))])


def total_all(value, axes, count):
    got = lax.all_to_all(jnp.broadcast_to(value, (count, 128)), axes, 0, 0, tiled=True)
    return jnp.sum(got[:, 0])


def pick(stack, index):
    return lax.dynamic_index_in_dim(stack, index, 0, keepdims=False)


def in_low(value):
    return lax.reduce_precision(value, 8, 7)


def two_parts(value):
    high = in_low(value)
    return high, in_low(value - high)


def share_sums(send, keep, small):
    low, wide = jnp.bfloat16, jnp.float32
    place = lax.axis_index(DP)
    seat_x = (place >> 1) & 1
    seat_y = (place >> 2) & 1
    layer = lax.axis_index(HOR)
    part_rows = OWN_ROWS // 4
    half = OWN_ROWS // 2

    def with_small(value, parts):
        return jnp.concatenate([value.reshape(-1, 128), parts[0], parts[1]], axis=0).astype(low)

    def small_of(got):
        tail = got[-128:].astype(wide)
        return tail[:64] + tail[64:]

    got = swap(send, DP, 1)
    grid = (keep + got[:-128].reshape(keep.shape).astype(wide)).reshape(2, 2, OWN_ROWS, 128)
    parts = two_parts(small + small_of(got))
    first, second = grid[:, :, :half], grid[:, :, half:]
    first_in = swap(
        with_small(lax.dynamic_index_in_dim(first, 1 - seat_x, 1, keepdims=False), parts), DP, 2
    )
    second_in = swap(pick(second, 1 - seat_y).astype(low), DP, 4)
    parts = two_parts(parts[0] + parts[1] + small_of(first_in))
    first = lax.dynamic_index_in_dim(first, seat_x, 1, keepdims=False)
    first = first + first_in[:-128].reshape(first.shape).astype(wide)
    second = pick(second, seat_y) + second_in.astype(wide)
    first_in = swap(with_small(pick(first, 1 - seat_y), parts), DP, 4)
    second_in = swap(pick(second, 1 - seat_x).astype(low), DP, 2)
    parts = two_parts(parts[0] + parts[1] + small_of(first_in))
    own = jnp.concatenate(
        [
            pick(first, seat_y) + first_in[:-128].astype(wide),
            pick(second, seat_x) + second_in.astype(wide),
        ],
        axis=0,
    ).reshape(4, part_rows, 128)
    arrived = [swap(with_small(pick(own, layer ^ bits), parts), HOR, bits) for bits in (1, 2, 3)]
    part = pick(own, layer)
    for value in arrived:
        part = part + value[:-128].astype(wide)
    smalls = jnp.stack([parts[0] + parts[1]] + [small_of(value) for value in arrived])
    small = sum(pick(smalls, layer ^ n) for n in range(4))
    return part, small


def all_parts(part):
    layer = lax.axis_index(HOR)
    part_low = in_low(part).astype(jnp.bfloat16)
    parts = jnp.stack([part_low] + [swap(part_low, HOR, bits) for bits in (1, 2, 3)])
    return jnp.concatenate([pick(parts, layer ^ n) for n in range(4)], axis=0)


def on_device(
    trajectories,
    dim_means,
    dim_stds,
    noise_draw,
    diffusion_steps,
    valid_mask,
    kernels,
    affine,
    kernel_momentum,
    kernel_average,
    affine_momentum,
    affine_average,
):
    ring = lax.axis_size(HOR)
    frames = trajectories.shape[1] * ring
    if trajectories.shape[0] != ring or ring != 4 or frames % 512 or lax.axis_size(DP) != 8:
        return on_device_xla(
            trajectories,
            dim_means,
            dim_stds,
            noise_draw,
            diffusion_steps,
            valid_mask,
            kernels,
            affine,
            kernel_momentum,
            kernel_average,
            affine_momentum,
            affine_average,
        )
    total = total_all(jnp.sum(valid_mask.astype(jnp.float32)), DP, lax.axis_size(DP))
    low_out, noise_out, counts = exchange_pieces(
        trajectories, noise_draw, valid_mask, signal_level(diffusion_steps), dim_means, dim_stds
    )
    low_out, total = lax.optimization_barrier((low_out, total))
    noisy = lax.all_to_all(low_out, HOR, 0, 0, tiled=True)
    row = lax.broadcasted_iota(jnp.int32, (4, 8, 128), 1)
    extra = jnp.where(row == 0, counts[:4, None, :], jnp.where(row == 1, total, 0.0))
    noise_out = lax.dynamic_update_slice(noise_out, extra, (0, noise_out.shape[1] - 8, 0))
    noise_out, packed = lax.optimization_barrier((noise_out, kernels))
    noise = lax.all_to_all(noise_out, HOR, 0, 0, tiled=True)
    own_step = lax.dynamic_slice_in_dim(diffusion_steps, lax.axis_index(HOR), 1)
    sinus = jnp.broadcast_to(sinusoid(own_step), (8, TE))
    place = lax.axis_index(DP)
    send, keep, small = whole_horizon(noisy, noise, sinus, place & 1, packed, affine)
    part, small = share_sums(send, keep, small)
    share_len = kernels.shape[0] // lax.axis_size(DP)
    owner_start = place * share_len
    lead = owner_start - place * NKER_ROWS * 128
    number = (
        lax.axis_index(HOR) * part.size
        + lax.broadcasted_iota(jnp.int32, part.shape, 0) * 128
        + lax.broadcasted_iota(jnp.int32, part.shape, 1)
    )
    inside = (number >= lead) & (number < lead + share_len)
    count = lax.axis_size(DP) * lax.axis_size(HOR)
    squares = total_all(jnp.sum(jnp.where(inside, part * part, 0.0)), (DP, HOR), count)
    whole = all_parts(part)
    small_flat = small.reshape(-1)
    affine_sum = jnp.concatenate([small_flat[:7127], small_flat[7168:7552]])
    noise_loss = jnp.sum(small[60])
    grad_norm = jnp.sqrt(squares + jnp.sum(affine_sum * affine_sum))
    kernel_own = lax.dynamic_slice_in_dim(whole.astype(jnp.float32).reshape(-1), lead, share_len)
    factor = jnp.minimum(1.0, MAX_NORM / (grad_norm + 1e-06))
    kernel_step = kernel_own * factor
    kernel_old = lax.dynamic_slice_in_dim(kernels, owner_start, share_len)
    kernel_mom_new = MOMENTUM * kernel_momentum + kernel_step
    kernel_new = kernel_old - LEARN_RATE * (kernel_step + MOMENTUM * kernel_mom_new)
    kernel_ema_new = EMA_DECAY * kernel_average + (1.0 - EMA_DECAY) * kernel_new
    affine_step = affine_sum * factor
    affine_mom_new = MOMENTUM * affine_momentum + affine_step
    affine_new = affine - AFFINE_RATE * (affine_step + MOMENTUM * affine_mom_new)
    affine_ema_new = EMA_DECAY * affine_average + (1.0 - EMA_DECAY) * affine_new
    return (
        noise_loss,
        grad_norm,
        kernel_new,
        kernel_mom_new,
        kernel_ema_new,
        kernel_new.astype(jnp.bfloat16),
        affine_new,
        affine_mom_new,
        affine_ema_new,
        affine_new.astype(jnp.bfloat16),
    )


def solution(mesh):
    in_specs = (
        P(DP, HOR, None),
        P(),
        P(),
        P(DP, HOR, None),
        P(DP),
        P(DP, HOR),
        P(),
        P(),
        P(DP),
        P(DP),
        P(),
        P(),
    )
    out_specs = (P(), P(), P(DP), P(DP), P(DP), P(DP), P(), P(), P(), P())
    return jax.shard_map(
        on_device, mesh=mesh, in_specs=in_specs, out_specs=out_specs, check_vma=False
    )
```

```python
import functools
import math
from types import SimpleNamespace

import jax
import jax.numpy as jnp
from jax import lax
from jax.experimental import pallas as pl
from jax.experimental.pallas import tpu as pltpu
from jax.sharding import PartitionSpec as P

TD = 23
C1 = 64
C2 = 128
C3 = 256
TE = 128
TH = 256
KSIZE = 5
GROUPS = 8
NSTEPS = 100


DP, HOR = "dp", "hor"
PRECISE = lax.Precision.HIGHEST
EPSILON = 1e-05
MAX_NORM = 0.02
LEARN_RATE = 200.0
AFFINE_RATE = 1500.0
MOMENTUM = 0.9
EMA_DECAY = 0.5


def padded_2(cells, sides, width):
    for axis, dim in sides:
        if axis is None:
            pads = [(0, 0)] * cells.ndim
            pads[dim] = (width, width)
            cells = jnp.pad(cells, pads)
            continue
        count = lax.axis_size(axis)
        ends = count - 1
        head = lax.slice_in_dim(cells, 0, width, axis=dim)
        tail = lax.slice_in_dim(cells, cells.shape[dim] - width, cells.shape[dim], axis=dim)
        cells = jnp.concatenate(
            [
                lax.ppermute(tail, axis, [(i, (i + 1) % count) for i in range(ends)]),
                cells,
                lax.ppermute(head, axis, [((i + 1) % count, i) for i in range(ends)]),
            ],
            axis=dim,
        )
    return cells


def sum_over(values, axis):
    return values if axis is None else lax.psum(values, axis)


def axis_length(axis):
    return 1 if axis is None else lax.axis_size(axis)


def layout_shapes():
    kernel_shapes = []
    affine_shapes = []
    for width_in, width_out in [
        (TD, C1),
        (C1, C2),
        (C2, C3),
        (C3, C3),
        (C3 + C3, C2),
        (C2 + C2, C1),
    ]:
        matrices = [
            ("conv_one", KSIZE * width_in, width_out),
            ("conv_two", KSIZE * width_out, width_out),
            ("time_proj", TE, width_out),
        ]
        vectors = [
            (entry_name, width_out)
            for entry_name in [
                "bias_one",
                "gain_one",
                "shift_one",
                "time_bias",
                "bias_two",
                "gain_two",
                "shift_two",
            ]
        ]
        if width_in != width_out:
            matrices.append(("res_proj", width_in, width_out))
            vectors.append(("res_bias", width_out))
        kernel_shapes.append(matrices)
        affine_shapes.append(vectors)
    kernel_shapes.append(
        [
            ("head_conv", KSIZE * C1, C1),
            ("head_out", C1, TD),
            ("embed_one", TE, TH),
            ("embed_two", TH, TE),
        ]
    )
    affine_shapes.append(
        [
            ("head_bias", C1),
            ("head_gain", C1),
            ("head_shift", C1),
            ("out_bias", TD),
            ("embed_bias_one", TH),
            ("embed_bias_two", TE),
        ]
    )
    return (kernel_shapes, affine_shapes)


def unpack(kernels, affine):
    kernel_shapes, affine_shapes = layout_shapes()
    members_all = []
    cursor = 0
    for entries in kernel_shapes:
        members = SimpleNamespace()
        for entry_name, height, breadth in entries:
            piece = kernels[cursor : cursor + height * breadth].reshape(height, breadth)
            setattr(members, entry_name, piece)
            cursor += height * breadth
        members_all.append(members)
    cursor = 0
    for position, entries in enumerate(affine_shapes):
        for entry_name, length in entries:
            setattr(members_all[position], entry_name, affine[cursor : cursor + length])
            cursor += length
    return members_all


def pack_flat(grad_list):
    kernel_shapes, affine_shapes = layout_shapes()
    kernel_pieces = []
    affine_pieces = []
    for position, entries in enumerate(kernel_shapes):
        for entry_name, height, breadth in entries:
            kernel_pieces.append(
                vars(grad_list[position])
                .get(entry_name, jnp.zeros((height, breadth), jnp.float32))
                .reshape(-1)
            )
    for position, entries in enumerate(affine_shapes):
        for entry_name, length in entries:
            affine_pieces.append(
                vars(grad_list[position]).get(entry_name, jnp.zeros((length,), jnp.float32))
            )
    return (jnp.concatenate(kernel_pieces), jnp.concatenate(affine_pieces))


def mish_act(value):
    return value * jnp.tanh(jax.nn.softplus(value))


def mish_grad(value, upstream):
    return jax.vjp(mish_act, value)[1](upstream)[0]


def sinusoid(steps_vec):
    half_width = TE // 2
    ladder = jnp.exp(
        -math.log(10000.0) * jnp.arange(half_width).astype(jnp.float32) / (half_width - 1)
    )
    angles = steps_vec.astype(jnp.float32)[:, None] * ladder[None, :]
    return jnp.concatenate([jnp.sin(angles), jnp.cos(angles)], axis=1)


def signal_level(steps_vec):
    ratio = (steps_vec.astype(jnp.float32) + 1.0) / NSTEPS
    cosine_now = jnp.cos((ratio + 0.008) / 1.008 * math.pi / 2)
    cosine_zero = math.cos(0.008 / 1.008 * math.pi / 2)
    return (cosine_now / cosine_zero) ** 2


def time_parts(kernel_flat, affine_flat, steps_vec):
    members_all = unpack(kernel_flat, affine_flat)
    last_group = members_all[6]
    hidden = mish_act(
        jnp.dot(sinusoid(steps_vec), last_group.embed_one, precision=PRECISE)
        + last_group.embed_bias_one
    )
    feature = mish_act(
        jnp.dot(hidden, last_group.embed_two, precision=PRECISE) + last_group.embed_bias_two
    )
    return tuple(
        (
            jnp.dot(feature, members_all[block_index].time_proj, precision=PRECISE)
            + members_all[block_index].time_bias
            for block_index in range(6)
        )
    )


def conv_forward(inputs_low, weight_low, axis):
    padded = padded_2(inputs_low, ((axis, 1),), 2)
    frames = inputs_low.shape[1]
    channels = inputs_low.shape[2]
    running = 0.0
    for offset in range(KSIZE):
        running = running + jnp.einsum(
            "blc,cd->bld",
            padded[:, offset : offset + frames],
            weight_low[offset * channels : (offset + 1) * channels],
            preferred_element_type=jnp.float32,
        )
    return (running, padded)


def conv_backward(grad_low, padded, weight_low, axis):
    grad_padded = padded_2(grad_low, ((axis, 1),), 2)
    frames = grad_low.shape[1]
    channels = padded.shape[2]
    pieces = []
    running = 0.0
    for offset in range(KSIZE):
        pieces.append(
            jnp.einsum(
                "blc,bld->cd",
                padded[:, offset : offset + frames],
                grad_low,
                preferred_element_type=jnp.float32,
            )
        )
        start_row = KSIZE - 1 - offset
        running = running + jnp.einsum(
            "bld,cd->blc",
            grad_padded[:, start_row : start_row + frames],
            weight_low[offset * channels : (offset + 1) * channels],
            preferred_element_type=jnp.float32,
        )
    return (running, jnp.concatenate(pieces, axis=0))


def group_norm(values, gain_vec, shift_vec, axis):
    horizons, frames, channels = values.shape
    grouped = values.reshape(horizons, frames, GROUPS, channels // GROUPS)
    sum_one, sum_two = sum_over(
        (jnp.sum(grouped, axis=(1, 3)), jnp.sum(grouped * grouped, axis=(1, 3))), axis
    )
    group_count = frames * axis_length(axis) * (channels // GROUPS)
    average = sum_one / group_count
    inverse = lax.rsqrt(sum_two / group_count - average * average + EPSILON)
    normed = ((grouped - average[:, None, :, None]) * inverse[:, None, :, None]).reshape(
        horizons, frames, channels
    )
    return (normed * gain_vec + shift_vec, (normed, inverse))


def group_norm_back(upstream, norm_stats, gain_vec, axis):
    normed, inverse = norm_stats
    horizons, frames, channels = normed.shape
    grad_gain = jnp.sum(upstream * normed, axis=(0, 1))
    grad_shift = jnp.sum(upstream, axis=(0, 1))
    scaled = (upstream * gain_vec).reshape(horizons, frames, GROUPS, channels // GROUPS)
    grouped = normed.reshape(horizons, frames, GROUPS, channels // GROUPS)
    sum_one, sum_two = sum_over(
        (jnp.sum(scaled, axis=(1, 3)), jnp.sum(scaled * grouped, axis=(1, 3))), axis
    )
    group_count = frames * axis_length(axis) * (channels // GROUPS)
    result = inverse[:, None, :, None] * (
        scaled
        - sum_one[:, None, :, None] / group_count
        - grouped * sum_two[:, None, :, None] / group_count
    )
    return (result.reshape(horizons, frames, channels), grad_gain, grad_shift)


def block_forward(inputs, members, time_term, axis):
    inputs_low = inputs.astype(jnp.bfloat16)
    weight_one = members.conv_one.astype(jnp.bfloat16)
    weight_two = members.conv_two.astype(jnp.bfloat16)
    conv_out, padded_one = conv_forward(inputs_low, weight_one, axis)
    normed_one, stats_one = group_norm(
        conv_out + members.bias_one, members.gain_one, members.shift_one, axis
    )
    hidden = mish_act(normed_one) + time_term[:, None, :]
    conv_out, padded_two = conv_forward(hidden.astype(jnp.bfloat16), weight_two, axis)
    normed_two, stats_two = group_norm(
        conv_out + members.bias_two, members.gain_two, members.shift_two, axis
    )
    result = mish_act(normed_two)
    if "res_proj" in vars(members):
        weight_side = members.res_proj.astype(jnp.bfloat16)
        result = (
            result
            + jnp.einsum("blc,cd->bld", inputs_low, weight_side, preferred_element_type=jnp.float32)
            + members.res_bias
        )
    else:
        weight_side = None
        result = result + inputs
    return (
        result,
        (
            padded_one,
            stats_one,
            padded_two,
            stats_two,
            inputs_low,
            weight_one,
            weight_two,
            weight_side,
        ),
    )


def block_backward(upstream, kept, members, axis):
    (
        padded_one,
        stats_one,
        padded_two,
        stats_two,
        inputs_low,
        weight_one,
        weight_two,
        weight_side,
    ) = kept
    grad_map = SimpleNamespace()
    grad_normed = mish_grad(stats_two[0] * members.gain_two + members.shift_two, upstream)
    grad_pre, grad_map.gain_two, grad_map.shift_two = group_norm_back(
        grad_normed, stats_two, members.gain_two, axis
    )
    grad_map.bias_two = jnp.sum(grad_pre, axis=(0, 1))
    grad_hidden, grad_map.conv_two = conv_backward(
        grad_pre.astype(jnp.bfloat16), padded_two, weight_two, axis
    )
    time_grad = jnp.sum(grad_hidden, axis=1)
    grad_normed = mish_grad(stats_one[0] * members.gain_one + members.shift_one, grad_hidden)
    grad_pre, grad_map.gain_one, grad_map.shift_one = group_norm_back(
        grad_normed, stats_one, members.gain_one, axis
    )
    grad_map.bias_one = jnp.sum(grad_pre, axis=(0, 1))
    grad_inputs, grad_map.conv_one = conv_backward(
        grad_pre.astype(jnp.bfloat16), padded_one, weight_one, axis
    )
    if weight_side is not None:
        upstream_low = upstream.astype(jnp.bfloat16)
        grad_map.res_bias = jnp.sum(upstream, axis=(0, 1))
        grad_map.res_proj = jnp.einsum(
            "blc,bld->cd", inputs_low, upstream_low, preferred_element_type=jnp.float32
        )
        grad_inputs = grad_inputs + jnp.einsum(
            "bld,cd->blc", upstream_low, weight_side, preferred_element_type=jnp.float32
        )
    else:
        grad_inputs = grad_inputs + upstream
    return (grad_inputs, time_grad, grad_map)


def head_forward(inputs, members, axis):
    weight_conv = members.head_conv.astype(jnp.bfloat16)
    weight_out = members.head_out.astype(jnp.bfloat16)
    conv_out, padded = conv_forward(inputs.astype(jnp.bfloat16), weight_conv, axis)
    normed, norm_stats = group_norm(
        conv_out + members.head_bias, members.head_gain, members.head_shift, axis
    )
    feature_low = mish_act(normed).astype(jnp.bfloat16)
    predicted = (
        jnp.einsum("blc,cd->bld", feature_low, weight_out, preferred_element_type=jnp.float32)
        + members.out_bias
    )
    return (predicted, (padded, norm_stats, feature_low, weight_conv, weight_out))


def head_backward(upstream, kept, members, axis):
    padded, norm_stats, feature_low, weight_conv, weight_out = kept
    grad_map = SimpleNamespace()
    upstream_low = upstream.astype(jnp.bfloat16)
    grad_map.out_bias = jnp.sum(upstream, axis=(0, 1))
    grad_map.head_out = jnp.einsum(
        "blc,bld->cd", feature_low, upstream_low, preferred_element_type=jnp.float32
    )
    grad_feature = jnp.einsum(
        "bld,cd->blc", upstream_low, weight_out, preferred_element_type=jnp.float32
    )
    grad_normed = mish_grad(
        norm_stats[0] * members.head_gain + members.head_shift, grad_feature
    )
    grad_pre, grad_map.head_gain, grad_map.head_shift = group_norm_back(
        grad_normed, norm_stats, members.head_gain, axis
    )
    grad_map.head_bias = jnp.sum(grad_pre, axis=(0, 1))
    grad_inputs, grad_map.head_conv = conv_backward(
        grad_pre.astype(jnp.bfloat16), padded, weight_conv, axis
    )
    return (grad_inputs, grad_map)


BF = jnp.bfloat16
F32 = jnp.float32
HALO = 32
ROW_STARTS = (0, 293, 1445, 5797, 11173, 15013)
LOAD_ROWS = (0, 296, 1448, 5800, 11176, 15016, 16008, 16696)
HEAD_ROW = 16005
OUT_ROW = 16165
EMB_ROW = 16176
FLAT_ROWS = 16696
TABLE_ROWS = 16720
LATE_START = 5792
LATE_ROWS = 16168 - LATE_START
OWN_ROWS = 2112
NKER_ROWS = 2086
OUT_START = OUT_ROW * 128
WIDTHS = ((TD, C1), (C1, C2), (C2, C3), (C3, C3), (C3 + C3, C2), (C2 + C2, C1))
AFF_ROWS = (0, 4, 12, 28, 42, 50)
LAYER_OUT = ((1, 128), (2, 128), (2, 256), (2, 256), (2, 128), (1, 128), (1, 128))
W_ONE = ((640, 128), (640, 256), (640, 256), (1280, 256), (2560, 128), (2560, 128), (640, 128))
W_TWO = ((640, 128), (640, 128), (1280, 256), (1280, 256), (640, 128), (640, 128))
W_RES = ((128, 128), (128, 256), (128, 256), None, (512, 128), (512, 128))
UP, DOWN = 1, 2
TN = (((0,), (0,)), ((), ()))
NT = (((1,), (1,)), ((), ()))


INPUTS = ((0,), (1,), (2,), (3,), (4, 3), (5, 2))


class Refs:
    def __init__(self, names, values):
        vars(self).update(zip(names, values))

    def of(self, kind, block):
        return vars(self).get(f"{kind}{block}")

    def one(self, block):
        return self.of("one", block)

    def two(self, block):
        return self.of("two", block)

    def res(self, block):
        return self.of("res", block)

    def pre_a(self, block):
        return self.of("pre_a", block)

    def pre_b(self, block):
        return self.of("pre_b", block)

    def up(self, block):
        return self.of("up", block)

    def x(self, number):
        return self.of("x", number)


def lanes_of(shape):
    return lax.broadcasted_iota(jnp.int32, shape, 1)


def rows_of(shape):
    return lax.broadcasted_iota(jnp.int32, shape, 0)


def fill_halo(ref):
    halves, padded_rows, lanes = ref.shape
    inner = padded_rows - 2 * HALO
    row = rows_of((16, lanes))
    lane = lanes_of((16, lanes))
    for group in range(2):
        start = inner + 16 * group
        moved = [pltpu.roll(ref[q, start : start + 16, :].astype(F32), 1, 0) for q in range(halves)]
        into = pl.ds(16 * group, 16)
        if halves == 1:
            edge = jnp.where(lane >= 64, pltpu.roll(moved[0], 64, 1), 0.0)
            ref[0, into, :] = jnp.where(row == 0, edge, moved[0]).astype(BF)
        else:
            ref[0, into, :] = jnp.where(row == 0, 0.0, moved[0]).astype(BF)
            ref[1, into, :] = jnp.where(row == 0, moved[0], moved[1]).astype(BF)
        start = HALO + 16 * group
        moved = [pltpu.roll(ref[q, start : start + 16, :].astype(F32), 15, 0) for q in range(halves)]
        into = pl.ds(HALO + inner + 16 * group, 16)
        if halves == 1:
            edge = jnp.where(lane < 64, pltpu.roll(moved[0], 64, 1), 0.0)
            ref[0, into, :] = jnp.where(row == 15, edge, moved[0]).astype(BF)
        else:
            ref[0, into, :] = jnp.where(row == 15, moved[1], moved[0]).astype(BF)
            ref[1, into, :] = jnp.where(row == 15, 0.0, moved[1]).astype(BF)


def exchange_kernel(traj, noise, mask, scale, mean, std, noisy_out, noise_out, counts, noisy_wide, noise_wide):
    pieces, frames, wide = traj.shape
    segment = frames // 8
    quarter = segment // 4
    rows = tile_rows(frames // 7) * 7 if frames % 7 == 0 else tile_rows(frames)

    for piece in range(pieces):

        def fill(index, carry):
            here = pl.ds(pl.multiple_of(index * rows, rows), rows)
            value = noise[piece, here, :]
            clean = (traj[piece, here, :] - mean[...]) / std[...]
            noisy_wide[here, 0:wide] = scale[piece : piece + 1, 0:wide] * clean + (
                scale[4 + piece : 5 + piece, 0:wide] * value
            )
            noise_wide[here, 0:wide] = value
            return carry

        lax.fori_loop(0, frames // rows, fill, 0)
        step = quarter // 2 if quarter % 4 == 0 else quarter

        def gather(index, carry):
            lane = lanes_of((8, 128))

            def one(source, place):
                total = 0.0
                for number in range(4):
                    value = source[pl.ds(quarter * number + place, 8, stride=segment), :]
                    value = jnp.where(lane < wide, value, 0.0)
                    total = total + (pltpu.roll(value, 32 * number, 1) if number else value)
                return total

            for inner in range(0, step, 2):
                place = index * step + inner
                at = pl.multiple_of(8 * place, 16)
                noisy_out[piece, pl.ds(at, 16), :] = jnp.concatenate(
                    [one(noisy_wide, place), one(noisy_wide, place + 1)], axis=0
                ).astype(BF)
                noise_out[piece, pl.ds(at, 8), :] = one(noise_wide, place)
                noise_out[piece, pl.ds(at + 8, 8), :] = one(noise_wide, place + 1)
            return carry

        lax.fori_loop(0, quarter // step, gather, 0)
        total = jnp.sum(mask[piece : piece + 1, :].astype(F32), axis=1, keepdims=True)
        counts[piece : piece + 1, :] = jnp.broadcast_to(total, (1, 128))


def take_apart(source, quarter, store):
    lane = lanes_of((16, 128))

    def step(index, carry):
        at = pl.multiple_of(16 * index, 16)
        got = [source[piece, pl.ds(at, 16), :].astype(F32) for piece in range(4)]
        for inner in range(2):
            here = slice(8 * inner, 8 * inner + 8)
            low = jnp.concatenate([got[0][here], got[1][here]], axis=0)
            high = jnp.concatenate([got[2][here], got[3][here]], axis=0)
            for number in range(4):
                left = pltpu.roll(low, (128 - 32 * number) % 128, 1) if number else low
                right = pltpu.roll(high, (192 - 32 * number) % 128, 1) if number != 2 else high
                value = jnp.where(lane < 64, left, right)
                store(quarter * number + 2 * index + inner, jnp.where(lane % 64 < 32, value, 0.0))
        return carry

    lax.fori_loop(0, quarter // 2, step, 0)


def mish_fast(value):
    grown = jnp.exp(jnp.minimum(value, 20.0))
    top = grown * (grown + 2.0)
    return value * (top / (top + 2.0))


def mish_both(value):
    grown = jnp.exp(jnp.minimum(value, 20.0))
    top = grown * (grown + 2.0)
    inverse = 1.0 / (top + 2.0)
    ratio = top * inverse
    slope = ratio + 4.0 * value * (top - grown) * (inverse * inverse)
    return value * ratio, slope


def fold_rows(value):
    rows, lanes = value.shape
    return jnp.sum(value.reshape(rows // 8, 8, lanes), axis=0)


def down_one_row(value):
    return jnp.sum(value, axis=0, keepdims=True)


def both_halves(row):
    return row + pltpu.roll(row, 64, 1)


def group_sums(first, second, packed):
    lanes = first.shape[1]
    row = rows_of((16, lanes))
    stacked = jnp.zeros((16, lanes), F32)
    for number, value in enumerate((first, second)):
        for part in range(3):
            high = value.astype(BF).astype(F32)
            stacked = jnp.where(row == 3 * number + part, high, stacked)
            value = value - high
    left = rows_of((lanes, lanes))
    right = lanes_of((lanes, lanes))
    if packed:
        same = (left % 64) // 8 == (right % 64) // 8
    else:
        size = lanes // GROUPS
        same = left // size == right // size
    same = jnp.where(same, 1.0, 0.0).astype(BF)
    summed = jnp.dot(stacked.astype(BF), same, preferred_element_type=F32)
    return down_one_row(summed[0:3, :]), down_one_row(summed[3:6, :])


def tile_rows(inner):
    for rows in (256, 128, 64, 32, 16):
        if inner % rows == 0:
            return rows


def sweep(halves, inner, body, carry):
    rows = tile_rows(inner)
    per_half = inner // rows

    def step(index, state):
        q = index // per_half
        start = pl.multiple_of((index - q * per_half) * rows, rows)
        return body(q, start, rows, state)

    return lax.fori_loop(0, halves * per_half, step, carry)


def vector(aff, row, width):
    if width == 256:
        base = int(row)
        return jnp.concatenate([aff[base : base + 1, :], aff[base + 1 : base + 2, :]], axis=1)
    base = int(row)
    whole = aff[base : base + 1, :]
    if width == 128:
        return whole
    turned = pltpu.roll(whole, 64, 1)
    lane = lanes_of((1, 128))
    if row == base:
        return jnp.where(lane < 64, whole, turned)
    return jnp.where(lane < 64, turned, whole)


def block_vector(aff, block, number):
    width = WIDTHS[block][1]
    return vector(aff, AFF_ROWS[block] + number * width / 128, width)


def head_vector(aff, number):
    return vector(aff, 54 + number / 2, 64)


def conv_input(xs, q, tap, inner):
    parts = [x[q, pl.ds(16 * tap, inner), :] for x in xs]
    return parts[0] if len(parts) == 1 else jnp.concatenate(parts, axis=1)


def conv_to(xs, weight, bias, out, crossing):
    halves, inner, lanes = out.shape
    zero = jnp.zeros((8, lanes), F32)

    def finish(q, total, state):
        total = total + bias
        out[q] = total
        return state[0] + fold_rows(total), state[1] + fold_rows(total * total)

    if crossing == UP:
        wide = jnp.concatenate([conv_input(xs, 0, k, inner) for k in range(KSIZE)], axis=1)
        total = jnp.dot(wide, weight[...], preferred_element_type=F32)
        state = finish(0, total[:, :lanes], (zero, zero))
        return finish(1, total[:, lanes:], state)

    def taps_across(parts):
        wide = jnp.concatenate(parts, axis=1)
        size = wide.shape[1]
        across = jnp.concatenate([weight[size * k : size * k + size, :] for k in range(KSIZE)], axis=1)
        value = jnp.dot(wide, across, preferred_element_type=F32)
        total = 0.0
        for k in range(KSIZE):
            total = total + value[16 * k : 16 * k + inner, lanes * k : lanes * k + lanes]
        return total

    if crossing == DOWN:
        return finish(0, taps_across([x[q] for q in range(2) for x in xs]), (zero, zero))
    if lanes == 128:
        return lax.fori_loop(0, halves, lambda q, state: finish(q, taps_across([x[q] for x in xs]), state), (zero, zero))

    def half(q, state):
        wide = jnp.concatenate([conv_input(xs, q, k, inner) for k in range(KSIZE)], axis=1)
        return finish(q, jnp.dot(wide, weight[...], preferred_element_type=F32), state)

    return lax.fori_loop(0, halves, half, (zero, zero))


def norm_fit(sums, gain, shift, count, packed, stats, layer):
    lanes = gain.shape[1]
    one = down_one_row(sums[0])
    two = down_one_row(sums[1])
    group_one, group_two = group_sums(one, two, packed)
    mean = group_one / count
    inverse = lax.rsqrt(group_two / count - mean * mean + EPSILON)
    scale = inverse * gain
    offset = shift - mean * scale
    for number, row in enumerate((scale, offset, mean, inverse, one)):
        stats[8 * layer + number : 8 * layer + number + 1, 0:lanes] = row
    return scale, offset


def norm_kept(stats, layer, lanes):
    return [stats[8 * layer + n : 8 * layer + n + 1, 0:lanes] for n in range(5)]


def norm_back_fit(sums, kept, gain, count, rows, packed):
    scale, _, mean, inverse, one = kept
    grad_shift = down_one_row(sums[0])
    grad_gain = inverse * (down_one_row(sums[1]) - mean * grad_shift)
    first, second = group_sums(gain * grad_shift, gain * grad_gain, packed)
    first = first / count
    second = second / count
    slope = -inverse * inverse * second
    level = -inverse * first - slope * mean
    grad_bias = scale * grad_shift + slope * one + level * rows
    if packed:
        grad_shift, grad_gain, grad_bias = [both_halves(v) for v in (grad_shift, grad_gain, grad_bias)]
    return slope, level, grad_bias, grad_gain, grad_shift


def in_steps(count, step, body):
    full = count // step

    def move(index, carry):
        body(pl.multiple_of(index * step, step), step)
        return carry

    if full > 1:
        lax.fori_loop(0, full, move, 0)
    elif full:
        body(0, step)
    if count % step:
        body(full * step, count % step)


def unpack_pairs(flat, start, count, out):
    def move(at, step):
        rows = flat[pl.ds(start + at, step), :]
        turned = pltpu.roll(rows, 64, 1)
        lane = lanes_of(rows.shape)
        out[pl.ds(2 * at, step, stride=2), :] = jnp.where(lane < 64, rows, turned)
        out[pl.ds(2 * at + 1, step, stride=2), :] = jnp.where(lane < 64, turned, rows)

    in_steps(count, 128, move)


def pack_pairs(source, out, start, count):
    def move(at, step):
        even = source[pl.ds(2 * at, step, stride=2), :]
        odd = pltpu.roll(source[pl.ds(2 * at + 1, step, stride=2), :], 64, 1)
        out[pl.ds(start + at, step), :] = jnp.where(lanes_of(even.shape) < 64, even, odd)

    in_steps(count, 128, move)


def spread_pairs(pairs, start, count, weight, to, size):
    rows = min(-(-count // 32) * 32, size)
    value = pairs[start : start + rows, :]
    keep = rows_of(value.shape) < count
    lane = lanes_of(value.shape)
    weight[to : to + rows, :] = jnp.where(keep & (lane < 64), value, 0.0).astype(BF)
    weight[to + size : to + size + rows, :] = jnp.where(keep & (lane >= 64), value, 0.0).astype(BF)


def straight_rows(flat, start, count, out, to):
    def move(at, step):
        out[pl.ds(to + at, step), :] = flat[pl.ds(start + at, step), :].astype(out.dtype)

    in_steps(count, 256, move)


def wide_rows(flat, start, count, out, to):
    def move(at, step):
        for half in range(2):
            out[pl.ds(to + at, step), 128 * half : 128 * half + 128] = flat[
                pl.ds(start + 2 * at + half, step, stride=2), :
            ].astype(out.dtype)

    in_steps(count, 128, move)


def prepare_block(block, c):
    flat = c.flat
    start = ROW_STARTS[block]
    width_in, width_out = WIDTHS[block]
    one, two = c.one(block), c.two(block)
    res = c.res(block)
    proj, at = c.proj, TE * block
    pairs = c.pairs
    if width_out == 64:
        chunks = 592 if block == 0 else 1984
        unpack_pairs(flat, start, chunks // 2, pairs)
        size = 64 if block == 0 else 256
        if block == 0:
            one[...] = jnp.zeros_like(one)
            res[...] = jnp.zeros_like(res)
        for k in range(KSIZE):
            spread_pairs(pairs, width_in * k, width_in, one, 2 * size * k, size)
            spread_pairs(pairs, KSIZE * width_in + 64 * k, 64, two, 128 * k, 64)
        cursor = KSIZE * (width_in + 64)
        proj[at : at + TE, 0:128] = pairs[cursor : cursor + TE, :]
        spread_pairs(pairs, cursor + TE, width_in, res, 0, size)
    elif width_out == 128:
        if block == 1:
            one[...] = jnp.zeros_like(one)
            res[...] = jnp.zeros_like(res)
            for k in range(KSIZE + 1):
                source = start + 64 * k if k < KSIZE else start + 320 + 640 + TE
                value = flat[source : source + 64, :].astype(BF)
                into, base = (one, 128 * k) if k < KSIZE else (res, 0)
                into[base : base + 64, 0:128] = value
                into[base + 64 : base + 128, 128:256] = value
        else:
            straight_rows(flat, start, KSIZE * width_in, one, 0)
            straight_rows(flat, start + KSIZE * width_in + 640 + TE, width_in, res, 0)
        straight_rows(flat, start + KSIZE * width_in, 640, two, 0)
        cursor = start + KSIZE * width_in + 640
        proj[at : at + TE, 0:128] = flat[cursor : cursor + TE, :]
    else:
        wide_rows(flat, start, KSIZE * width_in, one, 0)
        wide_rows(flat, start + 2 * KSIZE * width_in, 1280, two, 0)
        cursor = start + 2 * (KSIZE * width_in + 1280)
        wide_rows(flat, cursor, TE, proj, at)
        if res is not None:
            wide_rows(flat, cursor + 2 * TE, width_in, res, 0)


def column(row):
    return jnp.transpose(jnp.broadcast_to(row, (128, 128)))


def row_times(row, matrix):
    total = 0.0
    for at in range(0, row.shape[1], 128):
        wide = column(row[:, at : at + 128])
        if matrix.shape[1] == 256:
            wide = jnp.concatenate([wide, wide], axis=1)
        total = total + fold_rows(matrix[at : at + 128, :] * wide)
    return down_one_row(total)


def lane_sums(value):
    if value.shape[1] == 256:
        value = value[:, 0:128] + value[:, 128:256]
    parts = []
    for at in range(0, value.shape[0], 128):
        total = jnp.sum(value[at : at + 128, :], axis=1, keepdims=True)
        parts.append(jnp.transpose(jnp.broadcast_to(total, (128, 128)))[0:1, :])
    return parts[0] if len(parts) == 1 else jnp.concatenate(parts, axis=1)


def outer(left, right):
    wide = []
    for at in range(0, left.shape[1], 128):
        part = column(left[:, at : at + 128])
        if right.shape[1] == 256:
            part = jnp.concatenate([part, part], axis=1)
        wide.append(part * right)
    return wide[0] if len(wide) == 1 else jnp.concatenate(wide, axis=0)


CROSSING = (None, UP, None, None, None, DOWN)


def counts_of(frames, block):
    width = WIDTHS[block][1] if block < 6 else C1
    return frames * (width // GROUPS)


def forward_kernel(c, far, into, sems):
    aff, stats, terms = c.aff, c.stats, c.terms
    inner = c.pre_a0.shape[1]
    frames = 2 * inner
    saves = []

    def save(source, target):
        copy = pltpu.make_async_copy(source, target, sems.at[16 + len(saves)])
        copy.start()
        saves.append(copy)

    loads = []
    for number, (low, high) in enumerate(zip(LOAD_ROWS[:-1], LOAD_ROWS[1:])):
        part = pl.ds(low, high - low)
        copy = pltpu.make_async_copy(far.flat.at[part, :], c.flat.at[part, :], sems.at[number])
        loads.append(copy)
    order = (6, 0, 1, 2, 3, 4, 5)
    for number in order:
        loads[number].start()
    loads[6].wait()
    flat, pairs, embed = c.flat, c.pairs, c.embed_two
    unpack_pairs(flat, EMB_ROW, FLAT_ROWS - EMB_ROW, pairs)
    quarter = [pairs[pl.ds(1 + n, TE, stride=4), :] for n in range(4)]
    lane = lanes_of((TE, 128))
    embed_one = jnp.concatenate(
        [jnp.where(lane < 64, quarter[0], quarter[1]), jnp.where(lane < 64, quarter[2], quarter[3])], axis=1
    )
    embed[...] = jnp.where(
        lanes_of((TH, 128)) < 64, pairs[pl.ds(513, TH, stride=2), :], pairs[pl.ds(514, TH, stride=2), :]
    )
    sinus = c.sinus[...]
    bias = vector(aff, 56, 256)
    kept = c.kept
    hidden_pre = row_times(sinus[0:1, :], embed_one) + bias
    hidden = mish_fast(hidden_pre)
    feature_pre = row_times(hidden, embed[...]) + vector(aff, 58, 128)
    feature = mish_fast(feature_pre)
    for number, value in enumerate((hidden_pre, hidden, feature_pre, feature)):
        lanes = value.shape[1]
        kept[8 * number : 8 * number + 8, 0:lanes] = jnp.broadcast_to(value, (8, lanes))
    save(c.embed_two, into.embed_two)
    x0 = c.x0

    def put_noisy(group, value):
        x0[0, pl.ds(pl.multiple_of(HALO + 16 * group, 16), 16), :] = value.astype(BF)

    take_apart(c.noisy, inner // 64, put_noisy)
    fill_halo(x0)
    save(c.x0, into.x0)

    for block in range(6):
        loads[block].wait()
        prepare_block(block, c)
        for get in (Refs.one, Refs.two, Refs.res):
            if get(c, block) is not None:
                save(get(c, block), get(into, block))
        halves, lanes = LAYER_OUT[block]
        packed = halves == 1
        count = counts_of(frames, block)
        width = WIDTHS[block][1]
        lane_bias = block_vector(aff, block, 3)
        term = row_times(feature, c.proj[TE * block : TE * block + TE, 0:lanes]) + lane_bias
        terms[8 * block : 8 * block + 1, 0:lanes] = term
        xs = [c.x(number) for number in INPUTS[block]]
        pre_a, pre_b = c.pre_a(block), c.pre_b(block)
        sums = conv_to(xs, c.one(block), block_vector(aff, block, 0), pre_a, CROSSING[block])
        save(pre_a, into.pre_a(block))
        scale, offset = norm_fit(
            sums, block_vector(aff, block, 1), block_vector(aff, block, 2), count, packed, stats, 2 * block
        )
        hid = c.hid.at[0:halves, :, 0:lanes]

        def to_hidden(q, start, rows, carry):
            value = mish_fast(pre_a[q, pl.ds(start, rows), :] * scale + offset) + term
            hid[q, pl.ds(HALO + start, rows), :] = value.astype(BF)
            return carry

        sweep(halves, inner, to_hidden, 0)
        fill_halo(hid)
        sums = conv_to([hid], c.two(block), block_vector(aff, block, 4), pre_b, None)
        save(pre_b, into.pre_b(block))
        scale_b, offset_b = norm_fit(
            sums, block_vector(aff, block, 5), block_vector(aff, block, 6), count, packed, stats, 2 * block + 1
        )
        side = c.side
        res = c.res(block)
        if res is not None:
            res_bias = block_vector(aff, block, 7)
            if CROSSING[block] == UP:
                total = jnp.dot(conv_input(xs, 0, 2, inner), res[...], preferred_element_type=F32)
                side[0, :, 0:lanes] = total[:, :lanes] + res_bias
                side[1, :, 0:lanes] = total[:, lanes:] + res_bias
            elif CROSSING[block] == DOWN:
                wide = jnp.concatenate([conv_input(xs, q, 2, inner) for q in range(2)], axis=1)
                side[0, :, 0:lanes] = jnp.dot(wide, res[...], preferred_element_type=F32) + res_bias
            else:
                for q in range(halves):
                    side[q, :, 0:lanes] = (
                        jnp.dot(conv_input(xs, q, 2, inner), res[...], preferred_element_type=F32) + res_bias
                    )
        out = c.x(block + 1)

        def to_output(q, start, rows, carry):
            value = mish_fast(pre_b[q, pl.ds(start, rows), :] * scale_b + offset_b)
            value = value + side[q, pl.ds(start, rows), 0:lanes]
            if block == 2:
                side[q, pl.ds(start, rows), 0:lanes] = value
            out[q, pl.ds(HALO + start, rows), :] = value.astype(BF)
            return carry

        sweep(halves, inner, to_output, 0)
        fill_halo(out)
        save(out, into.x(block + 1))
    unpack_pairs(flat, HEAD_ROW, 160, pairs)
    for k in range(KSIZE):
        spread_pairs(pairs, 64 * k, 64, c.one6, 128 * k, 64)
    save(c.one6, into.one6)
    sums = conv_to([c.x6], c.one6, head_vector(aff, 0), c.pre_a6, None)
    save(c.pre_a6, into.pre_a6)
    norm_fit(sums, head_vector(aff, 1), head_vector(aff, 2), counts_of(frames, 6), True, stats, 12)
    for source, target in ((stats, into.stats), (terms, into.terms), (kept, into.kept), (c.proj, into.proj)):
        save(source, target)
    for copy in saves:
        copy.wait()


def put_rows(value, out, start):
    rows, lanes = value.shape
    if lanes == 128:
        out[start : start + rows, :] = value
    else:
        out[pl.ds(start, rows, stride=2), :] = value[:, 0:128]
        out[pl.ds(start + 1, rows, stride=2), :] = value[:, 128:256]


def conv_dx(dy, weight, size, inner, crossing, emit):
    halves = dy.shape[0]
    narrow = size == 128

    def rows_at(q, k):
        return dy[q] if narrow else conv_input([dy], q, k, inner)

    def taps(pick):
        if narrow:
            value = lax.dot_general(pick(0), weight[...], NT, preferred_element_type=F32)
            total = 0.0
            for k in range(KSIZE):
                first = 16 * (KSIZE - 1 - k)
                total = total + value[first : first + inner, size * k : size * k + size]
            return total
        wide = jnp.concatenate([pick(KSIZE - 1 - k) for k in range(KSIZE)], axis=1)
        across = jnp.concatenate([weight[size * k : size * k + size, :] for k in range(KSIZE)], axis=1)
        return lax.dot_general(wide, across, NT, preferred_element_type=F32)

    if crossing == UP:
        emit(0, taps(lambda k: jnp.concatenate([rows_at(q, k) for q in range(2)], axis=1)))
    elif halves == 1:
        emit(0, taps(lambda k: rows_at(0, k)))
    else:

        def half(q, carry):
            emit(q, taps(lambda k: rows_at(q, k)))
            return carry

        lax.fori_loop(0, halves, half, 0)


def conv_dw(xs, dy, inner, crossing, acc, extra=None):
    def dys(q):
        parts = [conv_input([dy], q, KSIZE - 1 - k, inner) for k in range(KSIZE)]
        if extra is not None:
            parts.append(extra[q, :, 0 : dy.shape[2]])
        return parts

    def product(left, right):
        return lax.dot_general(left, right, TN, preferred_element_type=F32)

    if crossing == UP:
        both = zip(dys(0), dys(1))
        value = product(conv_input(xs, 0, 2, inner), jnp.concatenate([p for pair in both for p in pair], axis=1))
        acc[0 : value.shape[0], 0 : value.shape[1]] = value
        return
    if crossing == DOWN:
        left = jnp.concatenate([conv_input(xs, q, 2, inner) for q in range(2)], axis=1)
        value = product(left, jnp.concatenate(dys(0), axis=1))
        acc[0 : value.shape[0], 0 : value.shape[1]] = value
        return
    for q in range(dy.shape[0]):
        value = product(conv_input(xs, q, 2, inner), jnp.concatenate(dys(q), axis=1))
        if q == 0:
            acc[0 : value.shape[0], 0 : value.shape[1]] = value
        else:
            acc[0 : value.shape[0], 0 : value.shape[1]] += value


def fold_pairs(acc, tap, size, rows):
    lanes = slice(128 * tap, 128 * tap + 128)
    return acc[0:rows, lanes] + pltpu.roll(acc[size : size + rows, lanes], 64, 1)


def put_vector(grads, row, width, value):
    base = int(row)
    if width == 256:
        grads[base : base + 1, :] = value[:, 0:128]
        grads[base + 1 : base + 2, :] = value[:, 128:256]
    elif width == 128:
        grads[base : base + 1, :] = value
    else:
        lane = lanes_of((1, 128))
        keep = lane < 64 if row == base else lane >= 64
        grads[base : base + 1, :] = jnp.where(keep, value, grads[base : base + 1, :])


def norm_backward(c, layer, pre, gain, count, packed, upstream, dy, also=None):
    halves, inner, lanes = pre.shape
    kept = norm_kept(c.stats, layer, lanes)
    dv = c.dv
    zero = jnp.zeros((8, lanes), F32)

    def first(q, start, rows, state):
        here = pl.ds(start, rows)
        value = pre[q, here, :]
        act, slope = mish_both(value * kept[0] + kept[1])
        up = upstream(q, here)
        if also is not None:
            also(q, here, act, up)
        grad = up * slope
        dv[q, here, 0:lanes] = grad
        return state[0] + fold_rows(grad), state[1] + fold_rows(grad * value), state[2] + fold_rows(up)

    sums = sweep(halves, inner, first, (zero, zero, zero))
    rows_each = float(inner * halves)
    slope, level, grad_bias, grad_gain, grad_shift = norm_back_fit(sums, kept, gain, count, rows_each, packed)
    scale = kept[0]

    def second(q, start, rows, carry):
        here = pl.ds(start, rows)
        value = scale * dv[q, here, 0:lanes] + (slope * pre[q, here, :] + level)
        dy[q, pl.ds(HALO + start, rows), :] = value.astype(BF)
        return carry

    sweep(halves, inner, second, 0)
    fill_halo(dy)
    total = down_one_row(sums[2])
    return grad_bias, grad_gain, grad_shift, both_halves(total) if packed else total


def backward_block(block, c, base, copies, need):
    aff, grads, table, acc = c.aff, c.agrad, c.table, c.acc
    halves, lanes = LAYER_OUT[block]
    packed = halves == 1
    width_in, width_out = WIDTHS[block]
    inner = c.pre_a(block).shape[1]
    count = counts_of(2 * inner, block)
    up = c.up(block)
    low = c.low
    dy = c.dy.at[0:halves, :, 0:lanes]
    act_low = c.act
    res = c.res(block)
    xs = [c.x(number) for number in INPUTS[block]]
    start = ROW_STARTS[block] - base
    spot = AFF_ROWS[block]
    unit = width_out / 128

    def keep_low(q, here, act, value):
        low[q, here, 0:lanes] = value.astype(BF)

    need(copies.pre_b(block), copies.up(block))
    got = norm_backward(
        c, 2 * block + 1, c.pre_b(block), block_vector(aff, block, 5), count, packed,
        lambda q, here: up[q, here, :], dy, keep_low if res is not None else None,
    )
    for number, value in zip((4, 5, 6, 7), got):
        if number < 7 or res is not None:
            put_vector(grads, spot + number * unit, width_out, value)
    dv = c.dv

    def emit_hidden(q, value):
        dv[q, :, 0:lanes] = value

    need(copies.two(block))
    conv_dx(dy, c.two(block), lanes, inner, None, emit_hidden)
    term = c.terms[8 * block : 8 * block + 1, 0:lanes]
    dy_two = dy
    dy_one = c.ey.at[0:halves, :, 0:lanes]

    def keep_act(q, here, act, value):
        act_low[q, here, 0:lanes] = (act + term).astype(BF)

    need(copies.pre_a(block))
    got = norm_backward(
        c, 2 * block, c.pre_a(block), block_vector(aff, block, 1), count, packed,
        lambda q, here: dv[q, here, 0:lanes], dy_one, keep_act,
    )
    for number, value in zip((0, 1, 2, 3), got):
        put_vector(grads, spot + number * unit, width_out, value)
    time_row = got[3]
    c.tgrad[8 * block : 8 * block + 1, 0:lanes] = time_row

    def plain_dw(left, right_ref):
        for q in range(halves):
            parts = jnp.concatenate([conv_input([right_ref], q, KSIZE - 1 - k, inner) for k in range(KSIZE)], axis=1)
            value = lax.dot_general(left[q, :, 0:lanes], parts, TN, preferred_element_type=F32)
            if q == 0:
                acc[0:lanes, 0 : KSIZE * lanes] = value
            else:
                acc[0:lanes, 0 : KSIZE * lanes] += value

    plain_dw(act_low, dy_two)
    pairs = c.pairs
    proj_grad = outer(c.kept[24:25, 0:128], time_row)
    if width_out == 64:
        at = KSIZE * width_in
        for k in range(KSIZE):
            pairs[at + 64 * k : at + 64 * k + 64, :] = fold_pairs(acc, k, 64, 64)
        pairs[at + 320 : at + 320 + TE, :] = proj_grad
    else:
        at = start + KSIZE * width_in * (width_out // 128)
        for k in range(KSIZE):
            put_rows(acc[0:lanes, lanes * k : lanes * k + lanes], table, at + k * lanes * (width_out // 128))
        put_rows(proj_grad, table, at + 5 * lanes * (width_out // 128))
    crossing = CROSSING[block]
    need(copies.one(block), copies.res(block), *[copies.x(number) for number in INPUTS[block]])
    if block == 2:
        need(copies.up(1))
    if block > 0:
        size = {None: sum(x.shape[2] for x in xs), UP: 128, DOWN: 512}[crossing]

        def emit(q, value):
            if res is not None:
                if crossing == UP:
                    side = jnp.concatenate([low[0, :, 0:lanes], low[1, :, 0:lanes]], axis=1)
                else:
                    side = low[q, :, 0:lanes]
                value = value + lax.dot_general(side, res[...], NT, preferred_element_type=F32)
            if block == 5:
                for h in range(2):
                    c.up4[h] = value[:, 256 * h : 256 * h + 128]
                    c.up1[h] = value[:, 256 * h + 128 : 256 * h + 256]
            elif block == 4:
                c.up3[q] = value[:, 0:256]
                c.up2[q] = value[:, 256:512]
            elif block == 3:
                c.up2[q] = c.up2[q] + (value + up[q])
            elif block == 2:
                c.up1[q] = c.up1[q] + value
            else:
                c.up0[0] = value

        conv_dx(dy_one, c.one(block), size, inner, crossing, emit)
    conv_dw(xs, dy_one, inner, crossing, acc, low if res is not None else None)
    if width_out == 64:
        size = 64 if block == 0 else 256
        rows = 24 if block == 0 else 256
        for k in range(KSIZE):
            value = fold_pairs(acc, k, size, rows)
            pairs[width_in * k : width_in * k + width_in, :] = value[0:width_in]
        at = KSIZE * (width_in + 64) + TE
        pairs[at : at + width_in, :] = fold_pairs(acc, KSIZE, size, rows)[0:width_in]
        if block == 0:
            after = table[288:296, :]
            pack_pairs(pairs, table, start, 296)
            table[288:296, :] = jnp.where(rows_of((8, 128)) < 5, table[288:296, :], after)
        else:
            pack_pairs(pairs, table, start, 992)
    else:
        unit_rows = width_out // 128
        for k in range(KSIZE + (0 if res is None else 1)):
            at = start + k * width_in * unit_rows
            if k == KSIZE:
                at = start + (KSIZE * (width_in + width_out) + TE) * unit_rows
            if crossing == UP:
                value = acc[0:64, 256 * k : 256 * k + 128] + acc[64:128, 256 * k + 128 : 256 * k + 256]
            else:
                value = acc[0:width_in, width_out * k : width_out * k + width_out]
            put_rows(value, table, at)


def load_all(c, far, sems):
    copies = {}
    for number, (name, source) in enumerate(vars(far).items()):
        if name in vars(c):
            copies[name] = pltpu.make_async_copy(source, vars(c)[name], sems.at[number])
            copies[name].start()
    done = set()

    def need(*wanted):
        for copy in wanted:
            if copy is not None and id(copy) not in done:
                done.add(id(copy))
                copy.wait()

    return Refs(copies.keys(), copies.values()), need


def late_kernel(c, far, into, sems):
    copies, need = load_all(c, far, sems)
    aff, grads = c.aff, c.agrad
    outs = []

    def give(source, target):
        copy = pltpu.make_async_copy(source, target, sems.at[len(vars(far)) + len(outs)])
        copy.start()
        outs.append(copy)

    grads[...] = jnp.zeros_like(grads)
    need(copies.noise_in)
    noise_in, noise = c.noise_in, c.noise
    last = noise_in.shape[1] - 8

    def put_noise(group, value):
        noise[pl.ds(pl.multiple_of(16 * group, 16), 16), :] = value

    take_apart(noise_in, c.pre_a6.shape[1] // 64, put_noise)
    tail = noise_in[0, last:, :] + noise_in[1, last:, :] + noise_in[2, last:, :] + noise_in[3, last:, :]
    length = tail[0:1, :]
    scale_out = 1.0 / (tail[1:2, :] * TD)
    need(copies.stats, copies.terms, copies.kept, copies.pre_a6)
    pre = c.pre_a6
    inner = pre.shape[1]
    kept = norm_kept(c.stats, 12, 128)
    act, low, up = c.act, c.low, c.up5
    lane = lanes_of((1, 128))
    spot = lane % 64
    out_row = aff[55:56, :]
    out_bias = jnp.where(spot < TD, jnp.where(lane < 64, pltpu.roll(out_row, 64, 1), out_row), 0.0)
    segment = inner // 16

    def to_feature(q, start, rows, carry):
        here = pl.ds(start, rows)
        act[0, here, 0:128] = mish_fast(pre[0, here, :] * kept[0] + kept[1]).astype(BF)
        return carry

    sweep(1, inner, to_feature, 0)
    dv = c.dv
    dv[0, :, 0:128] = jnp.dot(act[0, :, 0:128], c.wout[...], preferred_element_type=F32)

    def to_loss(q, start, rows, state):
        here = pl.ds(start, rows)
        shape = (rows, 128)
        place = rows_of(shape) + start
        lanes = lanes_of(shape)
        frame = (place % 16 + jnp.where(lanes >= 64, 16, 0)) * segment + place // 16
        weight = jnp.where((frame.astype(F32) < length) & (lanes % 64 < TD), 1.0, 0.0)
        difference = weight * (dv[0, here, 0:128] + out_bias - noise[here, :])
        grad = 2.0 * difference * scale_out
        low[0, here, 0:128] = grad.astype(BF)
        return state[0] + fold_rows(difference * difference), state[1] + fold_rows(grad)

    zero = jnp.zeros((8, 128), F32)
    loss, out_sum = sweep(1, inner, to_loss, (zero, zero))
    c.loss[...] = loss * scale_out
    out_sum = both_halves(down_one_row(out_sum))
    c.gout[...] = lax.dot_general(act[0, :, 0:128], low[0, :, 0:128], TN, preferred_element_type=F32)
    dv[0, :, 0:128] = lax.dot_general(low[0, :, 0:128], c.wout[...], NT, preferred_element_type=F32)
    dy = c.dy.at[0:1, :, 0:128]
    got = norm_backward(
        c, 12, pre, head_vector(aff, 1), counts_of(2 * inner, 6), True, lambda q, here: dv[q, here, 0:128], dy
    )
    grads[54:55, :] = jnp.where(lane < 64, got[0], got[1])
    grads[55:56, :] = jnp.where(lane < 64, got[2], jnp.where(spot < TD, out_sum, 0.0))

    def emit_head(q, value):
        up[0] = value

    need(copies.one6, copies.x6)
    conv_dx(dy, c.one6, 128, inner, None, emit_head)
    conv_dw([c.x6], dy, inner, None, c.acc)
    for k in range(KSIZE):
        c.pairs[64 * k : 64 * k + 64, :] = fold_pairs(c.acc, k, 64, 64)
    pack_pairs(c.pairs, c.table, HEAD_ROW - LATE_START, 160)
    c.tgrad[...] = jnp.zeros_like(c.tgrad)
    backward_block(5, c, LATE_START, copies, need)
    give(c.up1, into.up1)
    backward_block(4, c, LATE_START, copies, need)
    split = -(-(ROW_STARTS[4] - LATE_START) // 8) * 8
    give(c.table.at[split:LATE_ROWS], into.table.at[split:LATE_ROWS])
    backward_block(3, c, LATE_START, copies, need)
    give(c.table.at[0:split], into.table.at[0:split])
    for source, target in ((c.up2, into.up2), (c.tgrad, into.tgrad), (grads, into.agrad)):
        give(source, target)
    need(*vars(copies).values())
    for copy in outs:
        copy.wait()


def early_kernel(c, far, into, sems):
    copies, need = load_all(c, far, sems)
    aff, grads, table = c.aff, c.agrad, c.table
    outs = []
    after = len(vars(far))

    def own_copy(source, target):
        copy = pltpu.make_async_copy(source, target, sems.at[after + len(outs)])
        copy.start()
        outs.append(copy)

    own_copy(far.late.at[0:8], c.edge)
    own_copy(far.late.at[8:LATE_ROWS], table.at[LATE_START + 8 : LATE_START + LATE_ROWS])
    late_edge, late_rest = outs
    need(copies.stats, copies.terms, copies.kept, copies.agrad, copies.tgrad)
    backward_block(2, c, 0, copies, need)
    late_edge.wait()
    lead = rows_of((8, 128)) < ROW_STARTS[3] - LATE_START
    table[LATE_START : LATE_START + 8, :] = jnp.where(lead, table[LATE_START : LATE_START + 8, :], c.edge[...])
    backward_block(1, c, 0, copies, need)
    backward_block(0, c, 0, copies, need)
    need(*vars(copies).values())
    late_rest.wait()
    total = jnp.zeros((TE, 128), F32)
    for block in range(6):
        lanes = LAYER_OUT[block][1]
        first = c.tgrad[8 * block : 8 * block + 1, 0:lanes]
        if WIDTHS[block][1] == 64:
            first = jnp.where(lanes_of((1, lanes)) < 64, first, 0.0)
        value = c.proj[TE * block : TE * block + TE, 0:lanes] * first
        total = total + (value if lanes == 128 else value[:, 0:128] + value[:, 128:256])
    kept = c.kept
    hidden_pre, hidden = kept[0:1, :], kept[8:9, :]
    feature_pre = kept[16:17, 0:128]
    grad_feature = lane_sums(total) * mish_both(feature_pre)[1]
    pairs = c.pairs
    second = outer(hidden, grad_feature)
    put_vector(grads, 58, 128, grad_feature)
    grad_hidden = lane_sums(c.embed_two[...] * grad_feature) * mish_both(hidden_pre)[1]
    first = outer(c.sinus[0:1, :], grad_hidden)
    put_vector(grads, 56, 256, grad_hidden)
    grads[60:61, :] = down_one_row(c.loss[...])
    table[OUT_ROW : OUT_ROW + 12, :] = c.hograd[0:12, :]
    table[FLAT_ROWS:TABLE_ROWS, :] = jnp.zeros((TABLE_ROWS - FLAT_ROWS, 128), F32)
    pairs[1024:1040, :] = jnp.zeros((16, 128), F32)
    pairs[0:1, :] = c.hograd[11:12, :]
    for half in range(2):
        value = first[:, 128 * half : 128 * half + 128]
        pairs[pl.ds(1 + 2 * half, TE, stride=4), :] = value
        pairs[pl.ds(2 + 2 * half, TE, stride=4), :] = pltpu.roll(value, 64, 1)
    pairs[pl.ds(513, TH, stride=2), :] = second
    pairs[pl.ds(514, TH, stride=2), :] = pltpu.roll(second, 64, 1)
    pack_pairs(pairs, table, EMB_ROW, FLAT_ROWS - EMB_ROW)
    core = c.core[0]
    keep, send = c.keep, c.send
    share = NKER_ROWS
    step = 176

    for pair in range(4):

        def split(index, carry):
            at = pl.multiple_of(index * step, step)
            even = table[pl.ds(share * (2 * pair) + at, step), :]
            odd = table[pl.ds(share * (2 * pair + 1) + at, step), :]
            keep[pair, pl.ds(at, step), :] = jnp.where(core == 0, even, odd)
            send[pl.ds(OWN_ROWS * pair + at, step), :] = jnp.where(core == 0, odd, even).astype(BF)
            return carry

        lax.fori_loop(0, OWN_ROWS // step, split, 0)
        own_copy(keep.at[pair], into.keep.at[pair])
        span = pl.ds(OWN_ROWS * pair, OWN_ROWS)
        own_copy(send.at[span, :], into.send.at[span, :])
    value = grads[...]
    high = value.astype(BF)
    rest = (value - high.astype(F32)).astype(BF)
    send[4 * OWN_ROWS : 4 * OWN_ROWS + 64, :] = high
    send[4 * OWN_ROWS + 64 : 4 * OWN_ROWS + 128, :] = rest
    grads[...] = high.astype(F32) + rest.astype(F32)
    span = pl.ds(4 * OWN_ROWS, 128)
    own_copy(send.at[span, :], into.send.at[span, :])
    own_copy(grads, into.agrad)
    for copy in outs[2:]:
        copy.wait()


def shape_tables(inner):
    padded = inner + 2 * HALO
    first = dict(
        stats=((104, 256), F32),
        terms=((48, 256), F32),
        kept=((32, 256), F32),
        proj=((6 * TE, 256), F32),
        embed_two=((256, 128), F32),
    )
    other = dict(
        tgrad=((48, 256), F32),
        agrad=((64, 128), F32),
        flat=((FLAT_ROWS, 128), F32),
        pairs=((2048, 128), F32),
        table=((TABLE_ROWS, 128), F32),
        edge=((8, 128), F32),
        send=((4 * OWN_ROWS + 128, 128), BF),
        keep=((4, OWN_ROWS, 128), F32),
        acc=((512, 1536), F32),
        side=((2, inner, 256), F32),
        dv=((2, inner, 256), F32),
        low=((2, inner, 256), BF),
        act=((2, inner, 256), BF),
        noise=((inner, 128), F32),
        noise_in=((4, inner // 8 + 8, 128), F32),
        hid=((2, padded, 256), BF),
        dy=((2, padded, 256), BF),
        ey=((2, padded, 256), BF),
    )
    for number, (halves, lanes) in enumerate(((1, 128),) + LAYER_OUT[:6]):
        first[f"x{number}"] = ((halves, padded, lanes), BF)
    for block in range(7):
        halves, lanes = LAYER_OUT[block]
        first[f"pre_a{block}"] = ((halves, inner, lanes), F32)
        first[f"one{block}"] = (W_ONE[block], BF)
        if block < 6:
            other[f"up{block}"] = ((halves, inner, lanes), F32)
            first[f"pre_b{block}"] = ((halves, inner, lanes), F32)
            first[f"two{block}"] = (W_TWO[block], BF)
            if W_RES[block] is not None:
                first[f"res{block}"] = (W_RES[block], BF)
    return first, other


def run_kernel(body, vmem_in, smem_in, any_in, outs_vmem, outs_any, scratch, sems, cost):
    operands = list(vmem_in.values()) + list(smem_in.values()) + list(any_in.values())
    in_specs = (
        [pl.BlockSpec(memory_space=pltpu.VMEM)] * len(vmem_in)
        + [pl.BlockSpec(memory_space=pltpu.SMEM)] * len(smem_in)
        + [pl.BlockSpec(memory_space=pl.ANY)] * len(any_in)
    )
    out_specs = [pl.BlockSpec(memory_space=pltpu.VMEM)] * len(outs_vmem)
    out_specs += [pl.BlockSpec(memory_space=pl.ANY)] * len(outs_any)
    out_kinds = list(outs_vmem.values()) + list(outs_any.values())
    near = list(vmem_in) + list(smem_in)
    places = (len(near), len(operands), len(operands) + len(outs_vmem), len(operands) + len(out_kinds))

    def call(*refs):
        here, there, results, left, buffers = [
            refs[low:high] for low, high in zip((0,) + places, places + (len(refs) - 1,))
        ]
        c = Refs(near + list(outs_vmem) + list(scratch), here + results + buffers)
        body(c, Refs(any_in, there), Refs(outs_any, left), refs[-1])

    results = pl.pallas_call(
        call,
        out_shape=[jax.ShapeDtypeStruct(*kind) for kind in out_kinds],
        in_specs=in_specs,
        out_specs=out_specs,
        scratch_shapes=[pltpu.VMEM(*kind) for kind in scratch.values()] + [pltpu.SemaphoreType.DMA((sems,))],
        compiler_params=pltpu.CompilerParams(vmem_limit_bytes=VMEM_LIMIT),
        cost_estimate=pl.CostEstimate(flops=cost, bytes_accessed=40000000, transcendentals=0),
    )(*operands)
    return SimpleNamespace(**dict(zip(list(outs_vmem) + list(outs_any), results)))


VMEM_LIMIT = 67043328


def exchange_pieces(traj, noise, mask, signal, mean, std):
    pieces, frames, wide = traj.shape
    scale = jnp.concatenate([jnp.sqrt(signal), jnp.sqrt(1.0 - signal)])
    vmem = pl.BlockSpec(memory_space=pltpu.VMEM)
    return pl.pallas_call(
        exchange_kernel,
        out_shape=[
            jax.ShapeDtypeStruct((pieces, frames // 4, 128), BF),
            jax.ShapeDtypeStruct((pieces, frames // 4 + 8, 128), F32),
            jax.ShapeDtypeStruct((8, 128), F32),
        ],
        in_specs=[vmem] * 6,
        out_specs=[vmem] * 3,
        scratch_shapes=[pltpu.VMEM((frames, 128), F32)] * 2,
    )(traj, noise, mask, jnp.broadcast_to(scale[:, None], (2 * pieces, 128)), mean[None, :], std[None, :])


def whole_horizon(noisy, noise, sinus, core, kernels, affine):
    inner = 4 * noisy.shape[1] * 2
    first, other = shape_tables(inner)
    t = SimpleNamespace(**first, **other)
    flat = jnp.pad(kernels, (0, FLAT_ROWS * 128 - kernels.shape[0])).reshape(FLAT_ROWS, 128)
    aff = jnp.concatenate(
        [affine[:7127], jnp.zeros((41,), F32), affine[7127:], jnp.zeros((640,), F32)]
    ).reshape(64, 128)
    head_out = kernels[OUT_START : OUT_START + C1 * TD].reshape(C1, TD).astype(BF)
    wide_out = jnp.pad(head_out, ((0, 0), (0, 64 - TD)))
    nothing = jnp.zeros((C1, 64), BF)
    wout = jnp.concatenate(
        [jnp.concatenate([wide_out, nothing], axis=1), jnp.concatenate([nothing, wide_out], axis=1)], axis=0
    )
    f = run_kernel(
        forward_kernel,
        dict(noisy=noisy, aff=aff, sinus=sinus),
        {},
        dict(flat=flat),
        {},
        first,
        dict(first, flat=t.flat, pairs=t.pairs, side=t.side, hid=t.hid),
        16 + len(first),
        14000000000,
    )
    late_in = dict(noise_in=noise, stats=f.stats, terms=f.terms, kept=f.kept, pre_a6=f.pre_a6, one6=f.one6, x6=f.x6)
    late_in.update(pre_b5=f.pre_b5, two5=f.two5, pre_a5=f.pre_a5, one5=f.one5, res5=f.res5, x5=f.x5, x2=f.x2)
    late_in.update(pre_b4=f.pre_b4, two4=f.two4, pre_a4=f.pre_a4, one4=f.one4, res4=f.res4, x4=f.x4, x3=f.x3)
    late_in.update(pre_b3=f.pre_b3, two3=f.two3, pre_a3=f.pre_a3, one3=f.one3)
    late_out = dict(table=((LATE_ROWS, 128), F32), up1=t.up1, up2=t.up2, tgrad=t.tgrad, agrad=t.agrad)
    work = dict(dv=t.dv, low=t.low, act=t.act, acc=t.acc, pairs=t.pairs, dy=t.dy, ey=t.ey)
    late = run_kernel(
        late_kernel,
        dict(aff=aff, wout=wout),
        {},
        late_in,
        dict(loss=((8, 128), F32), gout=((128, 128), F32)),
        late_out,
        dict({n: vars(t)[n] for n in late_in}, **late_out, noise=t.noise, up5=t.up5, up4=t.up4, up3=t.up3, **work),
        len(late_in) + len(late_out) + 1,
        16000000000,
    )
    gout = late.gout
    head_grad = (gout[0:64, 0:TD] + gout[64:128, 64 : 64 + TD]).reshape(-1)
    early_in = dict(stats=f.stats, terms=f.terms, kept=f.kept, agrad=late.agrad, tgrad=late.tgrad)
    early_in.update(up2=late.up2, pre_b2=f.pre_b2, two2=f.two2, pre_a2=f.pre_a2, one2=f.one2, res2=f.res2, x2=f.x2)
    early_in.update(up1=late.up1, pre_b1=f.pre_b1, two1=f.two1, pre_a1=f.pre_a1, one1=f.one1, res1=f.res1, x1=f.x1)
    early_in.update(pre_b0=f.pre_b0, two0=f.two0, pre_a0=f.pre_a0, one0=f.one0, res0=f.res0, x0=f.x0)
    early_in.update(proj=f.proj, embed_two=f.embed_two)
    early = run_kernel(
        early_kernel,
        dict(
            aff=aff,
            sinus=jnp.where(jnp.arange(8)[:, None] == 0, sinus, 0.0),
            loss=late.loss,
            hograd=jnp.pad(head_grad, (0, 2048 - C1 * TD)).reshape(16, 128),
        ),
        dict(core=core.reshape(1)),
        dict(early_in, late=late.table),
        {},
        dict(send=t.send, keep=t.keep, agrad=t.agrad),
        dict(
            {n: vars(t)[n] for n in early_in}, table=t.table, send=t.send, keep=t.keep, up0=t.up0, edge=t.edge, **work
        ),
        len(early_in) + 16,
        10000000000,
    )
    return early.send, early.keep, early.agrad


def on_device_xla(
    trajectories,
    dim_means,
    dim_stds,
    noise_draw,
    diffusion_steps,
    valid_mask,
    kernels,
    affine,
    kernel_momentum,
    kernel_average,
    affine_momentum,
    affine_average,
):
    members_all = unpack(kernels, affine)
    valid_total = lax.psum(jnp.sum(valid_mask.astype(jnp.float32)), (DP, HOR))
    signal_now = signal_level(diffusion_steps)[:, None, None]
    clean_frames = (trajectories - dim_means) / dim_stds
    noisy_frames = jnp.sqrt(signal_now) * clean_frames + jnp.sqrt(1.0 - signal_now) * noise_draw

    ring = lax.axis_size(HOR)
    axis = HOR
    if trajectories.shape[0] % ring == 0:
        axis = None
        local = trajectories.shape[0] // ring
        part = lax.axis_index(HOR) * local
        low_frames = noisy_frames.astype(jnp.bfloat16)
        noisy_frames = lax.all_to_all(low_frames, HOR, 0, 1, tiled=True).astype(jnp.float32)
        noise_draw = lax.all_to_all(noise_draw, HOR, 0, 1, tiled=True)
        valid_mask = lax.all_to_all(valid_mask, HOR, 0, 1, tiled=True)
        diffusion_steps = lax.dynamic_slice_in_dim(diffusion_steps, part, local)

    def time_closed(kernel_flat, affine_flat):
        return time_parts(kernel_flat, affine_flat, diffusion_steps)

    time_list, time_pullback = jax.vjp(time_closed, kernels, affine)
    down_one, kept_one = block_forward(noisy_frames, members_all[0], time_list[0], axis)
    down_two, kept_two = block_forward(down_one, members_all[1], time_list[1], axis)
    down_three, kept_three = block_forward(down_two, members_all[2], time_list[2], axis)
    middle, kept_middle = block_forward(down_three, members_all[3], time_list[3], axis)
    up_one, kept_upper = block_forward(
        jnp.concatenate([middle, down_three], axis=2), members_all[4], time_list[4], axis)
    up_two, kept_lower = block_forward(
        jnp.concatenate([up_one, down_two], axis=2), members_all[5], time_list[5], axis)
    predicted, kept_head = head_forward(up_two, members_all[6], axis)
    weight_rows = valid_mask.astype(jnp.float32)[:, :, None]
    difference = predicted - noise_draw
    loss_scale = 1.0 / (valid_total * TD)
    loss_part = jnp.sum(weight_rows * difference * difference) * loss_scale
    grad_predicted = 2.0 * weight_rows * difference * loss_scale
    grad_up_two, head_grads = head_backward(grad_predicted, kept_head, members_all[6], axis)
    grad_joined, time_six, grads_six = block_backward(grad_up_two, kept_lower, members_all[5], axis)
    grad_up_one = grad_joined[:, :, :C2]
    grad_down_two = grad_joined[:, :, C2:]
    grad_joined, time_five, grads_five = block_backward(grad_up_one, kept_upper, members_all[4], axis)
    grad_middle = grad_joined[:, :, :C3]
    grad_down_three = grad_joined[:, :, C3:]
    grad_inputs, time_four, grads_four = block_backward(grad_middle, kept_middle, members_all[3], axis)
    grad_inputs, time_three, grads_three = block_backward(
        grad_down_three + grad_inputs, kept_three, members_all[2], axis
    )
    grad_inputs, time_two, grads_two = block_backward(
        grad_down_two + grad_inputs, kept_two, members_all[1], axis
    )
    grad_inputs, time_one, grads_one = block_backward(grad_inputs, kept_one, members_all[0], axis)
    kernel_grad, affine_grad = pack_flat(
        [grads_one, grads_two, grads_three, grads_four, grads_five, grads_six, head_grads]
    )
    time_kernel, time_affine = time_pullback(
        (time_one, time_two, time_three, time_four, time_five, time_six)
    )
    kernel_grad = kernel_grad + time_kernel
    affine_grad = affine_grad + time_affine
    share_len = kernels.shape[0] // lax.axis_size(DP)
    owner_start = lax.axis_index(DP) * share_len
    kernel_sum, affine_sum, noise_loss = lax.psum(
        (kernel_grad, affine_grad, loss_part), (DP, HOR)
    )
    kernel_own = lax.dynamic_slice_in_dim(kernel_sum, owner_start, share_len)
    squares = jnp.sum(kernel_sum * kernel_sum) + jnp.sum(affine_sum * affine_sum)
    grad_norm = jnp.sqrt(squares)
    factor = jnp.minimum(1.0, MAX_NORM / (grad_norm + 1e-06))
    kernel_step = kernel_own * factor
    kernel_old = lax.dynamic_slice_in_dim(kernels, owner_start, share_len)
    kernel_mom_new = MOMENTUM * kernel_momentum + kernel_step
    kernel_new = kernel_old - LEARN_RATE * (kernel_step + MOMENTUM * kernel_mom_new)
    kernel_ema_new = EMA_DECAY * kernel_average + (1.0 - EMA_DECAY) * kernel_new
    affine_step = affine_sum * factor
    affine_mom_new = MOMENTUM * affine_momentum + affine_step
    affine_new = affine - AFFINE_RATE * (affine_step + MOMENTUM * affine_mom_new)
    affine_ema_new = EMA_DECAY * affine_average + (1.0 - EMA_DECAY) * affine_new
    return (
        noise_loss,
        grad_norm,
        kernel_new,
        kernel_mom_new,
        kernel_ema_new,
        kernel_new.astype(jnp.bfloat16),
        affine_new,
        affine_mom_new,
        affine_ema_new,
        affine_new.astype(jnp.bfloat16),
    )


def swap(value, axis, bit):
    return lax.ppermute(value, axis, [(i, i ^ bit) for i in range(lax.axis_size(axis))])


def total_all(value, axes, count):
    got = lax.all_to_all(jnp.broadcast_to(value, (count, 128)), axes, 0, 0, tiled=True)
    return jnp.sum(got[:, 0])


def pick(stack, index):
    return lax.dynamic_index_in_dim(stack, index, 0, keepdims=False)


def in_low(value):
    return lax.reduce_precision(value, 8, 7)


def two_parts(value):
    high = in_low(value)
    return high, in_low(value - high)


def share_sums(send, keep, small):
    low, wide = jnp.bfloat16, jnp.float32
    place = lax.axis_index(DP)
    seat_x = (place >> 1) & 1
    seat_y = (place >> 2) & 1
    layer = lax.axis_index(HOR)
    part_rows = OWN_ROWS // 4
    half = OWN_ROWS // 2

    def with_small(value, parts):
        return jnp.concatenate([value.reshape(-1, 128), parts[0], parts[1]], axis=0).astype(low)

    def small_of(got):
        tail = got[-128:].astype(wide)
        return tail[:64] + tail[64:]

    got = swap(send, DP, 1)
    grid = (keep + got[:-128].reshape(keep.shape).astype(wide)).reshape(2, 2, OWN_ROWS, 128)
    parts = two_parts(small + small_of(got))
    first, second = grid[:, :, :half], grid[:, :, half:]
    first_in = swap(
        with_small(lax.dynamic_index_in_dim(first, 1 - seat_x, 1, keepdims=False), parts), DP, 2
    )
    second_in = swap(pick(second, 1 - seat_y).astype(low), DP, 4)
    parts = two_parts(parts[0] + parts[1] + small_of(first_in))
    first = lax.dynamic_index_in_dim(first, seat_x, 1, keepdims=False)
    first = first + first_in[:-128].reshape(first.shape).astype(wide)
    second = pick(second, seat_y) + second_in.astype(wide)
    first_in = swap(with_small(pick(first, 1 - seat_y), parts), DP, 4)
    second_in = swap(pick(second, 1 - seat_x).astype(low), DP, 2)
    parts = two_parts(parts[0] + parts[1] + small_of(first_in))
    own = jnp.concatenate(
        [
            pick(first, seat_y) + first_in[:-128].astype(wide),
            pick(second, seat_x) + second_in.astype(wide),
        ],
        axis=0,
    ).reshape(4, part_rows, 128)
    arrived = [swap(with_small(pick(own, layer ^ bits), parts), HOR, bits) for bits in (1, 2, 3)]
    part = pick(own, layer)
    for value in arrived:
        part = part + value[:-128].astype(wide)
    smalls = jnp.stack([parts[0] + parts[1]] + [small_of(value) for value in arrived])
    small = sum(pick(smalls, layer ^ n) for n in range(4))
    return part, small


def all_parts(part):
    layer = lax.axis_index(HOR)
    part_low = in_low(part).astype(jnp.bfloat16)
    parts = jnp.stack([part_low] + [swap(part_low, HOR, bits) for bits in (1, 2, 3)])
    return jnp.concatenate([pick(parts, layer ^ n) for n in range(4)], axis=0)


def on_device(
    trajectories,
    dim_means,
    dim_stds,
    noise_draw,
    diffusion_steps,
    valid_mask,
    kernels,
    affine,
    kernel_momentum,
    kernel_average,
    affine_momentum,
    affine_average,
):
    ring = lax.axis_size(HOR)
    frames = trajectories.shape[1] * ring
    if trajectories.shape[0] != ring or ring != 4 or frames % 512 or lax.axis_size(DP) != 8:
        return on_device_xla(
            trajectories,
            dim_means,
            dim_stds,
            noise_draw,
            diffusion_steps,
            valid_mask,
            kernels,
            affine,
            kernel_momentum,
            kernel_average,
            affine_momentum,
            affine_average,
        )
    total = total_all(jnp.sum(valid_mask.astype(jnp.float32)), DP, lax.axis_size(DP))
    low_out, noise_out, counts = exchange_pieces(
        trajectories, noise_draw, valid_mask, signal_level(diffusion_steps), dim_means, dim_stds
    )
    low_out, total = lax.optimization_barrier((low_out, total))
    noisy = lax.all_to_all(low_out, HOR, 0, 0, tiled=True)
    row = lax.broadcasted_iota(jnp.int32, (4, 8, 128), 1)
    extra = jnp.where(row == 0, counts[:4, None, :], jnp.where(row == 1, total, 0.0))
    noise_out = lax.dynamic_update_slice(noise_out, extra, (0, noise_out.shape[1] - 8, 0))
    noise_out, packed = lax.optimization_barrier((noise_out, kernels))
    noise = lax.all_to_all(noise_out, HOR, 0, 0, tiled=True)
    own_step = lax.dynamic_slice_in_dim(diffusion_steps, lax.axis_index(HOR), 1)
    sinus = jnp.broadcast_to(sinusoid(own_step), (8, TE))
    place = lax.axis_index(DP)
    send, keep, small = whole_horizon(noisy, noise, sinus, place & 1, packed, affine)
    part, small = share_sums(send, keep, small)
    share_len = kernels.shape[0] // lax.axis_size(DP)
    owner_start = place * share_len
    lead = owner_start - place * NKER_ROWS * 128
    number = (
        lax.axis_index(HOR) * part.size
        + lax.broadcasted_iota(jnp.int32, part.shape, 0) * 128
        + lax.broadcasted_iota(jnp.int32, part.shape, 1)
    )
    inside = (number >= lead) & (number < lead + share_len)
    count = lax.axis_size(DP) * lax.axis_size(HOR)
    squares = total_all(jnp.sum(jnp.where(inside, part * part, 0.0)), (DP, HOR), count)
    whole = all_parts(part)
    small_flat = small.reshape(-1)
    affine_sum = jnp.concatenate([small_flat[:7127], small_flat[7168:7552]])
    noise_loss = jnp.sum(small[60])
    grad_norm = jnp.sqrt(squares + jnp.sum(affine_sum * affine_sum))
    kernel_own = lax.dynamic_slice_in_dim(whole.astype(jnp.float32).reshape(-1), lead, share_len)
    factor = jnp.minimum(1.0, MAX_NORM / (grad_norm + 1e-06))
    kernel_step = kernel_own * factor
    kernel_old = lax.dynamic_slice_in_dim(kernels, owner_start, share_len)
    kernel_mom_new = MOMENTUM * kernel_momentum + kernel_step
    kernel_new = kernel_old - LEARN_RATE * (kernel_step + MOMENTUM * kernel_mom_new)
    kernel_ema_new = EMA_DECAY * kernel_average + (1.0 - EMA_DECAY) * kernel_new
    affine_step = affine_sum * factor
    affine_mom_new = MOMENTUM * affine_momentum + affine_step
    affine_new = affine - AFFINE_RATE * (affine_step + MOMENTUM * affine_mom_new)
    affine_ema_new = EMA_DECAY * affine_average + (1.0 - EMA_DECAY) * affine_new
    return (
        noise_loss,
        grad_norm,
        kernel_new,
        kernel_mom_new,
        kernel_ema_new,
        kernel_new.astype(jnp.bfloat16),
        affine_new,
        affine_mom_new,
        affine_ema_new,
        affine_new.astype(jnp.bfloat16),
    )


def solution(mesh):
    in_specs = (
        P(DP, HOR, None),
        P(),
        P(),
        P(DP, HOR, None),
        P(DP),
        P(DP, HOR),
        P(),
        P(),
        P(DP),
        P(DP),
        P(),
        P(),
    )
    out_specs = (P(), P(), P(DP), P(DP), P(DP), P(DP), P(), P(), P(), P())
    return jax.shard_map(
        on_device, mesh=mesh, in_specs=in_specs, out_specs=out_specs, check_vma=False
    )
```

```python
import functools
import math
from types import SimpleNamespace

import jax
import jax.numpy as jnp
from jax import lax
from jax.experimental import pallas as pl
from jax.experimental.pallas import tpu as pltpu
from jax.sharding import PartitionSpec as P

TD = 23
C1 = 64
C2 = 128
C3 = 256
TE = 128
TH = 256
KSIZE = 5
GROUPS = 8
NSTEPS = 100


DP, HOR = "dp", "hor"
PRECISE = lax.Precision.HIGHEST
EPSILON = 1e-05
MAX_NORM = 0.02
LEARN_RATE = 200.0
AFFINE_RATE = 1500.0
MOMENTUM = 0.9
EMA_DECAY = 0.5


def padded_2(cells, sides, width):
    for axis, dim in sides:
        if axis is None:
            pads = [(0, 0)] * cells.ndim
            pads[dim] = (width, width)
            cells = jnp.pad(cells, pads)
            continue
        count = lax.axis_size(axis)
        ends = count - 1
        head = lax.slice_in_dim(cells, 0, width, axis=dim)
        tail = lax.slice_in_dim(cells, cells.shape[dim] - width, cells.shape[dim], axis=dim)
        cells = jnp.concatenate(
            [
                lax.ppermute(tail, axis, [(i, (i + 1) % count) for i in range(ends)]),
                cells,
                lax.ppermute(head, axis, [((i + 1) % count, i) for i in range(ends)]),
            ],
            axis=dim,
        )
    return cells


def sum_over(values, axis):
    return values if axis is None else lax.psum(values, axis)


def axis_length(axis):
    return 1 if axis is None else lax.axis_size(axis)


def layout_shapes():
    kernel_shapes = []
    affine_shapes = []
    for width_in, width_out in [
        (TD, C1),
        (C1, C2),
        (C2, C3),
        (C3, C3),
        (C3 + C3, C2),
        (C2 + C2, C1),
    ]:
        matrices = [
            ("conv_one", KSIZE * width_in, width_out),
            ("conv_two", KSIZE * width_out, width_out),
            ("time_proj", TE, width_out),
        ]
        vectors = [
            (entry_name, width_out)
            for entry_name in [
                "bias_one",
                "gain_one",
                "shift_one",
                "time_bias",
                "bias_two",
                "gain_two",
                "shift_two",
            ]
        ]
        if width_in != width_out:
            matrices.append(("res_proj", width_in, width_out))
            vectors.append(("res_bias", width_out))
        kernel_shapes.append(matrices)
        affine_shapes.append(vectors)
    kernel_shapes.append(
        [
            ("head_conv", KSIZE * C1, C1),
            ("head_out", C1, TD),
            ("embed_one", TE, TH),
            ("embed_two", TH, TE),
        ]
    )
    affine_shapes.append(
        [
            ("head_bias", C1),
            ("head_gain", C1),
            ("head_shift", C1),
            ("out_bias", TD),
            ("embed_bias_one", TH),
            ("embed_bias_two", TE),
        ]
    )
    return (kernel_shapes, affine_shapes)


def unpack(kernels, affine):
    kernel_shapes, affine_shapes = layout_shapes()
    members_all = []
    cursor = 0
    for entries in kernel_shapes:
        members = SimpleNamespace()
        for entry_name, height, breadth in entries:
            piece = kernels[cursor : cursor + height * breadth].reshape(height, breadth)
            setattr(members, entry_name, piece)
            cursor += height * breadth
        members_all.append(members)
    cursor = 0
    for position, entries in enumerate(affine_shapes):
        for entry_name, length in entries:
            setattr(members_all[position], entry_name, affine[cursor : cursor + length])
            cursor += length
    return members_all


def pack_flat(grad_list):
    kernel_shapes, affine_shapes = layout_shapes()
    kernel_pieces = []
    affine_pieces = []
    for position, entries in enumerate(kernel_shapes):
        for entry_name, height, breadth in entries:
            kernel_pieces.append(
                vars(grad_list[position])
                .get(entry_name, jnp.zeros((height, breadth), jnp.float32))
                .reshape(-1)
            )
    for position, entries in enumerate(affine_shapes):
        for entry_name, length in entries:
            affine_pieces.append(
                vars(grad_list[position]).get(entry_name, jnp.zeros((length,), jnp.float32))
            )
    return (jnp.concatenate(kernel_pieces), jnp.concatenate(affine_pieces))


def mish_act(value):
    return value * jnp.tanh(jax.nn.softplus(value))


def mish_grad(value, upstream):
    return jax.vjp(mish_act, value)[1](upstream)[0]


def sinusoid(steps_vec):
    half_width = TE // 2
    ladder = jnp.exp(
        -math.log(10000.0) * jnp.arange(half_width).astype(jnp.float32) / (half_width - 1)
    )
    angles = steps_vec.astype(jnp.float32)[:, None] * ladder[None, :]
    return jnp.concatenate([jnp.sin(angles), jnp.cos(angles)], axis=1)


def signal_level(steps_vec):
    ratio = (steps_vec.astype(jnp.float32) + 1.0) / NSTEPS
    cosine_now = jnp.cos((ratio + 0.008) / 1.008 * math.pi / 2)
    cosine_zero = math.cos(0.008 / 1.008 * math.pi / 2)
    return (cosine_now / cosine_zero) ** 2


def time_parts(kernel_flat, affine_flat, steps_vec):
    members_all = unpack(kernel_flat, affine_flat)
    last_group = members_all[6]
    hidden = mish_act(
        jnp.dot(sinusoid(steps_vec), last_group.embed_one, precision=PRECISE)
        + last_group.embed_bias_one
    )
    feature = mish_act(
        jnp.dot(hidden, last_group.embed_two, precision=PRECISE) + last_group.embed_bias_two
    )
    return tuple(
        (
            jnp.dot(feature, members_all[block_index].time_proj, precision=PRECISE)
            + members_all[block_index].time_bias
            for block_index in range(6)
        )
    )


def conv_forward(inputs_low, weight_low, axis):
    padded = padded_2(inputs_low, ((axis, 1),), 2)
    frames = inputs_low.shape[1]
    channels = inputs_low.shape[2]
    running = 0.0
    for offset in range(KSIZE):
        running = running + jnp.einsum(
            "blc,cd->bld",
            padded[:, offset : offset + frames],
            weight_low[offset * channels : (offset + 1) * channels],
            preferred_element_type=jnp.float32,
        )
    return (running, padded)


def conv_backward(grad_low, padded, weight_low, axis):
    grad_padded = padded_2(grad_low, ((axis, 1),), 2)
    frames = grad_low.shape[1]
    channels = padded.shape[2]
    pieces = []
    running = 0.0
    for offset in range(KSIZE):
        pieces.append(
            jnp.einsum(
                "blc,bld->cd",
                padded[:, offset : offset + frames],
                grad_low,
                preferred_element_type=jnp.float32,
            )
        )
        start_row = KSIZE - 1 - offset
        running = running + jnp.einsum(
            "bld,cd->blc",
            grad_padded[:, start_row : start_row + frames],
            weight_low[offset * channels : (offset + 1) * channels],
            preferred_element_type=jnp.float32,
        )
    return (running, jnp.concatenate(pieces, axis=0))


def group_norm(values, gain_vec, shift_vec, axis):
    horizons, frames, channels = values.shape
    grouped = values.reshape(horizons, frames, GROUPS, channels // GROUPS)
    sum_one, sum_two = sum_over(
        (jnp.sum(grouped, axis=(1, 3)), jnp.sum(grouped * grouped, axis=(1, 3))), axis
    )
    group_count = frames * axis_length(axis) * (channels // GROUPS)
    average = sum_one / group_count
    inverse = lax.rsqrt(sum_two / group_count - average * average + EPSILON)
    normed = ((grouped - average[:, None, :, None]) * inverse[:, None, :, None]).reshape(
        horizons, frames, channels
    )
    return (normed * gain_vec + shift_vec, (normed, inverse))


def group_norm_back(upstream, norm_stats, gain_vec, axis):
    normed, inverse = norm_stats
    horizons, frames, channels = normed.shape
    grad_gain = jnp.sum(upstream * normed, axis=(0, 1))
    grad_shift = jnp.sum(upstream, axis=(0, 1))
    scaled = (upstream * gain_vec).reshape(horizons, frames, GROUPS, channels // GROUPS)
    grouped = normed.reshape(horizons, frames, GROUPS, channels // GROUPS)
    sum_one, sum_two = sum_over(
        (jnp.sum(scaled, axis=(1, 3)), jnp.sum(scaled * grouped, axis=(1, 3))), axis
    )
    group_count = frames * axis_length(axis) * (channels // GROUPS)
    result = inverse[:, None, :, None] * (
        scaled
        - sum_one[:, None, :, None] / group_count
        - grouped * sum_two[:, None, :, None] / group_count
    )
    return (result.reshape(horizons, frames, channels), grad_gain, grad_shift)


def block_forward(inputs, members, time_term, axis):
    inputs_low = inputs.astype(jnp.bfloat16)
    weight_one = members.conv_one.astype(jnp.bfloat16)
    weight_two = members.conv_two.astype(jnp.bfloat16)
    conv_out, padded_one = conv_forward(inputs_low, weight_one, axis)
    normed_one, stats_one = group_norm(
        conv_out + members.bias_one, members.gain_one, members.shift_one, axis
    )
    hidden = mish_act(normed_one) + time_term[:, None, :]
    conv_out, padded_two = conv_forward(hidden.astype(jnp.bfloat16), weight_two, axis)
    normed_two, stats_two = group_norm(
        conv_out + members.bias_two, members.gain_two, members.shift_two, axis
    )
    result = mish_act(normed_two)
    if "res_proj" in vars(members):
        weight_side = members.res_proj.astype(jnp.bfloat16)
        result = (
            result
            + jnp.einsum("blc,cd->bld", inputs_low, weight_side, preferred_element_type=jnp.float32)
            + members.res_bias
        )
    else:
        weight_side = None
        result = result + inputs
    return (
        result,
        (
            padded_one,
            stats_one,
            padded_two,
            stats_two,
            inputs_low,
            weight_one,
            weight_two,
            weight_side,
        ),
    )


def block_backward(upstream, kept, members, axis):
    (
        padded_one,
        stats_one,
        padded_two,
        stats_two,
        inputs_low,
        weight_one,
        weight_two,
        weight_side,
    ) = kept
    grad_map = SimpleNamespace()
    grad_normed = mish_grad(stats_two[0] * members.gain_two + members.shift_two, upstream)
    grad_pre, grad_map.gain_two, grad_map.shift_two = group_norm_back(
        grad_normed, stats_two, members.gain_two, axis
    )
    grad_map.bias_two = jnp.sum(grad_pre, axis=(0, 1))
    grad_hidden, grad_map.conv_two = conv_backward(
        grad_pre.astype(jnp.bfloat16), padded_two, weight_two, axis
    )
    time_grad = jnp.sum(grad_hidden, axis=1)
    grad_normed = mish_grad(stats_one[0] * members.gain_one + members.shift_one, grad_hidden)
    grad_pre, grad_map.gain_one, grad_map.shift_one = group_norm_back(
        grad_normed, stats_one, members.gain_one, axis
    )
    grad_map.bias_one = jnp.sum(grad_pre, axis=(0, 1))
    grad_inputs, grad_map.conv_one = conv_backward(
        grad_pre.astype(jnp.bfloat16), padded_one, weight_one, axis
    )
    if weight_side is not None:
        upstream_low = upstream.astype(jnp.bfloat16)
        grad_map.res_bias = jnp.sum(upstream, axis=(0, 1))
        grad_map.res_proj = jnp.einsum(
            "blc,bld->cd", inputs_low, upstream_low, preferred_element_type=jnp.float32
        )
        grad_inputs = grad_inputs + jnp.einsum(
            "bld,cd->blc", upstream_low, weight_side, preferred_element_type=jnp.float32
        )
    else:
        grad_inputs = grad_inputs + upstream
    return (grad_inputs, time_grad, grad_map)


def head_forward(inputs, members, axis):
    weight_conv = members.head_conv.astype(jnp.bfloat16)
    weight_out = members.head_out.astype(jnp.bfloat16)
    conv_out, padded = conv_forward(inputs.astype(jnp.bfloat16), weight_conv, axis)
    normed, norm_stats = group_norm(
        conv_out + members.head_bias, members.head_gain, members.head_shift, axis
    )
    feature_low = mish_act(normed).astype(jnp.bfloat16)
    predicted = (
        jnp.einsum("blc,cd->bld", feature_low, weight_out, preferred_element_type=jnp.float32)
        + members.out_bias
    )
    return (predicted, (padded, norm_stats, feature_low, weight_conv, weight_out))


def head_backward(upstream, kept, members, axis):
    padded, norm_stats, feature_low, weight_conv, weight_out = kept
    grad_map = SimpleNamespace()
    upstream_low = upstream.astype(jnp.bfloat16)
    grad_map.out_bias = jnp.sum(upstream, axis=(0, 1))
    grad_map.head_out = jnp.einsum(
        "blc,bld->cd", feature_low, upstream_low, preferred_element_type=jnp.float32
    )
    grad_feature = jnp.einsum(
        "bld,cd->blc", upstream_low, weight_out, preferred_element_type=jnp.float32
    )
    grad_normed = mish_grad(
        norm_stats[0] * members.head_gain + members.head_shift, grad_feature
    )
    grad_pre, grad_map.head_gain, grad_map.head_shift = group_norm_back(
        grad_normed, norm_stats, members.head_gain, axis
    )
    grad_map.head_bias = jnp.sum(grad_pre, axis=(0, 1))
    grad_inputs, grad_map.head_conv = conv_backward(
        grad_pre.astype(jnp.bfloat16), padded, weight_conv, axis
    )
    return (grad_inputs, grad_map)


BF = jnp.bfloat16
F32 = jnp.float32
HALO = 32
ROW_STARTS = (0, 293, 1445, 5797, 11173, 15013)
LOAD_ROWS = (0, 296, 1448, 5800, 11176, 15016, 16008, 16696)
HEAD_ROW = 16005
OUT_ROW = 16165
EMB_ROW = 16176
FLAT_ROWS = 16696
TABLE_ROWS = 16720
LATE_START = 5792
LATE_ROWS = 16168 - LATE_START
OWN_ROWS = 2112
NKER_ROWS = 2086
OUT_START = OUT_ROW * 128
WIDTHS = ((TD, C1), (C1, C2), (C2, C3), (C3, C3), (C3 + C3, C2), (C2 + C2, C1))
AFF_ROWS = (0, 4, 12, 28, 42, 50)
LAYER_OUT = ((1, 128), (2, 128), (2, 256), (2, 256), (2, 128), (1, 128), (1, 128))
W_ONE = ((640, 128), (640, 256), (640, 256), (1280, 256), (2560, 128), (2560, 128), (640, 128))
W_TWO = ((640, 128), (640, 128), (1280, 256), (1280, 256), (640, 128), (640, 128))
W_RES = ((128, 128), (128, 256), (128, 256), None, (512, 128), (512, 128))
UP, DOWN = 1, 2
TN = (((0,), (0,)), ((), ()))
NT = (((1,), (1,)), ((), ()))


INPUTS = ((0,), (1,), (2,), (3,), (4, 3), (5, 2))


class Refs:
    def __init__(self, names, values):
        vars(self).update(zip(names, values))

    def of(self, kind, block):
        return vars(self).get(f"{kind}{block}")

    def one(self, block):
        return self.of("one", block)

    def two(self, block):
        return self.of("two", block)

    def res(self, block):
        return self.of("res", block)

    def pre_a(self, block):
        return self.of("pre_a", block)

    def pre_b(self, block):
        return self.of("pre_b", block)

    def up(self, block):
        return self.of("up", block)

    def x(self, number):
        return self.of("x", number)


def lanes_of(shape):
    return lax.broadcasted_iota(jnp.int32, shape, 1)


def rows_of(shape):
    return lax.broadcasted_iota(jnp.int32, shape, 0)


def fill_halo(ref):
    halves, padded_rows, lanes = ref.shape
    inner = padded_rows - 2 * HALO
    row = rows_of((16, lanes))
    lane = lanes_of((16, lanes))
    for group in range(2):
        start = inner + 16 * group
        moved = [pltpu.roll(ref[q, start : start + 16, :].astype(F32), 1, 0) for q in range(halves)]
        into = pl.ds(16 * group, 16)
        if halves == 1:
            edge = jnp.where(lane >= 64, pltpu.roll(moved[0], 64, 1), 0.0)
            ref[0, into, :] = jnp.where(row == 0, edge, moved[0]).astype(BF)
        else:
            ref[0, into, :] = jnp.where(row == 0, 0.0, moved[0]).astype(BF)
            ref[1, into, :] = jnp.where(row == 0, moved[0], moved[1]).astype(BF)
        start = HALO + 16 * group
        moved = [pltpu.roll(ref[q, start : start + 16, :].astype(F32), 15, 0) for q in range(halves)]
        into = pl.ds(HALO + inner + 16 * group, 16)
        if halves == 1:
            edge = jnp.where(lane < 64, pltpu.roll(moved[0], 64, 1), 0.0)
            ref[0, into, :] = jnp.where(row == 15, edge, moved[0]).astype(BF)
        else:
            ref[0, into, :] = jnp.where(row == 15, moved[1], moved[0]).astype(BF)
            ref[1, into, :] = jnp.where(row == 15, 0.0, moved[1]).astype(BF)


def exchange_kernel(traj, noise, mask, scale, mean, std, noisy_out, noise_out, counts, noisy_wide, noise_wide):
    pieces, frames, wide = traj.shape
    segment = frames // 8
    quarter = segment // 4
    rows = tile_rows(frames // 7) * 7 if frames % 7 == 0 else tile_rows(frames)

    for piece in range(pieces):

        def fill(index, carry):
            here = pl.ds(pl.multiple_of(index * rows, rows), rows)
            value = noise[piece, here, :]
            clean = (traj[piece, here, :] - mean[...]) / std[...]
            noisy_wide[here, 0:wide] = scale[piece : piece + 1, 0:wide] * clean + (
                scale[4 + piece : 5 + piece, 0:wide] * value
            )
            noise_wide[here, 0:wide] = value
            return carry

        lax.fori_loop(0, frames // rows, fill, 0)
        step = quarter // 2 if quarter % 4 == 0 else quarter

        def gather(index, carry):
            lane = lanes_of((8, 128))

            def one(source, place):
                total = 0.0
                for number in range(4):
                    value = source[pl.ds(quarter * number + place, 8, stride=segment), :]
                    value = jnp.where(lane < wide, value, 0.0)
                    total = total + (pltpu.roll(value, 32 * number, 1) if number else value)
                return total

            for inner in range(0, step, 2):
                place = index * step + inner
                at = pl.multiple_of(8 * place, 16)
                noisy_out[piece, pl.ds(at, 16), :] = jnp.concatenate(
                    [one(noisy_wide, place), one(noisy_wide, place + 1)], axis=0
                ).astype(BF)
                noise_out[piece, pl.ds(at, 8), :] = one(noise_wide, place)
                noise_out[piece, pl.ds(at + 8, 8), :] = one(noise_wide, place + 1)
            return carry

        lax.fori_loop(0, quarter // step, gather, 0)
        total = jnp.sum(mask[piece : piece + 1, :].astype(F32), axis=1, keepdims=True)
        counts[piece : piece + 1, :] = jnp.broadcast_to(total, (1, 128))


def take_apart(source, quarter, store):
    lane = lanes_of((16, 128))

    def step(index, carry):
        at = pl.multiple_of(16 * index, 16)
        got = [source[piece, pl.ds(at, 16), :].astype(F32) for piece in range(4)]
        for inner in range(2):
            here = slice(8 * inner, 8 * inner + 8)
            low = jnp.concatenate([got[0][here], got[1][here]], axis=0)
            high = jnp.concatenate([got[2][here], got[3][here]], axis=0)
            for number in range(4):
                left = pltpu.roll(low, (128 - 32 * number) % 128, 1) if number else low
                right = pltpu.roll(high, (192 - 32 * number) % 128, 1) if number != 2 else high
                value = jnp.where(lane < 64, left, right)
                store(quarter * number + 2 * index + inner, jnp.where(lane % 64 < 32, value, 0.0))
        return carry

    lax.fori_loop(0, quarter // 2, step, 0)


def mish_fast(value):
    grown = jnp.exp(jnp.minimum(value, 20.0))
    top = grown * (grown + 2.0)
    return value * (top / (top + 2.0))


def mish_both(value):
    grown = jnp.exp(jnp.minimum(value, 20.0))
    top = grown * (grown + 2.0)
    inverse = 1.0 / (top + 2.0)
    ratio = top * inverse
    slope = ratio + 4.0 * value * (top - grown) * (inverse * inverse)
    return value * ratio, slope


def fold_rows(value):
    rows, lanes = value.shape
    return jnp.sum(value.reshape(rows // 8, 8, lanes), axis=0)


def down_one_row(value):
    return jnp.sum(value, axis=0, keepdims=True)


def both_halves(row):
    return row + pltpu.roll(row, 64, 1)


def group_sums(first, second, packed):
    lanes = first.shape[1]
    row = rows_of((16, lanes))
    stacked = jnp.zeros((16, lanes), F32)
    for number, value in enumerate((first, second)):
        for part in range(3):
            high = value.astype(BF).astype(F32)
            stacked = jnp.where(row == 3 * number + part, high, stacked)
            value = value - high
    left = rows_of((lanes, lanes))
    right = lanes_of((lanes, lanes))
    if packed:
        same = (left % 64) // 8 == (right % 64) // 8
    else:
        size = lanes // GROUPS
        same = left // size == right // size
    same = jnp.where(same, 1.0, 0.0).astype(BF)
    summed = jnp.dot(stacked.astype(BF), same, preferred_element_type=F32)
    return down_one_row(summed[0:3, :]), down_one_row(summed[3:6, :])


def tile_rows(inner):
    for rows in (896, 448, 256, 128, 64, 32, 16):
        if inner % rows == 0:
            return rows


def sweep(halves, inner, body, carry):
    rows = tile_rows(inner)
    per_half = inner // rows

    def step(index, state):
        q = index // per_half
        start = pl.multiple_of((index - q * per_half) * rows, rows)
        return body(q, start, rows, state)

    return lax.fori_loop(0, halves * per_half, step, carry)


def vector(aff, row, width):
    if width == 256:
        base = int(row)
        return jnp.concatenate([aff[base : base + 1, :], aff[base + 1 : base + 2, :]], axis=1)
    base = int(row)
    whole = aff[base : base + 1, :]
    if width == 128:
        return whole
    turned = pltpu.roll(whole, 64, 1)
    lane = lanes_of((1, 128))
    if row == base:
        return jnp.where(lane < 64, whole, turned)
    return jnp.where(lane < 64, turned, whole)


def block_vector(aff, block, number):
    width = WIDTHS[block][1]
    return vector(aff, AFF_ROWS[block] + number * width / 128, width)


def head_vector(aff, number):
    return vector(aff, 54 + number / 2, 64)


def conv_input(xs, q, tap, inner):
    parts = [x[q, pl.ds(16 * tap, inner), :] for x in xs]
    return parts[0] if len(parts) == 1 else jnp.concatenate(parts, axis=1)


def conv_to(xs, weight, bias, out, crossing, beside=None):
    halves, inner, lanes = out.shape
    zero = jnp.zeros((8, lanes), F32)

    def finish(q, total, state):
        total = total + bias
        out[q] = total
        return state[0] + fold_rows(total), state[1] + fold_rows(total * total)

    if crossing == UP:
        wide = jnp.concatenate([conv_input(xs, 0, k, inner) for k in range(KSIZE)], axis=1)
        total = jnp.dot(wide, weight[...], preferred_element_type=F32)
        state = finish(0, total[:, :lanes], (zero, zero))
        return finish(1, total[:, lanes:], state)

    def taps_across(q, parts):
        wide = jnp.concatenate(parts, axis=1)
        size = wide.shape[1]
        across = jnp.concatenate([weight[size * k : size * k + size, :] for k in range(KSIZE)], axis=1)
        if beside is not None:
            side, res, res_bias = beside
            across = jnp.concatenate([across, res[...]], axis=1)
        value = jnp.dot(wide, across, preferred_element_type=F32)
        if beside is not None:
            side[q, :, 0:lanes] = value[32 : 32 + inner, KSIZE * lanes :] + res_bias
        total = 0.0
        for k in range(KSIZE):
            total = total + value[16 * k : 16 * k + inner, lanes * k : lanes * k + lanes]
        return total

    if crossing == DOWN:
        return finish(0, taps_across(0, [x[q] for q in range(2) for x in xs]), (zero, zero))
    if lanes == 128:
        return lax.fori_loop(0, halves, lambda q, state: finish(q, taps_across(q, [x[q] for x in xs]), state), (zero, zero))

    def half(q, state):
        wide = jnp.concatenate([conv_input(xs, q, k, inner) for k in range(KSIZE)], axis=1)
        return finish(q, jnp.dot(wide, weight[...], preferred_element_type=F32), state)

    return lax.fori_loop(0, halves, half, (zero, zero))


def norm_fit(sums, gain, shift, count, packed, stats, layer):
    lanes = gain.shape[1]
    one = down_one_row(sums[0])
    two = down_one_row(sums[1])
    group_one, group_two = group_sums(one, two, packed)
    mean = group_one / count
    inverse = lax.rsqrt(group_two / count - mean * mean + EPSILON)
    scale = inverse * gain
    offset = shift - mean * scale
    for number, row in enumerate((scale, offset, mean, inverse, one)):
        stats[8 * layer + number : 8 * layer + number + 1, 0:lanes] = row
    return scale, offset


def norm_kept(stats, layer, lanes):
    return [stats[8 * layer + n : 8 * layer + n + 1, 0:lanes] for n in range(5)]


def norm_back_fit(sums, kept, gain, count, rows, packed):
    scale, _, mean, inverse, one = kept
    grad_shift = down_one_row(sums[0])
    grad_gain = inverse * (down_one_row(sums[1]) - mean * grad_shift)
    first, second = group_sums(gain * grad_shift, gain * grad_gain, packed)
    first = first / count
    second = second / count
    slope = -inverse * inverse * second
    level = -inverse * first - slope * mean
    grad_bias = scale * grad_shift + slope * one + level * rows
    if packed:
        grad_shift, grad_gain, grad_bias = [both_halves(v) for v in (grad_shift, grad_gain, grad_bias)]
    return slope, level, grad_bias, grad_gain, grad_shift


def in_steps(count, step, body):
    full = count // step

    def move(index, carry):
        body(pl.multiple_of(index * step, step), step)
        return carry

    if full > 1:
        lax.fori_loop(0, full, move, 0)
    elif full:
        body(0, step)
    if count % step:
        body(full * step, count % step)


def unpack_pairs(flat, start, count, out):
    def move(at, step):
        rows = flat[pl.ds(start + at, step), :]
        turned = pltpu.roll(rows, 64, 1)
        lane = lanes_of(rows.shape)
        out[pl.ds(2 * at, step, stride=2), :] = jnp.where(lane < 64, rows, turned)
        out[pl.ds(2 * at + 1, step, stride=2), :] = jnp.where(lane < 64, turned, rows)

    in_steps(count, 128, move)


def pack_pairs(source, out, start, count):
    def move(at, step):
        even = source[pl.ds(2 * at, step, stride=2), :]
        odd = pltpu.roll(source[pl.ds(2 * at + 1, step, stride=2), :], 64, 1)
        out[pl.ds(start + at, step), :] = jnp.where(lanes_of(even.shape) < 64, even, odd)

    in_steps(count, 128, move)


def spread_pairs(pairs, start, count, weight, to, size):
    rows = min(-(-count // 32) * 32, size)
    value = pairs[start : start + rows, :]
    keep = rows_of(value.shape) < count
    lane = lanes_of(value.shape)
    weight[to : to + rows, :] = jnp.where(keep & (lane < 64), value, 0.0).astype(BF)
    weight[to + size : to + size + rows, :] = jnp.where(keep & (lane >= 64), value, 0.0).astype(BF)


def straight_rows(flat, start, count, out, to):
    def move(at, step):
        out[pl.ds(to + at, step), :] = flat[pl.ds(start + at, step), :].astype(out.dtype)

    in_steps(count, 256, move)


def wide_rows(flat, start, count, out, to):
    def move(at, step):
        for half in range(2):
            out[pl.ds(to + at, step), 128 * half : 128 * half + 128] = flat[
                pl.ds(start + 2 * at + half, step, stride=2), :
            ].astype(out.dtype)

    in_steps(count, 128, move)


def prepare_block(block, c):
    flat = c.flat
    start = ROW_STARTS[block]
    width_in, width_out = WIDTHS[block]
    one, two = c.one(block), c.two(block)
    res = c.res(block)
    proj, at = c.proj, TE * block
    pairs = c.pairs
    if width_out == 64:
        chunks = 592 if block == 0 else 1984
        unpack_pairs(flat, start, chunks // 2, pairs)
        size = 64 if block == 0 else 256
        if block == 0:
            one[...] = jnp.zeros_like(one)
            res[...] = jnp.zeros_like(res)
        for k in range(KSIZE):
            spread_pairs(pairs, width_in * k, width_in, one, 2 * size * k, size)
            spread_pairs(pairs, KSIZE * width_in + 64 * k, 64, two, 128 * k, 64)
        cursor = KSIZE * (width_in + 64)
        proj[at : at + TE, 0:128] = pairs[cursor : cursor + TE, :]
        spread_pairs(pairs, cursor + TE, width_in, res, 0, size)
    elif width_out == 128:
        if block == 1:
            one[...] = jnp.zeros_like(one)
            res[...] = jnp.zeros_like(res)
            for k in range(KSIZE + 1):
                source = start + 64 * k if k < KSIZE else start + 320 + 640 + TE
                value = flat[source : source + 64, :].astype(BF)
                into, base = (one, 128 * k) if k < KSIZE else (res, 0)
                into[base : base + 64, 0:128] = value
                into[base + 64 : base + 128, 128:256] = value
        else:
            straight_rows(flat, start, KSIZE * width_in, one, 0)
            straight_rows(flat, start + KSIZE * width_in + 640 + TE, width_in, res, 0)
        straight_rows(flat, start + KSIZE * width_in, 640, two, 0)
        cursor = start + KSIZE * width_in + 640
        proj[at : at + TE, 0:128] = flat[cursor : cursor + TE, :]
    else:
        wide_rows(flat, start, KSIZE * width_in, one, 0)
        wide_rows(flat, start + 2 * KSIZE * width_in, 1280, two, 0)
        cursor = start + 2 * (KSIZE * width_in + 1280)
        wide_rows(flat, cursor, TE, proj, at)
        if res is not None:
            wide_rows(flat, cursor + 2 * TE, width_in, res, 0)


def column(row):
    return jnp.transpose(jnp.broadcast_to(row, (128, 128)))


def row_times(row, matrix):
    total = 0.0
    for at in range(0, row.shape[1], 128):
        wide = column(row[:, at : at + 128])
        if matrix.shape[1] == 256:
            wide = jnp.concatenate([wide, wide], axis=1)
        total = total + fold_rows(matrix[at : at + 128, :] * wide)
    return down_one_row(total)


def lane_sums(value):
    if value.shape[1] == 256:
        value = value[:, 0:128] + value[:, 128:256]
    parts = []
    for at in range(0, value.shape[0], 128):
        total = jnp.sum(value[at : at + 128, :], axis=1, keepdims=True)
        parts.append(jnp.transpose(jnp.broadcast_to(total, (128, 128)))[0:1, :])
    return parts[0] if len(parts) == 1 else jnp.concatenate(parts, axis=1)


def outer(left, right):
    wide = []
    for at in range(0, left.shape[1], 128):
        part = column(left[:, at : at + 128])
        if right.shape[1] == 256:
            part = jnp.concatenate([part, part], axis=1)
        wide.append(part * right)
    return wide[0] if len(wide) == 1 else jnp.concatenate(wide, axis=0)


CROSSING = (None, UP, None, None, None, DOWN)


def counts_of(frames, block):
    width = WIDTHS[block][1] if block < 6 else C1
    return frames * (width // GROUPS)


def forward_kernel(c, far, into, sems):
    aff, stats, terms = c.aff, c.stats, c.terms
    inner = c.pre_a0.shape[1]
    frames = 2 * inner
    saves = []

    def save(source, target):
        copy = pltpu.make_async_copy(source, target, sems.at[16 + len(saves)])
        copy.start()
        saves.append(copy)

    loads = []
    for number, (low, high) in enumerate(zip(LOAD_ROWS[:-1], LOAD_ROWS[1:])):
        part = pl.ds(low, high - low)
        copy = pltpu.make_async_copy(far.flat.at[part, :], c.flat.at[part, :], sems.at[number])
        loads.append(copy)
    order = (6, 0, 1, 2, 3, 4, 5)
    for number in order:
        loads[number].start()
    loads[6].wait()
    flat, pairs, embed = c.flat, c.pairs, c.embed_two
    unpack_pairs(flat, EMB_ROW, FLAT_ROWS - EMB_ROW, pairs)
    quarter = [pairs[pl.ds(1 + n, TE, stride=4), :] for n in range(4)]
    lane = lanes_of((TE, 128))
    embed_one = jnp.concatenate(
        [jnp.where(lane < 64, quarter[0], quarter[1]), jnp.where(lane < 64, quarter[2], quarter[3])], axis=1
    )
    embed[...] = jnp.where(
        lanes_of((TH, 128)) < 64, pairs[pl.ds(513, TH, stride=2), :], pairs[pl.ds(514, TH, stride=2), :]
    )
    sinus = c.sinus[...]
    bias = vector(aff, 56, 256)
    kept = c.kept
    hidden_pre = row_times(sinus[0:1, :], embed_one) + bias
    hidden = mish_fast(hidden_pre)
    feature_pre = row_times(hidden, embed[...]) + vector(aff, 58, 128)
    feature = mish_fast(feature_pre)
    for number, value in enumerate((hidden_pre, hidden, feature_pre, feature)):
        lanes = value.shape[1]
        kept[8 * number : 8 * number + 8, 0:lanes] = jnp.broadcast_to(value, (8, lanes))
    save(c.embed_two, into.embed_two)
    x0 = c.x0

    def put_noisy(group, value):
        x0[0, pl.ds(pl.multiple_of(HALO + 16 * group, 16), 16), :] = value.astype(BF)

    take_apart(c.noisy, inner // 64, put_noisy)
    fill_halo(x0)
    save(c.x0, into.x0)

    for block in range(6):
        loads[block].wait()
        prepare_block(block, c)
        for get in (Refs.one, Refs.two, Refs.res):
            if get(c, block) is not None:
                save(get(c, block), get(into, block))
        halves, lanes = LAYER_OUT[block]
        packed = halves == 1
        count = counts_of(frames, block)
        width = WIDTHS[block][1]
        lane_bias = block_vector(aff, block, 3)
        term = row_times(feature, c.proj[TE * block : TE * block + TE, 0:lanes]) + lane_bias
        terms[8 * block : 8 * block + 1, 0:lanes] = term
        xs = [c.x(number) for number in INPUTS[block]]
        pre_a, pre_b = c.pre_a(block), c.pre_b(block)
        side = c.side
        res = c.res(block)
        joined = res is not None and lanes == 128 and CROSSING[block] != UP
        beside = (side, res, block_vector(aff, block, 7)) if joined else None
        sums = conv_to(xs, c.one(block), block_vector(aff, block, 0), pre_a, CROSSING[block], beside)
        save(pre_a, into.pre_a(block))
        scale, offset = norm_fit(
            sums, block_vector(aff, block, 1), block_vector(aff, block, 2), count, packed, stats, 2 * block
        )
        hid = c.hid.at[0:halves, :, 0:lanes]

        def to_hidden(q, start, rows, carry):
            value = mish_fast(pre_a[q, pl.ds(start, rows), :] * scale + offset) + term
            hid[q, pl.ds(HALO + start, rows), :] = value.astype(BF)
            return carry

        sweep(halves, inner, to_hidden, 0)
        fill_halo(hid)
        sums = conv_to([hid], c.two(block), block_vector(aff, block, 4), pre_b, None)
        save(pre_b, into.pre_b(block))
        scale_b, offset_b = norm_fit(
            sums, block_vector(aff, block, 5), block_vector(aff, block, 6), count, packed, stats, 2 * block + 1
        )
        if res is not None and not joined:
            res_bias = block_vector(aff, block, 7)
            if CROSSING[block] == UP:
                total = jnp.dot(conv_input(xs, 0, 2, inner), res[...], preferred_element_type=F32)
                side[0, :, 0:lanes] = total[:, :lanes] + res_bias
                side[1, :, 0:lanes] = total[:, lanes:] + res_bias
            else:
                for q in range(halves):
                    side[q, :, 0:lanes] = (
                        jnp.dot(conv_input(xs, q, 2, inner), res[...], preferred_element_type=F32) + res_bias
                    )
        out = c.x(block + 1)

        def to_output(q, start, rows, carry):
            value = mish_fast(pre_b[q, pl.ds(start, rows), :] * scale_b + offset_b)
            value = value + side[q, pl.ds(start, rows), 0:lanes]
            if block == 2:
                side[q, pl.ds(start, rows), 0:lanes] = value
            out[q, pl.ds(HALO + start, rows), :] = value.astype(BF)
            return carry

        sweep(halves, inner, to_output, 0)
        fill_halo(out)
        save(out, into.x(block + 1))
    unpack_pairs(flat, HEAD_ROW, 160, pairs)
    for k in range(KSIZE):
        spread_pairs(pairs, 64 * k, 64, c.one6, 128 * k, 64)
    save(c.one6, into.one6)
    sums = conv_to([c.x6], c.one6, head_vector(aff, 0), c.pre_a6, None)
    save(c.pre_a6, into.pre_a6)
    norm_fit(sums, head_vector(aff, 1), head_vector(aff, 2), counts_of(frames, 6), True, stats, 12)
    for source, target in ((stats, into.stats), (terms, into.terms), (kept, into.kept), (c.proj, into.proj)):
        save(source, target)
    for copy in saves:
        copy.wait()


def put_rows(value, out, start):
    rows, lanes = value.shape
    if lanes == 128:
        out[start : start + rows, :] = value
    else:
        out[pl.ds(start, rows, stride=2), :] = value[:, 0:128]
        out[pl.ds(start + 1, rows, stride=2), :] = value[:, 128:256]


def conv_dx(dy, weight, size, inner, crossing, emit, beside=None):
    halves = dy.shape[0]
    narrow = size == 128

    def rows_at(q, k):
        return dy[q] if narrow else conv_input([dy], q, k, inner)

    def taps(pick, q=0):
        if narrow:
            value = lax.dot_general(pick(0), weight[...], NT, preferred_element_type=F32)
            total = 0.0
            for k in range(KSIZE):
                first = 16 * (KSIZE - 1 - k)
                total = total + value[first : first + inner, size * k : size * k + size]
            return total
        wide = jnp.concatenate([pick(KSIZE - 1 - k) for k in range(KSIZE)], axis=1)
        across = jnp.concatenate([weight[size * k : size * k + size, :] for k in range(KSIZE)], axis=1)
        if beside is not None:
            wide = jnp.concatenate([wide, beside[0][q, :, 0 : dy.shape[2]]], axis=1)
            across = jnp.concatenate([across, beside[1][...]], axis=1)
        return lax.dot_general(wide, across, NT, preferred_element_type=F32)

    if crossing == UP:
        emit(0, taps(lambda k: jnp.concatenate([rows_at(q, k) for q in range(2)], axis=1)))
    elif halves == 1:
        emit(0, taps(lambda k: rows_at(0, k)))
    else:

        def half(q, carry):
            emit(q, taps(lambda k: rows_at(q, k), q))
            return carry

        lax.fori_loop(0, halves, half, 0)


def conv_dw(xs, dy, inner, crossing, acc, extra=None):
    def dys(q):
        parts = [conv_input([dy], q, KSIZE - 1 - k, inner) for k in range(KSIZE)]
        if extra is not None:
            parts.append(extra[q, :, 0 : dy.shape[2]])
        return parts

    def product(left, right):
        return lax.dot_general(left, right, TN, preferred_element_type=F32)

    if crossing == UP:
        both = zip(dys(0), dys(1))
        value = product(conv_input(xs, 0, 2, inner), jnp.concatenate([p for pair in both for p in pair], axis=1))
        acc[0 : value.shape[0], 0 : value.shape[1]] = value
        return
    if crossing == DOWN:
        left = jnp.concatenate([conv_input(xs, q, 2, inner) for q in range(2)], axis=1)
        value = product(left, jnp.concatenate(dys(0), axis=1))
        acc[0 : value.shape[0], 0 : value.shape[1]] = value
        return
    for q in range(dy.shape[0]):
        value = product(conv_input(xs, q, 2, inner), jnp.concatenate(dys(q), axis=1))
        if q == 0:
            acc[0 : value.shape[0], 0 : value.shape[1]] = value
        else:
            acc[0 : value.shape[0], 0 : value.shape[1]] += value


def fold_pairs(acc, tap, size, rows):
    lanes = slice(128 * tap, 128 * tap + 128)
    return acc[0:rows, lanes] + pltpu.roll(acc[size : size + rows, lanes], 64, 1)


def put_vector(grads, row, width, value):
    base = int(row)
    if width == 256:
        grads[base : base + 1, :] = value[:, 0:128]
        grads[base + 1 : base + 2, :] = value[:, 128:256]
    elif width == 128:
        grads[base : base + 1, :] = value
    else:
        lane = lanes_of((1, 128))
        keep = lane < 64 if row == base else lane >= 64
        grads[base : base + 1, :] = jnp.where(keep, value, grads[base : base + 1, :])


def norm_backward(c, layer, pre, gain, count, packed, upstream, dy, also=None):
    halves, inner, lanes = pre.shape
    kept = norm_kept(c.stats, layer, lanes)
    dv = c.dv
    zero = jnp.zeros((8, lanes), F32)

    def first(q, start, rows, state):
        here = pl.ds(start, rows)
        value = pre[q, here, :]
        act, slope = mish_both(value * kept[0] + kept[1])
        up = upstream(q, here)
        if also is not None:
            also(q, here, act, up)
        grad = up * slope
        dv[q, here, 0:lanes] = grad
        return state[0] + fold_rows(grad), state[1] + fold_rows(grad * value), state[2] + fold_rows(up)

    sums = sweep(halves, inner, first, (zero, zero, zero))
    rows_each = float(inner * halves)
    slope, level, grad_bias, grad_gain, grad_shift = norm_back_fit(sums, kept, gain, count, rows_each, packed)
    scale = kept[0]

    def second(q, start, rows, carry):
        here = pl.ds(start, rows)
        value = scale * dv[q, here, 0:lanes] + (slope * pre[q, here, :] + level)
        dy[q, pl.ds(HALO + start, rows), :] = value.astype(BF)
        return carry

    sweep(halves, inner, second, 0)
    fill_halo(dy)
    total = down_one_row(sums[2])
    return grad_bias, grad_gain, grad_shift, both_halves(total) if packed else total


def backward_block(block, c, base, copies, need):
    aff, grads, table, acc = c.aff, c.agrad, c.table, c.acc
    halves, lanes = LAYER_OUT[block]
    packed = halves == 1
    width_in, width_out = WIDTHS[block]
    inner = c.pre_a(block).shape[1]
    count = counts_of(2 * inner, block)
    up = c.up(block)
    low = c.low
    dy = c.dy.at[0:halves, :, 0:lanes]
    act_low = c.act
    res = c.res(block)
    xs = [c.x(number) for number in INPUTS[block]]
    start = ROW_STARTS[block] - base
    spot = AFF_ROWS[block]
    unit = width_out / 128

    def keep_low(q, here, act, value):
        low[q, here, 0:lanes] = value.astype(BF)

    need(copies.pre_b(block), copies.up(block))
    got = norm_backward(
        c, 2 * block + 1, c.pre_b(block), block_vector(aff, block, 5), count, packed,
        lambda q, here: up[q, here, :], dy, keep_low if res is not None else None,
    )
    for number, value in zip((4, 5, 6, 7), got):
        if number < 7 or res is not None:
            put_vector(grads, spot + number * unit, width_out, value)
    dv = c.dv

    def emit_hidden(q, value):
        dv[q, :, 0:lanes] = value

    need(copies.two(block))
    conv_dx(dy, c.two(block), lanes, inner, None, emit_hidden)
    term = c.terms[8 * block : 8 * block + 1, 0:lanes]
    dy_two = dy
    dy_one = c.ey.at[0:halves, :, 0:lanes]

    def keep_act(q, here, act, value):
        act_low[q, here, 0:lanes] = (act + term).astype(BF)

    need(copies.pre_a(block))
    got = norm_backward(
        c, 2 * block, c.pre_a(block), block_vector(aff, block, 1), count, packed,
        lambda q, here: dv[q, here, 0:lanes], dy_one, keep_act,
    )
    for number, value in zip((0, 1, 2, 3), got):
        put_vector(grads, spot + number * unit, width_out, value)
    time_row = got[3]
    c.tgrad[8 * block : 8 * block + 1, 0:lanes] = time_row

    def plain_dw(left, right_ref):
        for q in range(halves):
            parts = jnp.concatenate([conv_input([right_ref], q, KSIZE - 1 - k, inner) for k in range(KSIZE)], axis=1)
            value = lax.dot_general(left[q, :, 0:lanes], parts, TN, preferred_element_type=F32)
            if q == 0:
                acc[0:lanes, 0 : KSIZE * lanes] = value
            else:
                acc[0:lanes, 0 : KSIZE * lanes] += value

    plain_dw(act_low, dy_two)
    pairs = c.pairs
    proj_grad = outer(c.kept[24:25, 0:128], time_row)
    if width_out == 64:
        at = KSIZE * width_in
        for k in range(KSIZE):
            pairs[at + 64 * k : at + 64 * k + 64, :] = fold_pairs(acc, k, 64, 64)
        pairs[at + 320 : at + 320 + TE, :] = proj_grad
    else:
        at = start + KSIZE * width_in * (width_out // 128)
        for k in range(KSIZE):
            put_rows(acc[0:lanes, lanes * k : lanes * k + lanes], table, at + k * lanes * (width_out // 128))
        put_rows(proj_grad, table, at + 5 * lanes * (width_out // 128))
    crossing = CROSSING[block]
    need(copies.one(block), copies.res(block), *[copies.x(number) for number in INPUTS[block]])
    if block == 2:
        need(copies.up(1))
    if block > 0:
        size = {None: sum(x.shape[2] for x in xs), UP: 128, DOWN: 512}[crossing]
        joined = res is not None and size != 128

        def emit(q, value):
            if res is not None and not joined:
                if crossing == UP:
                    side = jnp.concatenate([low[0, :, 0:lanes], low[1, :, 0:lanes]], axis=1)
                else:
                    side = low[q, :, 0:lanes]
                value = value + lax.dot_general(side, res[...], NT, preferred_element_type=F32)
            if block == 5:
                for h in range(2):
                    c.up4[h] = value[:, 256 * h : 256 * h + 128]
                    c.up1[h] = value[:, 256 * h + 128 : 256 * h + 256]
            elif block == 4:
                c.up3[q] = value[:, 0:256]
                c.up2[q] = value[:, 256:512]
            elif block == 3:
                c.up2[q] = c.up2[q] + (value + up[q])
            elif block == 2:
                c.up1[q] = c.up1[q] + value
            else:
                c.up0[0] = value

        conv_dx(dy_one, c.one(block), size, inner, crossing, emit, (low, res) if joined else None)
    conv_dw(xs, dy_one, inner, crossing, acc, low if res is not None else None)
    if width_out == 64:
        size = 64 if block == 0 else 256
        rows = 24 if block == 0 else 256
        for k in range(KSIZE):
            value = fold_pairs(acc, k, size, rows)
            pairs[width_in * k : width_in * k + width_in, :] = value[0:width_in]
        at = KSIZE * (width_in + 64) + TE
        pairs[at : at + width_in, :] = fold_pairs(acc, KSIZE, size, rows)[0:width_in]
        if block == 0:
            after = table[288:296, :]
            pack_pairs(pairs, table, start, 296)
            table[288:296, :] = jnp.where(rows_of((8, 128)) < 5, table[288:296, :], after)
        else:
            pack_pairs(pairs, table, start, 992)
    else:
        unit_rows = width_out // 128
        for k in range(KSIZE + (0 if res is None else 1)):
            at = start + k * width_in * unit_rows
            if k == KSIZE:
                at = start + (KSIZE * (width_in + width_out) + TE) * unit_rows
            if crossing == UP:
                value = acc[0:64, 256 * k : 256 * k + 128] + acc[64:128, 256 * k + 128 : 256 * k + 256]
            else:
                value = acc[0:width_in, width_out * k : width_out * k + width_out]
            put_rows(value, table, at)


def load_all(c, far, sems):
    copies = {}
    for number, (name, source) in enumerate(vars(far).items()):
        if name in vars(c):
            copies[name] = pltpu.make_async_copy(source, vars(c)[name], sems.at[number])
            copies[name].start()
    done = set()

    def need(*wanted):
        for copy in wanted:
            if copy is not None and id(copy) not in done:
                done.add(id(copy))
                copy.wait()

    return Refs(copies.keys(), copies.values()), need


def late_kernel(c, far, into, sems):
    copies, need = load_all(c, far, sems)
    aff, grads = c.aff, c.agrad
    outs = []

    def give(source, target):
        copy = pltpu.make_async_copy(source, target, sems.at[len(vars(far)) + len(outs)])
        copy.start()
        outs.append(copy)

    grads[...] = jnp.zeros_like(grads)
    need(copies.noise_in)
    noise_in, noise = c.noise_in, c.noise
    last = noise_in.shape[1] - 8

    def put_noise(group, value):
        noise[pl.ds(pl.multiple_of(16 * group, 16), 16), :] = value

    take_apart(noise_in, c.pre_a6.shape[1] // 64, put_noise)
    tail = noise_in[0, last:, :] + noise_in[1, last:, :] + noise_in[2, last:, :] + noise_in[3, last:, :]
    length = tail[0:1, :]
    scale_out = 1.0 / (tail[1:2, :] * TD)
    need(copies.stats, copies.terms, copies.kept, copies.pre_a6)
    pre = c.pre_a6
    inner = pre.shape[1]
    kept = norm_kept(c.stats, 12, 128)
    act, low, up = c.act, c.low, c.up5
    lane = lanes_of((1, 128))
    spot = lane % 64
    out_row = aff[55:56, :]
    out_bias = jnp.where(spot < TD, jnp.where(lane < 64, pltpu.roll(out_row, 64, 1), out_row), 0.0)
    segment = inner // 16

    def to_feature(q, start, rows, carry):
        here = pl.ds(start, rows)
        act[0, here, 0:128] = mish_fast(pre[0, here, :] * kept[0] + kept[1]).astype(BF)
        return carry

    sweep(1, inner, to_feature, 0)
    dv = c.dv
    dv[0, :, 0:128] = jnp.dot(act[0, :, 0:128], c.wout[...], preferred_element_type=F32)

    def to_loss(q, start, rows, state):
        here = pl.ds(start, rows)
        shape = (rows, 128)
        place = rows_of(shape) + start
        lanes = lanes_of(shape)
        frame = (place % 16 + jnp.where(lanes >= 64, 16, 0)) * segment + place // 16
        weight = jnp.where((frame.astype(F32) < length) & (lanes % 64 < TD), 1.0, 0.0)
        difference = weight * (dv[0, here, 0:128] + out_bias - noise[here, :])
        grad = 2.0 * difference * scale_out
        low[0, here, 0:128] = grad.astype(BF)
        return state[0] + fold_rows(difference * difference), state[1] + fold_rows(grad)

    zero = jnp.zeros((8, 128), F32)
    loss, out_sum = sweep(1, inner, to_loss, (zero, zero))
    c.loss[...] = loss * scale_out
    out_sum = both_halves(down_one_row(out_sum))
    c.gout[...] = lax.dot_general(act[0, :, 0:128], low[0, :, 0:128], TN, preferred_element_type=F32)
    dv[0, :, 0:128] = lax.dot_general(low[0, :, 0:128], c.wout[...], NT, preferred_element_type=F32)
    dy = c.dy.at[0:1, :, 0:128]
    got = norm_backward(
        c, 12, pre, head_vector(aff, 1), counts_of(2 * inner, 6), True, lambda q, here: dv[q, here, 0:128], dy
    )
    grads[54:55, :] = jnp.where(lane < 64, got[0], got[1])
    grads[55:56, :] = jnp.where(lane < 64, got[2], jnp.where(spot < TD, out_sum, 0.0))

    def emit_head(q, value):
        up[0] = value

    need(copies.one6, copies.x6)
    conv_dx(dy, c.one6, 128, inner, None, emit_head)
    conv_dw([c.x6], dy, inner, None, c.acc)
    for k in range(KSIZE):
        c.pairs[64 * k : 64 * k + 64, :] = fold_pairs(c.acc, k, 64, 64)
    pack_pairs(c.pairs, c.table, HEAD_ROW - LATE_START, 160)
    c.tgrad[...] = jnp.zeros_like(c.tgrad)
    backward_block(5, c, LATE_START, copies, need)
    give(c.up1, into.up1)
    backward_block(4, c, LATE_START, copies, need)
    split = -(-(ROW_STARTS[4] - LATE_START) // 8) * 8
    give(c.table.at[split:LATE_ROWS], into.table.at[split:LATE_ROWS])
    backward_block(3, c, LATE_START, copies, need)
    give(c.table.at[0:split], into.table.at[0:split])
    for source, target in ((c.up2, into.up2), (c.tgrad, into.tgrad), (grads, into.agrad)):
        give(source, target)
    need(*vars(copies).values())
    for copy in outs:
        copy.wait()


def early_kernel(c, far, into, sems):
    copies, need = load_all(c, far, sems)
    aff, grads, table = c.aff, c.agrad, c.table
    outs = []
    after = len(vars(far))

    def own_copy(source, target):
        copy = pltpu.make_async_copy(source, target, sems.at[after + len(outs)])
        copy.start()
        outs.append(copy)

    own_copy(far.late.at[0:8], c.edge)
    own_copy(far.late.at[8:LATE_ROWS], table.at[LATE_START + 8 : LATE_START + LATE_ROWS])
    late_edge, late_rest = outs
    need(copies.stats, copies.terms, copies.kept, copies.agrad, copies.tgrad)
    backward_block(2, c, 0, copies, need)
    late_edge.wait()
    lead = rows_of((8, 128)) < ROW_STARTS[3] - LATE_START
    table[LATE_START : LATE_START + 8, :] = jnp.where(lead, table[LATE_START : LATE_START + 8, :], c.edge[...])
    backward_block(1, c, 0, copies, need)
    backward_block(0, c, 0, copies, need)
    need(*vars(copies).values())
    late_rest.wait()
    total = jnp.zeros((TE, 128), F32)
    for block in range(6):
        lanes = LAYER_OUT[block][1]
        first = c.tgrad[8 * block : 8 * block + 1, 0:lanes]
        if WIDTHS[block][1] == 64:
            first = jnp.where(lanes_of((1, lanes)) < 64, first, 0.0)
        value = c.proj[TE * block : TE * block + TE, 0:lanes] * first
        total = total + (value if lanes == 128 else value[:, 0:128] + value[:, 128:256])
    kept = c.kept
    hidden_pre, hidden = kept[0:1, :], kept[8:9, :]
    feature_pre = kept[16:17, 0:128]
    grad_feature = lane_sums(total) * mish_both(feature_pre)[1]
    pairs = c.pairs
    second = outer(hidden, grad_feature)
    put_vector(grads, 58, 128, grad_feature)
    grad_hidden = lane_sums(c.embed_two[...] * grad_feature) * mish_both(hidden_pre)[1]
    first = outer(c.sinus[0:1, :], grad_hidden)
    put_vector(grads, 56, 256, grad_hidden)
    grads[60:61, :] = down_one_row(c.loss[...])
    table[OUT_ROW : OUT_ROW + 12, :] = c.hograd[0:12, :]
    table[FLAT_ROWS:TABLE_ROWS, :] = jnp.zeros((TABLE_ROWS - FLAT_ROWS, 128), F32)
    pairs[1024:1040, :] = jnp.zeros((16, 128), F32)
    pairs[0:1, :] = c.hograd[11:12, :]
    for half in range(2):
        value = first[:, 128 * half : 128 * half + 128]
        pairs[pl.ds(1 + 2 * half, TE, stride=4), :] = value
        pairs[pl.ds(2 + 2 * half, TE, stride=4), :] = pltpu.roll(value, 64, 1)
    pairs[pl.ds(513, TH, stride=2), :] = second
    pairs[pl.ds(514, TH, stride=2), :] = pltpu.roll(second, 64, 1)
    pack_pairs(pairs, table, EMB_ROW, FLAT_ROWS - EMB_ROW)
    core = c.core[0]
    keep, send = c.keep, c.send
    share = NKER_ROWS
    step = 176

    for pair in range(4):

        def split(index, carry):
            at = pl.multiple_of(index * step, step)
            even = table[pl.ds(share * (2 * pair) + at, step), :]
            odd = table[pl.ds(share * (2 * pair + 1) + at, step), :]
            keep[pair, pl.ds(at, step), :] = jnp.where(core == 0, even, odd)
            send[pl.ds(OWN_ROWS * pair + at, step), :] = jnp.where(core == 0, odd, even).astype(BF)
            return carry

        lax.fori_loop(0, OWN_ROWS // step, split, 0)
        own_copy(keep.at[pair], into.keep.at[pair])
        span = pl.ds(OWN_ROWS * pair, OWN_ROWS)
        own_copy(send.at[span, :], into.send.at[span, :])
    value = grads[...]
    high = value.astype(BF)
    rest = (value - high.astype(F32)).astype(BF)
    send[4 * OWN_ROWS : 4 * OWN_ROWS + 64, :] = high
    send[4 * OWN_ROWS + 64 : 4 * OWN_ROWS + 128, :] = rest
    grads[...] = high.astype(F32) + rest.astype(F32)
    span = pl.ds(4 * OWN_ROWS, 128)
    own_copy(send.at[span, :], into.send.at[span, :])
    own_copy(grads, into.agrad)
    for copy in outs[2:]:
        copy.wait()


def shape_tables(inner):
    padded = inner + 2 * HALO
    first = dict(
        stats=((104, 256), F32),
        terms=((48, 256), F32),
        kept=((32, 256), F32),
        proj=((6 * TE, 256), F32),
        embed_two=((256, 128), F32),
    )
    other = dict(
        tgrad=((48, 256), F32),
        agrad=((64, 128), F32),
        flat=((FLAT_ROWS, 128), F32),
        pairs=((2048, 128), F32),
        table=((TABLE_ROWS, 128), F32),
        edge=((8, 128), F32),
        send=((4 * OWN_ROWS + 128, 128), BF),
        keep=((4, OWN_ROWS, 128), F32),
        acc=((512, 1536), F32),
        side=((2, inner, 256), F32),
        dv=((2, inner, 256), F32),
        low=((2, inner, 256), BF),
        act=((2, inner, 256), BF),
        noise=((inner, 128), F32),
        noise_in=((4, inner // 8 + 8, 128), F32),
        hid=((2, padded, 256), BF),
        dy=((2, padded, 256), BF),
        ey=((2, padded, 256), BF),
    )
    for number, (halves, lanes) in enumerate(((1, 128),) + LAYER_OUT[:6]):
        first[f"x{number}"] = ((halves, padded, lanes), BF)
    for block in range(7):
        halves, lanes = LAYER_OUT[block]
        first[f"pre_a{block}"] = ((halves, inner, lanes), F32)
        first[f"one{block}"] = (W_ONE[block], BF)
        if block < 6:
            other[f"up{block}"] = ((halves, inner, lanes), F32)
            first[f"pre_b{block}"] = ((halves, inner, lanes), F32)
            first[f"two{block}"] = (W_TWO[block], BF)
            if W_RES[block] is not None:
                first[f"res{block}"] = (W_RES[block], BF)
    return first, other


def run_kernel(body, vmem_in, smem_in, any_in, outs_vmem, outs_any, scratch, sems, cost):
    operands = list(vmem_in.values()) + list(smem_in.values()) + list(any_in.values())
    in_specs = (
        [pl.BlockSpec(memory_space=pltpu.VMEM)] * len(vmem_in)
        + [pl.BlockSpec(memory_space=pltpu.SMEM)] * len(smem_in)
        + [pl.BlockSpec(memory_space=pl.ANY)] * len(any_in)
    )
    out_specs = [pl.BlockSpec(memory_space=pltpu.VMEM)] * len(outs_vmem)
    out_specs += [pl.BlockSpec(memory_space=pl.ANY)] * len(outs_any)
    out_kinds = list(outs_vmem.values()) + list(outs_any.values())
    near = list(vmem_in) + list(smem_in)
    places = (len(near), len(operands), len(operands) + len(outs_vmem), len(operands) + len(out_kinds))

    def call(*refs):
        here, there, results, left, buffers = [
            refs[low:high] for low, high in zip((0,) + places, places + (len(refs) - 1,))
        ]
        c = Refs(near + list(outs_vmem) + list(scratch), here + results + buffers)
        body(c, Refs(any_in, there), Refs(outs_any, left), refs[-1])

    results = pl.pallas_call(
        call,
        out_shape=[jax.ShapeDtypeStruct(*kind) for kind in out_kinds],
        in_specs=in_specs,
        out_specs=out_specs,
        scratch_shapes=[pltpu.VMEM(*kind) for kind in scratch.values()] + [pltpu.SemaphoreType.DMA((sems,))],
        compiler_params=pltpu.CompilerParams(vmem_limit_bytes=VMEM_LIMIT),
        cost_estimate=pl.CostEstimate(flops=cost, bytes_accessed=40000000, transcendentals=0),
    )(*operands)
    return SimpleNamespace(**dict(zip(list(outs_vmem) + list(outs_any), results)))


VMEM_LIMIT = 67043328


def exchange_pieces(traj, noise, mask, signal, mean, std):
    pieces, frames, wide = traj.shape
    scale = jnp.concatenate([jnp.sqrt(signal), jnp.sqrt(1.0 - signal)])
    vmem = pl.BlockSpec(memory_space=pltpu.VMEM)
    return pl.pallas_call(
        exchange_kernel,
        out_shape=[
            jax.ShapeDtypeStruct((pieces, frames // 4, 128), BF),
            jax.ShapeDtypeStruct((pieces, frames // 4 + 8, 128), F32),
            jax.ShapeDtypeStruct((8, 128), F32),
        ],
        in_specs=[vmem] * 6,
        out_specs=[vmem] * 3,
        scratch_shapes=[pltpu.VMEM((frames, 128), F32)] * 2,
    )(traj, noise, mask, jnp.broadcast_to(scale[:, None], (2 * pieces, 128)), mean[None, :], std[None, :])


def whole_horizon(noisy, noise, sinus, core, kernels, affine):
    inner = 4 * noisy.shape[1] * 2
    first, other = shape_tables(inner)
    t = SimpleNamespace(**first, **other)
    flat = jnp.pad(kernels, (0, FLAT_ROWS * 128 - kernels.shape[0])).reshape(FLAT_ROWS, 128)
    aff = jnp.concatenate(
        [affine[:7127], jnp.zeros((41,), F32), affine[7127:], jnp.zeros((640,), F32)]
    ).reshape(64, 128)
    head_out = kernels[OUT_START : OUT_START + C1 * TD].reshape(C1, TD).astype(BF)
    wide_out = jnp.pad(head_out, ((0, 0), (0, 64 - TD)))
    nothing = jnp.zeros((C1, 64), BF)
    wout = jnp.concatenate(
        [jnp.concatenate([wide_out, nothing], axis=1), jnp.concatenate([nothing, wide_out], axis=1)], axis=0
    )
    f = run_kernel(
        forward_kernel,
        dict(noisy=noisy, aff=aff, sinus=sinus),
        {},
        dict(flat=flat),
        {},
        first,
        dict(first, flat=t.flat, pairs=t.pairs, side=t.side, hid=t.hid),
        16 + len(first),
        14000000000,
    )
    late_in = dict(noise_in=noise, stats=f.stats, terms=f.terms, kept=f.kept, pre_a6=f.pre_a6, one6=f.one6, x6=f.x6)
    late_in.update(pre_b5=f.pre_b5, two5=f.two5, pre_a5=f.pre_a5, one5=f.one5, res5=f.res5, x5=f.x5, x2=f.x2)
    late_in.update(pre_b4=f.pre_b4, two4=f.two4, pre_a4=f.pre_a4, one4=f.one4, res4=f.res4, x4=f.x4, x3=f.x3)
    late_in.update(pre_b3=f.pre_b3, two3=f.two3, pre_a3=f.pre_a3, one3=f.one3)
    late_out = dict(table=((LATE_ROWS, 128), F32), up1=t.up1, up2=t.up2, tgrad=t.tgrad, agrad=t.agrad)
    work = dict(dv=t.dv, low=t.low, act=t.act, acc=t.acc, pairs=t.pairs, dy=t.dy, ey=t.ey)
    late = run_kernel(
        late_kernel,
        dict(aff=aff, wout=wout),
        {},
        late_in,
        dict(loss=((8, 128), F32), gout=((128, 128), F32)),
        late_out,
        dict({n: vars(t)[n] for n in late_in}, **late_out, noise=t.noise, up5=t.up5, up4=t.up4, up3=t.up3, **work),
        len(late_in) + len(late_out) + 1,
        16000000000,
    )
    gout = late.gout
    head_grad = (gout[0:64, 0:TD] + gout[64:128, 64 : 64 + TD]).reshape(-1)
    early_in = dict(stats=f.stats, terms=f.terms, kept=f.kept, agrad=late.agrad, tgrad=late.tgrad)
    early_in.update(up2=late.up2, pre_b2=f.pre_b2, two2=f.two2, pre_a2=f.pre_a2, one2=f.one2, res2=f.res2, x2=f.x2)
    early_in.update(up1=late.up1, pre_b1=f.pre_b1, two1=f.two1, pre_a1=f.pre_a1, one1=f.one1, res1=f.res1, x1=f.x1)
    early_in.update(pre_b0=f.pre_b0, two0=f.two0, pre_a0=f.pre_a0, one0=f.one0, res0=f.res0, x0=f.x0)
    early_in.update(proj=f.proj, embed_two=f.embed_two)
    early = run_kernel(
        early_kernel,
        dict(
            aff=aff,
            sinus=jnp.where(jnp.arange(8)[:, None] == 0, sinus, 0.0),
            loss=late.loss,
            hograd=jnp.pad(head_grad, (0, 2048 - C1 * TD)).reshape(16, 128),
        ),
        dict(core=core.reshape(1)),
        dict(early_in, late=late.table),
        {},
        dict(send=t.send, keep=t.keep, agrad=t.agrad),
        dict(
            {n: vars(t)[n] for n in early_in}, table=t.table, send=t.send, keep=t.keep, up0=t.up0, edge=t.edge, **work
        ),
        len(early_in) + 16,
        10000000000,
    )
    return early.send, early.keep, early.agrad


def on_device_xla(
    trajectories,
    dim_means,
    dim_stds,
    noise_draw,
    diffusion_steps,
    valid_mask,
    kernels,
    affine,
    kernel_momentum,
    kernel_average,
    affine_momentum,
    affine_average,
):
    members_all = unpack(kernels, affine)
    valid_total = lax.psum(jnp.sum(valid_mask.astype(jnp.float32)), (DP, HOR))
    signal_now = signal_level(diffusion_steps)[:, None, None]
    clean_frames = (trajectories - dim_means) / dim_stds
    noisy_frames = jnp.sqrt(signal_now) * clean_frames + jnp.sqrt(1.0 - signal_now) * noise_draw

    ring = lax.axis_size(HOR)
    axis = HOR
    if trajectories.shape[0] % ring == 0:
        axis = None
        local = trajectories.shape[0] // ring
        part = lax.axis_index(HOR) * local
        low_frames = noisy_frames.astype(jnp.bfloat16)
        noisy_frames = lax.all_to_all(low_frames, HOR, 0, 1, tiled=True).astype(jnp.float32)
        noise_draw = lax.all_to_all(noise_draw, HOR, 0, 1, tiled=True)
        valid_mask = lax.all_to_all(valid_mask, HOR, 0, 1, tiled=True)
        diffusion_steps = lax.dynamic_slice_in_dim(diffusion_steps, part, local)

    def time_closed(kernel_flat, affine_flat):
        return time_parts(kernel_flat, affine_flat, diffusion_steps)

    time_list, time_pullback = jax.vjp(time_closed, kernels, affine)
    down_one, kept_one = block_forward(noisy_frames, members_all[0], time_list[0], axis)
    down_two, kept_two = block_forward(down_one, members_all[1], time_list[1], axis)
    down_three, kept_three = block_forward(down_two, members_all[2], time_list[2], axis)
    middle, kept_middle = block_forward(down_three, members_all[3], time_list[3], axis)
    up_one, kept_upper = block_forward(
        jnp.concatenate([middle, down_three], axis=2), members_all[4], time_list[4], axis)
    up_two, kept_lower = block_forward(
        jnp.concatenate([up_one, down_two], axis=2), members_all[5], time_list[5], axis)
    predicted, kept_head = head_forward(up_two, members_all[6], axis)
    weight_rows = valid_mask.astype(jnp.float32)[:, :, None]
    difference = predicted - noise_draw
    loss_scale = 1.0 / (valid_total * TD)
    loss_part = jnp.sum(weight_rows * difference * difference) * loss_scale
    grad_predicted = 2.0 * weight_rows * difference * loss_scale
    grad_up_two, head_grads = head_backward(grad_predicted, kept_head, members_all[6], axis)
    grad_joined, time_six, grads_six = block_backward(grad_up_two, kept_lower, members_all[5], axis)
    grad_up_one = grad_joined[:, :, :C2]
    grad_down_two = grad_joined[:, :, C2:]
    grad_joined, time_five, grads_five = block_backward(grad_up_one, kept_upper, members_all[4], axis)
    grad_middle = grad_joined[:, :, :C3]
    grad_down_three = grad_joined[:, :, C3:]
    grad_inputs, time_four, grads_four = block_backward(grad_middle, kept_middle, members_all[3], axis)
    grad_inputs, time_three, grads_three = block_backward(
        grad_down_three + grad_inputs, kept_three, members_all[2], axis
    )
    grad_inputs, time_two, grads_two = block_backward(
        grad_down_two + grad_inputs, kept_two, members_all[1], axis
    )
    grad_inputs, time_one, grads_one = block_backward(grad_inputs, kept_one, members_all[0], axis)
    kernel_grad, affine_grad = pack_flat(
        [grads_one, grads_two, grads_three, grads_four, grads_five, grads_six, head_grads]
    )
    time_kernel, time_affine = time_pullback(
        (time_one, time_two, time_three, time_four, time_five, time_six)
    )
    kernel_grad = kernel_grad + time_kernel
    affine_grad = affine_grad + time_affine
    share_len = kernels.shape[0] // lax.axis_size(DP)
    owner_start = lax.axis_index(DP) * share_len
    kernel_sum, affine_sum, noise_loss = lax.psum(
        (kernel_grad, affine_grad, loss_part), (DP, HOR)
    )
    kernel_own = lax.dynamic_slice_in_dim(kernel_sum, owner_start, share_len)
    squares = jnp.sum(kernel_sum * kernel_sum) + jnp.sum(affine_sum * affine_sum)
    grad_norm = jnp.sqrt(squares)
    factor = jnp.minimum(1.0, MAX_NORM / (grad_norm + 1e-06))
    kernel_step = kernel_own * factor
    kernel_old = lax.dynamic_slice_in_dim(kernels, owner_start, share_len)
    kernel_mom_new = MOMENTUM * kernel_momentum + kernel_step
    kernel_new = kernel_old - LEARN_RATE * (kernel_step + MOMENTUM * kernel_mom_new)
    kernel_ema_new = EMA_DECAY * kernel_average + (1.0 - EMA_DECAY) * kernel_new
    affine_step = affine_sum * factor
    affine_mom_new = MOMENTUM * affine_momentum + affine_step
    affine_new = affine - AFFINE_RATE * (affine_step + MOMENTUM * affine_mom_new)
    affine_ema_new = EMA_DECAY * affine_average + (1.0 - EMA_DECAY) * affine_new
    return (
        noise_loss,
        grad_norm,
        kernel_new,
        kernel_mom_new,
        kernel_ema_new,
        kernel_new.astype(jnp.bfloat16),
        affine_new,
        affine_mom_new,
        affine_ema_new,
        affine_new.astype(jnp.bfloat16),
    )


def swap(value, axis, bit):
    return lax.ppermute(value, axis, [(i, i ^ bit) for i in range(lax.axis_size(axis))])


def total_all(value, axes, count):
    return jnp.sum(lax.all_to_all(jnp.broadcast_to(value, (count, value.shape[0])), axes, 0, 0, tiled=True))


def pick(stack, index):
    return lax.dynamic_index_in_dim(stack, index, 0, keepdims=False)


def in_low(value):
    return lax.reduce_precision(value, 8, 7)


def two_parts(value):
    high = in_low(value)
    return high, in_low(value - high)


def share_sums(send, keep, small):
    low, wide = jnp.bfloat16, jnp.float32
    place = lax.axis_index(DP)
    seat_x = (place >> 1) & 1
    seat_y = (place >> 2) & 1
    layer = lax.axis_index(HOR)
    part_rows = OWN_ROWS // 4
    half = OWN_ROWS // 2

    def with_small(value, parts):
        return jnp.concatenate([value.reshape(-1, 128), parts[0], parts[1]], axis=0).astype(low)

    def small_of(got):
        tail = got[-128:].astype(wide)
        return tail[:64] + tail[64:]

    got = swap(send, DP, 1)
    grid = (keep + got[:-128].reshape(keep.shape).astype(wide)).reshape(2, 2, OWN_ROWS, 128)
    parts = two_parts(small + small_of(got))
    first, second = grid[:, :, :half], grid[:, :, half:]
    first_in = swap(
        with_small(lax.dynamic_index_in_dim(first, 1 - seat_x, 1, keepdims=False), parts), DP, 2
    )
    second_in = swap(pick(second, 1 - seat_y).astype(low), DP, 4)
    parts = two_parts(parts[0] + parts[1] + small_of(first_in))
    first = lax.dynamic_index_in_dim(first, seat_x, 1, keepdims=False)
    first = first + first_in[:-128].reshape(first.shape).astype(wide)
    second = pick(second, seat_y) + second_in.astype(wide)
    first_in = swap(with_small(pick(first, 1 - seat_y), parts), DP, 4)
    second_in = swap(pick(second, 1 - seat_x).astype(low), DP, 2)
    parts = two_parts(parts[0] + parts[1] + small_of(first_in))
    own = jnp.concatenate(
        [
            pick(first, seat_y) + first_in[:-128].astype(wide),
            pick(second, seat_x) + second_in.astype(wide),
        ],
        axis=0,
    ).reshape(4, part_rows, 128)
    arrived = [swap(with_small(pick(own, layer ^ bits), parts), HOR, bits) for bits in (1, 2, 3)]
    part = pick(own, layer)
    for value in arrived:
        part = part + value[:-128].astype(wide)
    smalls = jnp.stack([parts[0] + parts[1]] + [small_of(value) for value in arrived])
    small = sum(pick(smalls, layer ^ n) for n in range(4))
    return part, small


def all_parts(part):
    layer = lax.axis_index(HOR)
    part_low = in_low(part).astype(jnp.bfloat16)
    parts = jnp.stack([part_low] + [swap(part_low, HOR, bits) for bits in (1, 2, 3)])
    return jnp.concatenate([pick(parts, layer ^ n) for n in range(4)], axis=0)


def on_device(
    trajectories,
    dim_means,
    dim_stds,
    noise_draw,
    diffusion_steps,
    valid_mask,
    kernels,
    affine,
    kernel_momentum,
    kernel_average,
    affine_momentum,
    affine_average,
):
    ring = lax.axis_size(HOR)
    frames = trajectories.shape[1] * ring
    if trajectories.shape[0] != ring or ring != 4 or frames % 512 or lax.axis_size(DP) != 8:
        return on_device_xla(
            trajectories,
            dim_means,
            dim_stds,
            noise_draw,
            diffusion_steps,
            valid_mask,
            kernels,
            affine,
            kernel_momentum,
            kernel_average,
            affine_momentum,
            affine_average,
        )
    total = total_all(jnp.sum(valid_mask.astype(jnp.float32), axis=0), DP, lax.axis_size(DP))
    low_out, noise_out, counts = exchange_pieces(
        trajectories, noise_draw, valid_mask, signal_level(diffusion_steps), dim_means, dim_stds
    )
    low_out, total = lax.optimization_barrier((low_out, total))
    noisy = lax.all_to_all(low_out, HOR, 0, 0, tiled=True)
    row = lax.broadcasted_iota(jnp.int32, (4, 8, 128), 1)
    extra = jnp.where(row == 0, counts[:4, None, :], jnp.where(row == 1, total, 0.0))
    noise_out = lax.dynamic_update_slice(noise_out, extra, (0, noise_out.shape[1] - 8, 0))
    noise_out, packed = lax.optimization_barrier((noise_out, kernels))
    noise = lax.all_to_all(noise_out, HOR, 0, 0, tiled=True)
    own_step = lax.dynamic_slice_in_dim(diffusion_steps, lax.axis_index(HOR), 1)
    sinus = jnp.broadcast_to(sinusoid(own_step), (8, TE))
    place = lax.axis_index(DP)
    send, keep, small = whole_horizon(noisy, noise, sinus, place & 1, packed, affine)
    part, small = share_sums(send, keep, small)
    share_len = kernels.shape[0] // lax.axis_size(DP)
    owner_start = place * share_len
    lead = owner_start - place * NKER_ROWS * 128
    number = (
        lax.axis_index(HOR) * part.size
        + lax.broadcasted_iota(jnp.int32, part.shape, 0) * 128
        + lax.broadcasted_iota(jnp.int32, part.shape, 1)
    )
    inside = (number >= lead) & (number < lead + share_len)
    count = lax.axis_size(DP) * lax.axis_size(HOR)
    squares = total_all(jnp.sum(jnp.where(inside, part * part, 0.0), axis=0), (DP, HOR), count)
    whole = all_parts(part)
    small_flat = small.reshape(-1)
    affine_sum = jnp.concatenate([small_flat[:7127], small_flat[7168:7552]])
    noise_loss = jnp.sum(small[60])
    grad_norm = jnp.sqrt(squares + jnp.sum(affine_sum * affine_sum))
    kernel_own = lax.dynamic_slice_in_dim(whole.astype(jnp.float32).reshape(-1), lead, share_len)
    factor = jnp.minimum(1.0, MAX_NORM / (grad_norm + 1e-06))
    kernel_step = kernel_own * factor
    kernel_old = lax.dynamic_slice_in_dim(kernels, owner_start, share_len)
    kernel_mom_new = MOMENTUM * kernel_momentum + kernel_step
    kernel_new = kernel_old - LEARN_RATE * (kernel_step + MOMENTUM * kernel_mom_new)
    kernel_ema_new = EMA_DECAY * kernel_average + (1.0 - EMA_DECAY) * kernel_new
    affine_step = affine_sum * factor
    affine_mom_new = MOMENTUM * affine_momentum + affine_step
    affine_new = affine - AFFINE_RATE * (affine_step + MOMENTUM * affine_mom_new)
    affine_ema_new = EMA_DECAY * affine_average + (1.0 - EMA_DECAY) * affine_new
    return (
        noise_loss,
        grad_norm,
        kernel_new,
        kernel_mom_new,
        kernel_ema_new,
        kernel_new.astype(jnp.bfloat16),
        affine_new,
        affine_mom_new,
        affine_ema_new,
        affine_new.astype(jnp.bfloat16),
    )


def solution(mesh):
    in_specs = (
        P(DP, HOR, None),
        P(),
        P(),
        P(DP, HOR, None),
        P(DP),
        P(DP, HOR),
        P(),
        P(),
        P(DP),
        P(DP),
        P(),
        P(),
    )
    out_specs = (P(), P(), P(DP), P(DP), P(DP), P(DP), P(), P(), P(), P())
    return jax.shard_map(
        on_device, mesh=mesh, in_specs=in_specs, out_specs=out_specs, check_vma=False
    )
```
